128 devices in a mesh: seq: 2 (over x_lo), fsdp: 64 (over y, z, x_hi, core).
Axes of the slice: x: 4 (x_hi: 2, x_lo: 2; x = x_hi * 2 + x_lo), y: 4, z: 4, core: 2. Of those that a mesh axis runs over, the one named last changes fastest.
Arguments:
- inputs: bfloat16 [64, 256, 1024], P('fsdp', 'seq'), may hold values from -8 to 8
- project_in: bfloat16 [1024, 2048], P('fsdp'), may hold values from -0.25 to 0.25
- project_out: bfloat16 [1024, 1024], P('fsdp'), may hold values from -0.75 to 0.75
- gain_attend: bfloat16 [1024], P('fsdp'), may hold values from 0.25 to 1.75
- gain_expert: bfloat16 [1024], P('fsdp'), may hold values from 0.25 to 1.75
- expert_gate: bfloat16 [16384, 1024], P('fsdp'), may hold values from -0.1875 to 0.1875
- expert_up: bfloat16 [16384, 1024], P('fsdp'), may hold values from -0.1875 to 0.1875
- expert_down: bfloat16 [16384, 1024], P('fsdp'), may hold values from -0.25 to 0.25
- routes: int32 [64, 256, 8], P('fsdp', 'seq'), may hold values from 0 to 31, all different within a row; in each aligned block of 128 rows (0 to 127, 128 to 255, ..., all dimensions but the last counted through in order) at most 36 rows name the same one
- route_weights: float32 [64, 256, 8], P('fsdp', 'seq'), may hold values from 0.03 to 0.4
- segments: int32 [64, 256], P('fsdp'), may hold values from 0 to 3, never falling along the last dimension, each value on 1 to 128 neighbouring positions
- cotangent: bfloat16 [64, 256, 1024], P('fsdp', 'seq'), may hold values from -6 to 6
Outputs:
- output: bfloat16 [64, 256, 1024], P('fsdp', 'seq')
- grad_inputs: bfloat16 [64, 256, 1024], P('fsdp', 'seq')
- grad_project_in: float32 [1024, 2048], P('fsdp')
- grad_project_out: float32 [1024, 1024], P('fsdp')
- grad_gain_attend: float32 [1024], P('fsdp')
- grad_gain_expert: float32 [1024], P('fsdp')
- grad_expert_gate: float32 [16384, 1024], P('fsdp')
- grad_expert_up: float32 [16384, 1024], P('fsdp')
- grad_expert_down: float32 [16384, 1024], P('fsdp')
The draws below stay inside these ranges and needn't reach their ends.
Inputs may be any that keep to these rules, and one draw needn't show every extreme that they name: `routes`: each token names 8 different experts. In each aligned block of 128 tokens (the tokens of one device) no expert is named by more than 36 tokens, a bound that some block reaches. `segments`: never falling along a sequence; each document spans 1 to 128 positions, one exactly 128.
All inputs are finite; a program needn't handle non-finite values.
Results may differ from the reference program's by a relative error of at most 0.014.
The reference program's roundings to bfloat16 on the way count: a program that leaves them out, or rounds other values in their place, can miss the bound.
Values may be sent and summed in bfloat16 or wider, within the bound.
A program may use at most 128 MiB of HBM per device.

```python
import math
import jax
import jax.numpy as jnp
import numpy as np
from jax import lax

MODEL_DIMENSION = 1024
HEADS = 16
KV_HEADS = 8
HEAD_DIM = 64
EXPERTS = 32
FF = 512
TOP = 8
TOK_DEV = 128
SEG_COUNT = 4
LEN = 256
SEQS = 64
CAP = 36
EXPERT_UNITS = 16384
HBLOCK = 256
SEG_MOST = 128
QKV_WIDTH = 2048
ATT_WIDTH = 1024
N_SEQ = 2


def draw_inputs(key, part):
    gaussian = jax.random.normal(jax.random.fold_in(key, 1), (SEQS, LEN, MODEL_DIMENSION), jnp.float32)
    return jnp.clip(gaussian, -6.0, 6.0).astype(jnp.bfloat16)


def draw_project_in(key, part):
    width_all = (HEADS + 2 * KV_HEADS) * HEAD_DIM
    gaussian = jax.random.normal(jax.random.fold_in(key, 5), (MODEL_DIMENSION, width_all), jnp.float32) / math.sqrt(MODEL_DIMENSION)
    gaussian = jnp.clip(gaussian, -0.2, 0.2)
    return gaussian.astype(jnp.bfloat16)


def block_scale(key, extent, cuts, low, largest):
    def one(dim, parts):
        draws = jax.random.uniform(jax.random.fold_in(jax.random.fold_in(key, 6), dim), (parts,), jnp.float32, low / len(cuts), largest / len(cuts))
        return jnp.repeat(jnp.exp(draws), extent[dim] // parts).reshape((-1,) + (1,) * (len(extent) - dim - 1))

    gain = one(*cuts[0])
    for cut in cuts[1:]:
        gain = gain * one(*cut)
    return gain


def split_up(number_of, total, limit, lean):
    weights = [(1 << 20) // math.isqrt(standing ** lean) + 1 for standing in range(2, number_of + 1)]
    rest, given = total - limit - (number_of - 1), [1] * (number_of - 1)
    while rest > 0:
        movable = [i for i in range(number_of - 1) if given[i] < limit]
        pool, remaining = sum([weights[i] for i in movable]), rest
        for i in movable:
            addition = min(limit - given[i], max(1, remaining * weights[i] // pool), rest)
            given[i] = given[i] + addition
            rest = rest - addition
    return np.array([limit] + given)


def uneven_parts(key, number_of, total, bound, skew):
    if number_of == 2:
        one = jax.random.randint(key, (), max(1, total - bound), min(bound, total - 1) + 1)
        return jnp.stack([one, total - one])
    lengths = jnp.asarray(split_up(number_of, total, bound, skew), jnp.int32)
    couples = (number_of - 1) // 2
    donor, sink = lengths[1:1 + 2 * couples:2], lengths[2:2 + 2 * couples:2]
    slack = jnp.minimum(donor - 1, bound - sink)
    moved = jax.random.randint(jax.random.fold_in(key, 1), (couples,), 0, 1 << 20) % (slack + 1)
    lengths = lengths.at[1:1 + 2 * couples:2].set(donor - moved).at[2:2 + 2 * couples:2].set(sink + moved)
    return lengths[jax.random.permutation(jax.random.fold_in(key, 2), number_of)]


def routed_block(own_key, own, number, rows, amount, top, reach, lean):
    order = jax.random.permutation(own_key, amount)
    crowded, common = portions_of(amount, rows * top, reach, lean, True), portions_of(amount, rows * top, reach, lean, False)
    places = jnp.arange(amount)

    def named(lengths, offset_by):
        used = int((lengths > 0).sum())
        fixed = max(1, used // 4)
        moved = fixed + (places - fixed + offset_by * (used - fixed)) % max(1, amount - fixed)
        return jnp.zeros((amount,), jnp.int32).at[order[jnp.where(places < fixed, places, moved)]].set(jnp.asarray(lengths, jnp.int32))

    lengths = jnp.where(number % 4 == 0, named(crowded, number // 4), named(common, number - number // 4 - 1))
    mixed = jax.random.permutation(jax.random.fold_in(own, 3), amount)
    donor, sink = mixed[0:amount // 2 * 2:2], mixed[1:amount // 2 * 2:2]
    room = jnp.minimum(lengths[donor] - 1, reach - lengths[sink]) // 2
    room = jnp.where((donor == order[0]) | (sink == order[0]) | (lengths[sink] == 0), 0, jnp.maximum(room, 0))
    moved = jax.random.randint(jax.random.fold_in(own, 4), (amount // 2,), 0, 1 << 20) % (room + 1)
    lengths = lengths.at[donor].add(-moved).at[sink].add(moved)
    members = jnp.searchsorted(jnp.cumsum(lengths), jnp.arange(rows * top), side="right").astype(jnp.int32)
    grid = members.reshape(top, rows).T
    grid = grid[jax.random.permutation(jax.random.fold_in(own, 1), rows)]
    offset_by = jax.random.randint(jax.random.fold_in(own, 2), (rows, 1), 0, top)
    return jnp.take_along_axis(grid, (jnp.arange(top)[None, :] + offset_by) % top, axis=1)


def portions_of(number_of, total, bound, slope, full):
    loads = [(1 << 20) // math.isqrt(standing ** slope) + 1 for standing in range(1, number_of + 1)]
    largest = bound if full else min(bound, max(-(-total // number_of), total * loads[0] // sum(loads)))
    least = 1 if total - largest >= number_of - 1 else 0
    holding, spare = [largest] + [least] * (number_of - 1), total - largest - least * (number_of - 1)
    while spare > 0:
        candidates = [i for i in range(1, number_of) if holding[i] < largest] or [i for i in range(1, number_of) if holding[i] < bound]
        whole, budget = sum([loads[i] for i in candidates]), spare
        for i in candidates:
            extra = min(bound - holding[i], max(1, budget * loads[i] // whole), spare)
            holding[i] = holding[i] + extra
            spare = spare - extra
    return np.array(holding)


def noise(stream_key, shape, spread, limit, cuts=(), dtype=jnp.bfloat16):
    values = spread * jax.random.normal(stream_key, shape, jnp.float32)
    if cuts:
        values = values * block_scale(stream_key, shape, cuts, -0.22, 0.18)
    return jnp.clip(values, -limit, limit).astype(dtype)


def setup_inputs(seed: int = 0) -> dict:
    seeds = jax.random.split(jax.random.key(seed), 13)
    inputs = draw_inputs(jax.random.fold_in(seeds[12], 71), 0)
    project_in = draw_project_in(jax.random.fold_in(seeds[12], 71), 0)
    project_out = noise(seeds[2], (ATT_WIDTH, MODEL_DIMENSION), (ATT_WIDTH // 16) ** -0.5, 0.75, ((0, 64),))
    gain_attend = jnp.clip(1.0 + 0.15 * jax.random.normal(seeds[3], (MODEL_DIMENSION,), jnp.float32), 0.25, 1.75).astype(jnp.bfloat16)
    gain_expert = jnp.clip(1.0 + 0.15 * jax.random.normal(seeds[4], (MODEL_DIMENSION,), jnp.float32), 0.25, 1.75).astype(jnp.bfloat16)
    expert_gate = noise(seeds[5], (EXPERT_UNITS, MODEL_DIMENSION), MODEL_DIMENSION ** -0.5, 0.1875, ((0, 64),))
    expert_up = noise(seeds[6], (EXPERT_UNITS, MODEL_DIMENSION), MODEL_DIMENSION ** -0.5, 0.1875, ((0, 64),))
    expert_down = noise(seeds[7], (EXPERT_UNITS, MODEL_DIMENSION), FF ** -0.5, 0.25, ((0, 64),))
    routes_keys = jax.random.split(jax.random.fold_in(seeds[8], 1), SEQS * LEN // TOK_DEV)
    routes_turns = jax.random.permutation(jax.random.fold_in(seeds[8], 3), SEQS * LEN // TOK_DEV)
    routes = jax.vmap(lambda own, number: routed_block(jax.random.fold_in(seeds[8], 2), own, number, TOK_DEV, EXPERTS, TOP, CAP, 1))(routes_keys, routes_turns).reshape((SEQS, LEN, TOP))
    route_weights = jnp.clip(jnp.exp(math.log(0.4) - 2.5902672 * jax.random.uniform(seeds[9], (SEQS, LEN, TOP), jnp.float32) ** block_scale(seeds[9], (SEQS, LEN, TOP), ((0, 64), (1, 2)), -0.2, 0.2)), 0.03, 0.4)
    segments = jax.vmap(lambda own: jnp.searchsorted(jnp.cumsum(uneven_parts(own, SEG_COUNT, LEN, SEG_MOST, 1)), jnp.arange(LEN), side="right"))(jax.random.split(seeds[10], SEQS)).reshape((SEQS, LEN)).astype(jnp.int32)
    cotangent = noise(seeds[11], (SEQS, LEN, MODEL_DIMENSION), 1.0, 6.0, ((0, 64), (1, 2)))
    return dict(inputs=inputs, project_in=project_in, project_out=project_out, gain_attend=gain_attend, gain_expert=gain_expert, expert_gate=expert_gate, expert_up=expert_up, expert_down=expert_down, routes=routes, route_weights=route_weights, segments=segments, cotangent=cotangent)


EPSILON = 1e-06
ROPE_BASE = 10000.0
block_limit = 512

def to_wide(narrow):
    return lax.optimization_barrier(narrow).astype(jnp.float32)

def rope_tables(positions):
    half_dim = HEAD_DIM // 2
    powers = jnp.arange(half_dim).astype(jnp.float32) * (2.0 / HEAD_DIM)
    inverse_freq = ROPE_BASE ** (-powers)
    angles = positions.astype(jnp.float32)[:, None] * inverse_freq[None, :]
    return (jnp.cos(angles), jnp.sin(angles))

def rotate(values, cosine_table, sine_table, turn_sign):
    half_dim = values.shape[-1] // 2
    leading = values[..., :half_dim]
    trailing = values[..., half_dim:]
    cosine_b = cosine_table[:, None, :]
    sine_b = sine_table[:, None, :] * turn_sign
    return jnp.concatenate([leading * cosine_b - trailing * sine_b, trailing * cosine_b + leading * sine_b], axis=-1)

def norm_forward(values, gain_vector):
    inverse = lax.rsqrt(lax.optimization_barrier(jnp.mean(values * values, axis=-1, keepdims=True)) + EPSILON)
    return ((values * inverse * gain_vector.astype(jnp.float32)).astype(jnp.bfloat16), inverse)

def norm_backward(values, inverse, gain_vector, upstream):
    scaled = upstream * gain_vector.astype(jnp.float32)
    grad_gain = lax.optimization_barrier(jnp.sum(upstream * values * inverse, axis=0))
    coupling = lax.optimization_barrier(jnp.mean(scaled * values, axis=-1, keepdims=True))
    return (inverse * scaled - values * inverse * inverse * inverse * coupling, grad_gain)

def block_scores(query_block, key_all, segments, start_row):
    block_len = query_block.shape[0]
    length = key_all.shape[0]
    scores = jnp.einsum('qkgd,skd->kgqs', query_block, key_all) * HEAD_DIM ** (-0.5)
    query_pos = start_row + jnp.arange(block_len)
    query_seg = lax.dynamic_slice_in_dim(segments, start_row, block_len)
    allowed = (jnp.arange(length)[None, :] <= query_pos[:, None]) & (segments[None, :] == query_seg[:, None])
    return jnp.where(allowed[None, None], scores, -1e+30)

def split_heads(query, keys, values):
    length = query.shape[0]
    block_len = min(block_limit, length)
    kv_count = keys.shape[1] // HEAD_DIM
    group_size = query.shape[1] // keys.shape[1]
    query_blocks = to_wide(query).reshape(length // block_len, block_len, kv_count, group_size, HEAD_DIM)
    key_all = to_wide(keys).reshape(length, kv_count, HEAD_DIM)
    value_all = to_wide(values).reshape(length, kv_count, HEAD_DIM)
    starts = (jnp.arange(length // block_len) * block_len).astype(jnp.int32)
    return (query_blocks, key_all, value_all, starts, block_len)

def attend_forward(query, keys, values, segments):
    length = query.shape[0]
    query_blocks, key_all, value_all, starts, block_len = split_heads(query, keys, values)

    def one_block(packed):
        query_block, start_row = packed
        scores = block_scores(query_block, key_all, segments, start_row)
        highest = lax.optimization_barrier(jnp.max(scores, axis=-1, keepdims=True))
        log_total = highest + jnp.log(lax.optimization_barrier(jnp.sum(jnp.exp(scores - highest), axis=-1, keepdims=True)))
        weights = jnp.exp(scores - log_total).astype(jnp.bfloat16)
        mixed = jnp.einsum('kgqs,skd->qkgd', to_wide(weights), value_all)
        return (mixed.astype(jnp.bfloat16).reshape(block_len, -1), log_total[..., 0])
    attended, log_totals = lax.map(one_block, (query_blocks, starts))
    return (attended.reshape(length, -1), log_totals)

def attend_backward(query, keys, values, segments, attended, log_totals, grad_attended):
    length = query.shape[0]
    query_blocks, key_all, value_all, starts, block_len = split_heads(query, keys, values)
    out_blocks = to_wide(attended).reshape(query_blocks.shape)
    grad_blocks = to_wide(grad_attended).reshape(query_blocks.shape)
    scale_factor = HEAD_DIM ** (-0.5)

    def one_block(sums_so_far, packed):
        grad_key_sum, grad_value_sum = sums_so_far
        query_block, out_block, grad_block, log_block, start_row = packed
        scores = block_scores(query_block, key_all, segments, start_row)
        weights = jnp.exp(scores - log_block[..., None])
        weights_low = to_wide(weights.astype(jnp.bfloat16))
        grad_value_sum = grad_value_sum + jnp.einsum('kgqs,qkgd->skd', weights_low, grad_block)
        grad_weights = jnp.einsum('qkgd,skd->kgqs', grad_block, value_all)
        row_delta = jnp.transpose(lax.optimization_barrier(jnp.sum(grad_block * out_block, axis=-1)), (1, 2, 0))
        grad_scores = to_wide((weights * (grad_weights - row_delta[..., None])).astype(jnp.bfloat16))
        grad_query = jnp.einsum('kgqs,skd->qkgd', grad_scores, key_all) * scale_factor
        grad_key_sum = grad_key_sum + jnp.einsum('kgqs,qkgd->skd', grad_scores, query_block) * scale_factor
        return ((grad_key_sum, grad_value_sum), grad_query.reshape(block_len, -1))
    zeros_kv = jnp.zeros(key_all.shape, jnp.float32)
    sums_end, grad_query = lax.scan(one_block, (zeros_kv, zeros_kv), (query_blocks, out_blocks, grad_blocks, log_totals, starts))
    return (grad_query.reshape(length, -1), sums_end[0].reshape(length, -1), sums_end[1].reshape(length, -1))

def expert_slots(route_ids):
    length = route_ids.shape[0]
    picked = (route_ids[:, :, None] == jnp.arange(EXPERTS)[None, None, :]).astype(jnp.int32)
    per_token = lax.optimization_barrier(jnp.sum(picked, axis=1)).reshape(N_SEQ, TOK_DEV, EXPERTS)
    before = (jnp.cumsum(per_token, axis=1) - per_token).reshape(length, EXPERTS)
    slot_rank = lax.optimization_barrier(jnp.sum(before[:, None, :] * picked, axis=2))
    block_index = (jnp.arange(length) // TOK_DEV)[:, None]
    return (route_ids * (N_SEQ * CAP) + block_index * CAP + slot_rank).astype(jnp.int32)

def reference(inputs, project_in, project_out, gain_attend, gain_expert, expert_gate, expert_up, expert_down, routes, route_weights, segments, cotangent):
    query_width = HEADS * HEAD_DIM
    kv_width = KV_HEADS * HEAD_DIM
    slot_count = N_SEQ * CAP
    blocks_per = FF // HBLOCK
    cosine_table, sine_table = rope_tables(jnp.arange(LEN))
    gate_wide = expert_gate.astype(jnp.float32).reshape(EXPERTS, FF, MODEL_DIMENSION)
    up_wide = expert_up.astype(jnp.float32).reshape(EXPERTS, FF, MODEL_DIMENSION)
    down_wide = expert_down.astype(jnp.float32).reshape(EXPERTS, FF, MODEL_DIMENSION)

    def one_sequence(sum_values, packed):
        input_low, route_ids, mix_weights, seg_ids, grad_low = packed
        row_values = input_low.astype(jnp.float32)
        normed_one, inverse_one = norm_forward(row_values, gain_attend)
        projected = jnp.dot(normed_one, project_in, preferred_element_type=jnp.float32)
        query = rotate(projected[:, :query_width].reshape(LEN, HEADS, HEAD_DIM), cosine_table, sine_table, 1.0).reshape(LEN, query_width).astype(jnp.bfloat16)
        keys = rotate(projected[:, query_width:query_width + kv_width].reshape(LEN, KV_HEADS, HEAD_DIM), cosine_table, sine_table, 1.0).reshape(LEN, kv_width).astype(jnp.bfloat16)
        values = projected[:, query_width + kv_width:].astype(jnp.bfloat16)
        attended, log_totals = attend_forward(query, keys, values, seg_ids)
        residual = row_values + jnp.dot(attended, project_out, preferred_element_type=jnp.float32)
        normed_two, inverse_two = norm_forward(residual, gain_expert)
        slot_index = expert_slots(route_ids).reshape(-1)
        copies = jnp.repeat(normed_two, TOP, axis=0)
        packed_rows = jnp.zeros((EXPERTS * slot_count, MODEL_DIMENSION), jnp.bfloat16).at[slot_index].set(copies)
        packed_wide = to_wide(packed_rows).reshape(EXPERTS, slot_count, MODEL_DIMENSION)
        gate_pre = jnp.einsum('ecd,efd->ecf', packed_wide, gate_wide)
        up_pre = jnp.einsum('ecd,efd->ecf', packed_wide, up_wide)
        hidden = (jax.nn.silu(gate_pre) * up_pre).astype(jnp.bfloat16)
        pieces = jnp.einsum('ecrh,erhd->ecrd', to_wide(hidden).reshape(EXPERTS, slot_count, blocks_per, HBLOCK), down_wide.reshape(EXPERTS, blocks_per, HBLOCK, MODEL_DIMENSION)).astype(jnp.bfloat16)
        expert_out = lax.optimization_barrier(jnp.sum(to_wide(pieces), axis=2)).reshape(EXPERTS * slot_count, MODEL_DIMENSION)
        chosen = expert_out[slot_index].reshape(LEN, TOP, MODEL_DIMENSION)
        output = (residual + lax.optimization_barrier(jnp.sum(chosen * mix_weights[:, :, None], axis=1))).astype(jnp.bfloat16)
        grad_out = grad_low.astype(jnp.float32)
        grad_mix = (grad_out[:, None, :] * mix_weights[:, :, None]).astype(jnp.bfloat16).reshape(LEN * TOP, MODEL_DIMENSION)
        grad_packed = to_wide(jnp.zeros((EXPERTS * slot_count, MODEL_DIMENSION), jnp.bfloat16).at[slot_index].set(grad_mix)).reshape(EXPERTS, slot_count, MODEL_DIMENSION)
        grad_hidden = jnp.einsum('ecd,efd->ecf', grad_packed, down_wide)
        sigmoid_gate = jax.nn.sigmoid(gate_pre)
        grad_gate_pre = to_wide((grad_hidden * up_pre * sigmoid_gate * (1.0 + gate_pre * (1.0 - sigmoid_gate))).astype(jnp.bfloat16))
        grad_up_pre = to_wide((grad_hidden * gate_pre * sigmoid_gate).astype(jnp.bfloat16))
        down_gradient_sequence = jnp.einsum('ecf,ecd->efd', to_wide(hidden), grad_packed)
        gate_gradient_sequence = jnp.einsum('ecf,ecd->efd', grad_gate_pre, packed_wide)
        up_gradient_sequence = jnp.einsum('ecf,ecd->efd', grad_up_pre, packed_wide)
        back_pieces = jnp.einsum('ecrh,erhd->ecrd', grad_gate_pre.reshape(EXPERTS, slot_count, blocks_per, HBLOCK), gate_wide.reshape(EXPERTS, blocks_per, HBLOCK, MODEL_DIMENSION))
        back_pieces = back_pieces + jnp.einsum('ecrh,erhd->ecrd', grad_up_pre.reshape(EXPERTS, slot_count, blocks_per, HBLOCK), up_wide.reshape(EXPERTS, blocks_per, HBLOCK, MODEL_DIMENSION))
        grad_slots = lax.optimization_barrier(jnp.sum(to_wide(back_pieces.astype(jnp.bfloat16)), axis=2)).reshape(EXPERTS * slot_count, MODEL_DIMENSION)
        grad_normed_two = lax.optimization_barrier(jnp.sum(grad_slots[slot_index].reshape(LEN, TOP, MODEL_DIMENSION), axis=1))
        grad_norm_two, second_gain_gradient = norm_backward(residual, inverse_two, gain_expert, grad_normed_two)
        grad_residual = grad_out + grad_norm_two
        grad_res_low = grad_residual.astype(jnp.bfloat16)
        output_gradient_sequence = jnp.dot(attended.T, grad_res_low, preferred_element_type=jnp.float32)
        grad_attended = jnp.dot(grad_res_low, project_out.T, preferred_element_type=jnp.float32).astype(jnp.bfloat16)
        grad_query, grad_keys, grad_values = attend_backward(query, keys, values, seg_ids, attended, log_totals, grad_attended)
        grad_query = rotate(grad_query.reshape(LEN, HEADS, HEAD_DIM), cosine_table, sine_table, -1.0).reshape(LEN, query_width)
        grad_keys = rotate(grad_keys.reshape(LEN, KV_HEADS, HEAD_DIM), cosine_table, sine_table, -1.0).reshape(LEN, kv_width)
        grad_projected = jnp.concatenate([grad_query, grad_keys, grad_values], axis=1).astype(jnp.bfloat16)
        input_gradient_sequence = jnp.dot(normed_one.T, grad_projected, preferred_element_type=jnp.float32)
        grad_normed_one = jnp.dot(grad_projected, project_in.T, preferred_element_type=jnp.float32)
        grad_norm_one, first_gain_gradient = norm_backward(row_values, inverse_one, gain_attend, grad_normed_one)
        grad_inputs = (grad_residual + grad_norm_one).astype(jnp.bfloat16)
        summand_terms = (input_gradient_sequence, output_gradient_sequence, first_gain_gradient, second_gain_gradient, gate_gradient_sequence.reshape(EXPERT_UNITS, MODEL_DIMENSION), up_gradient_sequence.reshape(EXPERT_UNITS, MODEL_DIMENSION), down_gradient_sequence.reshape(EXPERT_UNITS, MODEL_DIMENSION))
        updated_sum_values = tuple((running_sum_value + summand_term for running_sum_value, summand_term in zip(sum_values, summand_terms)))
        return (updated_sum_values, (output, grad_inputs))
    start_totals = (jnp.zeros((MODEL_DIMENSION, QKV_WIDTH), jnp.float32), jnp.zeros((ATT_WIDTH, MODEL_DIMENSION), jnp.float32), jnp.zeros((MODEL_DIMENSION,), jnp.float32), jnp.zeros((MODEL_DIMENSION,), jnp.float32), jnp.zeros((EXPERT_UNITS, MODEL_DIMENSION), jnp.float32), jnp.zeros((EXPERT_UNITS, MODEL_DIMENSION), jnp.float32), jnp.zeros((EXPERT_UNITS, MODEL_DIMENSION), jnp.float32))
    sum_values, (output, grad_inputs) = lax.scan(one_sequence, start_totals, (inputs, routes, route_weights, segments, cotangent))
    return (output, grad_inputs, sum_values[0], sum_values[1], sum_values[2], sum_values[3], sum_values[4], sum_values[5], sum_values[6])
```

```python
import jax
import jax.numpy as jnp
from jax import lax
from jax.experimental import pallas as pl
from jax.experimental.pallas import tpu as pltpu
from jax.sharding import Mesh, PartitionSpec as P

HEADS = 16
KV_HEADS = 8
HEAD_DIM = 64
EXPERTS = 32
FF = 512
TOP = 8
CAP = 36
SLOTS = 40
BLOCK = 256
ROW_BLOCK = 256

EPSILON = 1e-06
ROPE_BASE = 10000.0

f32 = jnp.float32
bf16 = jnp.bfloat16

RING = 4
MESH_ID = pl.DeviceIdType.MESH
SWAP = [(0, 1), (1, 0)]
NT = (((1,), (1,)), ((), ()))
TN = (((0,), (0,)), ((), ()))


def dot(a, b, dims=(((1,), (0,)), ((), ()))):
    return lax.dot_general(a, b, dims, preferred_element_type=f32)


def rope_tables(positions):
    half_dim = HEAD_DIM // 2
    powers = jnp.arange(half_dim).astype(f32) * (2.0 / HEAD_DIM)
    inverse_freq = ROPE_BASE ** (-powers)
    angles = positions.astype(f32)[:, None] * inverse_freq[None, :]
    return (jnp.cos(angles), jnp.sin(angles))


def rotate(values, cosine_table, sine_table, turn_sign):
    half_dim = values.shape[-1] // 2
    leading = values[..., :half_dim]
    trailing = values[..., half_dim:]
    cosine_b = cosine_table[:, None, :]
    sine_b = sine_table[:, None, :] * turn_sign
    return jnp.concatenate(
        [leading * cosine_b - trailing * sine_b, trailing * cosine_b + leading * sine_b], axis=-1
    )


def rotate_wide(values, cosine_table, sine_table, turn_sign):
    rows, width = values.shape
    heads = values.reshape(rows, width // HEAD_DIM, HEAD_DIM)
    return rotate(heads, cosine_table, sine_table, turn_sign).reshape(rows, width)


def norm_forward(values, gain_vector):
    inverse = lax.rsqrt(jnp.mean(values * values, axis=-1, keepdims=True) + EPSILON)
    return ((values * inverse * gain_vector.astype(f32)).astype(bf16), inverse)


def norm_backward(values, inverse, gain_vector, upstream):
    scaled = upstream * gain_vector.astype(f32)
    grad_gain = jnp.sum(upstream * values * inverse, axis=0)
    coupling = jnp.mean(scaled * values, axis=-1, keepdims=True)
    return (inverse * scaled - values * inverse * inverse * inverse * coupling, grad_gain)


def rounded(values):
    return lax.reduce_precision(values, exponent_bits=8, mantissa_bits=7)


def three_parts(values):
    first = rounded(values)
    second = rounded(values - first)
    third = values - first - second
    return (first.astype(bf16), second.astype(bf16), third.astype(bf16))


def masked_scores(query, keys, allowed):
    scores = jnp.einsum("qkgd,skd->kgqs", query, keys, preferred_element_type=f32)
    return jnp.where(allowed[None, None], scores * HEAD_DIM ** (-0.5), -1e30)


def attend_forward(query, keys, values, allowed):
    scores = masked_scores(query, keys, allowed)
    highest = jnp.max(scores, axis=-1, keepdims=True)
    log_total = highest + jnp.log(jnp.sum(jnp.exp(scores - highest), axis=-1, keepdims=True))
    weights = jnp.exp(scores - log_total).astype(bf16)
    mixed = jnp.einsum("kgqs,skd->qkgd", weights, values, preferred_element_type=f32)
    return (mixed.astype(bf16), log_total)


def attend_backward(query, keys, values, allowed, attended, log_total, grad_attended):
    scale_factor = HEAD_DIM ** (-0.5)
    weights = jnp.exp(masked_scores(query, keys, allowed) - log_total)
    grad_values = jnp.einsum(
        "kgqs,qkgd->skd", weights.astype(bf16), grad_attended, preferred_element_type=f32
    )
    grad_weights = jnp.einsum("qkgd,skd->kgqs", grad_attended, values, preferred_element_type=f32)
    row_delta = jnp.sum(grad_attended.astype(f32) * attended.astype(f32), axis=-1)
    row_delta = jnp.transpose(row_delta, (1, 2, 0))
    grad_scores = (weights * (grad_weights - row_delta[..., None])).astype(bf16)
    grad_query = jnp.einsum("kgqs,skd->qkgd", grad_scores, keys, preferred_element_type=f32)
    grad_keys = jnp.einsum("kgqs,qkgd->skd", grad_scores, query, preferred_element_type=f32)
    return (grad_query * scale_factor, grad_keys * scale_factor, grad_values)


def experts_first_body(x_ref, g_ref, pre_w_ref, down_w_ref, hidden_ref, grads_ref, back_ref):
    pre = dot(x_ref[...], pre_w_ref[...], NT)
    grad_hidden = dot(g_ref[...], down_w_ref[...], NT)
    back = None
    for b in range(FF // BLOCK):
        gate = pre[:, 2 * b * BLOCK : (2 * b + 1) * BLOCK]
        up = pre[:, (2 * b + 1) * BLOCK : (2 * b + 2) * BLOCK]
        grad_h = grad_hidden[:, b * BLOCK : (b + 1) * BLOCK]
        sigmoid_gate = 1.0 / (1.0 + jnp.exp(-gate))
        silu = gate * sigmoid_gate
        hidden_ref[:, b * BLOCK : (b + 1) * BLOCK] = (silu * up).astype(bf16)
        grad_gate = (grad_h * up * sigmoid_gate * (1.0 + gate * (1.0 - sigmoid_gate))).astype(bf16)
        grad_up = (grad_h * gate * sigmoid_gate).astype(bf16)
        both = jnp.concatenate([grad_gate, grad_up], axis=1)
        grads_ref[:, 2 * b * BLOCK : (2 * b + 2) * BLOCK] = both
        part = dot(both, pre_w_ref[2 * b * BLOCK : (2 * b + 2) * BLOCK, :]).astype(bf16).astype(f32)
        back = part if back is None else back + part
    back_ref[...] = back.astype(bf16)


def experts_first(arrived, grad_arrived, pre_w, down_w):
    rows, width = arrived.shape
    whole = lambda i: (0, 0)
    by_row = lambda i: (i, 0)
    return pl.pallas_call(
        experts_first_body,
        grid=(rows // ROW_BLOCK,),
        in_specs=[
            pl.BlockSpec((ROW_BLOCK, width), by_row),
            pl.BlockSpec((ROW_BLOCK, width), by_row),
            pl.BlockSpec((2 * FF, width), whole),
            pl.BlockSpec((FF, width), whole),
        ],
        out_specs=[
            pl.BlockSpec((ROW_BLOCK, FF), by_row),
            pl.BlockSpec((ROW_BLOCK, 2 * FF), by_row),
            pl.BlockSpec((ROW_BLOCK, width), by_row),
        ],
        out_shape=[
            jax.ShapeDtypeStruct((rows, FF), bf16),
            jax.ShapeDtypeStruct((rows, 2 * FF), bf16),
            jax.ShapeDtypeStruct((rows, width), bf16),
        ],
        cost_estimate=pl.CostEstimate(
            flops=2 * rows * width * FF * 5,
            bytes_accessed=rows * width * 2 * 5,
            transcendentals=rows * FF,
        ),
        name="experts_first",
    )(arrived, grad_arrived, pre_w, down_w)


def experts_second_body(x_ref, g_ref, hidden_ref, grads_ref, down_w_ref, out_ref, mine_ref, theirs_ref):
    @pl.when(pl.program_id(0) == 0)
    def _():
        mine_ref[...] = jnp.zeros_like(mine_ref)
        theirs_ref[...] = jnp.zeros_like(theirs_ref)

    out = None
    for b, total_ref in enumerate((mine_ref, theirs_ref)):
        hidden = hidden_ref[:, b * BLOCK : (b + 1) * BLOCK]
        part = dot(hidden, down_w_ref[b * BLOCK : (b + 1) * BLOCK, :]).astype(bf16).astype(f32)
        out = part if out is None else out + part
        total_ref[: 2 * BLOCK, :] += dot(
            grads_ref[:, 2 * b * BLOCK : (2 * b + 2) * BLOCK], x_ref[...], TN
        )
        total_ref[2 * BLOCK :, :] += dot(hidden, g_ref[...], TN)
    out_ref[...] = out.astype(bf16)


def experts_second(arrived, grad_arrived, hidden, grads, down_w):
    rows, width = arrived.shape
    whole = lambda i: (0, 0)
    by_row = lambda i: (i, 0)
    return pl.pallas_call(
        experts_second_body,
        grid=(rows // ROW_BLOCK,),
        in_specs=[
            pl.BlockSpec((ROW_BLOCK, width), by_row),
            pl.BlockSpec((ROW_BLOCK, width), by_row),
            pl.BlockSpec((ROW_BLOCK, FF), by_row),
            pl.BlockSpec((ROW_BLOCK, 2 * FF), by_row),
            pl.BlockSpec((FF, width), whole),
        ],
        out_specs=[
            pl.BlockSpec((ROW_BLOCK, width), by_row),
            pl.BlockSpec((3 * BLOCK, width), whole),
            pl.BlockSpec((3 * BLOCK, width), whole),
        ],
        out_shape=[
            jax.ShapeDtypeStruct((rows, width), bf16),
            jax.ShapeDtypeStruct((3 * BLOCK, width), f32),
            jax.ShapeDtypeStruct((3 * BLOCK, width), f32),
        ],
        cost_estimate=pl.CostEstimate(
            flops=2 * rows * width * FF * 4,
            bytes_accessed=rows * width * 2 * 5 + 6 * BLOCK * width * 4,
            transcendentals=0,
        ),
        name="experts_second",
    )(arrived, grad_arrived, hidden, grads, down_w)


def gather_body(shard_ref, out_ref, send_sem, recv_sem, local_sem):
    seq, chip, core = (lax.axis_index(name) for name in ("seq", "chip", "core"))
    y, z, half = (chip // (2 * RING), (chip // 2) % RING, chip % 2)

    def device(to_y, to_z, to_half, to_core):
        return (seq, (to_y * RING + to_z) * 2 + to_half, to_core)

    def first(step):
        return device((y + core * step) % RING, (z + (1 - core) * step) % RING, half, core)

    def last(step):
        return device((y + (1 - core) * step) % RING, (z + core * step) % RING, half, core)

    partner = device(y, z, half, 1 - core)
    across = device(y, z, 1 - half, core)
    ahead, behind = (1, RING - 1)
    barrier = pltpu.get_barrier_semaphore()
    for other in (partner, across, first(ahead), first(behind), last(ahead), last(behind)):
        pl.semaphore_signal(barrier, inc=1, device_id=other, device_id_type=MESH_ID)
    pl.semaphore_wait(barrier, 6)

    def send(i, src, dst, to):
        return pltpu.make_async_remote_copy(
            src_ref=src,
            dst_ref=dst,
            send_sem=send_sem.at[i],
            recv_sem=recv_sem.at[i],
            device_id=to,
            device_id_type=MESH_ID,
        )

    def line(c, step, part=None):
        cut = slice(None) if part is None else pl.ds(part * (RING // 2), RING // 2)
        if c == 0:
            return out_ref.at[(y + step) % RING, cut, :, 0]
        return out_ref.at[cut, (z + step) % RING, :, 1]

    def pair(c, step, part=None):
        cut = slice(None) if part is None else part
        if c == 0:
            return out_ref.at[y, (z + step) % RING, cut, 0]
        return out_ref.at[(y + step) % RING, z, cut, 1]

    def run(c):
        sent = []

        def go(i, region, to):
            copy = send(i, region, region, to)
            copy.start()
            sent.append(copy)

        def arrive(i, region):
            send(i, region, region, partner).wait_recv()

        own = out_ref.at[y, z, half, c]
        copy = send(0, shard_ref, own, across)
        copy.start()
        sent.append(copy)
        local = pltpu.make_async_copy(shard_ref, own, local_sem)
        local.start()
        local.wait()
        arrive(0, out_ref.at[y, z, 1 - half, c])
        go(1, pair(c, 0), first(ahead))
        go(2, pair(c, 0), first(behind))
        arrive(1, pair(c, behind))
        go(3, pair(c, behind, 0), first(ahead))
        arrive(2, pair(c, ahead))
        go(4, pair(c, ahead, 1), first(behind))
        arrive(3, pair(c, 2, 0))
        arrive(4, pair(c, 2, 1))
        go(5, line(c, 0), last(ahead))
        go(6, line(c, 0), last(behind))
        go(9, line(c, 0), partner)
        arrive(5, line(c, behind))
        go(7, line(c, behind, 0), last(ahead))
        go(10, line(c, behind), partner)
        arrive(6, line(c, ahead))
        go(8, line(c, ahead, 1), last(behind))
        go(11, line(c, ahead), partner)
        arrive(7, line(c, 2, 0))
        go(12, line(c, 2, 0), partner)
        arrive(8, line(c, 2, 1))
        go(13, line(c, 2, 1), partner)
        arrive(9, line(1 - c, 0))
        arrive(10, line(1 - c, behind))
        arrive(11, line(1 - c, ahead))
        arrive(12, line(1 - c, 2, 0))
        arrive(13, line(1 - c, 2, 1))
        for copy in sent:
            copy.wait_send()

    for c in (0, 1):
        pl.when(core == c)(lambda c=c: run(c))


def gather_weights(shard):
    rows, width = shard.shape
    out = pl.pallas_call(
        gather_body,
        out_shape=jax.ShapeDtypeStruct((RING, RING, 2, 2, rows, width), shard.dtype),
        in_specs=[pl.BlockSpec(memory_space=pltpu.VMEM)],
        out_specs=pl.BlockSpec(memory_space=pl.ANY),
        scratch_shapes=[
            pltpu.SemaphoreType.DMA((14,)),
            pltpu.SemaphoreType.DMA((14,)),
            pltpu.SemaphoreType.DMA,
        ],
        compiler_params=pltpu.CompilerParams(collective_id=0, has_side_effects=True),
        cost_estimate=pl.CostEstimate(
            flops=0, bytes_accessed=rows * width * 2 * 4 * RING * RING * 8, transcendentals=0
        ),
        name="gather_weights",
    )(shard)
    return out.reshape(4 * RING * RING * rows, width)


def projection_grads_body(mine_ref, sent_ref, gp_ref, gr_ref, gains_ref, total_ref, away_ref):
    width = gp_ref.shape[1]
    wide = width + gr_ref.shape[1]
    spread = lax.broadcasted_iota(jnp.int32, (8, 128), 0)
    lane = lax.broadcasted_iota(jnp.int32, (8, 128), 1)
    apart = ((spread == lane) & (spread < 6)).astype(bf16)
    tokens = gp_ref.shape[0]
    for ref, out_ref, which in ((mine_ref, total_ref, 0), (sent_ref, away_ref, 1)):
        out_ref[:, :width] = dot(ref[:tokens, :], gp_ref[...], TN).astype(out_ref.dtype)
        out_ref[:, width:wide] = dot(ref[tokens:, :], gr_ref[...], TN).astype(out_ref.dtype)
        out_ref[:, wide:] = dot(gains_ref[which], apart, TN).astype(out_ref.dtype)


def projection_grads(rows_mine, rows_sent, grad_projected, grad_res_low, gains):
    count = rows_mine.shape[1]
    width = grad_projected.shape[1] + grad_res_low.shape[1] + 128
    tile = 128
    whole = lambda i: (0, 0)
    by_column = lambda i: (0, i)
    by_row = lambda i: (i, 0)
    return pl.pallas_call(
        projection_grads_body,
        grid=(count // tile,),
        in_specs=[
            pl.BlockSpec((rows_mine.shape[0], tile), by_column),
            pl.BlockSpec((rows_sent.shape[0], tile), by_column),
            pl.BlockSpec(grad_projected.shape, whole),
            pl.BlockSpec(grad_res_low.shape, whole),
            pl.BlockSpec((2, 8, tile), lambda i: (0, 0, i)),
        ],
        out_specs=[pl.BlockSpec((tile, width), by_row), pl.BlockSpec((tile, width), by_row)],
        out_shape=[
            jax.ShapeDtypeStruct((count, width), f32),
            jax.ShapeDtypeStruct((count, width), bf16),
        ],
        name="projection_grads",
    )(rows_mine, rows_sent, grad_projected, grad_res_low, gains)


def merge_halves_body(mine_ref, came_ref, out_ref):
    wide = out_ref.shape[1] - 128
    out_ref[:, :wide] = (mine_ref[:, :wide] + came_ref[:, :wide].astype(f32)).astype(bf16)
    parts = mine_ref[:, wide:] + came_ref[:, wide:].astype(f32)
    lane = lax.broadcasted_iota(jnp.int32, parts.shape, 1)
    total = parts + pltpu.roll(parts, 126, 1) + pltpu.roll(parts, 124, 1)
    total = jnp.where(lane < 2, total, 0.0)
    one = total.astype(bf16).astype(f32)
    two = (total - one).astype(bf16).astype(f32)
    three = total - one - two
    out_ref[:, wide:] = (one + pltpu.roll(two, 2, 1) + pltpu.roll(three, 4, 1)).astype(bf16)


def merge_halves(mine, came):
    rows, width = mine.shape
    tile = 128
    by_row = lambda i: (i, 0)
    return pl.pallas_call(
        merge_halves_body,
        grid=(rows // tile,),
        in_specs=[pl.BlockSpec((tile, width), by_row), pl.BlockSpec((tile, width), by_row)],
        out_specs=pl.BlockSpec((tile, width), by_row),
        out_shape=jax.ShapeDtypeStruct((rows, width), bf16),
        name="merge_halves",
    )(mine, came)


def spread_plan(route_ids, mix_weights):
    token_count = route_ids.shape[0]
    expert_ids = jnp.arange(EXPERTS)[None, None, :]
    named = route_ids[:, :, None] == expert_ids
    picked = jnp.any(named, axis=1)
    token_weight = jnp.sum(jnp.where(named, mix_weights[:, :, None], 0.0), axis=1)
    earlier = jnp.arange(token_count)[None, :] < jnp.arange(token_count)[:, None]
    rank = dot(earlier.astype(bf16), picked.astype(bf16)).astype(jnp.int32)
    at_slot = jnp.where(picked, rank, -1).T[:, None, :] == jnp.arange(SLOTS)[None, :, None]
    placed = at_slot.astype(bf16).reshape(EXPERTS * SLOTS, token_count)
    weighted = jnp.where(at_slot, token_weight.T[:, None, :], 0.0)
    slot_weight = jnp.sum(weighted, axis=2).reshape(EXPERTS * SLOTS, 1)
    mixers = [part.reshape(EXPERTS * SLOTS, token_count) for part in three_parts(weighted)]
    return (placed, slot_weight, mixers)


def exchange(rows):
    width = rows.shape[-1]
    blocks = rows.reshape(EXPERTS, -1, width)
    return lax.all_to_all(blocks, "chip", split_axis=0, concat_axis=0, tiled=True).reshape(-1, width)


def on_device(
    inputs,
    project_in,
    project_out,
    gain_attend,
    gain_expert,
    expert_gate,
    expert_up,
    expert_down,
    routes,
    route_weights,
    segments,
    cotangent,
):
    token_count = inputs.shape[1]
    model_width = inputs.shape[2]
    query_width = HEADS * HEAD_DIM
    kv_width = KV_HEADS * HEAD_DIM
    group = HEADS // KV_HEADS
    seq = lax.axis_index("seq")
    core = lax.axis_index("core")
    own_low = inputs[0]
    other_low = lax.ppermute(own_low, "seq", SWAP)

    placed, slot_weight, mixers = spread_plan(routes[0], route_weights[0])
    grad_rows = (dot(placed, cotangent[0]) * slot_weight).astype(bf16)
    grad_arrived = exchange(grad_rows)

    own_units = jnp.concatenate([expert_gate, expert_up, expert_down], axis=0)
    other_units = lax.ppermute(own_units, "core", SWAP)
    pre_w = jnp.concatenate([own_units[: 2 * BLOCK], other_units[: 2 * BLOCK]], axis=0)
    down_w = jnp.concatenate([expert_down, other_units[2 * BLOCK :]], axis=0)

    share = gain_attend.shape[0]
    wide = query_width + 2 * kv_width + query_width
    filler = jnp.zeros((share, 126), bf16)
    gathered = gather_weights(
        jnp.concatenate(
            [project_in, project_out, gain_attend[:, None], gain_expert[:, None], filler], axis=1
        )
    )
    in_full = gathered[:, : query_width + 2 * kv_width]
    out_full = gathered[:, query_width + 2 * kv_width : wide]
    gain_one, gain_two = (gathered[:, wide], gathered[:, wide + 1])

    row_values = own_low.astype(f32)
    normed_one, inverse_one = norm_forward(row_values, gain_one)
    normed_other, _ = norm_forward(other_low.astype(f32), gain_one)
    kv_w = in_full[:, query_width:]
    projected = dot(normed_one, in_full)
    projected_other = dot(normed_other, kv_w)
    own_at = seq * token_count + jnp.arange(token_count)
    other_at = (1 - seq) * token_count + jnp.arange(token_count)
    own_cos, own_sin = rope_tables(own_at)
    other_cos, other_sin = rope_tables(other_at)
    query = rotate_wide(projected[:, :query_width], own_cos, own_sin, 1.0).astype(bf16)
    key_cut = query_width + kv_width
    own_keys = rotate_wide(projected[:, query_width:key_cut], own_cos, own_sin, 1.0)
    other_keys = rotate_wide(projected_other[:, :kv_width], other_cos, other_sin, 1.0)
    keys = jnp.concatenate([own_keys, other_keys], axis=0).astype(bf16)
    values = jnp.concatenate([projected[:, key_cut:], projected_other[:, kv_width:]], axis=0)
    query = query.reshape(token_count, KV_HEADS, group, HEAD_DIM)
    keys = keys.reshape(2 * token_count, KV_HEADS, HEAD_DIM)
    values = values.astype(bf16).reshape(2 * token_count, KV_HEADS, HEAD_DIM)
    seq_ids = segments[0]
    own_ids = lax.dynamic_slice(seq_ids, (seq * token_count,), (token_count,))
    other_ids = lax.dynamic_slice(seq_ids, ((1 - seq) * token_count,), (token_count,))
    key_at = jnp.concatenate([own_at, other_at])
    key_ids = jnp.concatenate([own_ids, other_ids])
    allowed = (key_at[None, :] <= own_at[:, None]) & (key_ids[None, :] == own_ids[:, None])
    attended, log_total = attend_forward(query, keys, values, allowed)
    mixed = attended.reshape(token_count, query_width)
    residual = row_values + dot(mixed, out_full)
    normed_two, inverse_two = norm_forward(residual, gain_two)

    arrived = exchange(dot(placed, normed_two).astype(bf16))
    hidden, grads, back = experts_first(arrived, grad_arrived, pre_w, down_w)
    grad_back = exchange(back)
    out_rows, mine, theirs = experts_second(arrived, grad_arrived, hidden, grads, down_w)
    grad_back, out_rows = lax.optimization_barrier((grad_back, out_rows))
    returned = exchange(out_rows)
    chip_total = mine + lax.ppermute(theirs, "core", SWAP)
    total_low = rounded(chip_total)
    total_other = lax.ppermute(total_low.astype(bf16), "seq", SWAP)

    grad_out = cotangent[0].astype(f32)
    grad_normed_two = dot(placed, grad_back, TN)
    grad_norm_two, gain_two_grad = norm_backward(residual, inverse_two, gain_two, grad_normed_two)
    grad_residual = grad_out + grad_norm_two
    grad_res_low = grad_residual.astype(bf16)
    grad_mixed = dot(grad_res_low, out_full, NT).astype(bf16)
    grad_query, grad_keys, grad_values = attend_backward(
        query, keys, values, allowed, attended, log_total, grad_mixed.reshape(attended.shape)
    )
    grad_query = grad_query.reshape(token_count, query_width)
    grad_keys = grad_keys.reshape(2 * token_count, kv_width)
    grad_values = grad_values.reshape(2 * token_count, kv_width)
    away_keys = rotate_wide(grad_keys[token_count:], other_cos, other_sin, -1.0)
    away = jnp.concatenate([away_keys, grad_values[token_count:]], axis=1).astype(bf16)
    came = lax.ppermute(away, "seq", SWAP).astype(f32)
    grad_query = rotate_wide(grad_query, own_cos, own_sin, -1.0)
    grad_keys = rotate_wide(grad_keys[:token_count], own_cos, own_sin, -1.0) + came[:, :kv_width]
    grad_values = grad_values[:token_count] + came[:, kv_width:]
    grad_projected = jnp.concatenate([grad_query, grad_keys, grad_values], axis=1).astype(bf16)
    grad_projected, total_other = lax.optimization_barrier((grad_projected, total_other))
    grad_units = total_low + total_other.astype(f32)
    grad_normed_one = dot(grad_projected, in_full, NT)
    grad_norm_one, gain_one_grad = norm_backward(row_values, inverse_one, gain_one, grad_normed_one)
    grad_inputs = (grad_residual + grad_norm_one).astype(bf16)

    owners = EXPERTS
    feature = jnp.arange(model_width)[:, None]
    slot = jnp.arange(model_width)[None, :]
    half_width = model_width // 2
    of_core = jnp.where(slot < half_width, core, 1 - core)
    at = slot % half_width
    chosen_half = feature == (2 * (at // share) + of_core) * share + at % share
    chosen_half = chosen_half.astype(bf16)
    features = dot(jnp.concatenate([normed_one, mixed], axis=0), chosen_half).astype(bf16)
    gain_pair = jnp.stack([gain_one_grad, gain_two_grad], axis=0)
    gain_parts = jnp.concatenate(three_parts(gain_pair) + (jnp.zeros_like(gain_pair, bf16),), axis=0)
    gain_parts = dot(gain_parts, chosen_half).astype(bf16)
    gain_parts = jnp.stack([gain_parts[:, :half_width], gain_parts[:, half_width:]], axis=0)
    grads_mine, grads_sent = projection_grads(
        features[:, :half_width], features[:, half_width:], grad_projected, grad_res_low, gain_parts
    )
    chip_rows = merge_halves(grads_mine, lax.ppermute(grads_sent, "core", SWAP))
    landed = lax.all_to_all(
        chip_rows.reshape(owners, share, wide + 128),
        "chip",
        split_axis=0,
        concat_axis=0,
        tiled=True,
    )
    totals = jnp.sum(landed.astype(f32), axis=0)
    totals = totals + lax.ppermute(totals, "seq", SWAP)
    gain_totals = totals[:, wide : wide + 2] + totals[:, wide + 2 : wide + 4]
    gain_totals = gain_totals + totals[:, wide + 4 : wide + 6]

    mix = jnp.concatenate(mixers, axis=1)
    chosen = dot(mix, returned, TN).reshape(3, token_count, model_width)
    output = (residual + (chosen[2] + chosen[1] + chosen[0])).astype(bf16)
    in_width = query_width + 2 * kv_width
    return (
        output.reshape(1, token_count, model_width),
        grad_inputs.reshape(1, token_count, model_width),
        totals[:, :in_width],
        totals[:, in_width:wide],
        gain_totals[:, 0],
        gain_totals[:, 1],
        grad_units[:BLOCK],
        grad_units[BLOCK : 2 * BLOCK],
        grad_units[2 * BLOCK :],
    )


def solution(mesh):
    devices = mesh.devices
    cores = Mesh(devices.reshape(devices.shape[0], -1, 2), ("seq", "chip", "core"))
    every = ("chip", "core")
    by_token = P(every, "seq", None)
    by_row = P(every, None)
    in_specs = (
        by_token,
        by_row,
        by_row,
        P(every),
        P(every),
        by_row,
        by_row,
        by_row,
        by_token,
        by_token,
        by_row,
        by_token,
    )
    out_specs = (by_token, by_token, by_row, by_row, P(every), P(every), by_row, by_row, by_row)
    return jax.shard_map(
        on_device, mesh=cores, in_specs=in_specs, out_specs=out_specs, check_vma=False
    )
```

```python
import jax
import jax.numpy as jnp
from jax import lax
from jax.experimental import pallas as pl
from jax.experimental.pallas import tpu as pltpu
from jax.sharding import Mesh, PartitionSpec as P

HEADS = 16
KV_HEADS = 8
HEAD_DIM = 64
EXPERTS = 32
FF = 512
TOP = 8
CAP = 36
SLOTS = 40
BLOCK = 256
ROW_BLOCK = 256

EPSILON = 1e-06
ROPE_BASE = 10000.0

f32 = jnp.float32
bf16 = jnp.bfloat16

RING = 4
MESH_ID = pl.DeviceIdType.MESH
SWAP = [(0, 1), (1, 0)]
NT = (((1,), (1,)), ((), ()))
TN = (((0,), (0,)), ((), ()))


def dot(a, b, dims=(((1,), (0,)), ((), ()))):
    return lax.dot_general(a, b, dims, preferred_element_type=f32)


def rope_tables(positions):
    half_dim = HEAD_DIM // 2
    powers = jnp.arange(half_dim).astype(f32) * (2.0 / HEAD_DIM)
    inverse_freq = ROPE_BASE ** (-powers)
    angles = positions.astype(f32)[:, None] * inverse_freq[None, :]
    return (jnp.cos(angles), jnp.sin(angles))


def rotate(values, cosine_table, sine_table, turn_sign):
    half_dim = values.shape[-1] // 2
    leading = values[..., :half_dim]
    trailing = values[..., half_dim:]
    cosine_b = cosine_table[:, None, :]
    sine_b = sine_table[:, None, :] * turn_sign
    return jnp.concatenate(
        [leading * cosine_b - trailing * sine_b, trailing * cosine_b + leading * sine_b], axis=-1
    )


def rotate_wide(values, cosine_table, sine_table, turn_sign):
    rows, width = values.shape
    heads = values.reshape(rows, width // HEAD_DIM, HEAD_DIM)
    return rotate(heads, cosine_table, sine_table, turn_sign).reshape(rows, width)


def norm_forward(values, gain_vector):
    inverse = lax.rsqrt(jnp.mean(values * values, axis=-1, keepdims=True) + EPSILON)
    return ((values * inverse * gain_vector.astype(f32)).astype(bf16), inverse)


def norm_backward(values, inverse, gain_vector, upstream):
    scaled = upstream * gain_vector.astype(f32)
    grad_gain = jnp.sum(upstream * values * inverse, axis=0)
    coupling = jnp.mean(scaled * values, axis=-1, keepdims=True)
    return (inverse * scaled - values * inverse * inverse * inverse * coupling, grad_gain)


def rounded(values):
    return lax.reduce_precision(values, exponent_bits=8, mantissa_bits=7)


def three_parts(values):
    first = rounded(values)
    second = rounded(values - first)
    third = values - first - second
    return (first.astype(bf16), second.astype(bf16), third.astype(bf16))


def masked_scores(query, keys, allowed):
    scores = jnp.einsum("qkgd,skd->kgqs", query, keys, preferred_element_type=f32)
    return jnp.where(allowed[None, None], scores * HEAD_DIM ** (-0.5), -1e30)


def attend_forward(query, keys, values, allowed):
    scores = masked_scores(query, keys, allowed)
    highest = jnp.max(scores, axis=-1, keepdims=True)
    log_total = highest + jnp.log(jnp.sum(jnp.exp(scores - highest), axis=-1, keepdims=True))
    weights = jnp.exp(scores - log_total).astype(bf16)
    mixed = jnp.einsum("kgqs,skd->qkgd", weights, values, preferred_element_type=f32)
    return (mixed.astype(bf16), log_total)


def attend_backward(query, keys, values, allowed, attended, log_total, grad_attended):
    scale_factor = HEAD_DIM ** (-0.5)
    weights = jnp.exp(masked_scores(query, keys, allowed) - log_total)
    grad_values = jnp.einsum(
        "kgqs,qkgd->skd", weights.astype(bf16), grad_attended, preferred_element_type=f32
    )
    grad_weights = jnp.einsum("qkgd,skd->kgqs", grad_attended, values, preferred_element_type=f32)
    row_delta = jnp.sum(grad_attended.astype(f32) * attended.astype(f32), axis=-1)
    row_delta = jnp.transpose(row_delta, (1, 2, 0))
    grad_scores = (weights * (grad_weights - row_delta[..., None])).astype(bf16)
    grad_query = jnp.einsum("kgqs,skd->qkgd", grad_scores, keys, preferred_element_type=f32)
    grad_keys = jnp.einsum("kgqs,qkgd->skd", grad_scores, query, preferred_element_type=f32)
    return (grad_query * scale_factor, grad_keys * scale_factor, grad_values)


def experts_first_body(x_ref, g_ref, pre_w_ref, down_w_ref, hidden_ref, grads_ref, back_ref):
    pre = dot(x_ref[...], pre_w_ref[...], NT)
    grad_hidden = dot(g_ref[...], down_w_ref[...], NT)
    back = None
    for b in range(FF // BLOCK):
        gate = pre[:, 2 * b * BLOCK : (2 * b + 1) * BLOCK]
        up = pre[:, (2 * b + 1) * BLOCK : (2 * b + 2) * BLOCK]
        grad_h = grad_hidden[:, b * BLOCK : (b + 1) * BLOCK]
        sigmoid_gate = 1.0 / (1.0 + jnp.exp(-gate))
        silu = gate * sigmoid_gate
        hidden_ref[:, b * BLOCK : (b + 1) * BLOCK] = (silu * up).astype(bf16)
        grad_gate = (grad_h * up * sigmoid_gate * (1.0 + gate * (1.0 - sigmoid_gate))).astype(bf16)
        grad_up = (grad_h * gate * sigmoid_gate).astype(bf16)
        both = jnp.concatenate([grad_gate, grad_up], axis=1)
        grads_ref[:, 2 * b * BLOCK : (2 * b + 2) * BLOCK] = both
        part = dot(both, pre_w_ref[2 * b * BLOCK : (2 * b + 2) * BLOCK, :]).astype(bf16).astype(f32)
        back = part if back is None else back + part
    back_ref[...] = back.astype(bf16)


def experts_first(arrived, grad_arrived, pre_w, down_w):
    rows, width = arrived.shape
    whole = lambda i: (0, 0)
    by_row = lambda i: (i, 0)
    return pl.pallas_call(
        experts_first_body,
        grid=(rows // ROW_BLOCK,),
        in_specs=[
            pl.BlockSpec((ROW_BLOCK, width), by_row),
            pl.BlockSpec((ROW_BLOCK, width), by_row),
            pl.BlockSpec((2 * FF, width), whole),
            pl.BlockSpec((FF, width), whole),
        ],
        out_specs=[
            pl.BlockSpec((ROW_BLOCK, FF), by_row),
            pl.BlockSpec((ROW_BLOCK, 2 * FF), by_row),
            pl.BlockSpec((ROW_BLOCK, width), by_row),
        ],
        out_shape=[
            jax.ShapeDtypeStruct((rows, FF), bf16),
            jax.ShapeDtypeStruct((rows, 2 * FF), bf16),
            jax.ShapeDtypeStruct((rows, width), bf16),
        ],
        cost_estimate=pl.CostEstimate(
            flops=2 * rows * width * FF * 5,
            bytes_accessed=rows * width * 2 * 5,
            transcendentals=rows * FF,
        ),
        name="experts_first",
    )(arrived, grad_arrived, pre_w, down_w)


def experts_second_body(
    x_ref,
    g_ref,
    hidden_ref,
    grads_ref,
    down_w_ref,
    out_ref,
    total_ref,
    theirs,
    came,
    low,
    low_came,
    send_sem,
    recv_sem,
):
    seq, chip, core = (lax.axis_index(name) for name in ("seq", "chip", "core"))
    partner = (seq, chip, 1 - core)
    mirror = (1 - seq, chip, core)
    barrier = pltpu.get_barrier_semaphore()
    for other in (partner, mirror):
        pl.semaphore_signal(barrier, inc=1, device_id=other, device_id_type=MESH_ID)
    pl.semaphore_wait(barrier, 2)
    width = x_ref.shape[1]

    def send(i, src, dst, to):
        return pltpu.make_async_remote_copy(
            src_ref=src,
            dst_ref=dst,
            send_sem=send_sem.at[i],
            recv_sem=recv_sem.at[i],
            device_id=to,
            device_id_type=MESH_ID,
        )

    def unit_grads(block, kind, store):
        if kind < 2:
            at = (2 * block + kind) * BLOCK
            left, right = (grads_ref, x_ref)
        else:
            at = block * BLOCK
            left, right = (hidden_ref, g_ref)

        @pl.loop(0, width // BLOCK)
        def _(n):
            columns = pl.ds(pl.multiple_of(n * BLOCK, BLOCK), BLOCK)
            store[kind, :, columns] = dot(left[:, at : at + BLOCK], right[:, columns], TN)

    away = [send(k, theirs.at[k], came.at[k], partner) for k in range(3)]
    across = [send(3 + k, low.at[k], low_came.at[k], mirror) for k in range(3)]
    for k in range(3):
        unit_grads(1, k, theirs)
        if k:
            away[k - 1].start()
    unit_grads(0, 0, total_ref)
    away[2].start()

    def join(k):
        away[k].wait_recv()

        @pl.loop(0, BLOCK // 32)
        def _(r):
            rows = pl.ds(pl.multiple_of(r * 32, 32), 32)
            low[k, rows, :] = (total_ref[k, rows, :] + came[k, rows, :]).astype(bf16)

    for k in range(3):
        join(k)
        if k < 2:
            unit_grads(0, k + 1, total_ref)
            across[k].start()

    @pl.loop(0, x_ref.shape[0] // ROW_BLOCK)
    def _(r):
        rows = pl.ds(pl.multiple_of(r * ROW_BLOCK, ROW_BLOCK), ROW_BLOCK)
        out = None
        for b in range(FF // BLOCK):
            units = slice(b * BLOCK, (b + 1) * BLOCK)
            part = dot(hidden_ref[rows, units], down_w_ref[units, :]).astype(bf16).astype(f32)
            out = part if out is None else out + part
        out_ref[rows, :] = out.astype(bf16)

        @pl.when(r == 0)
        def _():
            across[2].start()

    for k in range(3):
        across[k].wait_recv()

        @pl.loop(0, BLOCK // 32)
        def _(r):
            rows = pl.ds(pl.multiple_of(r * 32, 32), 32)
            total_ref[k, rows, :] = low[k, rows, :].astype(f32) + low_came[k, rows, :].astype(f32)

    for copy in away + across:
        copy.wait_send()


def experts_second(arrived, grad_arrived, hidden, grads, down_w):
    rows, width = arrived.shape
    return pl.pallas_call(
        experts_second_body,
        in_specs=[pl.BlockSpec(memory_space=pltpu.VMEM)] * 5,
        out_specs=[pl.BlockSpec(memory_space=pltpu.VMEM)] * 2,
        out_shape=[
            jax.ShapeDtypeStruct((rows, width), bf16),
            jax.ShapeDtypeStruct((3, BLOCK, width), f32),
        ],
        scratch_shapes=[
            pltpu.VMEM((3, BLOCK, width), f32),
            pltpu.VMEM((3, BLOCK, width), f32),
            pltpu.VMEM((3, BLOCK, width), bf16),
            pltpu.VMEM((3, BLOCK, width), bf16),
            pltpu.SemaphoreType.DMA((6,)),
            pltpu.SemaphoreType.DMA((6,)),
        ],
        compiler_params=pltpu.CompilerParams(collective_id=1, has_side_effects=True),
        cost_estimate=pl.CostEstimate(
            flops=2 * rows * width * FF * 4,
            bytes_accessed=rows * width * 2 * 20,
            transcendentals=0,
        ),
        name="experts_second",
    )(arrived, grad_arrived, hidden, grads, down_w)


def gather_body(shard_ref, out_ref, send_sem, recv_sem, local_sem):
    seq, chip, core = (lax.axis_index(name) for name in ("seq", "chip", "core"))
    y, z, half = (chip // (2 * RING), (chip // 2) % RING, chip % 2)

    def device(to_y, to_z, to_half, to_core):
        return (seq, (to_y * RING + to_z) * 2 + to_half, to_core)

    def first(step):
        return device((y + core * step) % RING, (z + (1 - core) * step) % RING, half, core)

    def last(step):
        return device((y + (1 - core) * step) % RING, (z + core * step) % RING, half, core)

    partner = device(y, z, half, 1 - core)
    across = device(y, z, 1 - half, core)
    ahead, behind = (1, RING - 1)
    barrier = pltpu.get_barrier_semaphore()
    for other in (partner, across, first(ahead), first(behind), last(ahead), last(behind)):
        pl.semaphore_signal(barrier, inc=1, device_id=other, device_id_type=MESH_ID)
    pl.semaphore_wait(barrier, 6)

    def send(i, src, dst, to):
        return pltpu.make_async_remote_copy(
            src_ref=src,
            dst_ref=dst,
            send_sem=send_sem.at[i],
            recv_sem=recv_sem.at[i],
            device_id=to,
            device_id_type=MESH_ID,
        )

    def line(c, step, part=None):
        cut = slice(None) if part is None else pl.ds(part * (RING // 2), RING // 2)
        if c == 0:
            return out_ref.at[(y + step) % RING, cut, :, 0]
        return out_ref.at[cut, (z + step) % RING, :, 1]

    def pair(c, step, part=None):
        cut = slice(None) if part is None else part
        if c == 0:
            return out_ref.at[y, (z + step) % RING, cut, 0]
        return out_ref.at[(y + step) % RING, z, cut, 1]

    def run(c):
        sent = []

        def go(i, region, to):
            copy = send(i, region, region, to)
            copy.start()
            sent.append(copy)

        def arrive(i, region):
            send(i, region, region, partner).wait_recv()

        own = out_ref.at[y, z, half, c]
        copy = send(0, shard_ref, own, across)
        copy.start()
        sent.append(copy)
        local = pltpu.make_async_copy(shard_ref, own, local_sem)
        local.start()
        local.wait()
        arrive(0, out_ref.at[y, z, 1 - half, c])
        go(1, pair(c, 0), first(ahead))
        go(2, pair(c, 0), first(behind))
        arrive(1, pair(c, behind))
        go(3, pair(c, behind, 0), first(ahead))
        arrive(2, pair(c, ahead))
        go(4, pair(c, ahead, 1), first(behind))
        arrive(3, pair(c, 2, 0))
        arrive(4, pair(c, 2, 1))
        go(5, line(c, 0), last(ahead))
        go(6, line(c, 0), last(behind))
        go(9, line(c, 0), partner)
        arrive(5, line(c, behind))
        go(7, line(c, behind, 0), last(ahead))
        go(10, line(c, behind), partner)
        arrive(6, line(c, ahead))
        go(8, line(c, ahead, 1), last(behind))
        go(11, line(c, ahead), partner)
        arrive(7, line(c, 2, 0))
        go(12, line(c, 2, 0), partner)
        arrive(8, line(c, 2, 1))
        go(13, line(c, 2, 1), partner)
        arrive(9, line(1 - c, 0))
        arrive(10, line(1 - c, behind))
        arrive(11, line(1 - c, ahead))
        arrive(12, line(1 - c, 2, 0))
        arrive(13, line(1 - c, 2, 1))
        for copy in sent:
            copy.wait_send()

    for c in (0, 1):
        pl.when(core == c)(lambda c=c: run(c))


def gather_weights(shard):
    rows, width = shard.shape
    out = pl.pallas_call(
        gather_body,
        out_shape=jax.ShapeDtypeStruct((RING, RING, 2, 2, rows, width), shard.dtype),
        in_specs=[pl.BlockSpec(memory_space=pltpu.VMEM)],
        out_specs=pl.BlockSpec(memory_space=pl.ANY),
        scratch_shapes=[
            pltpu.SemaphoreType.DMA((14,)),
            pltpu.SemaphoreType.DMA((14,)),
            pltpu.SemaphoreType.DMA,
        ],
        compiler_params=pltpu.CompilerParams(collective_id=0, has_side_effects=True),
        cost_estimate=pl.CostEstimate(
            flops=0, bytes_accessed=rows * width * 2 * 4 * RING * RING * 8, transcendentals=0
        ),
        name="gather_weights",
    )(shard)
    return out.reshape(4 * RING * RING * rows, width)


def projection_grads_body(mine_ref, sent_ref, gp_ref, gr_ref, gains_ref, total_ref, away_ref):
    width = gp_ref.shape[1]
    wide = width + gr_ref.shape[1]
    spread = lax.broadcasted_iota(jnp.int32, (8, 128), 0)
    lane = lax.broadcasted_iota(jnp.int32, (8, 128), 1)
    apart = ((spread == lane) & (spread < 6)).astype(bf16)
    tokens = gp_ref.shape[0]
    for ref, out_ref, which in ((mine_ref, total_ref, 0), (sent_ref, away_ref, 1)):
        out_ref[:, :width] = dot(ref[:tokens, :], gp_ref[...], TN).astype(out_ref.dtype)
        out_ref[:, width:wide] = dot(ref[tokens:, :], gr_ref[...], TN).astype(out_ref.dtype)
        out_ref[:, wide:] = dot(gains_ref[which], apart, TN).astype(out_ref.dtype)


def projection_grads(rows_mine, rows_sent, grad_projected, grad_res_low, gains):
    count = rows_mine.shape[1]
    width = grad_projected.shape[1] + grad_res_low.shape[1] + 128
    tile = 128
    whole = lambda i: (0, 0)
    by_column = lambda i: (0, i)
    by_row = lambda i: (i, 0)
    return pl.pallas_call(
        projection_grads_body,
        grid=(count // tile,),
        in_specs=[
            pl.BlockSpec((rows_mine.shape[0], tile), by_column),
            pl.BlockSpec((rows_sent.shape[0], tile), by_column),
            pl.BlockSpec(grad_projected.shape, whole),
            pl.BlockSpec(grad_res_low.shape, whole),
            pl.BlockSpec((2, 8, tile), lambda i: (0, 0, i)),
        ],
        out_specs=[pl.BlockSpec((tile, width), by_row), pl.BlockSpec((tile, width), by_row)],
        out_shape=[
            jax.ShapeDtypeStruct((count, width), f32),
            jax.ShapeDtypeStruct((count, width), bf16),
        ],
        name="projection_grads",
    )(rows_mine, rows_sent, grad_projected, grad_res_low, gains)


def merge_halves_body(mine_ref, came_ref, out_ref):
    wide = out_ref.shape[1] - 128
    out_ref[:, :wide] = (mine_ref[:, :wide] + came_ref[:, :wide].astype(f32)).astype(bf16)
    parts = mine_ref[:, wide:] + came_ref[:, wide:].astype(f32)
    lane = lax.broadcasted_iota(jnp.int32, parts.shape, 1)
    total = parts + pltpu.roll(parts, 126, 1) + pltpu.roll(parts, 124, 1)
    total = jnp.where(lane < 2, total, 0.0)
    one = total.astype(bf16).astype(f32)
    two = (total - one).astype(bf16).astype(f32)
    three = total - one - two
    out_ref[:, wide:] = (one + pltpu.roll(two, 2, 1) + pltpu.roll(three, 4, 1)).astype(bf16)


def merge_halves(mine, came):
    rows, width = mine.shape
    tile = 128
    by_row = lambda i: (i, 0)
    return pl.pallas_call(
        merge_halves_body,
        grid=(rows // tile,),
        in_specs=[pl.BlockSpec((tile, width), by_row), pl.BlockSpec((tile, width), by_row)],
        out_specs=pl.BlockSpec((tile, width), by_row),
        out_shape=jax.ShapeDtypeStruct((rows, width), bf16),
        name="merge_halves",
    )(mine, came)


def spread_plan(route_ids, mix_weights):
    token_count = route_ids.shape[0]
    expert_ids = jnp.arange(EXPERTS)[None, None, :]
    named = route_ids[:, :, None] == expert_ids
    picked = jnp.any(named, axis=1)
    token_weight = jnp.sum(jnp.where(named, mix_weights[:, :, None], 0.0), axis=1)
    earlier = jnp.arange(token_count)[None, :] < jnp.arange(token_count)[:, None]
    rank = dot(earlier.astype(bf16), picked.astype(bf16)).astype(jnp.int32)
    at_slot = jnp.where(picked, rank, -1).T[:, None, :] == jnp.arange(SLOTS)[None, :, None]
    placed = at_slot.astype(bf16).reshape(EXPERTS * SLOTS, token_count)
    weighted = jnp.where(at_slot, token_weight.T[:, None, :], 0.0)
    slot_weight = jnp.sum(weighted, axis=2).reshape(EXPERTS * SLOTS, 1)
    mixers = [part.reshape(EXPERTS * SLOTS, token_count) for part in three_parts(weighted)]
    return (placed, slot_weight, mixers)


def exchange(rows):
    width = rows.shape[-1]
    blocks = rows.reshape(EXPERTS, -1, width)
    return lax.all_to_all(blocks, "chip", split_axis=0, concat_axis=0, tiled=True).reshape(-1, width)


def on_device(
    inputs,
    project_in,
    project_out,
    gain_attend,
    gain_expert,
    expert_gate,
    expert_up,
    expert_down,
    routes,
    route_weights,
    segments,
    cotangent,
):
    token_count = inputs.shape[1]
    model_width = inputs.shape[2]
    query_width = HEADS * HEAD_DIM
    kv_width = KV_HEADS * HEAD_DIM
    group = HEADS // KV_HEADS
    seq = lax.axis_index("seq")
    core = lax.axis_index("core")
    own_low = inputs[0]
    other_low = lax.ppermute(own_low, "seq", SWAP)

    placed, slot_weight, mixers = spread_plan(routes[0], route_weights[0])
    grad_rows = (dot(placed, cotangent[0]) * slot_weight).astype(bf16)

    own_units = jnp.concatenate([expert_gate, expert_up, expert_down], axis=0)
    other_units = lax.ppermute(own_units, "core", SWAP)
    pre_w = jnp.concatenate([own_units[: 2 * BLOCK], other_units[: 2 * BLOCK]], axis=0)
    down_w = jnp.concatenate([expert_down, other_units[2 * BLOCK :]], axis=0)

    share = gain_attend.shape[0]
    wide = query_width + 2 * kv_width + query_width
    filler = jnp.zeros((share, 126), bf16)
    gathered = gather_weights(
        jnp.concatenate(
            [project_in, project_out, gain_attend[:, None], gain_expert[:, None], filler], axis=1
        )
    )
    gathered, grad_rows = lax.optimization_barrier((gathered, grad_rows))
    grad_arrived = exchange(grad_rows)
    in_full = gathered[:, : query_width + 2 * kv_width]
    out_full = gathered[:, query_width + 2 * kv_width : wide]
    gain_one, gain_two = (gathered[:, wide], gathered[:, wide + 1])

    row_values = own_low.astype(f32)
    normed_one, inverse_one = norm_forward(row_values, gain_one)
    normed_other, _ = norm_forward(other_low.astype(f32), gain_one)
    kv_w = in_full[:, query_width:]
    projected = dot(normed_one, in_full)
    projected_other = dot(normed_other, kv_w)
    own_at = seq * token_count + jnp.arange(token_count)
    other_at = (1 - seq) * token_count + jnp.arange(token_count)
    own_cos, own_sin = rope_tables(own_at)
    other_cos, other_sin = rope_tables(other_at)
    query = rotate_wide(projected[:, :query_width], own_cos, own_sin, 1.0).astype(bf16)
    key_cut = query_width + kv_width
    own_keys = rotate_wide(projected[:, query_width:key_cut], own_cos, own_sin, 1.0)
    other_keys = rotate_wide(projected_other[:, :kv_width], other_cos, other_sin, 1.0)
    keys = jnp.concatenate([own_keys, other_keys], axis=0).astype(bf16)
    values = jnp.concatenate([projected[:, key_cut:], projected_other[:, kv_width:]], axis=0)
    query = query.reshape(token_count, KV_HEADS, group, HEAD_DIM)
    keys = keys.reshape(2 * token_count, KV_HEADS, HEAD_DIM)
    values = values.astype(bf16).reshape(2 * token_count, KV_HEADS, HEAD_DIM)
    seq_ids = segments[0]
    own_ids = lax.dynamic_slice(seq_ids, (seq * token_count,), (token_count,))
    other_ids = lax.dynamic_slice(seq_ids, ((1 - seq) * token_count,), (token_count,))
    key_at = jnp.concatenate([own_at, other_at])
    key_ids = jnp.concatenate([own_ids, other_ids])
    allowed = (key_at[None, :] <= own_at[:, None]) & (key_ids[None, :] == own_ids[:, None])
    attended, log_total = attend_forward(query, keys, values, allowed)
    mixed = attended.reshape(token_count, query_width)
    residual = row_values + dot(mixed, out_full)
    normed_two, inverse_two = norm_forward(residual, gain_two)

    arrived = exchange(dot(placed, normed_two).astype(bf16))
    hidden, grads, back = experts_first(arrived, grad_arrived, pre_w, down_w)
    grad_back = exchange(back)
    out_rows, grad_units = experts_second(arrived, grad_arrived, hidden, grads, down_w)
    grad_back, out_rows = lax.optimization_barrier((grad_back, out_rows))
    returned = exchange(out_rows)

    grad_out = cotangent[0].astype(f32)
    grad_normed_two = dot(placed, grad_back, TN)
    grad_norm_two, gain_two_grad = norm_backward(residual, inverse_two, gain_two, grad_normed_two)
    grad_residual = grad_out + grad_norm_two
    grad_res_low = grad_residual.astype(bf16)
    grad_mixed = dot(grad_res_low, out_full, NT).astype(bf16)
    grad_query, grad_keys, grad_values = attend_backward(
        query, keys, values, allowed, attended, log_total, grad_mixed.reshape(attended.shape)
    )
    grad_query = grad_query.reshape(token_count, query_width)
    grad_keys = grad_keys.reshape(2 * token_count, kv_width)
    grad_values = grad_values.reshape(2 * token_count, kv_width)
    away_keys = rotate_wide(grad_keys[token_count:], other_cos, other_sin, -1.0)
    away = jnp.concatenate([away_keys, grad_values[token_count:]], axis=1).astype(bf16)
    came = lax.ppermute(away, "seq", SWAP).astype(f32)
    grad_query = rotate_wide(grad_query, own_cos, own_sin, -1.0)
    grad_keys = rotate_wide(grad_keys[:token_count], own_cos, own_sin, -1.0) + came[:, :kv_width]
    grad_values = grad_values[:token_count] + came[:, kv_width:]
    grad_projected = jnp.concatenate([grad_query, grad_keys, grad_values], axis=1).astype(bf16)
    grad_projected, returned = lax.optimization_barrier((grad_projected, returned))
    grad_normed_one = dot(grad_projected, in_full, NT)
    grad_norm_one, gain_one_grad = norm_backward(row_values, inverse_one, gain_one, grad_normed_one)
    grad_inputs = (grad_residual + grad_norm_one).astype(bf16)

    owners = EXPERTS
    feature = jnp.arange(model_width)[:, None]
    slot = jnp.arange(model_width)[None, :]
    half_width = model_width // 2
    of_core = jnp.where(slot < half_width, core, 1 - core)
    at = slot % half_width
    chosen_half = feature == (2 * (at // share) + of_core) * share + at % share
    chosen_half = chosen_half.astype(bf16)
    features = dot(jnp.concatenate([normed_one, mixed], axis=0), chosen_half).astype(bf16)
    gain_pair = jnp.stack([gain_one_grad, gain_two_grad], axis=0)
    gain_parts = jnp.concatenate(three_parts(gain_pair) + (jnp.zeros_like(gain_pair, bf16),), axis=0)
    gain_parts = dot(gain_parts, chosen_half).astype(bf16)
    gain_parts = jnp.stack([gain_parts[:, :half_width], gain_parts[:, half_width:]], axis=0)
    grads_mine, grads_sent = projection_grads(
        features[:, :half_width], features[:, half_width:], grad_projected, grad_res_low, gain_parts
    )
    chip_rows = merge_halves(grads_mine, lax.ppermute(grads_sent, "core", SWAP))
    landed = lax.all_to_all(
        chip_rows.reshape(owners, share, wide + 128),
        "chip",
        split_axis=0,
        concat_axis=0,
        tiled=True,
    )
    totals = jnp.sum(landed.astype(f32), axis=0)
    totals = totals + lax.ppermute(totals, "seq", SWAP)
    gain_totals = totals[:, wide : wide + 2] + totals[:, wide + 2 : wide + 4]
    gain_totals = gain_totals + totals[:, wide + 4 : wide + 6]

    mix = jnp.concatenate(mixers, axis=1)
    chosen = dot(mix, returned, TN).reshape(3, token_count, model_width)
    output = (residual + (chosen[2] + chosen[1] + chosen[0])).astype(bf16)
    in_width = query_width + 2 * kv_width
    return (
        output.reshape(1, token_count, model_width),
        grad_inputs.reshape(1, token_count, model_width),
        totals[:, :in_width],
        totals[:, in_width:wide],
        gain_totals[:, 0],
        gain_totals[:, 1],
        grad_units[0],
        grad_units[1],
        grad_units[2],
    )


def solution(mesh):
    devices = mesh.devices
    cores = Mesh(devices.reshape(devices.shape[0], -1, 2), ("seq", "chip", "core"))
    every = ("chip", "core")
    by_token = P(every, "seq", None)
    by_row = P(every, None)
    in_specs = (
        by_token,
        by_row,
        by_row,
        P(every),
        P(every),
        by_row,
        by_row,
        by_row,
        by_token,
        by_token,
        by_row,
        by_token,
    )
    out_specs = (by_token, by_token, by_row, by_row, P(every), P(every), by_row, by_row, by_row)
    return jax.shard_map(
        on_device, mesh=cores, in_specs=in_specs, out_specs=out_specs, check_vma=False
    )
```

```python
import jax
import jax.numpy as jnp
from jax import lax
from jax.experimental import pallas as pl
from jax.experimental.pallas import tpu as pltpu
from jax.sharding import Mesh, PartitionSpec as P

HEADS = 16
KV_HEADS = 8
HEAD_DIM = 64
EXPERTS = 32
FF = 512
TOP = 8
CAP = 36
SLOTS = 40
BLOCK = 256
ROW_BLOCK = 256

EPSILON = 1e-06
ROPE_BASE = 10000.0

f32 = jnp.float32
bf16 = jnp.bfloat16

RING = 4
MESH_ID = pl.DeviceIdType.MESH
SWAP = [(0, 1), (1, 0)]
NT = (((1,), (1,)), ((), ()))
TN = (((0,), (0,)), ((), ()))


def dot(a, b, dims=(((1,), (0,)), ((), ()))):
    return lax.dot_general(a, b, dims, preferred_element_type=f32)


def rope_tables(positions):
    half_dim = HEAD_DIM // 2
    powers = jnp.arange(half_dim).astype(f32) * (2.0 / HEAD_DIM)
    inverse_freq = ROPE_BASE ** (-powers)
    angles = positions.astype(f32)[:, None] * inverse_freq[None, :]
    return (jnp.cos(angles), jnp.sin(angles))


def rotate(values, cosine_table, sine_table, turn_sign):
    half_dim = values.shape[-1] // 2
    leading = values[..., :half_dim]
    trailing = values[..., half_dim:]
    cosine_b = cosine_table[:, None, :]
    sine_b = sine_table[:, None, :] * turn_sign
    return jnp.concatenate(
        [leading * cosine_b - trailing * sine_b, trailing * cosine_b + leading * sine_b], axis=-1
    )


def rotate_wide(values, cosine_table, sine_table, turn_sign):
    rows, width = values.shape
    heads = values.reshape(rows, width // HEAD_DIM, HEAD_DIM)
    return rotate(heads, cosine_table, sine_table, turn_sign).reshape(rows, width)


def norm_forward(values, gain_vector):
    inverse = lax.rsqrt(jnp.mean(values * values, axis=-1, keepdims=True) + EPSILON)
    return ((values * inverse * gain_vector.astype(f32)).astype(bf16), inverse)


def norm_backward(values, inverse, gain_vector, upstream):
    scaled = upstream * gain_vector.astype(f32)
    grad_gain = jnp.sum(upstream * values * inverse, axis=0)
    coupling = jnp.mean(scaled * values, axis=-1, keepdims=True)
    return (inverse * scaled - values * inverse * inverse * inverse * coupling, grad_gain)


def rounded(values):
    return lax.reduce_precision(values, exponent_bits=8, mantissa_bits=7)


def three_parts(values):
    first = rounded(values)
    second = rounded(values - first)
    third = values - first - second
    return (first.astype(bf16), second.astype(bf16), third.astype(bf16))


def masked_scores(query, keys, allowed):
    scores = jnp.einsum("qkgd,skd->kgqs", query, keys, preferred_element_type=f32)
    return jnp.where(allowed[None, None], scores * HEAD_DIM ** (-0.5), -1e30)


def attend_forward(query, keys, values, allowed):
    scores = masked_scores(query, keys, allowed)
    highest = jnp.max(scores, axis=-1, keepdims=True)
    log_total = highest + jnp.log(jnp.sum(jnp.exp(scores - highest), axis=-1, keepdims=True))
    weights = jnp.exp(scores - log_total).astype(bf16)
    mixed = jnp.einsum("kgqs,skd->qkgd", weights, values, preferred_element_type=f32)
    return (mixed.astype(bf16), log_total)


def attend_backward(query, keys, values, allowed, attended, log_total, grad_attended):
    scale_factor = HEAD_DIM ** (-0.5)
    weights = jnp.exp(masked_scores(query, keys, allowed) - log_total)
    grad_values = jnp.einsum(
        "kgqs,qkgd->skd", weights.astype(bf16), grad_attended, preferred_element_type=f32
    )
    grad_weights = jnp.einsum("qkgd,skd->kgqs", grad_attended, values, preferred_element_type=f32)
    row_delta = jnp.sum(grad_attended.astype(f32) * attended.astype(f32), axis=-1)
    row_delta = jnp.transpose(row_delta, (1, 2, 0))
    grad_scores = (weights * (grad_weights - row_delta[..., None])).astype(bf16)
    grad_query = jnp.einsum("kgqs,skd->qkgd", grad_scores, keys, preferred_element_type=f32)
    grad_keys = jnp.einsum("kgqs,qkgd->skd", grad_scores, query, preferred_element_type=f32)
    return (grad_query * scale_factor, grad_keys * scale_factor, grad_values)


def experts_first_body(x_ref, g_ref, pre_w_ref, down_w_ref, hidden_ref, grads_ref, back_ref):
    pre = dot(x_ref[...], pre_w_ref[...], NT)
    grad_hidden = dot(g_ref[...], down_w_ref[...], NT)
    back = None
    for b in range(FF // BLOCK):
        gate = pre[:, 2 * b * BLOCK : (2 * b + 1) * BLOCK]
        up = pre[:, (2 * b + 1) * BLOCK : (2 * b + 2) * BLOCK]
        grad_h = grad_hidden[:, b * BLOCK : (b + 1) * BLOCK]
        sigmoid_gate = 1.0 / (1.0 + jnp.exp(-gate))
        silu = gate * sigmoid_gate
        hidden_ref[:, b * BLOCK : (b + 1) * BLOCK] = (silu * up).astype(bf16)
        grad_gate = (grad_h * up * sigmoid_gate * (1.0 + gate * (1.0 - sigmoid_gate))).astype(bf16)
        grad_up = (grad_h * gate * sigmoid_gate).astype(bf16)
        both = jnp.concatenate([grad_gate, grad_up], axis=1)
        grads_ref[:, 2 * b * BLOCK : (2 * b + 2) * BLOCK] = both
        part = dot(both, pre_w_ref[2 * b * BLOCK : (2 * b + 2) * BLOCK, :]).astype(bf16).astype(f32)
        back = part if back is None else back + part
    back_ref[...] = back.astype(bf16)


def experts_first(arrived, grad_arrived, pre_w, down_w):
    rows, width = arrived.shape
    whole = lambda i: (0, 0)
    by_row = lambda i: (i, 0)
    return pl.pallas_call(
        experts_first_body,
        grid=(rows // ROW_BLOCK,),
        in_specs=[
            pl.BlockSpec((ROW_BLOCK, width), by_row),
            pl.BlockSpec((ROW_BLOCK, width), by_row),
            pl.BlockSpec((2 * FF, width), whole),
            pl.BlockSpec((FF, width), whole),
        ],
        out_specs=[
            pl.BlockSpec((ROW_BLOCK, FF), by_row),
            pl.BlockSpec((ROW_BLOCK, 2 * FF), by_row),
            pl.BlockSpec((ROW_BLOCK, width), by_row),
        ],
        out_shape=[
            jax.ShapeDtypeStruct((rows, FF), bf16),
            jax.ShapeDtypeStruct((rows, 2 * FF), bf16),
            jax.ShapeDtypeStruct((rows, width), bf16),
        ],
        cost_estimate=pl.CostEstimate(
            flops=2 * rows * width * FF * 5,
            bytes_accessed=rows * width * 2 * 5,
            transcendentals=rows * FF,
        ),
        name="experts_first",
    )(arrived, grad_arrived, pre_w, down_w)


def experts_second_body(
    x_ref,
    g_ref,
    hidden_ref,
    grads_ref,
    down_w_ref,
    out_ref,
    total_ref,
    third_ref,
    theirs,
    came,
    last,
    low,
    low_came,
    send_sem,
    recv_sem,
):
    seq, chip, core = (lax.axis_index(name) for name in ("seq", "chip", "core"))
    partner = (seq, chip, 1 - core)
    mirror = (1 - seq, chip, core)
    barrier = pltpu.get_barrier_semaphore()
    for other in (partner, mirror):
        pl.semaphore_signal(barrier, inc=1, device_id=other, device_id_type=MESH_ID)
    pl.semaphore_wait(barrier, 2)
    width = x_ref.shape[1]

    def send(i, src, dst, to):
        return pltpu.make_async_remote_copy(
            src_ref=src,
            dst_ref=dst,
            send_sem=send_sem.at[i],
            recv_sem=recv_sem.at[i],
            device_id=to,
            device_id_type=MESH_ID,
        )

    def unit_grads(block, kind, target):
        if kind < 2:
            at = (2 * block + kind) * BLOCK
            left, right = (grads_ref, x_ref)
        else:
            at = block * BLOCK
            left, right = (hidden_ref, g_ref)

        @pl.loop(0, width // BLOCK)
        def _(n):
            columns = pl.ds(pl.multiple_of(n * BLOCK, BLOCK), BLOCK)
            target[:, columns] = dot(left[:, at : at + BLOCK], right[:, columns], TN)

    away = [send(k, theirs.at[k], came.at[k], partner) for k in range(3)]
    across = [send(3 + k, low.at[k], low_came.at[k], mirror) for k in range(2)]
    mine = [total_ref.at[0], total_ref.at[1], last]
    lows = [low.at[0], low.at[1], third_ref]
    for k in range(3):
        unit_grads(1, k, theirs.at[k])
        if k:
            away[k - 1].start()
    unit_grads(0, 0, mine[0])
    away[2].start()

    def join(k):
        away[k].wait_recv()

        @pl.loop(0, BLOCK // 32)
        def _(r):
            rows = pl.ds(pl.multiple_of(r * 32, 32), 32)
            lows[k][rows, :] = (mine[k][rows, :] + came[k, rows, :]).astype(bf16)

    for k in range(3):
        join(k)
        if k < 2:
            unit_grads(0, k + 1, mine[k + 1])
            across[k].start()

    @pl.loop(0, x_ref.shape[0] // ROW_BLOCK)
    def _(r):
        rows = pl.ds(pl.multiple_of(r * ROW_BLOCK, ROW_BLOCK), ROW_BLOCK)
        out = None
        for b in range(FF // BLOCK):
            units = slice(b * BLOCK, (b + 1) * BLOCK)
            part = dot(hidden_ref[rows, units], down_w_ref[units, :]).astype(bf16).astype(f32)
            out = part if out is None else out + part
        out_ref[rows, :] = out.astype(bf16)

    for k in range(2):
        across[k].wait_recv()

        @pl.loop(0, BLOCK // 32)
        def _(r):
            rows = pl.ds(pl.multiple_of(r * 32, 32), 32)
            total_ref[k, rows, :] = low[k, rows, :].astype(f32) + low_came[k, rows, :].astype(f32)

    for copy in away + across:
        copy.wait_send()


def experts_second(arrived, grad_arrived, hidden, grads, down_w):
    rows, width = arrived.shape
    return pl.pallas_call(
        experts_second_body,
        in_specs=[pl.BlockSpec(memory_space=pltpu.VMEM)] * 5,
        out_specs=[pl.BlockSpec(memory_space=pltpu.VMEM)] * 3,
        out_shape=[
            jax.ShapeDtypeStruct((rows, width), bf16),
            jax.ShapeDtypeStruct((2, BLOCK, width), f32),
            jax.ShapeDtypeStruct((BLOCK, width), bf16),
        ],
        scratch_shapes=[
            pltpu.VMEM((3, BLOCK, width), f32),
            pltpu.VMEM((3, BLOCK, width), f32),
            pltpu.VMEM((BLOCK, width), f32),
            pltpu.VMEM((2, BLOCK, width), bf16),
            pltpu.VMEM((2, BLOCK, width), bf16),
            pltpu.SemaphoreType.DMA((5,)),
            pltpu.SemaphoreType.DMA((5,)),
        ],
        compiler_params=pltpu.CompilerParams(collective_id=1, has_side_effects=True),
        cost_estimate=pl.CostEstimate(
            flops=2 * rows * width * FF * 4,
            bytes_accessed=rows * width * 2 * 20,
            transcendentals=0,
        ),
        name="experts_second",
    )(arrived, grad_arrived, hidden, grads, down_w)


def gather_body(shard_ref, out_ref, send_sem, recv_sem, local_sem):
    seq, chip, core = (lax.axis_index(name) for name in ("seq", "chip", "core"))
    y, z, half = (chip // (2 * RING), (chip // 2) % RING, chip % 2)

    def device(to_y, to_z, to_half, to_core):
        return (seq, (to_y * RING + to_z) * 2 + to_half, to_core)

    def first(step):
        return device((y + core * step) % RING, (z + (1 - core) * step) % RING, half, core)

    def last(step):
        return device((y + (1 - core) * step) % RING, (z + core * step) % RING, half, core)

    partner = device(y, z, half, 1 - core)
    across = device(y, z, 1 - half, core)
    ahead, behind = (1, RING - 1)
    barrier = pltpu.get_barrier_semaphore()
    for other in (partner, across, first(ahead), first(behind), last(ahead), last(behind)):
        pl.semaphore_signal(barrier, inc=1, device_id=other, device_id_type=MESH_ID)
    pl.semaphore_wait(barrier, 6)

    def send(i, src, dst, to):
        return pltpu.make_async_remote_copy(
            src_ref=src,
            dst_ref=dst,
            send_sem=send_sem.at[i],
            recv_sem=recv_sem.at[i],
            device_id=to,
            device_id_type=MESH_ID,
        )

    def line(c, step, part=None):
        cut = slice(None) if part is None else pl.ds(part * (RING // 2), RING // 2)
        if c == 0:
            return out_ref.at[(y + step) % RING, cut, :, 0]
        return out_ref.at[cut, (z + step) % RING, :, 1]

    def pair(c, step, part=None):
        cut = slice(None) if part is None else part
        if c == 0:
            return out_ref.at[y, (z + step) % RING, cut, 0]
        return out_ref.at[(y + step) % RING, z, cut, 1]

    def run(c):
        sent = []

        def go(i, region, to):
            copy = send(i, region, region, to)
            copy.start()
            sent.append(copy)

        def arrive(i, region):
            send(i, region, region, partner).wait_recv()

        own = out_ref.at[y, z, half, c]
        copy = send(0, shard_ref, own, across)
        copy.start()
        sent.append(copy)
        local = pltpu.make_async_copy(shard_ref, own, local_sem)
        local.start()
        local.wait()
        arrive(0, out_ref.at[y, z, 1 - half, c])
        go(1, pair(c, 0), first(ahead))
        go(2, pair(c, 0), first(behind))
        arrive(1, pair(c, behind))
        go(3, pair(c, behind, 0), first(ahead))
        arrive(2, pair(c, ahead))
        go(4, pair(c, ahead, 1), first(behind))
        arrive(3, pair(c, 2, 0))
        arrive(4, pair(c, 2, 1))
        go(5, line(c, 0), last(ahead))
        go(6, line(c, 0), last(behind))
        go(9, line(c, 0), partner)
        arrive(5, line(c, behind))
        go(7, line(c, behind, 0), last(ahead))
        go(10, line(c, behind), partner)
        arrive(6, line(c, ahead))
        go(8, line(c, ahead, 1), last(behind))
        go(11, line(c, ahead), partner)
        arrive(7, line(c, 2, 0))
        go(12, line(c, 2, 0), partner)
        arrive(8, line(c, 2, 1))
        go(13, line(c, 2, 1), partner)
        arrive(9, line(1 - c, 0))
        arrive(10, line(1 - c, behind))
        arrive(11, line(1 - c, ahead))
        arrive(12, line(1 - c, 2, 0))
        arrive(13, line(1 - c, 2, 1))
        for copy in sent:
            copy.wait_send()

    for c in (0, 1):
        pl.when(core == c)(lambda c=c: run(c))


def gather_weights(shard):
    rows, width = shard.shape
    out = pl.pallas_call(
        gather_body,
        out_shape=jax.ShapeDtypeStruct((RING, RING, 2, 2, rows, width), shard.dtype),
        in_specs=[pl.BlockSpec(memory_space=pltpu.VMEM)],
        out_specs=pl.BlockSpec(memory_space=pl.ANY),
        scratch_shapes=[
            pltpu.SemaphoreType.DMA((14,)),
            pltpu.SemaphoreType.DMA((14,)),
            pltpu.SemaphoreType.DMA,
        ],
        compiler_params=pltpu.CompilerParams(collective_id=0, has_side_effects=True),
        cost_estimate=pl.CostEstimate(
            flops=0, bytes_accessed=rows * width * 2 * 4 * RING * RING * 8, transcendentals=0
        ),
        name="gather_weights",
    )(shard)
    return out.reshape(4 * RING * RING * rows, width)


def projection_grads_body(mine_ref, sent_ref, gq_ref, gkv_ref, gr_ref, gains_ref, total_ref, away_ref):
    query = gq_ref.shape[1]
    width = query + gkv_ref.shape[1]
    wide = width + gr_ref.shape[1]
    spread = lax.broadcasted_iota(jnp.int32, (8, 128), 0)
    lane = lax.broadcasted_iota(jnp.int32, (8, 128), 1)
    apart = ((spread == lane) & (spread < 6)).astype(bf16)
    tokens = gq_ref.shape[0]
    for ref, out_ref, which in ((mine_ref, total_ref, 0), (sent_ref, away_ref, 1)):
        out_ref[:, :query] = dot(ref[:tokens, :], gq_ref[...], TN).astype(out_ref.dtype)
        out_ref[:, query:width] = dot(ref[: 2 * tokens, :], gkv_ref[...], TN).astype(out_ref.dtype)
        out_ref[:, width:wide] = dot(ref[2 * tokens :, :], gr_ref[...], TN).astype(out_ref.dtype)
        out_ref[:, wide:] = dot(gains_ref[which], apart, TN).astype(out_ref.dtype)


def projection_grads(rows_mine, rows_sent, grad_query, grad_kv, grad_res_low, gains):
    count = rows_mine.shape[1]
    width = grad_query.shape[1] + grad_kv.shape[1] + grad_res_low.shape[1] + 128
    tile = 128
    whole = lambda i: (0, 0)
    by_column = lambda i: (0, i)
    by_row = lambda i: (i, 0)
    return pl.pallas_call(
        projection_grads_body,
        grid=(count // tile,),
        in_specs=[
            pl.BlockSpec((rows_mine.shape[0], tile), by_column),
            pl.BlockSpec((rows_sent.shape[0], tile), by_column),
            pl.BlockSpec(grad_query.shape, whole),
            pl.BlockSpec(grad_kv.shape, whole),
            pl.BlockSpec(grad_res_low.shape, whole),
            pl.BlockSpec((2, 8, tile), lambda i: (0, 0, i)),
        ],
        out_specs=[pl.BlockSpec((tile, width), by_row), pl.BlockSpec((tile, width), by_row)],
        out_shape=[
            jax.ShapeDtypeStruct((count, width), f32),
            jax.ShapeDtypeStruct((count, width), bf16),
        ],
        name="projection_grads",
    )(rows_mine, rows_sent, grad_query, grad_kv, grad_res_low, gains)


def packed(values):
    lane = lax.broadcasted_iota(jnp.int32, (values.shape[0], 128), 1)
    wide = values.shape[1] - 128
    parts = values[:, wide:]
    total = parts + pltpu.roll(parts, 126, 1) + pltpu.roll(parts, 124, 1)
    total = jnp.where(lane < 2, total, 0.0)
    one = total.astype(bf16).astype(f32)
    two = (total - one).astype(bf16).astype(f32)
    three = total - one - two
    tail = one + pltpu.roll(two, 2, 1) + pltpu.roll(three, 4, 1)
    return jnp.concatenate([values[:, :wide].astype(bf16), tail.astype(bf16)], axis=1)


def reduce_body(
    mine,
    sent,
    low,
    total_ref,
    unit_ref,
    came,
    acc,
    stage,
    in1,
    in2,
    stage_a,
    in_a1,
    in_a2,
    stage_x,
    in_x,
    own,
    in_own,
    low_came,
    chip_send,
    chip_recv,
    ring_send,
    ring_recv,
):
    seq, chip, core = (lax.axis_index(name) for name in ("seq", "chip", "core"))
    y, z, half = (chip // (2 * RING), (chip // 2) % RING, chip % 2)
    flip = 1 - core
    at_last = flip * y + core * z
    at_first = flip * z + core * y

    def device(to_y, to_z, to_half, to_core):
        return (seq, (to_y * RING + to_z) * 2 + to_half, to_core)

    def first(step):
        return device((y + core * step) % RING, (z + flip * step) % RING, half, core)

    def last(step):
        return device((y + flip * step) % RING, (z + core * step) % RING, half, core)

    partner = device(y, z, half, flip)
    across = device(y, z, 1 - half, core)
    mirror = (1 - seq, chip, core)
    ahead, behind = (1, RING - 1)
    barrier = pltpu.get_barrier_semaphore()
    others = (partner, across, mirror, first(ahead), first(behind), last(ahead), last(behind))
    for other in others:
        pl.semaphore_signal(barrier, inc=1, device_id=other, device_id_type=MESH_ID)
    pl.semaphore_wait(barrier, len(others))

    def send(i, src, dst, to):
        return pltpu.make_async_remote_copy(
            src_ref=src,
            dst_ref=dst,
            send_sem=ring_send.at[i],
            recv_sem=ring_recv.at[i],
            device_id=to,
            device_id_type=MESH_ID,
        )

    def on_chip(s, j, of_core):
        line = ((1 - of_core) * y + of_core * z + s) % RING
        a = (1 - of_core) * line + of_core * j
        b = (1 - of_core) * j + of_core * line
        return (
            a,
            b,
            pltpu.make_async_remote_copy(
                src_ref=sent.at[a, b],
                dst_ref=came.at[a, b],
                send_sem=chip_send.at[s, j],
                recv_sem=chip_recv.at[s, j],
                device_id=partner,
                device_id_type=MESH_ID,
            ),
        )

    order = (2, ahead, behind, 0)
    two = RING // 2
    units = send(12, low, low_came, mirror)
    units.start()
    for s in order:

        @pl.loop(0, RING)
        def _(j):
            on_chip(s, j, flip)[2].start()

    ring = [
        send(0, stage.at[2, :two], in1.at[0], last(ahead)),
        send(1, stage.at[2, two:], in1.at[1], last(behind)),
        send(2, stage.at[1, two:], in2.at[0, two:], last(ahead)),
        send(3, stage.at[1, :two], in2.at[0, :two], last(ahead)),
        send(4, stage.at[3, :two], in2.at[1, :two], last(behind)),
        send(5, stage.at[3, two:], in2.at[1, two:], last(behind)),
        send(6, stage_a.at[2, 0], in_a1.at[0], first(ahead)),
        send(7, stage_a.at[2, 1], in_a1.at[1], first(behind)),
        send(8, stage_a.at[1], in_a2.at[0], first(ahead)),
        send(9, stage_a.at[3], in_a2.at[1], first(behind)),
        send(10, stage_x, in_x, across),
        send(11, own, in_own, mirror),
    ]

    def merge(s, low_j, high_j, to_stage):
        @pl.loop(low_j, high_j)
        def _(j):
            a, b, copy = on_chip(s, j, core)
            copy.wait_recv()
            for h in range(2):
                value = mine[a, b, h] + came[a, b, h].astype(f32)
                if to_stage:
                    stage[s, j, h] = packed(value)
                if not to_stage or s != 2:
                    acc[s, j, h] = value

    merge(2, 0, RING, True)
    ring[0].start()
    ring[1].start()
    merge(ahead, 0, RING, True)
    ring[2].start()
    merge(behind, 0, RING, True)
    ring[4].start()
    merge(0, 0, RING, False)
    for i, s, source, first_j in ((0, ahead, 0, 0), (1, behind, 1, two)):
        ring[i].wait_recv()

        @pl.loop(0, two)
        def _(k):
            for h in range(2):
                value = acc[s, first_j + k, h] + in1[source, k, h].astype(f32)
                stage[s, first_j + k, h] = packed(value)

        ring[3 if i == 0 else 5].start()

    for i, source, first_j in ((2, 0, two), (4, 1, 0), (3, 0, 0), (5, 1, two)):
        ring[i].wait_recv()

        @pl.loop(first_j, first_j + two)
        def _(j):
            for h in range(2):
                acc[0, j, h] = acc[0, j, h] + in2[source, j, h].astype(f32)

    def at(step):
        return (at_first + step) % RING

    for h in range(2):
        stage_a[2, h] = packed(acc[0, at(2), h])
    ring[6].start()
    ring[7].start()
    stage_a[1, 1] = packed(acc[0, at(ahead), 1])
    stage_a[3, 0] = packed(acc[0, at(behind), 0])
    ring[6].wait_recv()
    stage_a[1, 0] = packed(acc[0, at(ahead), 0] + in_a1[0].astype(f32))
    ring[8].start()
    ring[7].wait_recv()
    stage_a[3, 1] = packed(acc[0, at(behind), 1] + in_a1[1].astype(f32))
    ring[9].start()
    ring[8].wait_recv()
    ring[9].wait_recv()
    away = 1 - half
    stage_x[...] = packed(
        acc[0, at_first, away] + in_a2[0, away].astype(f32) + in_a2[1, away].astype(f32)
    )
    ring[10].start()
    own[...] = acc[0, at_first, half] + in_a2[0, half].astype(f32) + in_a2[1, half].astype(f32)
    ring[10].wait_recv()
    own[...] = own[...] + in_x[...].astype(f32)
    ring[11].start()
    units.wait_recv()

    @pl.loop(0, low.shape[0] // 32)
    def _(r):
        rows = pl.ds(pl.multiple_of(r * 32, 32), 32)
        unit_ref[rows, :] = low[rows, :].astype(f32) + low_came[rows, :].astype(f32)

    ring[11].wait_recv()
    total_ref[...] = own[...] + in_own[...]
    units.wait_send()
    for copy in ring:
        copy.wait_send()
    for s in order:

        @pl.loop(0, RING)
        def _(j):
            on_chip(s, j, flip)[2].wait_send()


def reduce_grads(mine, sent, low):
    width = mine.shape[1]
    share = mine.shape[0] // (2 * RING * RING)
    shape = (RING, RING, 2, share, width)
    two = RING // 2
    pair = (2, share, width)
    return pl.pallas_call(
        reduce_body,
        in_specs=[pl.BlockSpec(memory_space=pltpu.VMEM)] * 3,
        out_specs=[pl.BlockSpec(memory_space=pltpu.VMEM)] * 2,
        out_shape=[
            jax.ShapeDtypeStruct((share, width), f32),
            jax.ShapeDtypeStruct(low.shape, f32),
        ],
        scratch_shapes=[
            pltpu.VMEM(shape, bf16),
            pltpu.VMEM(shape, f32),
            pltpu.VMEM(shape, bf16),
            pltpu.VMEM((2, two) + pair, bf16),
            pltpu.VMEM((2, RING) + pair, bf16),
            pltpu.VMEM((RING,) + pair, bf16),
            pltpu.VMEM(pair, bf16),
            pltpu.VMEM((2,) + pair, bf16),
            pltpu.VMEM((share, width), bf16),
            pltpu.VMEM((share, width), bf16),
            pltpu.VMEM((share, width), f32),
            pltpu.VMEM((share, width), f32),
            pltpu.VMEM(low.shape, bf16),
            pltpu.SemaphoreType.DMA((RING, RING)),
            pltpu.SemaphoreType.DMA((RING, RING)),
            pltpu.SemaphoreType.DMA((13,)),
            pltpu.SemaphoreType.DMA((13,)),
        ],
        compiler_params=pltpu.CompilerParams(collective_id=2, has_side_effects=True),
        cost_estimate=pl.CostEstimate(
            flops=mine.size * 8, bytes_accessed=mine.size * 60, transcendentals=0
        ),
        name="reduce_grads",
    )(mine.reshape(shape), sent.reshape(shape), low)


def spread_plan(route_ids, mix_weights):
    token_count = route_ids.shape[0]
    expert_ids = jnp.arange(EXPERTS)[None, None, :]
    named = route_ids[:, :, None] == expert_ids
    picked = jnp.any(named, axis=1)
    token_weight = jnp.sum(jnp.where(named, mix_weights[:, :, None], 0.0), axis=1)
    earlier = jnp.arange(token_count)[None, :] < jnp.arange(token_count)[:, None]
    rank = dot(earlier.astype(bf16), picked.astype(bf16)).astype(jnp.int32)
    at_slot = jnp.where(picked, rank, -1).T[:, None, :] == jnp.arange(SLOTS)[None, :, None]
    placed = at_slot.astype(bf16).reshape(EXPERTS * SLOTS, token_count)
    weighted = jnp.where(at_slot, token_weight.T[:, None, :], 0.0)
    slot_weight = jnp.sum(weighted, axis=2).reshape(EXPERTS * SLOTS, 1)
    mixers = [part.reshape(EXPERTS * SLOTS, token_count) for part in three_parts(weighted)]
    return (placed, slot_weight, mixers)


def exchange(rows):
    width = rows.shape[-1]
    blocks = rows.reshape(EXPERTS, -1, width)
    return lax.all_to_all(blocks, "chip", split_axis=0, concat_axis=0, tiled=True).reshape(-1, width)


def on_device(
    inputs,
    project_in,
    project_out,
    gain_attend,
    gain_expert,
    expert_gate,
    expert_up,
    expert_down,
    routes,
    route_weights,
    segments,
    cotangent,
):
    token_count = inputs.shape[1]
    model_width = inputs.shape[2]
    query_width = HEADS * HEAD_DIM
    kv_width = KV_HEADS * HEAD_DIM
    group = HEADS // KV_HEADS
    seq = lax.axis_index("seq")
    core = lax.axis_index("core")
    own_low = inputs[0]
    other_low = lax.ppermute(own_low, "seq", SWAP)

    placed, slot_weight, mixers = spread_plan(routes[0], route_weights[0])
    grad_rows = (dot(placed, cotangent[0]) * slot_weight).astype(bf16)

    own_units = jnp.concatenate([expert_gate, expert_up, expert_down], axis=0)
    other_units = lax.ppermute(own_units, "core", SWAP)
    pre_w = jnp.concatenate([own_units[: 2 * BLOCK], other_units[: 2 * BLOCK]], axis=0)
    down_w = jnp.concatenate([expert_down, other_units[2 * BLOCK :]], axis=0)

    share = gain_attend.shape[0]
    wide = query_width + 2 * kv_width + query_width
    filler = jnp.zeros((share, 126), bf16)
    gathered = gather_weights(
        jnp.concatenate(
            [project_in, project_out, gain_attend[:, None], gain_expert[:, None], filler], axis=1
        )
    )
    gathered, grad_rows = lax.optimization_barrier((gathered, grad_rows))
    grad_arrived = exchange(grad_rows)
    in_full = gathered[:, : query_width + 2 * kv_width]
    out_full = gathered[:, query_width + 2 * kv_width : wide]
    gain_one, gain_two = (gathered[:, wide], gathered[:, wide + 1])

    row_values = own_low.astype(f32)
    normed_one, inverse_one = norm_forward(row_values, gain_one)
    normed_other, inverse_other = norm_forward(other_low.astype(f32), gain_one)
    kv_w = in_full[:, query_width:]
    projected = dot(normed_one, in_full)
    projected_other = dot(normed_other, kv_w)
    own_at = seq * token_count + jnp.arange(token_count)
    other_at = (1 - seq) * token_count + jnp.arange(token_count)
    own_cos, own_sin = rope_tables(own_at)
    other_cos, other_sin = rope_tables(other_at)
    query = rotate_wide(projected[:, :query_width], own_cos, own_sin, 1.0).astype(bf16)
    key_cut = query_width + kv_width
    own_keys = rotate_wide(projected[:, query_width:key_cut], own_cos, own_sin, 1.0)
    other_keys = rotate_wide(projected_other[:, :kv_width], other_cos, other_sin, 1.0)
    keys = jnp.concatenate([own_keys, other_keys], axis=0).astype(bf16)
    values = jnp.concatenate([projected[:, key_cut:], projected_other[:, kv_width:]], axis=0)
    query = query.reshape(token_count, KV_HEADS, group, HEAD_DIM)
    keys = keys.reshape(2 * token_count, KV_HEADS, HEAD_DIM)
    values = values.astype(bf16).reshape(2 * token_count, KV_HEADS, HEAD_DIM)
    seq_ids = segments[0]
    own_ids = lax.dynamic_slice(seq_ids, (seq * token_count,), (token_count,))
    other_ids = lax.dynamic_slice(seq_ids, ((1 - seq) * token_count,), (token_count,))
    key_at = jnp.concatenate([own_at, other_at])
    key_ids = jnp.concatenate([own_ids, other_ids])
    allowed = (key_at[None, :] <= own_at[:, None]) & (key_ids[None, :] == own_ids[:, None])
    attended, log_total = attend_forward(query, keys, values, allowed)
    mixed = attended.reshape(token_count, query_width)
    residual = row_values + dot(mixed, out_full)
    normed_two, inverse_two = norm_forward(residual, gain_two)

    arrived = exchange(dot(placed, normed_two).astype(bf16))
    hidden, grads, back = experts_first(arrived, grad_arrived, pre_w, down_w)
    grad_back = exchange(back)
    out_rows, grad_units, third_low = experts_second(arrived, grad_arrived, hidden, grads, down_w)
    grad_back, out_rows = lax.optimization_barrier((grad_back, out_rows))
    returned = exchange(out_rows)

    grad_out = cotangent[0].astype(f32)
    grad_normed_two = dot(placed, grad_back, TN)
    grad_norm_two, gain_two_grad = norm_backward(residual, inverse_two, gain_two, grad_normed_two)
    grad_residual = grad_out + grad_norm_two
    grad_res_low = grad_residual.astype(bf16)
    grad_mixed = dot(grad_res_low, out_full, NT).astype(bf16)
    grad_query, grad_keys, grad_values = attend_backward(
        query, keys, values, allowed, attended, log_total, grad_mixed.reshape(attended.shape)
    )
    grad_query = grad_query.reshape(token_count, query_width)
    grad_keys = grad_keys.reshape(2 * token_count, kv_width)
    grad_values = grad_values.reshape(2 * token_count, kv_width)
    away_keys = rotate_wide(grad_keys[token_count:], other_cos, other_sin, -1.0)
    away = jnp.concatenate([away_keys, grad_values[token_count:]], axis=1).astype(bf16)
    came = lax.ppermute(away, "seq", SWAP)
    grad_query = rotate_wide(grad_query, own_cos, own_sin, -1.0).astype(bf16)
    grad_keys = rotate_wide(grad_keys[:token_count], own_cos, own_sin, -1.0)
    grad_kv = jnp.concatenate([grad_keys, grad_values[:token_count]], axis=1).astype(bf16)
    from_query = dot(grad_query, in_full[:, :query_width], NT)
    from_kv = dot(jnp.concatenate([grad_kv, away], axis=0), kv_w, NT)
    from_own = from_query + from_kv[:token_count]
    other_values = other_low.astype(f32)
    gain_one_grad = jnp.sum(from_own * row_values * inverse_one, axis=0)
    gain_one_grad += jnp.sum(from_kv[token_count:] * other_values * inverse_other, axis=0)

    feature = jnp.arange(model_width)[:, None]
    slot = jnp.arange(model_width)[None, :]
    half_width = model_width // 2
    of_core = jnp.where(slot < half_width, core, 1 - core)
    at = slot % half_width
    chosen_half = feature == (2 * (at // share) + of_core) * share + at % share
    chosen_half = chosen_half.astype(bf16)
    features = jnp.concatenate([normed_one, normed_other, mixed], axis=0)
    features = dot(features, chosen_half).astype(bf16)
    gain_pair = jnp.stack([gain_one_grad, gain_two_grad], axis=0)
    gain_parts = jnp.concatenate(three_parts(gain_pair) + (jnp.zeros_like(gain_pair, bf16),), axis=0)
    gain_parts = dot(gain_parts, chosen_half).astype(bf16)
    gain_parts = jnp.stack([gain_parts[:, :half_width], gain_parts[:, half_width:]], axis=0)
    grads_mine, grads_sent = projection_grads(
        features[:, :half_width],
        features[:, half_width:],
        grad_query,
        jnp.concatenate([grad_kv, away], axis=0),
        grad_res_low,
        gain_parts,
    )
    totals, third_total = reduce_grads(grads_mine, grads_sent, third_low)
    gain_totals = totals[:, wide : wide + 2] + totals[:, wide + 2 : wide + 4]
    gain_totals = gain_totals + totals[:, wide + 4 : wide + 6]

    grad_normed_one = from_own + dot(came, kv_w, NT)
    grad_norm_one, _ = norm_backward(row_values, inverse_one, gain_one, grad_normed_one)
    grad_inputs = (grad_residual + grad_norm_one).astype(bf16)

    mix = jnp.concatenate(mixers, axis=1)
    chosen = dot(mix, returned, TN).reshape(3, token_count, model_width)
    output = (residual + (chosen[2] + chosen[1] + chosen[0])).astype(bf16)
    in_width = query_width + 2 * kv_width
    return (
        output.reshape(1, token_count, model_width),
        grad_inputs.reshape(1, token_count, model_width),
        totals[:, :in_width],
        totals[:, in_width:wide],
        gain_totals[:, 0],
        gain_totals[:, 1],
        grad_units[0],
        grad_units[1],
        third_total,
    )


def solution(mesh):
    devices = mesh.devices
    cores = Mesh(devices.reshape(devices.shape[0], -1, 2), ("seq", "chip", "core"))
    every = ("chip", "core")
    by_token = P(every, "seq", None)
    by_row = P(every, None)
    in_specs = (
        by_token,
        by_row,
        by_row,
        P(every),
        P(every),
        by_row,
        by_row,
        by_row,
        by_token,
        by_token,
        by_row,
        by_token,
    )
    out_specs = (by_token, by_token, by_row, by_row, P(every), P(every), by_row, by_row, by_row)
    return jax.shard_map(
        on_device, mesh=cores, in_specs=in_specs, out_specs=out_specs, check_vma=False
    )
```

```python
import jax
import jax.numpy as jnp
from jax import lax
from jax.experimental import pallas as pl
from jax.experimental.pallas import tpu as pltpu
from jax.sharding import Mesh, PartitionSpec as P

HEADS = 16
KV_HEADS = 8
HEAD_DIM = 64
EXPERTS = 32
FF = 512
TOP = 8
CAP = 36
SLOTS = 40
BLOCK = 256
ROW_BLOCK = 256

EPSILON = 1e-06
ROPE_BASE = 10000.0

f32 = jnp.float32
bf16 = jnp.bfloat16

RING = 4
MESH_ID = pl.DeviceIdType.MESH
SWAP = [(0, 1), (1, 0)]
NT = (((1,), (1,)), ((), ()))
TN = (((0,), (0,)), ((), ()))


def dot(a, b, dims=(((1,), (0,)), ((), ()))):
    return lax.dot_general(a, b, dims, preferred_element_type=f32)


def rope_tables(positions):
    half_dim = HEAD_DIM // 2
    powers = jnp.arange(half_dim).astype(f32) * (2.0 / HEAD_DIM)
    inverse_freq = ROPE_BASE ** (-powers)
    angles = positions.astype(f32)[:, None] * inverse_freq[None, :]
    return (jnp.cos(angles), jnp.sin(angles))


def rotate(values, cosine_table, sine_table, turn_sign):
    half_dim = values.shape[-1] // 2
    leading = values[..., :half_dim]
    trailing = values[..., half_dim:]
    cosine_b = cosine_table[:, None, :]
    sine_b = sine_table[:, None, :] * turn_sign
    return jnp.concatenate(
        [leading * cosine_b - trailing * sine_b, trailing * cosine_b + leading * sine_b], axis=-1
    )


def rotate_wide(values, cosine_table, sine_table, turn_sign):
    rows, width = values.shape
    heads = values.reshape(rows, width // HEAD_DIM, HEAD_DIM)
    return rotate(heads, cosine_table, sine_table, turn_sign).reshape(rows, width)


def norm_forward(values, gain_vector):
    inverse = lax.rsqrt(jnp.mean(values * values, axis=-1, keepdims=True) + EPSILON)
    return ((values * inverse * gain_vector.astype(f32)).astype(bf16), inverse)


def norm_backward(values, inverse, gain_vector, upstream):
    scaled = upstream * gain_vector.astype(f32)
    grad_gain = jnp.sum(upstream * values * inverse, axis=0)
    coupling = jnp.mean(scaled * values, axis=-1, keepdims=True)
    return (inverse * scaled - values * inverse * inverse * inverse * coupling, grad_gain)


def rounded(values):
    return lax.reduce_precision(values, exponent_bits=8, mantissa_bits=7)


def three_parts(values):
    first = rounded(values)
    second = rounded(values - first)
    third = values - first - second
    return (first.astype(bf16), second.astype(bf16), third.astype(bf16))


def masked_scores(query, keys, allowed):
    scores = jnp.einsum("qkgd,skd->kgqs", query, keys, preferred_element_type=f32)
    return jnp.where(allowed[None, None], scores * HEAD_DIM ** (-0.5), -1e30)


def attend_forward(query, keys, values, allowed):
    scores = masked_scores(query, keys, allowed)
    highest = jnp.max(scores, axis=-1, keepdims=True)
    log_total = highest + jnp.log(jnp.sum(jnp.exp(scores - highest), axis=-1, keepdims=True))
    weights = jnp.exp(scores - log_total).astype(bf16)
    mixed = jnp.einsum("kgqs,skd->qkgd", weights, values, preferred_element_type=f32)
    return (mixed.astype(bf16), log_total)


def attend_backward(query, keys, values, allowed, attended, log_total, grad_attended):
    scale_factor = HEAD_DIM ** (-0.5)
    weights = jnp.exp(masked_scores(query, keys, allowed) - log_total)
    grad_values = jnp.einsum(
        "kgqs,qkgd->skd", weights.astype(bf16), grad_attended, preferred_element_type=f32
    )
    grad_weights = jnp.einsum("qkgd,skd->kgqs", grad_attended, values, preferred_element_type=f32)
    row_delta = jnp.sum(grad_attended.astype(f32) * attended.astype(f32), axis=-1)
    row_delta = jnp.transpose(row_delta, (1, 2, 0))
    grad_scores = (weights * (grad_weights - row_delta[..., None])).astype(bf16)
    grad_query = jnp.einsum("kgqs,skd->qkgd", grad_scores, keys, preferred_element_type=f32)
    grad_keys = jnp.einsum("kgqs,qkgd->skd", grad_scores, query, preferred_element_type=f32)
    return (grad_query * scale_factor, grad_keys * scale_factor, grad_values)


def experts_first_body(x_ref, g_ref, pre_w_ref, down_w_ref, hidden_ref, grads_ref, back_ref):
    pre = dot(x_ref[...], pre_w_ref[...], NT)
    grad_hidden = dot(g_ref[...], down_w_ref[...], NT)
    back = None
    for b in range(FF // BLOCK):
        gate = pre[:, 2 * b * BLOCK : (2 * b + 1) * BLOCK]
        up = pre[:, (2 * b + 1) * BLOCK : (2 * b + 2) * BLOCK]
        grad_h = grad_hidden[:, b * BLOCK : (b + 1) * BLOCK]
        sigmoid_gate = 1.0 / (1.0 + jnp.exp(-gate))
        silu = gate * sigmoid_gate
        hidden_ref[:, b * BLOCK : (b + 1) * BLOCK] = (silu * up).astype(bf16)
        grad_gate = (grad_h * up * sigmoid_gate * (1.0 + gate * (1.0 - sigmoid_gate))).astype(bf16)
        grad_up = (grad_h * gate * sigmoid_gate).astype(bf16)
        both = jnp.concatenate([grad_gate, grad_up], axis=1)
        grads_ref[:, 2 * b * BLOCK : (2 * b + 2) * BLOCK] = both
        part = dot(both, pre_w_ref[2 * b * BLOCK : (2 * b + 2) * BLOCK, :]).astype(bf16).astype(f32)
        back = part if back is None else back + part
    back_ref[...] = back.astype(bf16)


def experts_first(arrived, grad_arrived, pre_w, down_w):
    rows, width = arrived.shape
    whole = lambda i: (0, 0)
    by_row = lambda i: (i, 0)
    return pl.pallas_call(
        experts_first_body,
        grid=(rows // ROW_BLOCK,),
        in_specs=[
            pl.BlockSpec((ROW_BLOCK, width), by_row),
            pl.BlockSpec((ROW_BLOCK, width), by_row),
            pl.BlockSpec((2 * FF, width), whole),
            pl.BlockSpec((FF, width), whole),
        ],
        out_specs=[
            pl.BlockSpec((ROW_BLOCK, FF), by_row),
            pl.BlockSpec((ROW_BLOCK, 2 * FF), by_row),
            pl.BlockSpec((ROW_BLOCK, width), by_row),
        ],
        out_shape=[
            jax.ShapeDtypeStruct((rows, FF), bf16),
            jax.ShapeDtypeStruct((rows, 2 * FF), bf16),
            jax.ShapeDtypeStruct((rows, width), bf16),
        ],
        cost_estimate=pl.CostEstimate(
            flops=2 * rows * width * FF * 5,
            bytes_accessed=rows * width * 2 * 5,
            transcendentals=rows * FF,
        ),
        name="experts_first",
    )(arrived, grad_arrived, pre_w, down_w)


def experts_second_body(
    x_ref,
    g_ref,
    hidden_ref,
    grads_ref,
    down_w_ref,
    out_ref,
    total_ref,
    rest_ref,
    theirs,
    came,
    last,
    low,
    low_came,
    send_sem,
    recv_sem,
):
    seq, chip, core = (lax.axis_index(name) for name in ("seq", "chip", "core"))
    partner = (seq, chip, 1 - core)
    mirror = (1 - seq, chip, core)
    barrier = pltpu.get_barrier_semaphore()
    for other in (partner, mirror):
        pl.semaphore_signal(barrier, inc=1, device_id=other, device_id_type=MESH_ID)
    pl.semaphore_wait(barrier, 2)
    width = x_ref.shape[1]

    def send(i, src, dst, to):
        return pltpu.make_async_remote_copy(
            src_ref=src,
            dst_ref=dst,
            send_sem=send_sem.at[i],
            recv_sem=recv_sem.at[i],
            device_id=to,
            device_id_type=MESH_ID,
        )

    def unit_grads(block, kind, target):
        if kind < 2:
            at = (2 * block + kind) * BLOCK
            left, right = (grads_ref, x_ref)
        else:
            at = block * BLOCK
            left, right = (hidden_ref, g_ref)

        @pl.loop(0, width // BLOCK)
        def _(n):
            columns = pl.ds(pl.multiple_of(n * BLOCK, BLOCK), BLOCK)
            target[:, columns] = dot(left[:, at : at + BLOCK], right[:, columns], TN)

    away = [send(k, theirs.at[k], came.at[k], partner) for k in range(3)]
    across = [send(3 + k, low.at[k], low_came.at[k], mirror) for k in range(1)]
    mine = [total_ref, last.at[0], last.at[1]]
    lows = [low.at[0], rest_ref.at[0], rest_ref.at[1]]
    for k in range(3):
        unit_grads(1, k, theirs.at[k])
        if k:
            away[k - 1].start()
    unit_grads(0, 0, mine[0])
    away[2].start()

    def join(k):
        away[k].wait_recv()

        @pl.loop(0, BLOCK // 32)
        def _(r):
            rows = pl.ds(pl.multiple_of(r * 32, 32), 32)
            lows[k][rows, :] = (mine[k][rows, :] + came[k, rows, :]).astype(bf16)

    for k in range(3):
        join(k)
        if k < 2:
            unit_grads(0, k + 1, mine[k + 1])
        if k < len(across):
            across[k].start()

    @pl.loop(0, x_ref.shape[0] // ROW_BLOCK)
    def _(r):
        rows = pl.ds(pl.multiple_of(r * ROW_BLOCK, ROW_BLOCK), ROW_BLOCK)
        out = None
        for b in range(FF // BLOCK):
            units = slice(b * BLOCK, (b + 1) * BLOCK)
            part = dot(hidden_ref[rows, units], down_w_ref[units, :]).astype(bf16).astype(f32)
            out = part if out is None else out + part
        out_ref[rows, :] = out.astype(bf16)

    for k in range(len(across)):
        across[k].wait_recv()

        @pl.loop(0, BLOCK // 32)
        def _(r):
            rows = pl.ds(pl.multiple_of(r * 32, 32), 32)
            mine[k][rows, :] = low[k, rows, :].astype(f32) + low_came[k, rows, :].astype(f32)

    for copy in away + across:
        copy.wait_send()


def experts_second(arrived, grad_arrived, hidden, grads, down_w):
    rows, width = arrived.shape
    return pl.pallas_call(
        experts_second_body,
        in_specs=[pl.BlockSpec(memory_space=pltpu.VMEM)] * 5,
        out_specs=[pl.BlockSpec(memory_space=pltpu.VMEM)] * 3,
        out_shape=[
            jax.ShapeDtypeStruct((rows, width), bf16),
            jax.ShapeDtypeStruct((BLOCK, width), f32),
            jax.ShapeDtypeStruct((2, BLOCK, width), bf16),
        ],
        scratch_shapes=[
            pltpu.VMEM((3, BLOCK, width), f32),
            pltpu.VMEM((3, BLOCK, width), f32),
            pltpu.VMEM((2, BLOCK, width), f32),
            pltpu.VMEM((1, BLOCK, width), bf16),
            pltpu.VMEM((1, BLOCK, width), bf16),
            pltpu.SemaphoreType.DMA((4,)),
            pltpu.SemaphoreType.DMA((4,)),
        ],
        compiler_params=pltpu.CompilerParams(collective_id=1, has_side_effects=True),
        cost_estimate=pl.CostEstimate(
            flops=2 * rows * width * FF * 4,
            bytes_accessed=rows * width * 2 * 20,
            transcendentals=0,
        ),
        name="experts_second",
    )(arrived, grad_arrived, hidden, grads, down_w)


def gather_body(shard_ref, out_ref, send_sem, recv_sem, local_sem):
    seq, chip, core = (lax.axis_index(name) for name in ("seq", "chip", "core"))
    y, z, half = (chip // (2 * RING), (chip // 2) % RING, chip % 2)

    def device(to_y, to_z, to_half, to_core):
        return (seq, (to_y * RING + to_z) * 2 + to_half, to_core)

    def first(step):
        return device((y + core * step) % RING, (z + (1 - core) * step) % RING, half, core)

    def last(step):
        return device((y + (1 - core) * step) % RING, (z + core * step) % RING, half, core)

    partner = device(y, z, half, 1 - core)
    across = (1 - seq, chip + 1 - 2 * half, core)
    ahead, behind = (1, RING - 1)
    barrier = pltpu.get_barrier_semaphore()
    for other in (partner, across, first(ahead), first(behind), last(ahead), last(behind)):
        pl.semaphore_signal(barrier, inc=1, device_id=other, device_id_type=MESH_ID)
    pl.semaphore_wait(barrier, 6)

    def send(i, src, dst, to):
        return pltpu.make_async_remote_copy(
            src_ref=src,
            dst_ref=dst,
            send_sem=send_sem.at[i],
            recv_sem=recv_sem.at[i],
            device_id=to,
            device_id_type=MESH_ID,
        )

    def pair(c, f, l, part=None):
        cut = slice(None) if part is None else part
        to_y, to_z = (l, f) if c == 0 else (f, l)
        return out_ref.at[(y + to_y) % RING, (z + to_z) % RING, cut, c]

    def run(c):
        sent = []

        def go(i, region, to):
            copy = send(i, region, region, to)
            copy.start()
            sent.append(copy)

        def arrive(i, region):
            send(i, region, region, partner).wait_recv()

        def spread(f):
            go(5 + 2 * f, pair(c, f, 0), last(ahead))
            go(6 + 2 * f, pair(c, f, 0), last(behind))
            go(21 + 5 * f, pair(c, f, 0), partner)

        def relay(f):
            arrive(5 + 2 * f, pair(c, f, behind))
            go(13 + 2 * f, pair(c, f, behind, 0), last(ahead))
            go(22 + 5 * f, pair(c, f, behind), partner)
            arrive(6 + 2 * f, pair(c, f, ahead))
            go(14 + 2 * f, pair(c, f, ahead, 1), last(behind))
            go(23 + 5 * f, pair(c, f, ahead), partner)

        own = out_ref.at[y, z, half, c]
        copy = send(0, shard_ref, own, across)
        copy.start()
        sent.append(copy)
        local = pltpu.make_async_copy(shard_ref, own, local_sem)
        local.start()
        local.wait()
        arrive(0, out_ref.at[y, z, 1 - half, c])
        go(1, pair(c, 0, 0), first(ahead))
        go(2, pair(c, 0, 0), first(behind))
        spread(0)
        arrive(1, pair(c, behind, 0))
        go(3, pair(c, behind, 0, 0), first(ahead))
        spread(behind)
        arrive(2, pair(c, ahead, 0))
        go(4, pair(c, ahead, 0, 1), first(behind))
        spread(ahead)
        relay(0)
        arrive(3, pair(c, 2, 0, 0))
        arrive(4, pair(c, 2, 0, 1))
        spread(2)
        for f in (behind, ahead, 2):
            relay(f)
        for f in (0, behind, ahead, 2):
            for part in range(2):
                arrive(13 + 2 * f + part, pair(c, f, 2, part))
                go(24 + 5 * f + part, pair(c, f, 2, part), partner)
        for f in (0, behind, ahead, 2):
            arrive(21 + 5 * f, pair(1 - c, f, 0))
            arrive(22 + 5 * f, pair(1 - c, f, behind))
            arrive(23 + 5 * f, pair(1 - c, f, ahead))
            for part in range(2):
                arrive(24 + 5 * f + part, pair(1 - c, f, 2, part))
        for copy in sent:
            copy.wait_send()

    for c in (0, 1):
        pl.when(core == c)(lambda c=c: run(c))


def gather_weights(shard):
    rows, width = shard.shape
    out = pl.pallas_call(
        gather_body,
        out_shape=jax.ShapeDtypeStruct((RING, RING, 2, 2, rows, width), shard.dtype),
        in_specs=[pl.BlockSpec(memory_space=pltpu.VMEM)],
        out_specs=pl.BlockSpec(memory_space=pl.ANY),
        scratch_shapes=[
            pltpu.SemaphoreType.DMA((41,)),
            pltpu.SemaphoreType.DMA((41,)),
            pltpu.SemaphoreType.DMA,
        ],
        compiler_params=pltpu.CompilerParams(collective_id=0, has_side_effects=True),
        cost_estimate=pl.CostEstimate(
            flops=0, bytes_accessed=rows * width * 2 * 4 * RING * RING * 8, transcendentals=0
        ),
        name="gather_weights",
    )(shard)
    return out.reshape(4 * RING * RING * rows, width)


def projection_grads_body(mine_ref, sent_ref, gq_ref, gkv_ref, gr_ref, gains_ref, total_ref, away_ref):
    query = gq_ref.shape[1]
    width = query + gkv_ref.shape[1]
    wide = width + gr_ref.shape[1]
    spread = lax.broadcasted_iota(jnp.int32, (8, 128), 0)
    lane = lax.broadcasted_iota(jnp.int32, (8, 128), 1)
    apart = ((spread == lane) & (spread < 6)).astype(bf16)
    tokens = gq_ref.shape[0]
    for ref, out_ref, which in ((mine_ref, total_ref, 0), (sent_ref, away_ref, 1)):
        out_ref[:, :query] = dot(ref[:tokens, :], gq_ref[...], TN).astype(out_ref.dtype)
        out_ref[:, query:width] = dot(ref[: 2 * tokens, :], gkv_ref[...], TN).astype(out_ref.dtype)
        out_ref[:, width:wide] = dot(ref[2 * tokens :, :], gr_ref[...], TN).astype(out_ref.dtype)
        out_ref[:, wide:] = dot(gains_ref[which], apart, TN).astype(out_ref.dtype)


def projection_grads(rows_mine, rows_sent, grad_query, grad_kv, grad_res_low, gains):
    count = rows_mine.shape[1]
    width = grad_query.shape[1] + grad_kv.shape[1] + grad_res_low.shape[1] + 128
    tile = 128
    whole = lambda i: (0, 0)
    by_column = lambda i: (0, i)
    by_row = lambda i: (i, 0)
    return pl.pallas_call(
        projection_grads_body,
        grid=(count // tile,),
        in_specs=[
            pl.BlockSpec((rows_mine.shape[0], tile), by_column),
            pl.BlockSpec((rows_sent.shape[0], tile), by_column),
            pl.BlockSpec(grad_query.shape, whole),
            pl.BlockSpec(grad_kv.shape, whole),
            pl.BlockSpec(grad_res_low.shape, whole),
            pl.BlockSpec((2, 8, tile), lambda i: (0, 0, i)),
        ],
        out_specs=[pl.BlockSpec((tile, width), by_row), pl.BlockSpec((tile, width), by_row)],
        out_shape=[
            jax.ShapeDtypeStruct((count, width), f32),
            jax.ShapeDtypeStruct((count, width), bf16),
        ],
        name="projection_grads",
    )(rows_mine, rows_sent, grad_query, grad_kv, grad_res_low, gains)


def packed(values):
    lane = lax.broadcasted_iota(jnp.int32, (values.shape[0], 128), 1)
    wide = values.shape[1] - 128
    parts = values[:, wide:]
    total = parts + pltpu.roll(parts, 126, 1) + pltpu.roll(parts, 124, 1)
    total = jnp.where(lane < 2, total, 0.0)
    one = total.astype(bf16).astype(f32)
    two = (total - one).astype(bf16).astype(f32)
    three = total - one - two
    tail = one + pltpu.roll(two, 2, 1) + pltpu.roll(three, 4, 1)
    return jnp.concatenate([values[:, :wide].astype(bf16), tail.astype(bf16)], axis=1)


def reduce_body(
    mine,
    sent,
    low,
    in_ref,
    out_ref,
    gain_ref,
    up_ref,
    down_ref,
    came,
    acc,
    stage,
    in1,
    in2,
    stage_a,
    in_a1,
    in_a2,
    stage_x,
    in_x,
    own,
    in_own,
    low_came,
    chip_send,
    chip_recv,
    ring_send,
    ring_recv,
):
    seq, chip, core = (lax.axis_index(name) for name in ("seq", "chip", "core"))
    y, z, half = (chip // (2 * RING), (chip // 2) % RING, chip % 2)
    flip = 1 - core
    at_last = flip * y + core * z
    at_first = flip * z + core * y

    def device(to_y, to_z, to_half, to_core):
        return (seq, (to_y * RING + to_z) * 2 + to_half, to_core)

    def first(step):
        return device((y + core * step) % RING, (z + flip * step) % RING, half, core)

    def last(step):
        return device((y + flip * step) % RING, (z + core * step) % RING, half, core)

    partner = device(y, z, half, flip)
    across = device(y, z, 1 - half, core)
    mirror = (1 - seq, chip, core)
    ahead, behind = (1, RING - 1)
    barrier = pltpu.get_barrier_semaphore()
    others = (partner, across, mirror, first(ahead), first(behind), last(ahead), last(behind))
    for other in others:
        pl.semaphore_signal(barrier, inc=1, device_id=other, device_id_type=MESH_ID)
    pl.semaphore_wait(barrier, len(others))

    def send(i, src, dst, to):
        return pltpu.make_async_remote_copy(
            src_ref=src,
            dst_ref=dst,
            send_sem=ring_send.at[i],
            recv_sem=ring_recv.at[i],
            device_id=to,
            device_id_type=MESH_ID,
        )

    def on_chip(s, j, of_core):
        line = ((1 - of_core) * y + of_core * z + s) % RING
        a = (1 - of_core) * line + of_core * j
        b = (1 - of_core) * j + of_core * line
        return (
            a,
            b,
            pltpu.make_async_remote_copy(
                src_ref=sent.at[a, b],
                dst_ref=came.at[a, b],
                send_sem=chip_send.at[s, j],
                recv_sem=chip_recv.at[s, j],
                device_id=partner,
                device_id_type=MESH_ID,
            ),
        )

    order = (2, ahead, behind, 0)
    two = RING // 2
    units = send(12, low, low_came, mirror)
    units.start()
    for s in order:

        @pl.loop(0, RING)
        def _(j):
            on_chip(s, j, flip)[2].start()

    ring = [
        send(0, stage.at[2, :two], in1.at[0], last(ahead)),
        send(1, stage.at[2, two:], in1.at[1], last(behind)),
        send(2, stage.at[1, two:], in2.at[0, two:], last(ahead)),
        send(3, stage.at[1, :two], in2.at[0, :two], last(ahead)),
        send(4, stage.at[3, :two], in2.at[1, :two], last(behind)),
        send(5, stage.at[3, two:], in2.at[1, two:], last(behind)),
        send(6, stage_a.at[2, 0], in_a1.at[0], first(ahead)),
        send(7, stage_a.at[2, 1], in_a1.at[1], first(behind)),
        send(8, stage_a.at[1], in_a2.at[0], first(ahead)),
        send(9, stage_a.at[3], in_a2.at[1], first(behind)),
        send(10, stage_x, in_x, across),
        send(11, own, in_own, mirror),
    ]

    def merge(s, low_j, high_j, to_stage):
        @pl.loop(low_j, high_j)
        def _(j):
            a, b, copy = on_chip(s, j, core)
            copy.wait_recv()
            for h in range(2):
                value = mine[a, b, h] + came[a, b, h].astype(f32)
                if to_stage:
                    stage[s, j, h] = packed(value)
                if not to_stage or s != 2:
                    acc[s, j, h] = value

    merge(2, 0, RING, True)
    ring[0].start()
    ring[1].start()
    merge(ahead, 0, RING, True)
    ring[2].start()
    merge(behind, 0, RING, True)
    ring[4].start()
    merge(0, 0, RING, False)
    for i, s, source, first_j in ((0, ahead, 0, 0), (1, behind, 1, two)):
        ring[i].wait_recv()

        @pl.loop(0, two)
        def _(k):
            for h in range(2):
                value = acc[s, first_j + k, h] + in1[source, k, h].astype(f32)
                stage[s, first_j + k, h] = packed(value)

        ring[3 if i == 0 else 5].start()

    for i, source, first_j in ((2, 0, two), (4, 1, 0), (3, 0, 0), (5, 1, two)):
        ring[i].wait_recv()

        @pl.loop(first_j, first_j + two)
        def _(j):
            for h in range(2):
                acc[0, j, h] = acc[0, j, h] + in2[source, j, h].astype(f32)

    def at(step):
        return (at_first + step) % RING

    for h in range(2):
        stage_a[2, h] = packed(acc[0, at(2), h])
    ring[6].start()
    ring[7].start()
    stage_a[1, 1] = packed(acc[0, at(ahead), 1])
    stage_a[3, 0] = packed(acc[0, at(behind), 0])
    ring[6].wait_recv()
    stage_a[1, 0] = packed(acc[0, at(ahead), 0] + in_a1[0].astype(f32))
    ring[8].start()
    ring[7].wait_recv()
    stage_a[3, 1] = packed(acc[0, at(behind), 1] + in_a1[1].astype(f32))
    ring[9].start()
    ring[8].wait_recv()
    ring[9].wait_recv()
    away = 1 - half
    stage_x[...] = packed(
        acc[0, at_first, away] + in_a2[0, away].astype(f32) + in_a2[1, away].astype(f32)
    )
    ring[10].start()
    own[...] = acc[0, at_first, half] + in_a2[0, half].astype(f32) + in_a2[1, half].astype(f32)
    ring[10].wait_recv()
    own[...] = own[...] + in_x[...].astype(f32)
    ring[11].start()
    units.wait_recv()

    @pl.loop(0, low.shape[1] // 32)
    def _(r):
        rows = pl.ds(pl.multiple_of(r * 32, 32), 32)
        up_ref[rows, :] = low[0, rows, :].astype(f32) + low_came[0, rows, :].astype(f32)
        down_ref[rows, :] = low[1, rows, :].astype(f32) + low_came[1, rows, :].astype(f32)

    ring[11].wait_recv()
    total = own[...] + in_own[...]
    cut = in_ref.shape[1]
    wide = cut + out_ref.shape[1]
    in_ref[...] = total[:, :cut]
    out_ref[...] = total[:, cut:wide]
    gain_ref[...] = total[:, wide:]
    units.wait_send()
    for copy in ring:
        copy.wait_send()
    for s in order:

        @pl.loop(0, RING)
        def _(j):
            on_chip(s, j, flip)[2].wait_send()


def reduce_grads(mine, sent, low, cut):
    width = mine.shape[1]
    share = mine.shape[0] // (2 * RING * RING)
    shape = (RING, RING, 2, share, width)
    two = RING // 2
    pair = (2, share, width)
    return pl.pallas_call(
        reduce_body,
        in_specs=[pl.BlockSpec(memory_space=pltpu.VMEM)] * 3,
        out_specs=[pl.BlockSpec(memory_space=pltpu.VMEM)] * 5,
        out_shape=[
            jax.ShapeDtypeStruct((share, cut), f32),
            jax.ShapeDtypeStruct((share, width - cut - 128), f32),
            jax.ShapeDtypeStruct((share, 128), f32),
            jax.ShapeDtypeStruct(low.shape[1:], f32),
            jax.ShapeDtypeStruct(low.shape[1:], f32),
        ],
        scratch_shapes=[
            pltpu.VMEM(shape, bf16),
            pltpu.VMEM(shape, f32),
            pltpu.VMEM(shape, bf16),
            pltpu.VMEM((2, two) + pair, bf16),
            pltpu.VMEM((2, RING) + pair, bf16),
            pltpu.VMEM((RING,) + pair, bf16),
            pltpu.VMEM(pair, bf16),
            pltpu.VMEM((2,) + pair, bf16),
            pltpu.VMEM((share, width), bf16),
            pltpu.VMEM((share, width), bf16),
            pltpu.VMEM((share, width), f32),
            pltpu.VMEM((share, width), f32),
            pltpu.VMEM(low.shape, bf16),
            pltpu.SemaphoreType.DMA((RING, RING)),
            pltpu.SemaphoreType.DMA((RING, RING)),
            pltpu.SemaphoreType.DMA((13,)),
            pltpu.SemaphoreType.DMA((13,)),
        ],
        compiler_params=pltpu.CompilerParams(collective_id=2, has_side_effects=True),
        cost_estimate=pl.CostEstimate(
            flops=mine.size * 8, bytes_accessed=mine.size * 60, transcendentals=0
        ),
        name="reduce_grads",
    )(mine.reshape(shape), sent.reshape(shape), low)


def spread_plan(route_ids, mix_weights):
    token_count = route_ids.shape[0]
    expert_ids = jnp.arange(EXPERTS)[None, None, :]
    named = route_ids[:, :, None] == expert_ids
    picked = jnp.any(named, axis=1)
    token_weight = jnp.sum(jnp.where(named, mix_weights[:, :, None], 0.0), axis=1)
    earlier = jnp.arange(token_count)[None, :] < jnp.arange(token_count)[:, None]
    rank = dot(earlier.astype(bf16), picked.astype(bf16)).astype(jnp.int32)
    at_slot = jnp.where(picked, rank, -1).T[:, None, :] == jnp.arange(SLOTS)[None, :, None]
    placed = at_slot.astype(bf16).reshape(EXPERTS * SLOTS, token_count)
    weighted = jnp.where(at_slot, token_weight.T[:, None, :], 0.0)
    slot_weight = jnp.sum(weighted, axis=2).reshape(EXPERTS * SLOTS, 1)
    mixers = [part.reshape(EXPERTS * SLOTS, token_count) for part in three_parts(weighted)]
    return (placed, slot_weight, mixers)


def exchange(rows):
    width = rows.shape[-1]
    blocks = rows.reshape(EXPERTS, -1, width)
    return lax.all_to_all(blocks, "chip", split_axis=0, concat_axis=0, tiled=True).reshape(-1, width)


def on_device(
    inputs,
    project_in,
    project_out,
    gain_attend,
    gain_expert,
    expert_gate,
    expert_up,
    expert_down,
    routes,
    route_weights,
    segments,
    cotangent,
):
    token_count = inputs.shape[1]
    model_width = inputs.shape[2]
    query_width = HEADS * HEAD_DIM
    kv_width = KV_HEADS * HEAD_DIM
    group = HEADS // KV_HEADS
    seq = lax.axis_index("seq")
    core = lax.axis_index("core")
    own_low = inputs[0]
    other_low = lax.ppermute(own_low, "seq", SWAP)

    placed, slot_weight, mixers = spread_plan(routes[0], route_weights[0])
    grad_rows = (dot(placed, cotangent[0]) * slot_weight).astype(bf16)

    own_units = jnp.concatenate([expert_gate, expert_up, expert_down], axis=0)
    other_units = lax.ppermute(own_units, "core", SWAP)
    pre_w = jnp.concatenate([own_units[: 2 * BLOCK], other_units[: 2 * BLOCK]], axis=0)
    down_w = jnp.concatenate([expert_down, other_units[2 * BLOCK :]], axis=0)

    share = gain_attend.shape[0]
    wide = query_width + 2 * kv_width + query_width
    filler = jnp.zeros((share, 126), bf16)
    gathered = gather_weights(
        jnp.concatenate(
            [project_in, project_out, gain_attend[:, None], gain_expert[:, None], filler], axis=1
        )
    )
    gathered, grad_rows = lax.optimization_barrier((gathered, grad_rows))
    grad_arrived = exchange(grad_rows)
    in_full = gathered[:, : query_width + 2 * kv_width]
    out_full = gathered[:, query_width + 2 * kv_width : wide]
    gain_one, gain_two = (gathered[:, wide], gathered[:, wide + 1])

    row_values = own_low.astype(f32)
    normed_one, inverse_one = norm_forward(row_values, gain_one)
    normed_other, inverse_other = norm_forward(other_low.astype(f32), gain_one)
    kv_w = in_full[:, query_width:]
    projected = dot(normed_one, in_full)
    projected_other = dot(normed_other, kv_w)
    own_at = seq * token_count + jnp.arange(token_count)
    other_at = (1 - seq) * token_count + jnp.arange(token_count)
    own_cos, own_sin = rope_tables(own_at)
    other_cos, other_sin = rope_tables(other_at)
    query = rotate_wide(projected[:, :query_width], own_cos, own_sin, 1.0).astype(bf16)
    key_cut = query_width + kv_width
    own_keys = rotate_wide(projected[:, query_width:key_cut], own_cos, own_sin, 1.0)
    other_keys = rotate_wide(projected_other[:, :kv_width], other_cos, other_sin, 1.0)
    keys = jnp.concatenate([own_keys, other_keys], axis=0).astype(bf16)
    values = jnp.concatenate([projected[:, key_cut:], projected_other[:, kv_width:]], axis=0)
    query = query.reshape(token_count, KV_HEADS, group, HEAD_DIM)
    keys = keys.reshape(2 * token_count, KV_HEADS, HEAD_DIM)
    values = values.astype(bf16).reshape(2 * token_count, KV_HEADS, HEAD_DIM)
    seq_ids = segments[0]
    own_ids = lax.dynamic_slice(seq_ids, (seq * token_count,), (token_count,))
    other_ids = lax.dynamic_slice(seq_ids, ((1 - seq) * token_count,), (token_count,))
    key_at = jnp.concatenate([own_at, other_at])
    key_ids = jnp.concatenate([own_ids, other_ids])
    allowed = (key_at[None, :] <= own_at[:, None]) & (key_ids[None, :] == own_ids[:, None])
    attended, log_total = attend_forward(query, keys, values, allowed)
    mixed = attended.reshape(token_count, query_width)
    residual = row_values + dot(mixed, out_full)
    normed_two, inverse_two = norm_forward(residual, gain_two)

    arrived = exchange(dot(placed, normed_two).astype(bf16))
    hidden, grads, back = experts_first(arrived, grad_arrived, pre_w, down_w)
    grad_back = exchange(back)
    out_rows, gate_total, rest_low = experts_second(arrived, grad_arrived, hidden, grads, down_w)
    grad_back, out_rows = lax.optimization_barrier((grad_back, out_rows))
    returned = exchange(out_rows)

    grad_out = cotangent[0].astype(f32)
    grad_normed_two = dot(placed, grad_back, TN)
    grad_norm_two, gain_two_grad = norm_backward(residual, inverse_two, gain_two, grad_normed_two)
    grad_residual = grad_out + grad_norm_two
    grad_res_low = grad_residual.astype(bf16)
    grad_mixed = dot(grad_res_low, out_full, NT).astype(bf16)
    grad_query, grad_keys, grad_values = attend_backward(
        query, keys, values, allowed, attended, log_total, grad_mixed.reshape(attended.shape)
    )
    grad_query = grad_query.reshape(token_count, query_width)
    grad_keys = grad_keys.reshape(2 * token_count, kv_width)
    grad_values = grad_values.reshape(2 * token_count, kv_width)
    away_keys = rotate_wide(grad_keys[token_count:], other_cos, other_sin, -1.0)
    away = jnp.concatenate([away_keys, grad_values[token_count:]], axis=1).astype(bf16)
    came = lax.ppermute(away, "seq", SWAP)
    grad_query = rotate_wide(grad_query, own_cos, own_sin, -1.0).astype(bf16)
    grad_keys = rotate_wide(grad_keys[:token_count], own_cos, own_sin, -1.0)
    grad_kv = jnp.concatenate([grad_keys, grad_values[:token_count]], axis=1).astype(bf16)
    from_query = dot(grad_query, in_full[:, :query_width], NT)
    from_kv = dot(jnp.concatenate([grad_kv, away], axis=0), kv_w, NT)
    from_own = from_query + from_kv[:token_count]
    other_values = other_low.astype(f32)
    gain_one_grad = jnp.sum(from_own * row_values * inverse_one, axis=0)
    gain_one_grad += jnp.sum(from_kv[token_count:] * other_values * inverse_other, axis=0)

    feature = jnp.arange(model_width)[:, None]
    slot = jnp.arange(model_width)[None, :]
    half_width = model_width // 2
    of_core = jnp.where(slot < half_width, core, 1 - core)
    at = slot % half_width
    chosen_half = feature == (2 * (at // share) + of_core) * share + at % share
    chosen_half = chosen_half.astype(bf16)
    features = jnp.concatenate([normed_one, normed_other, mixed], axis=0)
    features = dot(features, chosen_half).astype(bf16)
    gain_pair = jnp.stack([gain_one_grad, gain_two_grad], axis=0)
    gain_parts = jnp.concatenate(three_parts(gain_pair) + (jnp.zeros_like(gain_pair, bf16),), axis=0)
    gain_parts = dot(gain_parts, chosen_half).astype(bf16)
    gain_parts = jnp.stack([gain_parts[:, :half_width], gain_parts[:, half_width:]], axis=0)
    grads_mine, grads_sent = projection_grads(
        features[:, :half_width],
        features[:, half_width:],
        grad_query,
        jnp.concatenate([grad_kv, away], axis=0),
        grad_res_low,
        gain_parts,
    )
    in_width = query_width + 2 * kv_width
    in_total, out_total, gain_total, up_total, down_total = reduce_grads(
        grads_mine, grads_sent, rest_low, in_width
    )
    gain_total = gain_total[:, :2] + gain_total[:, 2:4] + gain_total[:, 4:6]

    came, gain_total = lax.optimization_barrier((came, gain_total))
    grad_normed_one = from_own + dot(came, kv_w, NT)
    grad_norm_one, _ = norm_backward(row_values, inverse_one, gain_one, grad_normed_one)
    grad_inputs = (grad_residual + grad_norm_one).astype(bf16)

    mix = jnp.concatenate(mixers, axis=1)
    chosen = dot(mix, returned, TN).reshape(3, token_count, model_width)
    output = (residual + (chosen[2] + chosen[1] + chosen[0])).astype(bf16)
    return (
        output.reshape(1, token_count, model_width),
        grad_inputs.reshape(1, token_count, model_width),
        in_total,
        out_total,
        gain_total[:, 0],
        gain_total[:, 1],
        gate_total,
        up_total,
        down_total,
    )


def solution(mesh):
    devices = mesh.devices
    cores = Mesh(devices.reshape(devices.shape[0], -1, 2), ("seq", "chip", "core"))
    every = ("chip", "core")
    by_token = P(every, "seq", None)
    by_row = P(every, None)
    in_specs = (
        by_token,
        by_row,
        by_row,
        P(every),
        P(every),
        by_row,
        by_row,
        by_row,
        by_token,
        by_token,
        by_row,
        by_token,
    )
    out_specs = (by_token, by_token, by_row, by_row, P(every), P(every), by_row, by_row, by_row)
    return jax.shard_map(
        on_device, mesh=cores, in_specs=in_specs, out_specs=out_specs, check_vma=False
    )
```

```python
import jax
import jax.numpy as jnp
from jax import lax
from jax.experimental import pallas as pl
from jax.experimental.pallas import tpu as pltpu
from jax.sharding import Mesh, PartitionSpec as P

HEADS = 16
KV_HEADS = 8
HEAD_DIM = 64
EXPERTS = 32
FF = 512
TOP = 8
CAP = 36
SLOTS = 40
BLOCK = 256
ROW_BLOCK = 256

EPSILON = 1e-06
ROPE_BASE = 10000.0

f32 = jnp.float32
bf16 = jnp.bfloat16

RING = 4
MESH_ID = pl.DeviceIdType.MESH
SWAP = [(0, 1), (1, 0)]
NT = (((1,), (1,)), ((), ()))
TN = (((0,), (0,)), ((), ()))


def dot(a, b, dims=(((1,), (0,)), ((), ()))):
    return lax.dot_general(a, b, dims, preferred_element_type=f32)


def rope_tables(positions):
    half_dim = HEAD_DIM // 2
    powers = jnp.arange(half_dim).astype(f32) * (2.0 / HEAD_DIM)
    inverse_freq = ROPE_BASE ** (-powers)
    angles = positions.astype(f32)[:, None] * inverse_freq[None, :]
    return (jnp.cos(angles), jnp.sin(angles))


def rotate(values, cosine_table, sine_table, turn_sign):
    half_dim = values.shape[-1] // 2
    leading = values[..., :half_dim]
    trailing = values[..., half_dim:]
    cosine_b = cosine_table[:, None, :]
    sine_b = sine_table[:, None, :] * turn_sign
    return jnp.concatenate(
        [leading * cosine_b - trailing * sine_b, trailing * cosine_b + leading * sine_b], axis=-1
    )


def rotate_wide(values, cosine_table, sine_table, turn_sign):
    rows, width = values.shape
    heads = values.reshape(rows, width // HEAD_DIM, HEAD_DIM)
    return rotate(heads, cosine_table, sine_table, turn_sign).reshape(rows, width)


def norm_forward(values, gain_vector):
    inverse = lax.rsqrt(jnp.mean(values * values, axis=-1, keepdims=True) + EPSILON)
    return ((values * inverse * gain_vector.astype(f32)).astype(bf16), inverse)


def norm_backward(values, inverse, gain_vector, upstream):
    scaled = upstream * gain_vector.astype(f32)
    grad_gain = jnp.sum(upstream * values * inverse, axis=0)
    coupling = jnp.mean(scaled * values, axis=-1, keepdims=True)
    return (inverse * scaled - values * inverse * inverse * inverse * coupling, grad_gain)


def rounded(values):
    return lax.reduce_precision(values, exponent_bits=8, mantissa_bits=7)


def three_parts(values):
    first = rounded(values)
    second = rounded(values - first)
    third = values - first - second
    return (first.astype(bf16), second.astype(bf16), third.astype(bf16))


def masked_scores(query, keys, allowed):
    scores = jnp.einsum("qkgd,skd->kgqs", query, keys, preferred_element_type=f32)
    return jnp.where(allowed[None, None], scores * HEAD_DIM ** (-0.5), -1e30)


def attend_forward(query, keys, values, allowed):
    scores = masked_scores(query, keys, allowed)
    highest = jnp.max(scores, axis=-1, keepdims=True)
    log_total = highest + jnp.log(jnp.sum(jnp.exp(scores - highest), axis=-1, keepdims=True))
    weights = jnp.exp(scores - log_total).astype(bf16)
    mixed = jnp.einsum("kgqs,skd->qkgd", weights, values, preferred_element_type=f32)
    return (mixed.astype(bf16), log_total)


def attend_backward(query, keys, values, allowed, attended, log_total, grad_attended):
    scale_factor = HEAD_DIM ** (-0.5)
    weights = jnp.exp(masked_scores(query, keys, allowed) - log_total)
    grad_values = jnp.einsum(
        "kgqs,qkgd->skd", weights.astype(bf16), grad_attended, preferred_element_type=f32
    )
    grad_weights = jnp.einsum("qkgd,skd->kgqs", grad_attended, values, preferred_element_type=f32)
    row_delta = jnp.sum(grad_attended.astype(f32) * attended.astype(f32), axis=-1)
    row_delta = jnp.transpose(row_delta, (1, 2, 0))
    grad_scores = (weights * (grad_weights - row_delta[..., None])).astype(bf16)
    grad_query = jnp.einsum("kgqs,skd->qkgd", grad_scores, keys, preferred_element_type=f32)
    grad_keys = jnp.einsum("kgqs,qkgd->skd", grad_scores, query, preferred_element_type=f32)
    return (grad_query * scale_factor, grad_keys * scale_factor, grad_values)


def experts_first_body(x_ref, g_ref, pre_w_ref, down_w_ref, hidden_ref, grads_ref, back_ref):
    pre = dot(x_ref[...], pre_w_ref[...], NT)
    grad_hidden = dot(g_ref[...], down_w_ref[...], NT)
    back = None
    for b in range(FF // BLOCK):
        gate = pre[:, 2 * b * BLOCK : (2 * b + 1) * BLOCK]
        up = pre[:, (2 * b + 1) * BLOCK : (2 * b + 2) * BLOCK]
        grad_h = grad_hidden[:, b * BLOCK : (b + 1) * BLOCK]
        sigmoid_gate = 1.0 / (1.0 + jnp.exp(-gate))
        silu = gate * sigmoid_gate
        hidden_ref[:, b * BLOCK : (b + 1) * BLOCK] = (silu * up).astype(bf16)
        grad_gate = (grad_h * up * sigmoid_gate * (1.0 + gate * (1.0 - sigmoid_gate))).astype(bf16)
        grad_up = (grad_h * gate * sigmoid_gate).astype(bf16)
        both = jnp.concatenate([grad_gate, grad_up], axis=1)
        grads_ref[:, 2 * b * BLOCK : (2 * b + 2) * BLOCK] = both
        part = dot(both, pre_w_ref[2 * b * BLOCK : (2 * b + 2) * BLOCK, :]).astype(bf16).astype(f32)
        back = part if back is None else back + part
    back_ref[...] = back.astype(bf16)


def experts_first(arrived, grad_arrived, pre_w, down_w):
    rows, width = arrived.shape
    whole = lambda i: (0, 0)
    by_row = lambda i: (i, 0)
    return pl.pallas_call(
        experts_first_body,
        grid=(rows // ROW_BLOCK,),
        in_specs=[
            pl.BlockSpec((ROW_BLOCK, width), by_row),
            pl.BlockSpec((ROW_BLOCK, width), by_row),
            pl.BlockSpec((2 * FF, width), whole),
            pl.BlockSpec((FF, width), whole),
        ],
        out_specs=[
            pl.BlockSpec((ROW_BLOCK, FF), by_row),
            pl.BlockSpec((ROW_BLOCK, 2 * FF), by_row),
            pl.BlockSpec((ROW_BLOCK, width), by_row),
        ],
        out_shape=[
            jax.ShapeDtypeStruct((rows, FF), bf16),
            jax.ShapeDtypeStruct((rows, 2 * FF), bf16),
            jax.ShapeDtypeStruct((rows, width), bf16),
        ],
        cost_estimate=pl.CostEstimate(
            flops=2 * rows * width * FF * 5,
            bytes_accessed=rows * width * 2 * 5,
            transcendentals=rows * FF,
        ),
        name="experts_first",
    )(arrived, grad_arrived, pre_w, down_w)


def experts_second_body(
    x_ref,
    g_ref,
    hidden_ref,
    grads_ref,
    down_w_ref,
    out_ref,
    gate_ref,
    up_ref,
    third_ref,
    theirs,
    came,
    last,
    low,
    low_came,
    send_sem,
    recv_sem,
):
    seq, chip, core = (lax.axis_index(name) for name in ("seq", "chip", "core"))
    partner = (seq, chip, 1 - core)
    mirror = (1 - seq, chip, core)
    barrier = pltpu.get_barrier_semaphore()
    for other in (partner, mirror):
        pl.semaphore_signal(barrier, inc=1, device_id=other, device_id_type=MESH_ID)
    pl.semaphore_wait(barrier, 2)
    width = x_ref.shape[1]

    def send(i, src, dst, to):
        return pltpu.make_async_remote_copy(
            src_ref=src,
            dst_ref=dst,
            send_sem=send_sem.at[i],
            recv_sem=recv_sem.at[i],
            device_id=to,
            device_id_type=MESH_ID,
        )

    def unit_grads(block, kind, target):
        if kind < 2:
            at = (2 * block + kind) * BLOCK
            left, right = (grads_ref, x_ref)
        else:
            at = block * BLOCK
            left, right = (hidden_ref, g_ref)

        @pl.loop(0, width // BLOCK)
        def _(n):
            columns = pl.ds(pl.multiple_of(n * BLOCK, BLOCK), BLOCK)
            target[:, columns] = dot(left[:, at : at + BLOCK], right[:, columns], TN)

    away = [send(k, theirs.at[k], came.at[k], partner) for k in range(3)]
    across = [send(3 + k, low.at[k], low_came.at[k], mirror) for k in range(2)]
    mine = [gate_ref, up_ref, last]
    lows = [low.at[0], low.at[1], third_ref]
    for k in range(3):
        unit_grads(1, k, theirs.at[k])
        if k:
            away[k - 1].start()
    unit_grads(0, 0, mine[0])
    away[2].start()

    def join(k):
        away[k].wait_recv()

        @pl.loop(0, BLOCK // 32)
        def _(r):
            rows = pl.ds(pl.multiple_of(r * 32, 32), 32)
            lows[k][rows, :] = (mine[k][rows, :] + came[k, rows, :]).astype(bf16)

    for k in range(3):
        join(k)
        if k < 2:
            unit_grads(0, k + 1, mine[k + 1])
            across[k].start()

    @pl.loop(0, x_ref.shape[0] // ROW_BLOCK)
    def _(r):
        rows = pl.ds(pl.multiple_of(r * ROW_BLOCK, ROW_BLOCK), ROW_BLOCK)
        out = None
        for b in range(FF // BLOCK):
            units = slice(b * BLOCK, (b + 1) * BLOCK)
            part = dot(hidden_ref[rows, units], down_w_ref[units, :]).astype(bf16).astype(f32)
            out = part if out is None else out + part
        out_ref[rows, :] = out.astype(bf16)

    for k in range(2):
        across[k].wait_recv()

        @pl.loop(0, BLOCK // 32)
        def _(r):
            rows = pl.ds(pl.multiple_of(r * 32, 32), 32)
            mine[k][rows, :] = low[k, rows, :].astype(f32) + low_came[k, rows, :].astype(f32)

    for copy in away + across:
        copy.wait_send()


def experts_second(arrived, grad_arrived, hidden, grads, down_w):
    rows, width = arrived.shape
    return pl.pallas_call(
        experts_second_body,
        in_specs=[pl.BlockSpec(memory_space=pltpu.VMEM)] * 5,
        out_specs=[pl.BlockSpec(memory_space=pltpu.VMEM)] * 4,
        out_shape=[
            jax.ShapeDtypeStruct((rows, width), bf16),
            jax.ShapeDtypeStruct((BLOCK, width), f32),
            jax.ShapeDtypeStruct((BLOCK, width), f32),
            jax.ShapeDtypeStruct((BLOCK, width), bf16),
        ],
        scratch_shapes=[
            pltpu.VMEM((3, BLOCK, width), f32),
            pltpu.VMEM((3, BLOCK, width), f32),
            pltpu.VMEM((BLOCK, width), f32),
            pltpu.VMEM((2, BLOCK, width), bf16),
            pltpu.VMEM((2, BLOCK, width), bf16),
            pltpu.SemaphoreType.DMA((5,)),
            pltpu.SemaphoreType.DMA((5,)),
        ],
        compiler_params=pltpu.CompilerParams(collective_id=1, has_side_effects=True),
        cost_estimate=pl.CostEstimate(
            flops=2 * rows * width * FF * 4,
            bytes_accessed=rows * width * 2 * 20,
            transcendentals=0,
        ),
        name="experts_second",
    )(arrived, grad_arrived, hidden, grads, down_w)


def gather_body(shard_ref, out_ref, send_sem, recv_sem, local_sem):
    seq, chip, core = (lax.axis_index(name) for name in ("seq", "chip", "core"))
    y, z, half = (chip // (2 * RING), (chip // 2) % RING, chip % 2)

    def device(to_y, to_z, to_half, to_core):
        return (seq, (to_y * RING + to_z) * 2 + to_half, to_core)

    def first(step):
        return device((y + core * step) % RING, (z + (1 - core) * step) % RING, half, core)

    def last(step):
        return device((y + (1 - core) * step) % RING, (z + core * step) % RING, half, core)

    partner = device(y, z, half, 1 - core)
    across = (1 - seq, chip + 1 - 2 * half, core)
    ahead, behind = (1, RING - 1)
    barrier = pltpu.get_barrier_semaphore()
    for other in (partner, across, first(ahead), first(behind), last(ahead), last(behind)):
        pl.semaphore_signal(barrier, inc=1, device_id=other, device_id_type=MESH_ID)
    pl.semaphore_wait(barrier, 6)

    def send(i, src, dst, to):
        return pltpu.make_async_remote_copy(
            src_ref=src,
            dst_ref=dst,
            send_sem=send_sem.at[i],
            recv_sem=recv_sem.at[i],
            device_id=to,
            device_id_type=MESH_ID,
        )

    def pair(c, f, l, part=None):
        cut = slice(None) if part is None else part
        to_y, to_z = (l, f) if c == 0 else (f, l)
        return out_ref.at[(y + to_y) % RING, (z + to_z) % RING, cut, c]

    def run(c):
        sent = []

        def go(i, region, to):
            copy = send(i, region, region, to)
            copy.start()
            sent.append(copy)

        def arrive(i, region):
            send(i, region, region, partner).wait_recv()

        def spread(f):
            go(5 + 2 * f, pair(c, f, 0), last(ahead))
            go(6 + 2 * f, pair(c, f, 0), last(behind))
            go(21 + 5 * f, pair(c, f, 0), partner)

        def relay(f):
            arrive(5 + 2 * f, pair(c, f, behind))
            go(13 + 2 * f, pair(c, f, behind, 0), last(ahead))
            go(22 + 5 * f, pair(c, f, behind), partner)
            arrive(6 + 2 * f, pair(c, f, ahead))
            go(14 + 2 * f, pair(c, f, ahead, 1), last(behind))
            go(23 + 5 * f, pair(c, f, ahead), partner)

        own = out_ref.at[y, z, half, c]
        copy = send(0, shard_ref, own, across)
        copy.start()
        sent.append(copy)
        local = pltpu.make_async_copy(shard_ref, own, local_sem)
        local.start()
        local.wait()
        arrive(0, out_ref.at[y, z, 1 - half, c])
        go(1, pair(c, 0, 0), first(ahead))
        go(2, pair(c, 0, 0), first(behind))
        spread(0)
        arrive(1, pair(c, behind, 0))
        go(3, pair(c, behind, 0, 0), first(ahead))
        spread(behind)
        arrive(2, pair(c, ahead, 0))
        go(4, pair(c, ahead, 0, 1), first(behind))
        spread(ahead)
        relay(0)
        arrive(3, pair(c, 2, 0, 0))
        arrive(4, pair(c, 2, 0, 1))
        spread(2)
        for f in (behind, ahead, 2):
            relay(f)
        for f in (0, behind, ahead, 2):
            for part in range(2):
                arrive(13 + 2 * f + part, pair(c, f, 2, part))
                go(24 + 5 * f + part, pair(c, f, 2, part), partner)
        for f in (0, behind, ahead, 2):
            arrive(21 + 5 * f, pair(1 - c, f, 0))
            arrive(22 + 5 * f, pair(1 - c, f, behind))
            arrive(23 + 5 * f, pair(1 - c, f, ahead))
            for part in range(2):
                arrive(24 + 5 * f + part, pair(1 - c, f, 2, part))
        for copy in sent:
            copy.wait_send()

    for c in (0, 1):
        pl.when(core == c)(lambda c=c: run(c))


def gather_weights(shard):
    rows, width = shard.shape
    out = pl.pallas_call(
        gather_body,
        out_shape=jax.ShapeDtypeStruct((RING, RING, 2, 2, rows, width), shard.dtype),
        in_specs=[pl.BlockSpec(memory_space=pltpu.VMEM)],
        out_specs=pl.BlockSpec(memory_space=pl.ANY),
        scratch_shapes=[
            pltpu.SemaphoreType.DMA((41,)),
            pltpu.SemaphoreType.DMA((41,)),
            pltpu.SemaphoreType.DMA,
        ],
        compiler_params=pltpu.CompilerParams(collective_id=0, has_side_effects=True),
        cost_estimate=pl.CostEstimate(
            flops=0, bytes_accessed=rows * width * 2 * 4 * RING * RING * 8, transcendentals=0
        ),
        name="gather_weights",
    )(shard)
    return out.reshape(4 * RING * RING * rows, width)


def projection_grads_body(mine_ref, sent_ref, gq_ref, gkv_ref, gr_ref, gains_ref, total_ref, away_ref):
    query = gq_ref.shape[1]
    width = query + gkv_ref.shape[1]
    wide = width + gr_ref.shape[1]
    spread = lax.broadcasted_iota(jnp.int32, (8, 128), 0)
    lane = lax.broadcasted_iota(jnp.int32, (8, 128), 1)
    apart = ((spread == lane) & (spread < 6)).astype(bf16)
    tokens = gq_ref.shape[0]
    for ref, out_ref, which in ((mine_ref, total_ref, 0), (sent_ref, away_ref, 1)):
        out_ref[:, :query] = dot(ref[:tokens, :], gq_ref[...], TN).astype(out_ref.dtype)
        out_ref[:, query:width] = dot(ref[: 2 * tokens, :], gkv_ref[...], TN).astype(out_ref.dtype)
        out_ref[:, width:wide] = dot(ref[2 * tokens :, :], gr_ref[...], TN).astype(out_ref.dtype)
        out_ref[:, wide:] = dot(gains_ref[which], apart, TN).astype(out_ref.dtype)


def projection_grads(rows_mine, rows_sent, grad_query, grad_kv, grad_res_low, gains):
    count = rows_mine.shape[1]
    width = grad_query.shape[1] + grad_kv.shape[1] + grad_res_low.shape[1] + 128
    tile = 128
    whole = lambda i: (0, 0)
    by_column = lambda i: (0, i)
    by_row = lambda i: (i, 0)
    return pl.pallas_call(
        projection_grads_body,
        grid=(count // tile,),
        in_specs=[
            pl.BlockSpec((rows_mine.shape[0], tile), by_column),
            pl.BlockSpec((rows_sent.shape[0], tile), by_column),
            pl.BlockSpec(grad_query.shape, whole),
            pl.BlockSpec(grad_kv.shape, whole),
            pl.BlockSpec(grad_res_low.shape, whole),
            pl.BlockSpec((2, 8, tile), lambda i: (0, 0, i)),
        ],
        out_specs=[pl.BlockSpec((tile, width), by_row), pl.BlockSpec((tile, width), by_row)],
        out_shape=[
            jax.ShapeDtypeStruct((count, width), f32),
            jax.ShapeDtypeStruct((count, width), bf16),
        ],
        name="projection_grads",
    )(rows_mine, rows_sent, grad_query, grad_kv, grad_res_low, gains)


def packed(values):
    lane = lax.broadcasted_iota(jnp.int32, (values.shape[0], 128), 1)
    wide = values.shape[1] - 128
    parts = values[:, wide:]
    total = parts + pltpu.roll(parts, 126, 1) + pltpu.roll(parts, 124, 1)
    total = jnp.where(lane < 2, total, 0.0)
    one = total.astype(bf16).astype(f32)
    two = (total - one).astype(bf16).astype(f32)
    three = total - one - two
    tail = one + pltpu.roll(two, 2, 1) + pltpu.roll(three, 4, 1)
    return jnp.concatenate([values[:, :wide].astype(bf16), tail.astype(bf16)], axis=1)


def reduce_body(
    mine,
    sent,
    low,
    in_ref,
    out_ref,
    gain_ref,
    unit_ref,
    came,
    acc,
    stage,
    in1,
    in2,
    stage_a,
    in_a1,
    in_a2,
    stage_x,
    in_x,
    own,
    in_own,
    low_came,
    chip_send,
    chip_recv,
    ring_send,
    ring_recv,
):
    seq, chip, core = (lax.axis_index(name) for name in ("seq", "chip", "core"))
    y, z, half = (chip // (2 * RING), (chip // 2) % RING, chip % 2)
    flip = 1 - core
    at_last = flip * y + core * z
    at_first = flip * z + core * y

    def device(to_y, to_z, to_half, to_core):
        return (seq, (to_y * RING + to_z) * 2 + to_half, to_core)

    def first(step):
        return device((y + core * step) % RING, (z + flip * step) % RING, half, core)

    def last(step):
        return device((y + flip * step) % RING, (z + core * step) % RING, half, core)

    partner = device(y, z, half, flip)
    across = (1 - seq, chip + 1 - 2 * half, core)
    mirror = (1 - seq, chip, core)
    ahead, behind = (1, RING - 1)
    barrier = pltpu.get_barrier_semaphore()
    others = (partner, across, mirror, first(ahead), first(behind), last(ahead), last(behind))
    for other in others:
        pl.semaphore_signal(barrier, inc=1, device_id=other, device_id_type=MESH_ID)
    pl.semaphore_wait(barrier, len(others))

    def send(i, src, dst, to):
        return pltpu.make_async_remote_copy(
            src_ref=src,
            dst_ref=dst,
            send_sem=ring_send.at[i],
            recv_sem=ring_recv.at[i],
            device_id=to,
            device_id_type=MESH_ID,
        )

    def on_chip(s, j, of_core):
        line = ((1 - of_core) * y + of_core * z + s) % RING
        a = (1 - of_core) * line + of_core * j
        b = (1 - of_core) * j + of_core * line
        return (
            a,
            b,
            pltpu.make_async_remote_copy(
                src_ref=sent.at[a, b],
                dst_ref=came.at[a, b],
                send_sem=chip_send.at[s, j],
                recv_sem=chip_recv.at[s, j],
                device_id=partner,
                device_id_type=MESH_ID,
            ),
        )

    order = (2, ahead, behind, 0)
    two = RING // 2
    units = send(12, low, low_came, mirror)
    units.start()
    for s in order:

        @pl.loop(0, RING)
        def _(j):
            on_chip(s, j, flip)[2].start()

    ring = [
        send(0, stage.at[2, :two], in1.at[0], last(ahead)),
        send(1, stage.at[2, two:], in1.at[1], last(behind)),
        send(2, stage.at[1, two:], in2.at[0, two:], last(ahead)),
        send(3, stage.at[1, :two], in2.at[0, :two], last(ahead)),
        send(4, stage.at[3, :two], in2.at[1, :two], last(behind)),
        send(5, stage.at[3, two:], in2.at[1, two:], last(behind)),
        send(6, stage_a.at[2, 0], in_a1.at[0], first(ahead)),
        send(7, stage_a.at[2, 1], in_a1.at[1], first(behind)),
        send(8, stage_a.at[1], in_a2.at[0], first(ahead)),
        send(9, stage_a.at[3], in_a2.at[1], first(behind)),
        send(10, stage_x, in_x, across),
        send(11, own, in_own, mirror),
    ]

    def merge(s, low_j, high_j, to_stage):
        @pl.loop(low_j, high_j)
        def _(j):
            a, b, copy = on_chip(s, j, core)
            copy.wait_recv()
            for h in range(2):
                value = mine[a, b, h] + came[a, b, h].astype(f32)
                if to_stage:
                    stage[s, j, h] = packed(value)
                if not to_stage or s != 2:
                    acc[s, j, h] = value

    merge(2, 0, RING, True)
    ring[0].start()
    ring[1].start()
    merge(ahead, 0, RING, True)
    ring[2].start()
    merge(behind, 0, RING, True)
    ring[4].start()
    merge(0, 0, RING, False)
    for i, s, source, first_j in ((0, ahead, 0, 0), (1, behind, 1, two)):
        ring[i].wait_recv()

        @pl.loop(0, two)
        def _(k):
            for h in range(2):
                value = acc[s, first_j + k, h] + in1[source, k, h].astype(f32)
                stage[s, first_j + k, h] = packed(value)

        ring[3 if i == 0 else 5].start()

    for i, source, first_j in ((2, 0, two), (4, 1, 0), (3, 0, 0), (5, 1, two)):
        ring[i].wait_recv()

        @pl.loop(first_j, first_j + two)
        def _(j):
            for h in range(2):
                acc[0, j, h] = acc[0, j, h] + in2[source, j, h].astype(f32)

    def at(step):
        return (at_first + step) % RING

    for h in range(2):
        stage_a[2, h] = packed(acc[0, at(2), h])
    ring[6].start()
    ring[7].start()
    stage_a[1, 1] = packed(acc[0, at(ahead), 1])
    stage_a[3, 0] = packed(acc[0, at(behind), 0])
    ring[6].wait_recv()
    stage_a[1, 0] = packed(acc[0, at(ahead), 0] + in_a1[0].astype(f32))
    ring[8].start()
    ring[7].wait_recv()
    stage_a[3, 1] = packed(acc[0, at(behind), 1] + in_a1[1].astype(f32))
    ring[9].start()
    ring[8].wait_recv()
    ring[9].wait_recv()
    away = 1 - half
    stage_x[...] = packed(
        acc[0, at_first, away] + in_a2[0, away].astype(f32) + in_a2[1, away].astype(f32)
    )
    ring[10].start()
    own[...] = acc[0, at_first, half] + in_a2[0, half].astype(f32) + in_a2[1, half].astype(f32)
    ring[10].wait_recv()
    own[...] = own[...] + in_x[...].astype(f32)
    ring[11].start()
    units.wait_recv()

    @pl.loop(0, low.shape[0] // 32)
    def _(r):
        rows = pl.ds(pl.multiple_of(r * 32, 32), 32)
        unit_ref[rows, :] = low[rows, :].astype(f32) + low_came[rows, :].astype(f32)

    ring[11].wait_recv()
    total = own[...] + in_own[...]
    cut = in_ref.shape[1]
    wide = cut + out_ref.shape[1]
    in_ref[...] = total[:, :cut]
    out_ref[...] = total[:, cut:wide]
    gain_ref[...] = total[:, wide:]
    units.wait_send()
    for copy in ring:
        copy.wait_send()
    for s in order:

        @pl.loop(0, RING)
        def _(j):
            on_chip(s, j, flip)[2].wait_send()


def reduce_grads(mine, sent, low, cut):
    width = mine.shape[1]
    share = mine.shape[0] // (2 * RING * RING)
    shape = (RING, RING, 2, share, width)
    two = RING // 2
    pair = (2, share, width)
    return pl.pallas_call(
        reduce_body,
        in_specs=[pl.BlockSpec(memory_space=pltpu.VMEM)] * 3,
        out_specs=[pl.BlockSpec(memory_space=pltpu.VMEM)] * 4,
        out_shape=[
            jax.ShapeDtypeStruct((share, cut), f32),
            jax.ShapeDtypeStruct((share, width - cut - 128), f32),
            jax.ShapeDtypeStruct((share, 128), f32),
            jax.ShapeDtypeStruct(low.shape, f32),
        ],
        scratch_shapes=[
            pltpu.VMEM(shape, bf16),
            pltpu.VMEM(shape, f32),
            pltpu.VMEM(shape, bf16),
            pltpu.VMEM((2, two) + pair, bf16),
            pltpu.VMEM((2, RING) + pair, bf16),
            pltpu.VMEM((RING,) + pair, bf16),
            pltpu.VMEM(pair, bf16),
            pltpu.VMEM((2,) + pair, bf16),
            pltpu.VMEM((share, width), bf16),
            pltpu.VMEM((share, width), bf16),
            pltpu.VMEM((share, width), f32),
            pltpu.VMEM((share, width), f32),
            pltpu.VMEM(low.shape, bf16),
            pltpu.SemaphoreType.DMA((RING, RING)),
            pltpu.SemaphoreType.DMA((RING, RING)),
            pltpu.SemaphoreType.DMA((13,)),
            pltpu.SemaphoreType.DMA((13,)),
        ],
        compiler_params=pltpu.CompilerParams(collective_id=2, has_side_effects=True),
        cost_estimate=pl.CostEstimate(
            flops=mine.size * 8, bytes_accessed=mine.size * 60, transcendentals=0
        ),
        name="reduce_grads",
    )(mine.reshape(shape), sent.reshape(shape), low)


def spread_plan(route_ids, mix_weights):
    token_count = route_ids.shape[0]
    expert_ids = jnp.arange(EXPERTS)[None, None, :]
    named = route_ids[:, :, None] == expert_ids
    picked = jnp.any(named, axis=1)
    token_weight = jnp.sum(jnp.where(named, mix_weights[:, :, None], 0.0), axis=1)
    earlier = jnp.arange(token_count)[None, :] < jnp.arange(token_count)[:, None]
    rank = dot(earlier.astype(bf16), picked.astype(bf16)).astype(jnp.int32)
    at_slot = jnp.where(picked, rank, -1).T[:, None, :] == jnp.arange(SLOTS)[None, :, None]
    placed = at_slot.astype(bf16).reshape(EXPERTS * SLOTS, token_count)
    weighted = jnp.where(at_slot, token_weight.T[:, None, :], 0.0)
    slot_weight = jnp.sum(weighted, axis=2).reshape(EXPERTS * SLOTS, 1)
    mixers = [part.reshape(EXPERTS * SLOTS, token_count) for part in three_parts(weighted)]
    return (placed, slot_weight, mixers)


def exchange(rows):
    width = rows.shape[-1]
    blocks = rows.reshape(EXPERTS, -1, width)
    groups = [[(g ^ (c % 2)) * EXPERTS + c for c in range(EXPERTS)] for g in range(2)]
    landed = lax.all_to_all(
        blocks,
        ("seq", "chip"),
        split_axis=0,
        concat_axis=0,
        axis_index_groups=groups,
        tiled=True,
    )
    return landed.reshape(-1, width)


def on_device(
    inputs,
    project_in,
    project_out,
    gain_attend,
    gain_expert,
    expert_gate,
    expert_up,
    expert_down,
    routes,
    route_weights,
    segments,
    cotangent,
):
    token_count = inputs.shape[1]
    model_width = inputs.shape[2]
    query_width = HEADS * HEAD_DIM
    kv_width = KV_HEADS * HEAD_DIM
    group = HEADS // KV_HEADS
    seq = lax.axis_index("seq")
    core = lax.axis_index("core")
    own_low = inputs[0]
    other_low = lax.ppermute(own_low, "seq", SWAP)

    placed, slot_weight, mixers = spread_plan(routes[0], route_weights[0])
    grad_rows = (dot(placed, cotangent[0]) * slot_weight).astype(bf16)

    own_units = jnp.concatenate([expert_gate, expert_up, expert_down], axis=0)
    other_units = lax.ppermute(own_units, "core", SWAP)
    pre_w = jnp.concatenate([own_units[: 2 * BLOCK], other_units[: 2 * BLOCK]], axis=0)
    down_w = jnp.concatenate([expert_down, other_units[2 * BLOCK :]], axis=0)

    share = gain_attend.shape[0]
    wide = query_width + 2 * kv_width + query_width
    filler = jnp.zeros((share, 126), bf16)
    gathered = gather_weights(
        jnp.concatenate(
            [project_in, project_out, gain_attend[:, None], gain_expert[:, None], filler], axis=1
        )
    )
    gathered, grad_rows = lax.optimization_barrier((gathered, grad_rows))
    grad_arrived = exchange(grad_rows)
    in_full = gathered[:, : query_width + 2 * kv_width]
    out_full = gathered[:, query_width + 2 * kv_width : wide]
    gain_one, gain_two = (gathered[:, wide], gathered[:, wide + 1])

    row_values = own_low.astype(f32)
    normed_one, inverse_one = norm_forward(row_values, gain_one)
    normed_other, inverse_other = norm_forward(other_low.astype(f32), gain_one)
    kv_w = in_full[:, query_width:]
    projected = dot(normed_one, in_full)
    projected_other = dot(normed_other, kv_w)
    own_at = seq * token_count + jnp.arange(token_count)
    other_at = (1 - seq) * token_count + jnp.arange(token_count)
    own_cos, own_sin = rope_tables(own_at)
    other_cos, other_sin = rope_tables(other_at)
    query = rotate_wide(projected[:, :query_width], own_cos, own_sin, 1.0).astype(bf16)
    key_cut = query_width + kv_width
    own_keys = rotate_wide(projected[:, query_width:key_cut], own_cos, own_sin, 1.0)
    other_keys = rotate_wide(projected_other[:, :kv_width], other_cos, other_sin, 1.0)
    keys = jnp.concatenate([own_keys, other_keys], axis=0).astype(bf16)
    values = jnp.concatenate([projected[:, key_cut:], projected_other[:, kv_width:]], axis=0)
    query = query.reshape(token_count, KV_HEADS, group, HEAD_DIM)
    keys = keys.reshape(2 * token_count, KV_HEADS, HEAD_DIM)
    values = values.astype(bf16).reshape(2 * token_count, KV_HEADS, HEAD_DIM)
    seq_ids = segments[0]
    own_ids = lax.dynamic_slice(seq_ids, (seq * token_count,), (token_count,))
    other_ids = lax.dynamic_slice(seq_ids, ((1 - seq) * token_count,), (token_count,))
    key_at = jnp.concatenate([own_at, other_at])
    key_ids = jnp.concatenate([own_ids, other_ids])
    allowed = (key_at[None, :] <= own_at[:, None]) & (key_ids[None, :] == own_ids[:, None])
    attended, log_total = attend_forward(query, keys, values, allowed)
    mixed = attended.reshape(token_count, query_width)
    residual = row_values + dot(mixed, out_full)
    normed_two, inverse_two = norm_forward(residual, gain_two)

    arrived = exchange(dot(placed, normed_two).astype(bf16))
    hidden, grads, back = experts_first(arrived, grad_arrived, pre_w, down_w)
    grad_back = exchange(back)
    out_rows, gate_total, up_total, down_low = experts_second(arrived, grad_arrived, hidden, grads, down_w)
    grad_back, out_rows = lax.optimization_barrier((grad_back, out_rows))
    returned = exchange(out_rows)

    grad_out = cotangent[0].astype(f32)
    grad_normed_two = dot(placed, grad_back, TN)
    grad_norm_two, gain_two_grad = norm_backward(residual, inverse_two, gain_two, grad_normed_two)
    grad_residual = grad_out + grad_norm_two
    grad_res_low = grad_residual.astype(bf16)
    grad_mixed = dot(grad_res_low, out_full, NT).astype(bf16)
    grad_query, grad_keys, grad_values = attend_backward(
        query, keys, values, allowed, attended, log_total, grad_mixed.reshape(attended.shape)
    )
    grad_query = grad_query.reshape(token_count, query_width)
    grad_keys = grad_keys.reshape(2 * token_count, kv_width)
    grad_values = grad_values.reshape(2 * token_count, kv_width)
    away_keys = rotate_wide(grad_keys[token_count:], other_cos, other_sin, -1.0)
    away = jnp.concatenate([away_keys, grad_values[token_count:]], axis=1).astype(bf16)
    came = lax.ppermute(away, "seq", SWAP)
    grad_query = rotate_wide(grad_query, own_cos, own_sin, -1.0).astype(bf16)
    grad_keys = rotate_wide(grad_keys[:token_count], own_cos, own_sin, -1.0)
    grad_kv = jnp.concatenate([grad_keys, grad_values[:token_count]], axis=1).astype(bf16)
    from_query = dot(grad_query, in_full[:, :query_width], NT)
    from_kv = dot(jnp.concatenate([grad_kv, away], axis=0), kv_w, NT)
    from_own = from_query + from_kv[:token_count]
    other_values = other_low.astype(f32)
    gain_one_grad = jnp.sum(from_own * row_values * inverse_one, axis=0)
    gain_one_grad += jnp.sum(from_kv[token_count:] * other_values * inverse_other, axis=0)

    feature = jnp.arange(model_width)[:, None]
    slot = jnp.arange(model_width)[None, :]
    half_width = model_width // 2
    of_core = jnp.where(slot < half_width, core, 1 - core)
    at = slot % half_width
    chosen_half = feature == (2 * (at // share) + of_core) * share + at % share
    chosen_half = chosen_half.astype(bf16)
    features = jnp.concatenate([normed_one, normed_other, mixed], axis=0)
    features = dot(features, chosen_half).astype(bf16)
    gain_pair = jnp.stack([gain_one_grad, gain_two_grad], axis=0)
    gain_parts = jnp.concatenate(three_parts(gain_pair) + (jnp.zeros_like(gain_pair, bf16),), axis=0)
    gain_parts = dot(gain_parts, chosen_half).astype(bf16)
    gain_parts = jnp.stack([gain_parts[:, :half_width], gain_parts[:, half_width:]], axis=0)
    grads_mine, grads_sent = projection_grads(
        features[:, :half_width],
        features[:, half_width:],
        grad_query,
        jnp.concatenate([grad_kv, away], axis=0),
        grad_res_low,
        gain_parts,
    )
    in_width = query_width + 2 * kv_width
    in_total, out_total, gain_total, down_total = reduce_grads(
        grads_mine, grads_sent, down_low, in_width
    )
    gain_total = gain_total[:, :2] + gain_total[:, 2:4] + gain_total[:, 4:6]

    came, gain_total = lax.optimization_barrier((came, gain_total))
    grad_normed_one = from_own + dot(came, kv_w, NT)
    grad_norm_one, _ = norm_backward(row_values, inverse_one, gain_one, grad_normed_one)
    grad_inputs = (grad_residual + grad_norm_one).astype(bf16)

    mix = jnp.concatenate(mixers, axis=1)
    chosen = dot(mix, returned, TN).reshape(3, token_count, model_width)
    output = (residual + (chosen[2] + chosen[1] + chosen[0])).astype(bf16)
    return (
        output.reshape(1, token_count, model_width),
        grad_inputs.reshape(1, token_count, model_width),
        in_total,
        out_total,
        gain_total[:, 0],
        gain_total[:, 1],
        gate_total,
        up_total,
        down_total,
    )


def solution(mesh):
    devices = mesh.devices
    cores = Mesh(devices.reshape(devices.shape[0], -1, 2), ("seq", "chip", "core"))
    every = ("chip", "core")
    by_token = P(every, "seq", None)
    by_row = P(every, None)
    in_specs = (
        by_token,
        by_row,
        by_row,
        P(every),
        P(every),
        by_row,
        by_row,
        by_row,
        by_token,
        by_token,
        by_row,
        by_token,
    )
    out_specs = (by_token, by_token, by_row, by_row, P(every), P(every), by_row, by_row, by_row)
    return jax.shard_map(
        on_device, mesh=cores, in_specs=in_specs, out_specs=out_specs, check_vma=False
    )
```

```python
import jax
import jax.numpy as jnp
from jax import lax
from jax.experimental import pallas as pl
from jax.experimental.pallas import tpu as pltpu
from jax.sharding import Mesh, PartitionSpec as P

HEADS = 16
KV_HEADS = 8
HEAD_DIM = 64
EXPERTS = 32
FF = 512
TOP = 8
CAP = 36
SLOTS = 40
BLOCK = 256
ROW_BLOCK = 256

EPSILON = 1e-06
ROPE_BASE = 10000.0

f32 = jnp.float32
bf16 = jnp.bfloat16

RING = 4
MESH_ID = pl.DeviceIdType.MESH
SWAP = [(0, 1), (1, 0)]
NT = (((1,), (1,)), ((), ()))
TN = (((0,), (0,)), ((), ()))


def dot(a, b, dims=(((1,), (0,)), ((), ()))):
    return lax.dot_general(a, b, dims, preferred_element_type=f32)


def rope_tables(positions):
    half_dim = HEAD_DIM // 2
    powers = jnp.arange(half_dim).astype(f32) * (2.0 / HEAD_DIM)
    inverse_freq = ROPE_BASE ** (-powers)
    angles = positions.astype(f32)[:, None] * inverse_freq[None, :]
    return (jnp.cos(angles), jnp.sin(angles))


def rotate(values, cosine_table, sine_table, turn_sign):
    half_dim = values.shape[-1] // 2
    leading = values[..., :half_dim]
    trailing = values[..., half_dim:]
    cosine_b = cosine_table[:, None, :]
    sine_b = sine_table[:, None, :] * turn_sign
    return jnp.concatenate(
        [leading * cosine_b - trailing * sine_b, trailing * cosine_b + leading * sine_b], axis=-1
    )


def rotate_wide(values, cosine_table, sine_table, turn_sign):
    rows, width = values.shape
    heads = values.reshape(rows, width // HEAD_DIM, HEAD_DIM)
    return rotate(heads, cosine_table, sine_table, turn_sign).reshape(rows, width)


def norm_forward(values, gain_vector):
    inverse = lax.rsqrt(jnp.mean(values * values, axis=-1, keepdims=True) + EPSILON)
    return ((values * inverse * gain_vector.astype(f32)).astype(bf16), inverse)


def norm_backward(values, inverse, gain_vector, upstream):
    scaled = upstream * gain_vector.astype(f32)
    grad_gain = jnp.sum(upstream * values * inverse, axis=0)
    coupling = jnp.mean(scaled * values, axis=-1, keepdims=True)
    return (inverse * scaled - values * inverse * inverse * inverse * coupling, grad_gain)


def rounded(values):
    return lax.reduce_precision(values, exponent_bits=8, mantissa_bits=7)


def three_parts(values):
    first = rounded(values)
    second = rounded(values - first)
    third = values - first - second
    return (first.astype(bf16), second.astype(bf16), third.astype(bf16))


def masked_scores(query, keys, allowed):
    scores = jnp.einsum("qkgd,skd->kgqs", query, keys, preferred_element_type=f32)
    return jnp.where(allowed[None, None], scores * HEAD_DIM ** (-0.5), -1e30)


def attend_forward(query, keys, values, allowed):
    scores = masked_scores(query, keys, allowed)
    highest = jnp.max(scores, axis=-1, keepdims=True)
    log_total = highest + jnp.log(jnp.sum(jnp.exp(scores - highest), axis=-1, keepdims=True))
    weights = jnp.exp(scores - log_total).astype(bf16)
    mixed = jnp.einsum("kgqs,skd->qkgd", weights, values, preferred_element_type=f32)
    return (mixed.astype(bf16), log_total)


def experts_first_body(x_ref, g_ref, pre_w_ref, down_w_ref, hidden_ref, grads_ref, back_ref):
    pre = dot(x_ref[...], pre_w_ref[...], NT)
    grad_hidden = dot(g_ref[...], down_w_ref[...], NT)
    back = None
    for b in range(FF // BLOCK):
        gate = pre[:, 2 * b * BLOCK : (2 * b + 1) * BLOCK]
        up = pre[:, (2 * b + 1) * BLOCK : (2 * b + 2) * BLOCK]
        grad_h = grad_hidden[:, b * BLOCK : (b + 1) * BLOCK]
        sigmoid_gate = 1.0 / (1.0 + jnp.exp(-gate))
        silu = gate * sigmoid_gate
        hidden_ref[:, b * BLOCK : (b + 1) * BLOCK] = (silu * up).astype(bf16)
        grad_gate = (grad_h * up * sigmoid_gate * (1.0 + gate * (1.0 - sigmoid_gate))).astype(bf16)
        grad_up = (grad_h * gate * sigmoid_gate).astype(bf16)
        both = jnp.concatenate([grad_gate, grad_up], axis=1)
        grads_ref[:, 2 * b * BLOCK : (2 * b + 2) * BLOCK] = both
        part = dot(both, pre_w_ref[2 * b * BLOCK : (2 * b + 2) * BLOCK, :]).astype(bf16).astype(f32)
        back = part if back is None else back + part
    back_ref[...] = back.astype(bf16)


def experts_first(arrived, grad_arrived, pre_w, down_w):
    rows, width = arrived.shape
    whole = lambda i: (0, 0)
    by_row = lambda i: (i, 0)
    return pl.pallas_call(
        experts_first_body,
        grid=(rows // ROW_BLOCK,),
        in_specs=[
            pl.BlockSpec((ROW_BLOCK, width), by_row),
            pl.BlockSpec((ROW_BLOCK, width), by_row),
            pl.BlockSpec((2 * FF, width), whole),
            pl.BlockSpec((FF, width), whole),
        ],
        out_specs=[
            pl.BlockSpec((ROW_BLOCK, FF), by_row),
            pl.BlockSpec((ROW_BLOCK, 2 * FF), by_row),
            pl.BlockSpec((ROW_BLOCK, width), by_row),
        ],
        out_shape=[
            jax.ShapeDtypeStruct((rows, FF), bf16),
            jax.ShapeDtypeStruct((rows, 2 * FF), bf16),
            jax.ShapeDtypeStruct((rows, width), bf16),
        ],
        cost_estimate=pl.CostEstimate(
            flops=2 * rows * width * FF * 5,
            bytes_accessed=rows * width * 2 * 5,
            transcendentals=rows * FF,
        ),
        name="experts_first",
    )(arrived, grad_arrived, pre_w, down_w)


def experts_second_body(
    x_ref,
    g_ref,
    hidden_ref,
    grads_ref,
    down_w_ref,
    out_ref,
    gate_ref,
    up_ref,
    third_ref,
    theirs,
    came,
    last,
    low,
    low_came,
    send_sem,
    recv_sem,
):
    seq, chip, core = (lax.axis_index(name) for name in ("seq", "chip", "core"))
    partner = (seq, chip, 1 - core)
    mirror = (1 - seq, chip, core)
    barrier = pltpu.get_barrier_semaphore()
    for other in (partner, mirror):
        pl.semaphore_signal(barrier, inc=1, device_id=other, device_id_type=MESH_ID)
    pl.semaphore_wait(barrier, 2)
    width = x_ref.shape[1]

    def send(i, src, dst, to):
        return pltpu.make_async_remote_copy(
            src_ref=src,
            dst_ref=dst,
            send_sem=send_sem.at[i],
            recv_sem=recv_sem.at[i],
            device_id=to,
            device_id_type=MESH_ID,
        )

    def unit_grads(block, kind, target):
        if kind < 2:
            at = (2 * block + kind) * BLOCK
            left, right = (grads_ref, x_ref)
        else:
            at = block * BLOCK
            left, right = (hidden_ref, g_ref)

        @pl.loop(0, width // BLOCK)
        def _(n):
            columns = pl.ds(pl.multiple_of(n * BLOCK, BLOCK), BLOCK)
            target[:, columns] = dot(left[:, at : at + BLOCK], right[:, columns], TN)

    away = [send(k, theirs.at[k], came.at[k], partner) for k in range(3)]
    across = [send(3 + k, low.at[k], low_came.at[k], mirror) for k in range(2)]
    mine = [gate_ref, up_ref, last]
    lows = [low.at[0], low.at[1], third_ref]
    for k in range(3):
        unit_grads(1, k, theirs.at[k])
        if k:
            away[k - 1].start()
    unit_grads(0, 0, mine[0])
    away[2].start()

    def join(k):
        away[k].wait_recv()

        @pl.loop(0, BLOCK // 32)
        def _(r):
            rows = pl.ds(pl.multiple_of(r * 32, 32), 32)
            lows[k][rows, :] = (mine[k][rows, :] + came[k, rows, :]).astype(bf16)

    for k in range(3):
        join(k)
        if k < 2:
            unit_grads(0, k + 1, mine[k + 1])
            across[k].start()

    @pl.loop(0, x_ref.shape[0] // ROW_BLOCK)
    def _(r):
        rows = pl.ds(pl.multiple_of(r * ROW_BLOCK, ROW_BLOCK), ROW_BLOCK)
        out = None
        for b in range(FF // BLOCK):
            units = slice(b * BLOCK, (b + 1) * BLOCK)
            part = dot(hidden_ref[rows, units], down_w_ref[units, :]).astype(bf16).astype(f32)
            out = part if out is None else out + part
        out_ref[rows, :] = out.astype(bf16)

    for k in range(2):
        across[k].wait_recv()

        @pl.loop(0, BLOCK // 32)
        def _(r):
            rows = pl.ds(pl.multiple_of(r * 32, 32), 32)
            mine[k][rows, :] = low[k, rows, :].astype(f32) + low_came[k, rows, :].astype(f32)

    for copy in away + across:
        copy.wait_send()


def experts_second(arrived, grad_arrived, hidden, grads, down_w):
    rows, width = arrived.shape
    return pl.pallas_call(
        experts_second_body,
        in_specs=[pl.BlockSpec(memory_space=pltpu.VMEM)] * 5,
        out_specs=[pl.BlockSpec(memory_space=pltpu.VMEM)] * 4,
        out_shape=[
            jax.ShapeDtypeStruct((rows, width), bf16),
            jax.ShapeDtypeStruct((BLOCK, width), f32),
            jax.ShapeDtypeStruct((BLOCK, width), f32),
            jax.ShapeDtypeStruct((BLOCK, width), bf16),
        ],
        scratch_shapes=[
            pltpu.VMEM((3, BLOCK, width), f32),
            pltpu.VMEM((3, BLOCK, width), f32),
            pltpu.VMEM((BLOCK, width), f32),
            pltpu.VMEM((2, BLOCK, width), bf16),
            pltpu.VMEM((2, BLOCK, width), bf16),
            pltpu.SemaphoreType.DMA((5,)),
            pltpu.SemaphoreType.DMA((5,)),
        ],
        compiler_params=pltpu.CompilerParams(collective_id=1, has_side_effects=True),
        cost_estimate=pl.CostEstimate(
            flops=2 * rows * width * FF * 4,
            bytes_accessed=rows * width * 2 * 20,
            transcendentals=0,
        ),
        name="experts_second",
    )(arrived, grad_arrived, hidden, grads, down_w)


def gather_body(shard_ref, out_ref, send_sem, recv_sem, local_sem):
    seq, chip, core = (lax.axis_index(name) for name in ("seq", "chip", "core"))
    y, z, half = (chip // (2 * RING), (chip // 2) % RING, chip % 2)

    def device(to_y, to_z, to_half, to_core):
        return (seq, (to_y * RING + to_z) * 2 + to_half, to_core)

    def first(step):
        return device((y + core * step) % RING, (z + (1 - core) * step) % RING, half, core)

    def last(step):
        return device((y + (1 - core) * step) % RING, (z + core * step) % RING, half, core)

    partner = device(y, z, half, 1 - core)
    across = (1 - seq, chip + 1 - 2 * half, core)
    ahead, behind = (1, RING - 1)
    barrier = pltpu.get_barrier_semaphore()
    for other in (partner, across, first(ahead), first(behind), last(ahead), last(behind)):
        pl.semaphore_signal(barrier, inc=1, device_id=other, device_id_type=MESH_ID)
    pl.semaphore_wait(barrier, 6)

    def send(i, src, dst, to):
        return pltpu.make_async_remote_copy(
            src_ref=src,
            dst_ref=dst,
            send_sem=send_sem.at[i],
            recv_sem=recv_sem.at[i],
            device_id=to,
            device_id_type=MESH_ID,
        )

    def pair(c, f, l, part=None):
        cut = slice(None) if part is None else part
        to_y, to_z = (l, f) if c == 0 else (f, l)
        return out_ref.at[(y + to_y) % RING, (z + to_z) % RING, cut, c]

    def run(c):
        sent = []

        def go(i, region, to):
            copy = send(i, region, region, to)
            copy.start()
            sent.append(copy)

        def arrive(i, region):
            send(i, region, region, partner).wait_recv()

        def spread(f):
            go(5 + 2 * f, pair(c, f, 0), last(ahead))
            go(6 + 2 * f, pair(c, f, 0), last(behind))
            go(21 + 5 * f, pair(c, f, 0), partner)

        def relay(f):
            arrive(5 + 2 * f, pair(c, f, behind))
            go(13 + 2 * f, pair(c, f, behind, 0), last(ahead))
            go(22 + 5 * f, pair(c, f, behind), partner)
            arrive(6 + 2 * f, pair(c, f, ahead))
            go(14 + 2 * f, pair(c, f, ahead, 1), last(behind))
            go(23 + 5 * f, pair(c, f, ahead), partner)

        own = out_ref.at[y, z, half, c]
        copy = send(0, shard_ref, own, across)
        copy.start()
        sent.append(copy)
        local = pltpu.make_async_copy(shard_ref, own, local_sem)
        local.start()
        local.wait()
        arrive(0, out_ref.at[y, z, 1 - half, c])
        go(1, pair(c, 0, 0), first(ahead))
        go(2, pair(c, 0, 0), first(behind))
        spread(0)
        arrive(1, pair(c, behind, 0))
        go(3, pair(c, behind, 0, 0), first(ahead))
        spread(behind)
        arrive(2, pair(c, ahead, 0))
        go(4, pair(c, ahead, 0, 1), first(behind))
        spread(ahead)
        relay(0)
        arrive(3, pair(c, 2, 0, 0))
        arrive(4, pair(c, 2, 0, 1))
        spread(2)
        for f in (behind, ahead, 2):
            relay(f)
        for f in (0, behind, ahead, 2):
            for part in range(2):
                arrive(13 + 2 * f + part, pair(c, f, 2, part))
                go(24 + 5 * f + part, pair(c, f, 2, part), partner)
        for f in (0, behind, ahead, 2):
            arrive(21 + 5 * f, pair(1 - c, f, 0))
            arrive(22 + 5 * f, pair(1 - c, f, behind))
            arrive(23 + 5 * f, pair(1 - c, f, ahead))
            for part in range(2):
                arrive(24 + 5 * f + part, pair(1 - c, f, 2, part))
        for copy in sent:
            copy.wait_send()

    for c in (0, 1):
        pl.when(core == c)(lambda c=c: run(c))


def gather_weights(shard):
    rows, width = shard.shape
    out = pl.pallas_call(
        gather_body,
        out_shape=jax.ShapeDtypeStruct((RING, RING, 2, 2, rows, width), shard.dtype),
        in_specs=[pl.BlockSpec(memory_space=pltpu.VMEM)],
        out_specs=pl.BlockSpec(memory_space=pl.ANY),
        scratch_shapes=[
            pltpu.SemaphoreType.DMA((41,)),
            pltpu.SemaphoreType.DMA((41,)),
            pltpu.SemaphoreType.DMA,
        ],
        compiler_params=pltpu.CompilerParams(collective_id=0, has_side_effects=True),
        cost_estimate=pl.CostEstimate(
            flops=0, bytes_accessed=rows * width * 2 * 4 * RING * RING * 8, transcendentals=0
        ),
        name="gather_weights",
    )(shard)
    return out.reshape(4 * RING * RING * rows, width)


def projection_grads_body(mine_ref, sent_ref, gq_ref, gkv_ref, gr_ref, gains_ref, total_ref, away_ref):
    query = gq_ref.shape[1]
    width = query + gkv_ref.shape[1]
    wide = width + gr_ref.shape[1]
    spread = lax.broadcasted_iota(jnp.int32, (8, 128), 0)
    lane = lax.broadcasted_iota(jnp.int32, (8, 128), 1)
    apart = ((spread == lane) & (spread < 6)).astype(bf16)
    tokens = gq_ref.shape[0]
    for ref, out_ref, which in ((mine_ref, total_ref, 0), (sent_ref, away_ref, 1)):
        out_ref[:, :query] = dot(ref[:tokens, :], gq_ref[...], TN).astype(out_ref.dtype)
        out_ref[:, query:width] = dot(ref[: 2 * tokens, :], gkv_ref[...], TN).astype(out_ref.dtype)
        out_ref[:, width:wide] = dot(ref[2 * tokens :, :], gr_ref[...], TN).astype(out_ref.dtype)
        out_ref[:, wide:] = dot(gains_ref[which], apart, TN).astype(out_ref.dtype)


def projection_grads(rows_mine, rows_sent, grad_query, grad_kv, grad_res_low, gains):
    count = rows_mine.shape[1]
    width = grad_query.shape[1] + grad_kv.shape[1] + grad_res_low.shape[1] + 128
    tile = 128
    whole = lambda i: (0, 0)
    by_column = lambda i: (0, i)
    by_row = lambda i: (i, 0)
    return pl.pallas_call(
        projection_grads_body,
        grid=(count // tile,),
        in_specs=[
            pl.BlockSpec((rows_mine.shape[0], tile), by_column),
            pl.BlockSpec((rows_sent.shape[0], tile), by_column),
            pl.BlockSpec(grad_query.shape, whole),
            pl.BlockSpec(grad_kv.shape, whole),
            pl.BlockSpec(grad_res_low.shape, whole),
            pl.BlockSpec((2, 8, tile), lambda i: (0, 0, i)),
        ],
        out_specs=[pl.BlockSpec((tile, width), by_row), pl.BlockSpec((tile, width), by_row)],
        out_shape=[
            jax.ShapeDtypeStruct((count, width), f32),
            jax.ShapeDtypeStruct((count, width), bf16),
        ],
        name="projection_grads",
    )(rows_mine, rows_sent, grad_query, grad_kv, grad_res_low, gains)


def packed(values):
    lane = lax.broadcasted_iota(jnp.int32, (values.shape[0], 128), 1)
    wide = values.shape[1] - 128
    parts = values[:, wide:]
    total = parts + pltpu.roll(parts, 126, 1) + pltpu.roll(parts, 124, 1)
    total = jnp.where(lane < 2, total, 0.0)
    one = total.astype(bf16).astype(f32)
    two = (total - one).astype(bf16).astype(f32)
    three = total - one - two
    tail = one + pltpu.roll(two, 2, 1) + pltpu.roll(three, 4, 1)
    return jnp.concatenate([values[:, :wide].astype(bf16), tail.astype(bf16)], axis=1)


def reduce_body(
    mine,
    sent,
    low,
    in_ref,
    out_ref,
    gain_ref,
    unit_ref,
    came,
    acc,
    stage,
    in1,
    in2,
    stage_a,
    in_a1,
    in_a2,
    stage_x,
    in_x,
    own,
    in_own,
    low_came,
    chip_send,
    chip_recv,
    ring_send,
    ring_recv,
):
    seq, chip, core = (lax.axis_index(name) for name in ("seq", "chip", "core"))
    y, z, half = (chip // (2 * RING), (chip // 2) % RING, chip % 2)
    flip = 1 - core
    at_last = flip * y + core * z
    at_first = flip * z + core * y

    def device(to_y, to_z, to_half, to_core):
        return (seq, (to_y * RING + to_z) * 2 + to_half, to_core)

    def first(step):
        return device((y + core * step) % RING, (z + flip * step) % RING, half, core)

    def last(step):
        return device((y + flip * step) % RING, (z + core * step) % RING, half, core)

    partner = device(y, z, half, flip)
    across = (1 - seq, chip + 1 - 2 * half, core)
    mirror = (1 - seq, chip, core)
    ahead, behind = (1, RING - 1)
    barrier = pltpu.get_barrier_semaphore()
    others = (partner, across, mirror, first(ahead), first(behind), last(ahead), last(behind))
    for other in others:
        pl.semaphore_signal(barrier, inc=1, device_id=other, device_id_type=MESH_ID)
    pl.semaphore_wait(barrier, len(others))

    def send(i, src, dst, to):
        return pltpu.make_async_remote_copy(
            src_ref=src,
            dst_ref=dst,
            send_sem=ring_send.at[i],
            recv_sem=ring_recv.at[i],
            device_id=to,
            device_id_type=MESH_ID,
        )

    def on_chip(s, j, of_core):
        line = ((1 - of_core) * y + of_core * z + s) % RING
        a = (1 - of_core) * line + of_core * j
        b = (1 - of_core) * j + of_core * line
        return (
            a,
            b,
            pltpu.make_async_remote_copy(
                src_ref=sent.at[a, b],
                dst_ref=came.at[a, b],
                send_sem=chip_send.at[s, j],
                recv_sem=chip_recv.at[s, j],
                device_id=partner,
                device_id_type=MESH_ID,
            ),
        )

    order = (2, ahead, behind, 0)
    two = RING // 2
    units = send(12, low, low_came, mirror)
    units.start()
    for s in order:

        @pl.loop(0, RING)
        def _(j):
            on_chip(s, j, flip)[2].start()

    ring = [
        send(0, stage.at[2, :two], in1.at[0], last(ahead)),
        send(1, stage.at[2, two:], in1.at[1], last(behind)),
        send(2, stage.at[1, two:], in2.at[0, two:], last(ahead)),
        send(3, stage.at[1, :two], in2.at[0, :two], last(ahead)),
        send(4, stage.at[3, :two], in2.at[1, :two], last(behind)),
        send(5, stage.at[3, two:], in2.at[1, two:], last(behind)),
        send(6, stage_a.at[2, 0], in_a1.at[0], first(ahead)),
        send(7, stage_a.at[2, 1], in_a1.at[1], first(behind)),
        send(8, stage_a.at[1], in_a2.at[0], first(ahead)),
        send(9, stage_a.at[3], in_a2.at[1], first(behind)),
        send(10, stage_x, in_x, across),
        send(11, own, in_own, mirror),
    ]

    def merge(s, low_j, high_j, to_stage):
        @pl.loop(low_j, high_j)
        def _(j):
            a, b, copy = on_chip(s, j, core)
            copy.wait_recv()
            for h in range(2):
                value = mine[a, b, h] + came[a, b, h].astype(f32)
                if to_stage:
                    stage[s, j, h] = packed(value)
                if not to_stage or s != 2:
                    acc[s, j, h] = value

    merge(2, 0, RING, True)
    ring[0].start()
    ring[1].start()
    merge(ahead, 0, RING, True)
    ring[2].start()
    merge(behind, 0, RING, True)
    ring[4].start()
    merge(0, 0, RING, False)
    for i, s, source, first_j in ((0, ahead, 0, 0), (1, behind, 1, two)):
        ring[i].wait_recv()

        @pl.loop(0, two)
        def _(k):
            for h in range(2):
                value = acc[s, first_j + k, h] + in1[source, k, h].astype(f32)
                stage[s, first_j + k, h] = packed(value)

        ring[3 if i == 0 else 5].start()

    for i, source, first_j in ((2, 0, two), (4, 1, 0), (3, 0, 0), (5, 1, two)):
        ring[i].wait_recv()

        @pl.loop(first_j, first_j + two)
        def _(j):
            for h in range(2):
                acc[0, j, h] = acc[0, j, h] + in2[source, j, h].astype(f32)

    def at(step):
        return (at_first + step) % RING

    for h in range(2):
        stage_a[2, h] = packed(acc[0, at(2), h])
    ring[6].start()
    ring[7].start()
    stage_a[1, 1] = packed(acc[0, at(ahead), 1])
    stage_a[3, 0] = packed(acc[0, at(behind), 0])
    ring[6].wait_recv()
    stage_a[1, 0] = packed(acc[0, at(ahead), 0] + in_a1[0].astype(f32))
    ring[8].start()
    ring[7].wait_recv()
    stage_a[3, 1] = packed(acc[0, at(behind), 1] + in_a1[1].astype(f32))
    ring[9].start()
    ring[8].wait_recv()
    ring[9].wait_recv()
    away = 1 - half
    stage_x[...] = packed(
        acc[0, at_first, away] + in_a2[0, away].astype(f32) + in_a2[1, away].astype(f32)
    )
    ring[10].start()
    own[...] = acc[0, at_first, half] + in_a2[0, half].astype(f32) + in_a2[1, half].astype(f32)
    ring[10].wait_recv()
    own[...] = own[...] + in_x[...].astype(f32)
    ring[11].start()
    units.wait_recv()

    @pl.loop(0, low.shape[0] // 32)
    def _(r):
        rows = pl.ds(pl.multiple_of(r * 32, 32), 32)
        unit_ref[rows, :] = low[rows, :].astype(f32) + low_came[rows, :].astype(f32)

    ring[11].wait_recv()
    total = own[...] + in_own[...]
    cut = in_ref.shape[1]
    wide = cut + out_ref.shape[1]
    in_ref[...] = total[:, :cut]
    out_ref[...] = total[:, cut:wide]
    gain_ref[...] = total[:, wide:]
    units.wait_send()
    for copy in ring:
        copy.wait_send()
    for s in order:

        @pl.loop(0, RING)
        def _(j):
            on_chip(s, j, flip)[2].wait_send()


def reduce_grads(mine, sent, low, cut):
    width = mine.shape[1]
    share = mine.shape[0] // (2 * RING * RING)
    shape = (RING, RING, 2, share, width)
    two = RING // 2
    pair = (2, share, width)
    return pl.pallas_call(
        reduce_body,
        in_specs=[pl.BlockSpec(memory_space=pltpu.VMEM)] * 3,
        out_specs=[pl.BlockSpec(memory_space=pltpu.VMEM)] * 4,
        out_shape=[
            jax.ShapeDtypeStruct((share, cut), f32),
            jax.ShapeDtypeStruct((share, width - cut - 128), f32),
            jax.ShapeDtypeStruct((share, 128), f32),
            jax.ShapeDtypeStruct(low.shape, f32),
        ],
        scratch_shapes=[
            pltpu.VMEM(shape, bf16),
            pltpu.VMEM(shape, f32),
            pltpu.VMEM(shape, bf16),
            pltpu.VMEM((2, two) + pair, bf16),
            pltpu.VMEM((2, RING) + pair, bf16),
            pltpu.VMEM((RING,) + pair, bf16),
            pltpu.VMEM(pair, bf16),
            pltpu.VMEM((2,) + pair, bf16),
            pltpu.VMEM((share, width), bf16),
            pltpu.VMEM((share, width), bf16),
            pltpu.VMEM((share, width), f32),
            pltpu.VMEM((share, width), f32),
            pltpu.VMEM(low.shape, bf16),
            pltpu.SemaphoreType.DMA((RING, RING)),
            pltpu.SemaphoreType.DMA((RING, RING)),
            pltpu.SemaphoreType.DMA((13,)),
            pltpu.SemaphoreType.DMA((13,)),
        ],
        compiler_params=pltpu.CompilerParams(collective_id=2, has_side_effects=True),
        cost_estimate=pl.CostEstimate(
            flops=mine.size, bytes_accessed=mine.size, transcendentals=0
        ),
        name="reduce_grads",
    )(mine.reshape(shape), sent.reshape(shape), low)


def rotated(block, cosine, sine, first_half):
    partner = jnp.where(first_half, pltpu.roll(block, 96, 1), pltpu.roll(block, 32, 1))
    return block * cosine + partner * sine


def block_backward_body(
    placed_ref,
    back_ref,
    residual_ref,
    inverse_ref,
    gain_ref,
    cotangent_ref,
    weights_hbm,
    query_ref,
    keys_ref,
    values_ref,
    allowed_ref,
    attended_ref,
    log_ref,
    cosine_ref,
    sine_ref,
    own_ref,
    other_ref,
    residual_out,
    low_out,
    query_out,
    kv_out,
    from_out,
    gains_out,
    weights,
    sems,
):
    tokens, width = residual_ref.shape
    kv_width = keys_ref.shape[1]
    in_width = width + 2 * kv_width
    out_part = pltpu.make_async_copy(
        weights_hbm.at[:, in_width : in_width + width],
        weights.at[:, in_width : in_width + width],
        sems.at[0],
    )
    in_part = pltpu.make_async_copy(
        weights_hbm.at[:, :in_width], weights.at[:, :in_width], sems.at[1]
    )
    out_part.start()
    in_part.start()
    residual = residual_ref[...]
    inverse = inverse_ref[...]
    upstream = dot(placed_ref[...], back_ref[...], TN)
    gains_out[1:2, :] = jnp.sum(upstream * residual * inverse, axis=0, keepdims=True)
    scaled = upstream * gain_ref[...]
    coupling = jnp.mean(scaled * residual, axis=-1, keepdims=True)
    grad = inverse * scaled - residual * inverse * inverse * inverse * coupling
    grad = cotangent_ref[...].astype(f32) + grad
    residual_out[...] = grad
    low = grad.astype(bf16)
    low_out[...] = low
    out_part.wait()
    grad_mixed = dot(low, weights[:, in_width : in_width + width], NT).astype(bf16)

    lane = lax.broadcasted_iota(jnp.int32, (1, 128), 1)
    low_lanes = lane < HEAD_DIM
    first_half = lane % HEAD_DIM < HEAD_DIM // 2
    allowed = allowed_ref[...] != 0
    cosine, sine = (cosine_ref[...], sine_ref[...])
    scale = HEAD_DIM ** (-0.5)

    def doubled(block, place):
        wide = block.astype(f32)
        turned = pltpu.roll(wide, HEAD_DIM, 1)
        pair = (wide, turned) if place == 0 else (turned, wide)
        return jnp.where(low_lanes, pair[0], pair[1]).astype(bf16)

    for m in range(KV_HEADS // 2):
        kv_lanes = slice(m * 128, (m + 1) * 128)
        key_parts, value_parts = ([], [])
        for place in range(2):
            j = 2 * m + place
            lanes = slice(j * 128, (j + 1) * 128)
            keys = doubled(keys_ref[:, kv_lanes], place)
            values = doubled(values_ref[:, kv_lanes], place)
            grad_block = grad_mixed[:, lanes].astype(f32)
            product = grad_block * attended_ref[:, lanes].astype(f32)
            query_block = query_ref[:, lanes].astype(f32)
            grad_query = []
            grad_keys, grad_values = (None, None)
            for part in range(2):
                mine = low_lanes if part == 0 else jnp.logical_not(low_lanes)
                query = jnp.where(mine, query_block, 0.0).astype(bf16)
                upper = jnp.where(mine, grad_block, 0.0).astype(bf16)
                scores = jnp.where(allowed, dot(query, keys, NT) * scale, -1e30)
                exact = jnp.exp(scores - log_ref[:, 2 * j + part : 2 * j + part + 1])
                delta = jnp.sum(jnp.where(mine, product, 0.0), axis=-1, keepdims=True)
                grad_scores = (exact * (dot(upper, values, NT) - delta)).astype(bf16)
                grad_query.append(dot(grad_scores, keys))
                to_keys = dot(grad_scores, query, TN)
                to_values = dot(exact.astype(bf16), upper, TN)
                grad_keys = to_keys if part == 0 else grad_keys + to_keys
                grad_values = to_values if part == 0 else grad_values + to_values
            both = jnp.where(low_lanes, grad_query[0], grad_query[1]) * scale
            both = rotated(both, cosine[:tokens], sine[:tokens], first_half)
            query_out[:, lanes] = both.astype(bf16)
            key_parts.append(grad_keys + pltpu.roll(grad_keys, HEAD_DIM, 1))
            value_parts.append(grad_values + pltpu.roll(grad_values, HEAD_DIM, 1))
        grad_keys = jnp.where(low_lanes, key_parts[0], key_parts[1]) * scale
        kv_out[:, kv_lanes] = rotated(grad_keys, cosine, sine, first_half).astype(bf16)
        value_lanes = slice(kv_width + m * 128, kv_width + (m + 1) * 128)
        kv_out[:, value_lanes] = jnp.where(low_lanes, value_parts[0], value_parts[1]).astype(bf16)

    in_part.wait()
    from_kv = dot(kv_out[...], weights[:, width:in_width], NT)
    from_own = dot(query_out[...], weights[:, :width], NT) + from_kv[:tokens]
    from_out[...] = from_own
    gain = jnp.sum(from_own * own_ref[...], axis=0, keepdims=True)
    gain += jnp.sum(from_kv[tokens:] * other_ref[...], axis=0, keepdims=True)
    gains_out[0:1, :] = gain


def block_backward(
    placed, back, residual, inverse, gain, cotangent, weights, heads, masks, tables, scaled_inputs
):
    tokens, width = residual.shape
    query, keys, values = heads
    vmem = pl.BlockSpec(memory_space=pltpu.VMEM)
    return pl.pallas_call(
        block_backward_body,
        in_specs=[vmem] * 6 + [pl.BlockSpec(memory_space=pl.ANY)] + [vmem] * 10,
        out_specs=[vmem] * 6,
        out_shape=[
            jax.ShapeDtypeStruct((tokens, width), f32),
            jax.ShapeDtypeStruct((tokens, width), bf16),
            jax.ShapeDtypeStruct((tokens, width), bf16),
            jax.ShapeDtypeStruct((2 * tokens, 2 * keys.shape[1]), bf16),
            jax.ShapeDtypeStruct((tokens, width), f32),
            jax.ShapeDtypeStruct((2, width), f32),
        ],
        scratch_shapes=[pltpu.VMEM(weights.shape, bf16), pltpu.SemaphoreType.DMA((2,))],
        cost_estimate=pl.CostEstimate(
            flops=3_000_000_000, bytes_accessed=12_000_000, transcendentals=600_000
        ),
        name="block_backward",
    )(
        placed,
        back,
        residual,
        inverse,
        gain,
        cotangent,
        weights,
        query,
        keys,
        values,
        *masks,
        *tables,
        *scaled_inputs,
    )


def spread_plan(route_ids, mix_weights):
    token_count = route_ids.shape[0]
    expert_ids = jnp.arange(EXPERTS)[None, None, :]
    named = route_ids[:, :, None] == expert_ids
    picked = jnp.any(named, axis=1)
    token_weight = jnp.sum(jnp.where(named, mix_weights[:, :, None], 0.0), axis=1)
    earlier = jnp.arange(token_count)[None, :] < jnp.arange(token_count)[:, None]
    rank = dot(earlier.astype(bf16), picked.astype(bf16)).astype(jnp.int32)
    at_slot = jnp.where(picked, rank, -1).T[:, None, :] == jnp.arange(SLOTS)[None, :, None]
    placed = at_slot.astype(bf16).reshape(EXPERTS * SLOTS, token_count)
    weighted = jnp.where(at_slot, token_weight.T[:, None, :], 0.0)
    slot_weight = jnp.sum(weighted, axis=2).reshape(EXPERTS * SLOTS, 1)
    mixers = [part.reshape(EXPERTS * SLOTS, token_count) for part in three_parts(weighted)]
    return (placed, slot_weight, mixers)


def exchange(rows):
    width = rows.shape[-1]
    blocks = rows.reshape(EXPERTS, -1, width)
    groups = [[(g ^ (c % 2)) * EXPERTS + c for c in range(EXPERTS)] for g in range(2)]
    landed = lax.all_to_all(
        blocks,
        ("seq", "chip"),
        split_axis=0,
        concat_axis=0,
        axis_index_groups=groups,
        tiled=True,
    )
    return landed.reshape(-1, width)


def on_device(
    inputs,
    project_in,
    project_out,
    gain_attend,
    gain_expert,
    expert_gate,
    expert_up,
    expert_down,
    routes,
    route_weights,
    segments,
    cotangent,
):
    token_count = inputs.shape[1]
    model_width = inputs.shape[2]
    query_width = HEADS * HEAD_DIM
    kv_width = KV_HEADS * HEAD_DIM
    group = HEADS // KV_HEADS
    seq = lax.axis_index("seq")
    core = lax.axis_index("core")
    own_low = inputs[0]
    other_low = lax.ppermute(own_low, "seq", SWAP)

    placed, slot_weight, mixers = spread_plan(routes[0], route_weights[0])
    grad_rows = (dot(placed, cotangent[0]) * slot_weight).astype(bf16)

    own_units = jnp.concatenate([expert_gate, expert_up, expert_down], axis=0)
    other_units = lax.ppermute(own_units, "core", SWAP)
    pre_w = jnp.concatenate([own_units[: 2 * BLOCK], other_units[: 2 * BLOCK]], axis=0)
    down_w = jnp.concatenate([expert_down, other_units[2 * BLOCK :]], axis=0)

    share = gain_attend.shape[0]
    wide = query_width + 2 * kv_width + query_width
    filler = jnp.zeros((share, 126), bf16)
    gathered = gather_weights(
        jnp.concatenate(
            [project_in, project_out, gain_attend[:, None], gain_expert[:, None], filler], axis=1
        )
    )
    gathered, grad_rows = lax.optimization_barrier((gathered, grad_rows))
    grad_arrived = exchange(grad_rows)
    in_full = gathered[:, : query_width + 2 * kv_width]
    out_full = gathered[:, query_width + 2 * kv_width : wide]
    gain_one, gain_two = (gathered[:, wide], gathered[:, wide + 1])

    row_values = own_low.astype(f32)
    normed_one, inverse_one = norm_forward(row_values, gain_one)
    normed_other, inverse_other = norm_forward(other_low.astype(f32), gain_one)
    kv_w = in_full[:, query_width:]
    projected = dot(normed_one, in_full)
    projected_other = dot(normed_other, kv_w)
    own_at = seq * token_count + jnp.arange(token_count)
    other_at = (1 - seq) * token_count + jnp.arange(token_count)
    own_cos, own_sin = rope_tables(own_at)
    other_cos, other_sin = rope_tables(other_at)
    query = rotate_wide(projected[:, :query_width], own_cos, own_sin, 1.0).astype(bf16)
    key_cut = query_width + kv_width
    own_keys = rotate_wide(projected[:, query_width:key_cut], own_cos, own_sin, 1.0)
    other_keys = rotate_wide(projected_other[:, :kv_width], other_cos, other_sin, 1.0)
    keys = jnp.concatenate([own_keys, other_keys], axis=0).astype(bf16)
    values = jnp.concatenate([projected[:, key_cut:], projected_other[:, kv_width:]], axis=0)
    flat_heads = (query, keys, values.astype(bf16))
    query = query.reshape(token_count, KV_HEADS, group, HEAD_DIM)
    keys = keys.reshape(2 * token_count, KV_HEADS, HEAD_DIM)
    values = values.astype(bf16).reshape(2 * token_count, KV_HEADS, HEAD_DIM)
    seq_ids = segments[0]
    own_ids = lax.dynamic_slice(seq_ids, (seq * token_count,), (token_count,))
    other_ids = lax.dynamic_slice(seq_ids, ((1 - seq) * token_count,), (token_count,))
    key_at = jnp.concatenate([own_at, other_at])
    key_ids = jnp.concatenate([own_ids, other_ids])
    allowed = (key_at[None, :] <= own_at[:, None]) & (key_ids[None, :] == own_ids[:, None])
    attended, log_total = attend_forward(query, keys, values, allowed)
    mixed = attended.reshape(token_count, query_width)
    residual = row_values + dot(mixed, out_full)
    normed_two, inverse_two = norm_forward(residual, gain_two)

    arrived = exchange(dot(placed, normed_two).astype(bf16))
    hidden, grads, back = experts_first(arrived, grad_arrived, pre_w, down_w)
    grad_back = exchange(back)
    out_rows, gate_total, up_total, down_low = experts_second(arrived, grad_arrived, hidden, grads, down_w)
    grad_back, out_rows = lax.optimization_barrier((grad_back, out_rows))
    returned = exchange(out_rows)

    log_rows = log_total.reshape(HEADS, token_count).T
    lanes = jnp.arange(128)
    cosine = jnp.concatenate([own_cos, other_cos], axis=0)[:, lanes % (HEAD_DIM // 2)]
    sine = jnp.concatenate([own_sin, other_sin], axis=0)[:, lanes % (HEAD_DIM // 2)]
    sine = jnp.where(lanes % HEAD_DIM < HEAD_DIM // 2, sine, -sine)
    grad_residual, grad_res_low, grad_query, grad_kv, from_own, gain_pair = block_backward(
        placed,
        grad_back,
        residual,
        inverse_two,
        gain_two.astype(f32)[None, :],
        cotangent[0],
        gathered,
        flat_heads,
        (allowed.astype(jnp.int32), mixed, log_rows),
        (cosine, sine),
        (row_values * inverse_one, other_low.astype(f32) * inverse_other),
    )
    came = lax.ppermute(grad_kv[token_count:], "seq", SWAP)

    feature = jnp.arange(model_width)[:, None]
    slot = jnp.arange(model_width)[None, :]
    half_width = model_width // 2
    of_core = jnp.where(slot < half_width, core, 1 - core)
    at = slot % half_width
    chosen_half = feature == (2 * (at // share) + of_core) * share + at % share
    chosen_half = chosen_half.astype(bf16)
    features = jnp.concatenate([normed_one, normed_other, mixed], axis=0)
    features = dot(features, chosen_half).astype(bf16)
    gain_parts = jnp.concatenate(three_parts(gain_pair) + (jnp.zeros_like(gain_pair, bf16),), axis=0)
    gain_parts = dot(gain_parts, chosen_half).astype(bf16)
    gain_parts = jnp.stack([gain_parts[:, :half_width], gain_parts[:, half_width:]], axis=0)
    grads_mine, grads_sent = projection_grads(
        features[:, :half_width],
        features[:, half_width:],
        grad_query,
        grad_kv,
        grad_res_low,
        gain_parts,
    )
    in_width = query_width + 2 * kv_width
    in_total, out_total, gain_total, down_total = reduce_grads(
        grads_mine, grads_sent, down_low, in_width
    )
    gain_total = gain_total[:, :2] + gain_total[:, 2:4] + gain_total[:, 4:6]

    came, gain_total = lax.optimization_barrier((came, gain_total))
    grad_normed_one = from_own + dot(came, kv_w, NT)
    grad_norm_one, _ = norm_backward(row_values, inverse_one, gain_one, grad_normed_one)
    grad_inputs = (grad_residual + grad_norm_one).astype(bf16)

    mix = jnp.concatenate(mixers, axis=1)
    chosen = dot(mix, returned, TN).reshape(3, token_count, model_width)
    output = (residual + (chosen[2] + chosen[1] + chosen[0])).astype(bf16)
    return (
        output.reshape(1, token_count, model_width),
        grad_inputs.reshape(1, token_count, model_width),
        in_total,
        out_total,
        gain_total[:, 0],
        gain_total[:, 1],
        gate_total,
        up_total,
        down_total,
    )


def solution(mesh):
    devices = mesh.devices
    cores = Mesh(devices.reshape(devices.shape[0], -1, 2), ("seq", "chip", "core"))
    every = ("chip", "core")
    by_token = P(every, "seq", None)
    by_row = P(every, None)
    in_specs = (
        by_token,
        by_row,
        by_row,
        P(every),
        P(every),
        by_row,
        by_row,
        by_row,
        by_token,
        by_token,
        by_row,
        by_token,
    )
    out_specs = (by_token, by_token, by_row, by_row, P(every), P(every), by_row, by_row, by_row)
    return jax.shard_map(
        on_device, mesh=cores, in_specs=in_specs, out_specs=out_specs, check_vma=False
    )
```

```python
import jax
import jax.numpy as jnp
from jax import lax
from jax.experimental import pallas as pl
from jax.experimental.pallas import tpu as pltpu
from jax.sharding import Mesh, PartitionSpec as P

HEADS = 16
KV_HEADS = 8
HEAD_DIM = 64
EXPERTS = 32
FF = 512
TOP = 8
CAP = 36
SLOTS = 40
BLOCK = 256
ROW_BLOCK = 256

EPSILON = 1e-06
ROPE_BASE = 10000.0

f32 = jnp.float32
bf16 = jnp.bfloat16

RING = 4
MESH_ID = pl.DeviceIdType.MESH
SWAP = [(0, 1), (1, 0)]
NT = (((1,), (1,)), ((), ()))
TN = (((0,), (0,)), ((), ()))


def dot(a, b, dims=(((1,), (0,)), ((), ()))):
    return lax.dot_general(a, b, dims, preferred_element_type=f32)


def rope_tables(positions):
    half_dim = HEAD_DIM // 2
    powers = jnp.arange(half_dim).astype(f32) * (2.0 / HEAD_DIM)
    inverse_freq = ROPE_BASE ** (-powers)
    angles = positions.astype(f32)[:, None] * inverse_freq[None, :]
    return (jnp.cos(angles), jnp.sin(angles))


def wide_tables(positions):
    place = jnp.arange(128) % HEAD_DIM
    powers = (place % (HEAD_DIM // 2)).astype(f32) * (2.0 / HEAD_DIM)
    angles = positions.astype(f32)[:, None] * (ROPE_BASE ** (-powers))[None, :]
    sine = jnp.sin(angles)
    return (jnp.cos(angles), jnp.where(place < HEAD_DIM // 2, sine, -sine))


def rotate(values, cosine_table, sine_table, turn_sign):
    half_dim = values.shape[-1] // 2
    leading = values[..., :half_dim]
    trailing = values[..., half_dim:]
    cosine_b = cosine_table[:, None, :]
    sine_b = sine_table[:, None, :] * turn_sign
    return jnp.concatenate(
        [leading * cosine_b - trailing * sine_b, trailing * cosine_b + leading * sine_b], axis=-1
    )


def rotate_wide(values, cosine_table, sine_table, turn_sign):
    rows, width = values.shape
    heads = values.reshape(rows, width // HEAD_DIM, HEAD_DIM)
    return rotate(heads, cosine_table, sine_table, turn_sign).reshape(rows, width)


def norm_forward(values, gain_vector):
    inverse = lax.rsqrt(jnp.mean(values * values, axis=-1, keepdims=True) + EPSILON)
    return ((values * inverse * gain_vector.astype(f32)).astype(bf16), inverse)


def norm_backward(values, inverse, gain_vector, upstream):
    scaled = upstream * gain_vector.astype(f32)
    grad_gain = jnp.sum(upstream * values * inverse, axis=0)
    coupling = jnp.mean(scaled * values, axis=-1, keepdims=True)
    return (inverse * scaled - values * inverse * inverse * inverse * coupling, grad_gain)


def rounded(values):
    return lax.reduce_precision(values, exponent_bits=8, mantissa_bits=7)


def three_parts(values):
    first = rounded(values)
    second = rounded(values - first)
    third = values - first - second
    return (first.astype(bf16), second.astype(bf16), third.astype(bf16))


def masked_scores(query, keys, allowed):
    scores = jnp.einsum("qkgd,skd->kgqs", query, keys, preferred_element_type=f32)
    return jnp.where(allowed[None, None], scores * HEAD_DIM ** (-0.5), -1e30)


def attend_forward(query, keys, values, allowed):
    scores = masked_scores(query, keys, allowed)
    highest = jnp.max(scores, axis=-1, keepdims=True)
    log_total = highest + jnp.log(jnp.sum(jnp.exp(scores - highest), axis=-1, keepdims=True))
    weights = jnp.exp(scores - log_total).astype(bf16)
    mixed = jnp.einsum("kgqs,skd->qkgd", weights, values, preferred_element_type=f32)
    return (mixed.astype(bf16), log_total)


def experts_first_body(x_ref, g_ref, pre_w_ref, down_w_ref, hidden_ref, grads_ref, back_ref):
    pre = dot(x_ref[...], pre_w_ref[...], NT)
    grad_hidden = dot(g_ref[...], down_w_ref[...], NT)
    back = None
    for b in range(FF // BLOCK):
        gate = pre[:, 2 * b * BLOCK : (2 * b + 1) * BLOCK]
        up = pre[:, (2 * b + 1) * BLOCK : (2 * b + 2) * BLOCK]
        grad_h = grad_hidden[:, b * BLOCK : (b + 1) * BLOCK]
        sigmoid_gate = 1.0 / (1.0 + jnp.exp(-gate))
        silu = gate * sigmoid_gate
        hidden_ref[:, b * BLOCK : (b + 1) * BLOCK] = (silu * up).astype(bf16)
        grad_gate = (grad_h * up * sigmoid_gate * (1.0 + gate * (1.0 - sigmoid_gate))).astype(bf16)
        grad_up = (grad_h * gate * sigmoid_gate).astype(bf16)
        both = jnp.concatenate([grad_gate, grad_up], axis=1)
        grads_ref[:, 2 * b * BLOCK : (2 * b + 2) * BLOCK] = both
        part = dot(both, pre_w_ref[2 * b * BLOCK : (2 * b + 2) * BLOCK, :]).astype(bf16).astype(f32)
        back = part if back is None else back + part
    back_ref[...] = back.astype(bf16)


def experts_first(arrived, grad_arrived, pre_w, down_w):
    rows, width = arrived.shape
    whole = lambda i: (0, 0)
    by_row = lambda i: (i, 0)
    return pl.pallas_call(
        experts_first_body,
        grid=(rows // ROW_BLOCK,),
        in_specs=[
            pl.BlockSpec((ROW_BLOCK, width), by_row),
            pl.BlockSpec((ROW_BLOCK, width), by_row),
            pl.BlockSpec((2 * FF, width), whole),
            pl.BlockSpec((FF, width), whole),
        ],
        out_specs=[
            pl.BlockSpec((ROW_BLOCK, FF), by_row),
            pl.BlockSpec((ROW_BLOCK, 2 * FF), by_row),
            pl.BlockSpec((ROW_BLOCK, width), by_row),
        ],
        out_shape=[
            jax.ShapeDtypeStruct((rows, FF), bf16),
            jax.ShapeDtypeStruct((rows, 2 * FF), bf16),
            jax.ShapeDtypeStruct((rows, width), bf16),
        ],
        cost_estimate=pl.CostEstimate(
            flops=2 * rows * width * FF * 5,
            bytes_accessed=rows * width * 2 * 5,
            transcendentals=rows * FF,
        ),
        name="experts_first",
    )(arrived, grad_arrived, pre_w, down_w)


def experts_second_body(
    x_ref,
    g_ref,
    hidden_ref,
    grads_ref,
    down_w_ref,
    out_ref,
    gate_ref,
    up_ref,
    third_ref,
    theirs,
    came,
    last,
    low,
    low_came,
    send_sem,
    recv_sem,
):
    seq, chip, core = (lax.axis_index(name) for name in ("seq", "chip", "core"))
    partner = (seq, chip, 1 - core)
    mirror = (1 - seq, chip, core)
    barrier = pltpu.get_barrier_semaphore()
    for other in (partner, mirror):
        pl.semaphore_signal(barrier, inc=1, device_id=other, device_id_type=MESH_ID)
    pl.semaphore_wait(barrier, 2)
    width = x_ref.shape[1]

    def send(i, src, dst, to):
        return pltpu.make_async_remote_copy(
            src_ref=src,
            dst_ref=dst,
            send_sem=send_sem.at[i],
            recv_sem=recv_sem.at[i],
            device_id=to,
            device_id_type=MESH_ID,
        )

    def unit_grads(block, kind, target):
        if kind < 2:
            at = (2 * block + kind) * BLOCK
            left, right = (grads_ref, x_ref)
        else:
            at = block * BLOCK
            left, right = (hidden_ref, g_ref)

        @pl.loop(0, width // BLOCK)
        def _(n):
            columns = pl.ds(pl.multiple_of(n * BLOCK, BLOCK), BLOCK)
            target[:, columns] = dot(left[:, at : at + BLOCK], right[:, columns], TN)

    away = [send(k, theirs.at[k], came.at[k], partner) for k in range(3)]
    across = [send(3 + k, low.at[k], low_came.at[k], mirror) for k in range(2)]
    mine = [gate_ref, up_ref, last]
    lows = [low.at[0], low.at[1], third_ref]
    for k in range(3):
        unit_grads(1, k, theirs.at[k])
        if k:
            away[k - 1].start()
    unit_grads(0, 0, mine[0])
    away[2].start()

    def join(k):
        away[k].wait_recv()

        @pl.loop(0, BLOCK // 32)
        def _(r):
            rows = pl.ds(pl.multiple_of(r * 32, 32), 32)
            lows[k][rows, :] = (mine[k][rows, :] + came[k, rows, :]).astype(bf16)

    for k in range(3):
        join(k)
        if k < 2:
            unit_grads(0, k + 1, mine[k + 1])
            across[k].start()

    @pl.loop(0, x_ref.shape[0] // ROW_BLOCK)
    def _(r):
        rows = pl.ds(pl.multiple_of(r * ROW_BLOCK, ROW_BLOCK), ROW_BLOCK)
        out = None
        for b in range(FF // BLOCK):
            units = slice(b * BLOCK, (b + 1) * BLOCK)
            part = dot(hidden_ref[rows, units], down_w_ref[units, :]).astype(bf16).astype(f32)
            out = part if out is None else out + part
        out_ref[rows, :] = out.astype(bf16)

    for k in range(2):
        across[k].wait_recv()

        @pl.loop(0, BLOCK // 32)
        def _(r):
            rows = pl.ds(pl.multiple_of(r * 32, 32), 32)
            mine[k][rows, :] = low[k, rows, :].astype(f32) + low_came[k, rows, :].astype(f32)

    for copy in away + across:
        copy.wait_send()


def experts_second(arrived, grad_arrived, hidden, grads, down_w):
    rows, width = arrived.shape
    return pl.pallas_call(
        experts_second_body,
        in_specs=[pl.BlockSpec(memory_space=pltpu.VMEM)] * 5,
        out_specs=[pl.BlockSpec(memory_space=pltpu.VMEM)] * 4,
        out_shape=[
            jax.ShapeDtypeStruct((rows, width), bf16),
            jax.ShapeDtypeStruct((BLOCK, width), f32),
            jax.ShapeDtypeStruct((BLOCK, width), f32),
            jax.ShapeDtypeStruct((BLOCK, width), bf16),
        ],
        scratch_shapes=[
            pltpu.VMEM((3, BLOCK, width), f32),
            pltpu.VMEM((3, BLOCK, width), f32),
            pltpu.VMEM((BLOCK, width), f32),
            pltpu.VMEM((2, BLOCK, width), bf16),
            pltpu.VMEM((2, BLOCK, width), bf16),
            pltpu.SemaphoreType.DMA((5,)),
            pltpu.SemaphoreType.DMA((5,)),
        ],
        compiler_params=pltpu.CompilerParams(collective_id=1, has_side_effects=True),
        cost_estimate=pl.CostEstimate(
            flops=2 * rows * width * FF * 4,
            bytes_accessed=rows * width * 2 * 20,
            transcendentals=0,
        ),
        name="experts_second",
    )(arrived, grad_arrived, hidden, grads, down_w)


def gather_body(shard_ref, out_ref, send_sem, recv_sem, local_sem):
    seq, chip, core = (lax.axis_index(name) for name in ("seq", "chip", "core"))
    y, z, half = (chip // (2 * RING), (chip // 2) % RING, chip % 2)

    def device(to_y, to_z, to_half, to_core):
        return (seq, (to_y * RING + to_z) * 2 + to_half, to_core)

    def first(step):
        return device((y + core * step) % RING, (z + (1 - core) * step) % RING, half, core)

    def last(step):
        return device((y + (1 - core) * step) % RING, (z + core * step) % RING, half, core)

    partner = device(y, z, half, 1 - core)
    across = (1 - seq, chip + 1 - 2 * half, core)
    ahead, behind = (1, RING - 1)
    barrier = pltpu.get_barrier_semaphore()
    for other in (partner, across, first(ahead), first(behind), last(ahead), last(behind)):
        pl.semaphore_signal(barrier, inc=1, device_id=other, device_id_type=MESH_ID)
    pl.semaphore_wait(barrier, 6)

    def send(i, src, dst, to):
        return pltpu.make_async_remote_copy(
            src_ref=src,
            dst_ref=dst,
            send_sem=send_sem.at[i],
            recv_sem=recv_sem.at[i],
            device_id=to,
            device_id_type=MESH_ID,
        )

    def pair(c, f, l, part=None):
        cut = slice(None) if part is None else part
        to_y, to_z = (l, f) if c == 0 else (f, l)
        return out_ref.at[(y + to_y) % RING, (z + to_z) % RING, cut, c]

    def run(c):
        sent = []

        def go(i, region, to):
            copy = send(i, region, region, to)
            copy.start()
            sent.append(copy)

        def arrive(i, region):
            send(i, region, region, partner).wait_recv()

        def spread(f):
            go(5 + 2 * f, pair(c, f, 0), last(ahead))
            go(6 + 2 * f, pair(c, f, 0), last(behind))
            go(21 + 5 * f, pair(c, f, 0), partner)

        def relay(f):
            arrive(5 + 2 * f, pair(c, f, behind))
            go(13 + 2 * f, pair(c, f, behind, 0), last(ahead))
            go(22 + 5 * f, pair(c, f, behind), partner)
            arrive(6 + 2 * f, pair(c, f, ahead))
            go(14 + 2 * f, pair(c, f, ahead, 1), last(behind))
            go(23 + 5 * f, pair(c, f, ahead), partner)

        own = out_ref.at[y, z, half, c]
        copy = send(0, shard_ref, own, across)
        copy.start()
        sent.append(copy)
        local = pltpu.make_async_copy(shard_ref, own, local_sem)
        local.start()
        local.wait()
        arrive(0, out_ref.at[y, z, 1 - half, c])
        go(1, pair(c, 0, 0), first(ahead))
        go(2, pair(c, 0, 0), first(behind))
        spread(0)
        arrive(1, pair(c, behind, 0))
        go(3, pair(c, behind, 0, 0), first(ahead))
        spread(behind)
        arrive(2, pair(c, ahead, 0))
        go(4, pair(c, ahead, 0, 1), first(behind))
        spread(ahead)
        relay(0)
        arrive(3, pair(c, 2, 0, 0))
        arrive(4, pair(c, 2, 0, 1))
        spread(2)
        for f in (behind, ahead, 2):
            relay(f)
        for f in (0, behind, ahead, 2):
            for part in range(2):
                arrive(13 + 2 * f + part, pair(c, f, 2, part))
                go(24 + 5 * f + part, pair(c, f, 2, part), partner)
        for f in (0, behind, ahead, 2):
            arrive(21 + 5 * f, pair(1 - c, f, 0))
            arrive(22 + 5 * f, pair(1 - c, f, behind))
            arrive(23 + 5 * f, pair(1 - c, f, ahead))
            for part in range(2):
                arrive(24 + 5 * f + part, pair(1 - c, f, 2, part))
        for copy in sent:
            copy.wait_send()

    for c in (0, 1):
        pl.when(core == c)(lambda c=c: run(c))


def gather_weights(shard):
    rows, width = shard.shape
    out = pl.pallas_call(
        gather_body,
        out_shape=jax.ShapeDtypeStruct((RING, RING, 2, 2, rows, width), shard.dtype),
        in_specs=[pl.BlockSpec(memory_space=pltpu.VMEM)],
        out_specs=pl.BlockSpec(memory_space=pl.ANY),
        scratch_shapes=[
            pltpu.SemaphoreType.DMA((41,)),
            pltpu.SemaphoreType.DMA((41,)),
            pltpu.SemaphoreType.DMA,
        ],
        compiler_params=pltpu.CompilerParams(collective_id=0, has_side_effects=True),
        cost_estimate=pl.CostEstimate(
            flops=0, bytes_accessed=rows * width * 2 * 4 * RING * RING * 8, transcendentals=0
        ),
        name="gather_weights",
    )(shard)
    return out.reshape(4 * RING * RING * rows, width)


def projection_grads_body(
    mine_ref,
    sent_ref,
    gq_ref,
    gkv_ref,
    gr_ref,
    gains_ref,
    chosen_mine_ref,
    chosen_sent_ref,
    total_ref,
    away_ref,
):
    query = gq_ref.shape[1]
    width = query + gkv_ref.shape[1]
    wide = width + gr_ref.shape[1]
    spread = lax.broadcasted_iota(jnp.int32, (8, 128), 0)
    lane = lax.broadcasted_iota(jnp.int32, (8, 128), 1)
    apart = ((spread == lane) & (spread < 6)).astype(bf16)
    tokens = gq_ref.shape[0]
    halves = (
        (mine_ref, total_ref, chosen_mine_ref),
        (sent_ref, away_ref, chosen_sent_ref),
    )
    for ref, out_ref, chosen_ref in halves:
        out_ref[:, :query] = dot(ref[:tokens, :], gq_ref[...], TN).astype(out_ref.dtype)
        out_ref[:, query:width] = dot(ref[: 2 * tokens, :], gkv_ref[...], TN).astype(out_ref.dtype)
        out_ref[:, width:wide] = dot(ref[2 * tokens :, :], gr_ref[...], TN).astype(out_ref.dtype)
        picked = dot(gains_ref[...], chosen_ref[...]).astype(bf16)
        out_ref[:, wide:] = dot(picked, apart, TN).astype(out_ref.dtype)


def projection_grads(rows_mine, rows_sent, grad_query, grad_kv, grad_res_low, gains, chosen):
    count = rows_mine.shape[1]
    width = grad_query.shape[1] + grad_kv.shape[1] + grad_res_low.shape[1] + 128
    tile = 128
    whole = lambda i: (0, 0)
    by_column = lambda i: (0, i)
    by_row = lambda i: (i, 0)
    return pl.pallas_call(
        projection_grads_body,
        grid=(count // tile,),
        in_specs=[
            pl.BlockSpec((rows_mine.shape[0], tile), by_column),
            pl.BlockSpec((rows_sent.shape[0], tile), by_column),
            pl.BlockSpec(grad_query.shape, whole),
            pl.BlockSpec(grad_kv.shape, whole),
            pl.BlockSpec(grad_res_low.shape, whole),
            pl.BlockSpec(gains.shape, whole),
            pl.BlockSpec((chosen.shape[0], tile), by_column),
            pl.BlockSpec((chosen.shape[0], tile), lambda i: (0, i + count // tile)),
        ],
        out_specs=[pl.BlockSpec((tile, width), by_row), pl.BlockSpec((tile, width), by_row)],
        out_shape=[
            jax.ShapeDtypeStruct((count, width), f32),
            jax.ShapeDtypeStruct((count, width), bf16),
        ],
        name="projection_grads",
    )(rows_mine, rows_sent, grad_query, grad_kv, grad_res_low, gains, chosen, chosen)


def packed(values):
    lane = lax.broadcasted_iota(jnp.int32, (values.shape[0], 128), 1)
    wide = values.shape[1] - 128
    parts = values[:, wide:]
    total = parts + pltpu.roll(parts, 126, 1) + pltpu.roll(parts, 124, 1)
    total = jnp.where(lane < 2, total, 0.0)
    one = total.astype(bf16).astype(f32)
    two = (total - one).astype(bf16).astype(f32)
    three = total - one - two
    tail = one + pltpu.roll(two, 2, 1) + pltpu.roll(three, 4, 1)
    return jnp.concatenate([values[:, :wide].astype(bf16), tail.astype(bf16)], axis=1)


def reduce_body(
    mine,
    sent,
    low,
    in_ref,
    out_ref,
    gain_ref,
    unit_ref,
    came,
    acc,
    stage,
    in1,
    in2,
    stage_a,
    in_a1,
    in_a2,
    stage_x,
    in_x,
    own,
    in_own,
    low_came,
    chip_send,
    chip_recv,
    ring_send,
    ring_recv,
):
    seq, chip, core = (lax.axis_index(name) for name in ("seq", "chip", "core"))
    y, z, half = (chip // (2 * RING), (chip // 2) % RING, chip % 2)
    flip = 1 - core
    at_last = flip * y + core * z
    at_first = flip * z + core * y

    def device(to_y, to_z, to_half, to_core):
        return (seq, (to_y * RING + to_z) * 2 + to_half, to_core)

    def first(step):
        return device((y + core * step) % RING, (z + flip * step) % RING, half, core)

    def last(step):
        return device((y + flip * step) % RING, (z + core * step) % RING, half, core)

    partner = device(y, z, half, flip)
    across = (1 - seq, chip + 1 - 2 * half, core)
    mirror = (1 - seq, chip, core)
    ahead, behind = (1, RING - 1)
    barrier = pltpu.get_barrier_semaphore()
    others = (partner, across, mirror, first(ahead), first(behind), last(ahead), last(behind))
    for other in others:
        pl.semaphore_signal(barrier, inc=1, device_id=other, device_id_type=MESH_ID)
    pl.semaphore_wait(barrier, len(others))

    def send(i, src, dst, to):
        return pltpu.make_async_remote_copy(
            src_ref=src,
            dst_ref=dst,
            send_sem=ring_send.at[i],
            recv_sem=ring_recv.at[i],
            device_id=to,
            device_id_type=MESH_ID,
        )

    def on_chip(s, j, of_core):
        line = ((1 - of_core) * y + of_core * z + s) % RING
        a = (1 - of_core) * line + of_core * j
        b = (1 - of_core) * j + of_core * line
        return (
            a,
            b,
            pltpu.make_async_remote_copy(
                src_ref=sent.at[a, b],
                dst_ref=came.at[a, b],
                send_sem=chip_send.at[s, j],
                recv_sem=chip_recv.at[s, j],
                device_id=partner,
                device_id_type=MESH_ID,
            ),
        )

    order = (2, ahead, behind, 0)
    two = RING // 2
    units = send(12, low, low_came, mirror)
    units.start()
    for s in order:

        @pl.loop(0, RING)
        def _(j):
            on_chip(s, j, flip)[2].start()

    ring = [
        send(0, stage.at[2, :two], in1.at[0], last(ahead)),
        send(1, stage.at[2, two:], in1.at[1], last(behind)),
        send(2, stage.at[1, two:], in2.at[0, two:], last(ahead)),
        send(3, stage.at[1, :two], in2.at[0, :two], last(ahead)),
        send(4, stage.at[3, :two], in2.at[1, :two], last(behind)),
        send(5, stage.at[3, two:], in2.at[1, two:], last(behind)),
        send(6, stage_a.at[2, 0], in_a1.at[0], first(ahead)),
        send(7, stage_a.at[2, 1], in_a1.at[1], first(behind)),
        send(8, stage_a.at[1], in_a2.at[0], first(ahead)),
        send(9, stage_a.at[3], in_a2.at[1], first(behind)),
        send(10, stage_x, in_x, across),
        send(11, own, in_own, mirror),
    ]

    def merge(s, low_j, high_j, to_stage):
        @pl.loop(low_j, high_j)
        def _(j):
            a, b, copy = on_chip(s, j, core)
            copy.wait_recv()
            for h in range(2):
                value = mine[a, b, h] + came[a, b, h].astype(f32)
                if to_stage:
                    stage[s, j, h] = packed(value)
                if not to_stage or s != 2:
                    acc[s, j, h] = value

    merge(2, 0, RING, True)
    ring[0].start()
    ring[1].start()
    merge(ahead, 0, RING, True)
    ring[2].start()
    merge(behind, 0, RING, True)
    ring[4].start()
    merge(0, 0, RING, False)
    for i, s, source, first_j in ((0, ahead, 0, 0), (1, behind, 1, two)):
        ring[i].wait_recv()

        @pl.loop(0, two)
        def _(k):
            for h in range(2):
                value = acc[s, first_j + k, h] + in1[source, k, h].astype(f32)
                stage[s, first_j + k, h] = packed(value)

        ring[3 if i == 0 else 5].start()

    for i, source, first_j in ((2, 0, two), (4, 1, 0), (3, 0, 0), (5, 1, two)):
        ring[i].wait_recv()

        @pl.loop(first_j, first_j + two)
        def _(j):
            for h in range(2):
                acc[0, j, h] = acc[0, j, h] + in2[source, j, h].astype(f32)

    def at(step):
        return (at_first + step) % RING

    for h in range(2):
        stage_a[2, h] = packed(acc[0, at(2), h])
    ring[6].start()
    ring[7].start()
    stage_a[1, 1] = packed(acc[0, at(ahead), 1])
    stage_a[3, 0] = packed(acc[0, at(behind), 0])
    ring[6].wait_recv()
    stage_a[1, 0] = packed(acc[0, at(ahead), 0] + in_a1[0].astype(f32))
    ring[8].start()
    ring[7].wait_recv()
    stage_a[3, 1] = packed(acc[0, at(behind), 1] + in_a1[1].astype(f32))
    ring[9].start()
    ring[8].wait_recv()
    ring[9].wait_recv()
    away = 1 - half
    stage_x[...] = packed(
        acc[0, at_first, away] + in_a2[0, away].astype(f32) + in_a2[1, away].astype(f32)
    )
    ring[10].start()
    own[...] = acc[0, at_first, half] + in_a2[0, half].astype(f32) + in_a2[1, half].astype(f32)
    ring[10].wait_recv()
    own[...] = own[...] + in_x[...].astype(f32)
    ring[11].start()
    units.wait_recv()

    @pl.loop(0, low.shape[0] // 32)
    def _(r):
        rows = pl.ds(pl.multiple_of(r * 32, 32), 32)
        unit_ref[rows, :] = low[rows, :].astype(f32) + low_came[rows, :].astype(f32)

    ring[11].wait_recv()
    total = own[...] + in_own[...]
    cut = in_ref.shape[1]
    wide = cut + out_ref.shape[1]
    in_ref[...] = total[:, :cut]
    out_ref[...] = total[:, cut:wide]
    gain_ref[...] = total[:, wide:]
    units.wait_send()
    for copy in ring:
        copy.wait_send()
    for s in order:

        @pl.loop(0, RING)
        def _(j):
            on_chip(s, j, flip)[2].wait_send()


def reduce_grads(mine, sent, low, cut):
    width = mine.shape[1]
    share = mine.shape[0] // (2 * RING * RING)
    shape = (RING, RING, 2, share, width)
    two = RING // 2
    pair = (2, share, width)
    return pl.pallas_call(
        reduce_body,
        in_specs=[pl.BlockSpec(memory_space=pltpu.VMEM)] * 3,
        out_specs=[pl.BlockSpec(memory_space=pltpu.VMEM)] * 4,
        out_shape=[
            jax.ShapeDtypeStruct((share, cut), f32),
            jax.ShapeDtypeStruct((share, width - cut - 128), f32),
            jax.ShapeDtypeStruct((share, 128), f32),
            jax.ShapeDtypeStruct(low.shape, f32),
        ],
        scratch_shapes=[
            pltpu.VMEM(shape, bf16),
            pltpu.VMEM(shape, f32),
            pltpu.VMEM(shape, bf16),
            pltpu.VMEM((2, two) + pair, bf16),
            pltpu.VMEM((2, RING) + pair, bf16),
            pltpu.VMEM((RING,) + pair, bf16),
            pltpu.VMEM(pair, bf16),
            pltpu.VMEM((2,) + pair, bf16),
            pltpu.VMEM((share, width), bf16),
            pltpu.VMEM((share, width), bf16),
            pltpu.VMEM((share, width), f32),
            pltpu.VMEM((share, width), f32),
            pltpu.VMEM(low.shape, bf16),
            pltpu.SemaphoreType.DMA((RING, RING)),
            pltpu.SemaphoreType.DMA((RING, RING)),
            pltpu.SemaphoreType.DMA((13,)),
            pltpu.SemaphoreType.DMA((13,)),
        ],
        compiler_params=pltpu.CompilerParams(collective_id=2, has_side_effects=True),
        cost_estimate=pl.CostEstimate(
            flops=mine.size, bytes_accessed=mine.size, transcendentals=0
        ),
        name="reduce_grads",
    )(mine.reshape(shape), sent.reshape(shape), low)


def rotated(block, cosine, sine, first_half):
    partner = jnp.where(first_half, pltpu.roll(block, 96, 1), pltpu.roll(block, 32, 1))
    return block * cosine + partner * sine


def block_backward_body(
    placed_ref,
    back_ref,
    residual_ref,
    inverse_ref,
    gain_ref,
    cotangent_ref,
    weights_hbm,
    query_ref,
    keys_ref,
    values_ref,
    allowed_ref,
    attended_ref,
    log_ref,
    cosine_ref,
    sine_ref,
    own_ref,
    other_ref,
    residual_out,
    low_out,
    query_out,
    kv_out,
    from_out,
    gains_out,
    weights,
    sems,
):
    tokens, width = residual_ref.shape
    kv_width = keys_ref.shape[1]
    in_width = width + 2 * kv_width
    out_part = pltpu.make_async_copy(
        weights_hbm.at[:, in_width : in_width + width],
        weights.at[:, in_width : in_width + width],
        sems.at[0],
    )
    in_part = pltpu.make_async_copy(
        weights_hbm.at[:, :in_width], weights.at[:, :in_width], sems.at[1]
    )
    out_part.start()
    in_part.start()
    residual = residual_ref[...]
    inverse = inverse_ref[...]
    upstream = dot(placed_ref[...], back_ref[...], TN)
    gain_two = jnp.sum(upstream * residual * inverse, axis=0, keepdims=True)
    scaled = upstream * gain_ref[...]
    coupling = jnp.mean(scaled * residual, axis=-1, keepdims=True)
    grad = inverse * scaled - residual * inverse * inverse * inverse * coupling
    grad = cotangent_ref[...].astype(f32) + grad
    residual_out[...] = grad
    low = grad.astype(bf16)
    low_out[...] = low
    out_part.wait()
    grad_mixed = dot(low, weights[:, in_width : in_width + width], NT).astype(bf16)

    lane = lax.broadcasted_iota(jnp.int32, (1, 128), 1)
    low_lanes = lane < HEAD_DIM
    first_half = lane % HEAD_DIM < HEAD_DIM // 2
    allowed = allowed_ref[...] != 0
    cosine, sine = (cosine_ref[...], sine_ref[...])
    scale = HEAD_DIM ** (-0.5)

    def doubled(block, place):
        wide = block.astype(f32)
        turned = pltpu.roll(wide, HEAD_DIM, 1)
        pair = (wide, turned) if place == 0 else (turned, wide)
        return jnp.where(low_lanes, pair[0], pair[1]).astype(bf16)

    for m in range(KV_HEADS // 2):
        kv_lanes = slice(m * 128, (m + 1) * 128)
        key_parts, value_parts = ([], [])
        for place in range(2):
            j = 2 * m + place
            lanes = slice(j * 128, (j + 1) * 128)
            keys = doubled(keys_ref[:, kv_lanes], place)
            values = doubled(values_ref[:, kv_lanes], place)
            grad_block = grad_mixed[:, lanes].astype(f32)
            product = grad_block * attended_ref[:, lanes].astype(f32)
            query_block = query_ref[:, lanes].astype(f32)
            grad_query = []
            grad_keys, grad_values = (None, None)
            for part in range(2):
                mine = low_lanes if part == 0 else jnp.logical_not(low_lanes)
                query = jnp.where(mine, query_block, 0.0).astype(bf16)
                upper = jnp.where(mine, grad_block, 0.0).astype(bf16)
                scores = jnp.where(allowed, dot(query, keys, NT) * scale, -1e30)
                exact = jnp.exp(scores - log_ref[:, 2 * j + part : 2 * j + part + 1])
                delta = jnp.sum(jnp.where(mine, product, 0.0), axis=-1, keepdims=True)
                grad_scores = (exact * (dot(upper, values, NT) - delta)).astype(bf16)
                grad_query.append(dot(grad_scores, keys))
                to_keys = dot(grad_scores, query, TN)
                to_values = dot(exact.astype(bf16), upper, TN)
                grad_keys = to_keys if part == 0 else grad_keys + to_keys
                grad_values = to_values if part == 0 else grad_values + to_values
            both = jnp.where(low_lanes, grad_query[0], grad_query[1]) * scale
            both = rotated(both, cosine[:tokens], sine[:tokens], first_half)
            query_out[:, lanes] = both.astype(bf16)
            key_parts.append(grad_keys + pltpu.roll(grad_keys, HEAD_DIM, 1))
            value_parts.append(grad_values + pltpu.roll(grad_values, HEAD_DIM, 1))
        grad_keys = jnp.where(low_lanes, key_parts[0], key_parts[1]) * scale
        kv_out[:, kv_lanes] = rotated(grad_keys, cosine, sine, first_half).astype(bf16)
        value_lanes = slice(kv_width + m * 128, kv_width + (m + 1) * 128)
        kv_out[:, value_lanes] = jnp.where(low_lanes, value_parts[0], value_parts[1]).astype(bf16)

    in_part.wait()
    from_kv = dot(kv_out[...], weights[:, width:in_width], NT)
    from_own = dot(query_out[...], weights[:, :width], NT) + from_kv[:tokens]
    from_out[...] = from_own
    gain = jnp.sum(from_own * own_ref[...], axis=0, keepdims=True)
    gain += jnp.sum(from_kv[tokens:] * other_ref[...], axis=0, keepdims=True)
    gains = jnp.concatenate([gain, gain_two], axis=0)
    one = gains.astype(bf16).astype(f32)
    two = (gains - one).astype(bf16).astype(f32)
    three = gains - one - two
    parts = jnp.concatenate([one, two, three, jnp.zeros_like(gains)], axis=0)
    gains_out[...] = parts.astype(bf16)


def block_backward(
    placed, back, residual, inverse, gain, cotangent, weights, heads, masks, tables, scaled_inputs
):
    tokens, width = residual.shape
    query, keys, values = heads
    vmem = pl.BlockSpec(memory_space=pltpu.VMEM)
    return pl.pallas_call(
        block_backward_body,
        in_specs=[vmem] * 6 + [pl.BlockSpec(memory_space=pl.ANY)] + [vmem] * 10,
        out_specs=[vmem] * 6,
        out_shape=[
            jax.ShapeDtypeStruct((tokens, width), f32),
            jax.ShapeDtypeStruct((tokens, width), bf16),
            jax.ShapeDtypeStruct((tokens, width), bf16),
            jax.ShapeDtypeStruct((2 * tokens, 2 * keys.shape[1]), bf16),
            jax.ShapeDtypeStruct((tokens, width), f32),
            jax.ShapeDtypeStruct((8, width), bf16),
        ],
        scratch_shapes=[pltpu.VMEM(weights.shape, bf16), pltpu.SemaphoreType.DMA((2,))],
        cost_estimate=pl.CostEstimate(
            flops=3_000_000_000, bytes_accessed=12_000_000, transcendentals=600_000
        ),
        name="block_backward",
    )(
        placed,
        back,
        residual,
        inverse,
        gain,
        cotangent,
        weights,
        query,
        keys,
        values,
        *masks,
        *tables,
        *scaled_inputs,
    )


def spread_plan(route_ids, mix_weights):
    token_count = route_ids.shape[0]
    expert_ids = jnp.arange(EXPERTS)[None, None, :]
    named = route_ids[:, :, None] == expert_ids
    picked = jnp.any(named, axis=1)
    token_weight = jnp.sum(jnp.where(named, mix_weights[:, :, None], 0.0), axis=1)
    earlier = jnp.arange(token_count)[None, :] < jnp.arange(token_count)[:, None]
    rank = dot(earlier.astype(bf16), picked.astype(bf16)).astype(jnp.int32)
    at_slot = jnp.where(picked, rank, -1).T[:, None, :] == jnp.arange(SLOTS)[None, :, None]
    placed = at_slot.astype(bf16).reshape(EXPERTS * SLOTS, token_count)
    weighted = jnp.where(at_slot, token_weight.T[:, None, :], 0.0)
    slot_weight = jnp.sum(weighted, axis=2).reshape(EXPERTS * SLOTS, 1)
    mixers = [part.reshape(EXPERTS * SLOTS, token_count) for part in three_parts(weighted)]
    return (placed, slot_weight, mixers)


def exchange(rows):
    width = rows.shape[-1]
    blocks = rows.reshape(EXPERTS, -1, width)
    groups = [[(g ^ (c % 2)) * EXPERTS + c for c in range(EXPERTS)] for g in range(2)]
    landed = lax.all_to_all(
        blocks,
        ("seq", "chip"),
        split_axis=0,
        concat_axis=0,
        axis_index_groups=groups,
        tiled=True,
    )
    return landed.reshape(-1, width)


def on_device(
    inputs,
    project_in,
    project_out,
    gain_attend,
    gain_expert,
    expert_gate,
    expert_up,
    expert_down,
    routes,
    route_weights,
    segments,
    cotangent,
):
    token_count = inputs.shape[1]
    model_width = inputs.shape[2]
    query_width = HEADS * HEAD_DIM
    kv_width = KV_HEADS * HEAD_DIM
    group = HEADS // KV_HEADS
    seq = lax.axis_index("seq")
    core = lax.axis_index("core")
    own_low = inputs[0]
    other_low = lax.ppermute(own_low, "seq", SWAP)

    placed, slot_weight, mixers = spread_plan(routes[0], route_weights[0])
    grad_rows = (dot(placed, cotangent[0]) * slot_weight).astype(bf16)

    own_units = jnp.concatenate([expert_gate, expert_up, expert_down], axis=0)
    other_units = lax.ppermute(own_units, "core", SWAP)
    pre_w = jnp.concatenate([own_units[: 2 * BLOCK], other_units[: 2 * BLOCK]], axis=0)
    down_w = jnp.concatenate([expert_down, other_units[2 * BLOCK :]], axis=0)

    share = gain_attend.shape[0]
    wide = query_width + 2 * kv_width + query_width
    filler = jnp.zeros((share, 126), bf16)
    gathered = gather_weights(
        jnp.concatenate(
            [project_in, project_out, gain_attend[:, None], gain_expert[:, None], filler], axis=1
        )
    )
    gathered, grad_rows = lax.optimization_barrier((gathered, grad_rows))
    grad_arrived = exchange(grad_rows)
    in_full = gathered[:, : query_width + 2 * kv_width]
    out_full = gathered[:, query_width + 2 * kv_width : wide]
    gain_one, gain_two = (gathered[:, wide], gathered[:, wide + 1])

    row_values = own_low.astype(f32)
    normed_one, inverse_one = norm_forward(row_values, gain_one)
    normed_other, inverse_other = norm_forward(other_low.astype(f32), gain_one)
    kv_w = in_full[:, query_width:]
    projected = dot(normed_one, in_full)
    projected_other = dot(normed_other, kv_w)
    own_at = seq * token_count + jnp.arange(token_count)
    other_at = (1 - seq) * token_count + jnp.arange(token_count)
    own_cos, own_sin = rope_tables(own_at)
    other_cos, other_sin = rope_tables(other_at)
    query = rotate_wide(projected[:, :query_width], own_cos, own_sin, 1.0).astype(bf16)
    key_cut = query_width + kv_width
    own_keys = rotate_wide(projected[:, query_width:key_cut], own_cos, own_sin, 1.0)
    other_keys = rotate_wide(projected_other[:, :kv_width], other_cos, other_sin, 1.0)
    keys = jnp.concatenate([own_keys, other_keys], axis=0).astype(bf16)
    values = jnp.concatenate([projected[:, key_cut:], projected_other[:, kv_width:]], axis=0)
    flat_heads = (query, keys, values.astype(bf16))
    query = query.reshape(token_count, KV_HEADS, group, HEAD_DIM)
    keys = keys.reshape(2 * token_count, KV_HEADS, HEAD_DIM)
    values = values.astype(bf16).reshape(2 * token_count, KV_HEADS, HEAD_DIM)
    seq_ids = segments[0]
    own_ids = lax.dynamic_slice(seq_ids, (seq * token_count,), (token_count,))
    other_ids = lax.dynamic_slice(seq_ids, ((1 - seq) * token_count,), (token_count,))
    key_at = jnp.concatenate([own_at, other_at])
    key_ids = jnp.concatenate([own_ids, other_ids])
    allowed = (key_at[None, :] <= own_at[:, None]) & (key_ids[None, :] == own_ids[:, None])
    attended, log_total = attend_forward(query, keys, values, allowed)
    mixed = attended.reshape(token_count, query_width)
    residual = row_values + dot(mixed, out_full)
    normed_two, inverse_two = norm_forward(residual, gain_two)

    rows = dot(placed, normed_two).astype(bf16)
    rows, grad_arrived = lax.optimization_barrier((rows, grad_arrived))
    arrived = exchange(rows)

    log_rows = log_total.reshape(HEADS, token_count).T
    cosine, sine = wide_tables(key_at)
    feature = jnp.arange(model_width)[:, None]
    slot = jnp.arange(model_width)[None, :]
    half_width = model_width // 2
    of_core = jnp.where(slot < half_width, core, 1 - core)
    at = slot % half_width
    chosen_half = feature == (2 * (at // share) + of_core) * share + at % share
    chosen_half = chosen_half.astype(bf16)
    features = jnp.concatenate([normed_one, normed_other, mixed], axis=0)
    features = dot(features, chosen_half).astype(bf16)
    ready = (
        features[:, :half_width],
        features[:, half_width:],
        chosen_half,
        flat_heads,
        (allowed.astype(jnp.int32), mixed, log_rows),
        (cosine, sine),
        (row_values * inverse_one, other_low.astype(f32) * inverse_other),
    )
    arrived, ready = lax.optimization_barrier((arrived, ready))
    features_mine, features_sent, chosen_half, flat_heads, masks, tables, scaled_inputs = ready

    hidden, grads, back = experts_first(arrived, grad_arrived, pre_w, down_w)
    grad_back = exchange(back)
    out_rows, gate_total, up_total, down_low = experts_second(arrived, grad_arrived, hidden, grads, down_w)
    grad_back, out_rows = lax.optimization_barrier((grad_back, out_rows))
    returned = exchange(out_rows)

    grad_residual, grad_res_low, grad_query, grad_kv, from_own, gain_parts = block_backward(
        placed,
        grad_back,
        residual,
        inverse_two,
        gain_two.astype(f32)[None, :],
        cotangent[0],
        gathered,
        flat_heads,
        masks,
        tables,
        scaled_inputs,
    )
    came = lax.ppermute(grad_kv[token_count:], "seq", SWAP)

    grads_mine, grads_sent = projection_grads(
        features_mine, features_sent, grad_query, grad_kv, grad_res_low, gain_parts, chosen_half
    )
    in_width = query_width + 2 * kv_width
    in_total, out_total, gain_total, down_total = reduce_grads(
        grads_mine, grads_sent, down_low, in_width
    )
    gain_total = gain_total[:, :2] + gain_total[:, 2:4] + gain_total[:, 4:6]

    came, gain_total = lax.optimization_barrier((came, gain_total))
    grad_normed_one = from_own + dot(came, kv_w, NT)
    grad_norm_one, _ = norm_backward(row_values, inverse_one, gain_one, grad_normed_one)
    grad_inputs = (grad_residual + grad_norm_one).astype(bf16)

    mix = jnp.concatenate(mixers, axis=1)
    chosen = dot(mix, returned, TN).reshape(3, token_count, model_width)
    output = (residual + (chosen[2] + chosen[1] + chosen[0])).astype(bf16)
    return (
        output.reshape(1, token_count, model_width),
        grad_inputs.reshape(1, token_count, model_width),
        in_total,
        out_total,
        gain_total[:, 0],
        gain_total[:, 1],
        gate_total,
        up_total,
        down_total,
    )


def solution(mesh):
    devices = mesh.devices
    cores = Mesh(devices.reshape(devices.shape[0], -1, 2), ("seq", "chip", "core"))
    every = ("chip", "core")
    by_token = P(every, "seq", None)
    by_row = P(every, None)
    in_specs = (
        by_token,
        by_row,
        by_row,
        P(every),
        P(every),
        by_row,
        by_row,
        by_row,
        by_token,
        by_token,
        by_row,
        by_token,
    )
    out_specs = (by_token, by_token, by_row, by_row, P(every), P(every), by_row, by_row, by_row)
    return jax.shard_map(
        on_device, mesh=cores, in_specs=in_specs, out_specs=out_specs, check_vma=False
    )
```

```python
import jax
import jax.numpy as jnp
from jax import lax
from jax.experimental import pallas as pl
from jax.experimental.pallas import tpu as pltpu
from jax.sharding import Mesh, PartitionSpec as P

HEADS = 16
KV_HEADS = 8
HEAD_DIM = 64
EXPERTS = 32
FF = 512
TOP = 8
CAP = 36
SLOTS = 40
BLOCK = 256
ROW_BLOCK = 256

EPSILON = 1e-06
ROPE_BASE = 10000.0

f32 = jnp.float32
bf16 = jnp.bfloat16

RING = 4
MESH_ID = pl.DeviceIdType.MESH
SWAP = [(0, 1), (1, 0)]
NT = (((1,), (1,)), ((), ()))
TN = (((0,), (0,)), ((), ()))


def dot(a, b, dims=(((1,), (0,)), ((), ()))):
    return lax.dot_general(a, b, dims, preferred_element_type=f32)


def rope_tables(positions):
    half_dim = HEAD_DIM // 2
    powers = jnp.arange(half_dim).astype(f32) * (2.0 / HEAD_DIM)
    inverse_freq = ROPE_BASE ** (-powers)
    angles = positions.astype(f32)[:, None] * inverse_freq[None, :]
    return (jnp.cos(angles), jnp.sin(angles))


def wide_tables(positions):
    place = jnp.arange(128) % HEAD_DIM
    powers = (place % (HEAD_DIM // 2)).astype(f32) * (2.0 / HEAD_DIM)
    angles = positions.astype(f32)[:, None] * (ROPE_BASE ** (-powers))[None, :]
    sine = jnp.sin(angles)
    return (jnp.cos(angles), jnp.where(place < HEAD_DIM // 2, sine, -sine))


def rotate(values, cosine_table, sine_table, turn_sign):
    half_dim = values.shape[-1] // 2
    leading = values[..., :half_dim]
    trailing = values[..., half_dim:]
    cosine_b = cosine_table[:, None, :]
    sine_b = sine_table[:, None, :] * turn_sign
    return jnp.concatenate(
        [leading * cosine_b - trailing * sine_b, trailing * cosine_b + leading * sine_b], axis=-1
    )


def rotate_wide(values, cosine_table, sine_table, turn_sign):
    rows, width = values.shape
    heads = values.reshape(rows, width // HEAD_DIM, HEAD_DIM)
    return rotate(heads, cosine_table, sine_table, turn_sign).reshape(rows, width)


def norm_forward(values, gain_vector):
    inverse = lax.rsqrt(jnp.mean(values * values, axis=-1, keepdims=True) + EPSILON)
    return ((values * inverse * gain_vector.astype(f32)).astype(bf16), inverse)


def norm_backward(values, inverse, gain_vector, upstream):
    scaled = upstream * gain_vector.astype(f32)
    grad_gain = jnp.sum(upstream * values * inverse, axis=0)
    coupling = jnp.mean(scaled * values, axis=-1, keepdims=True)
    return (inverse * scaled - values * inverse * inverse * inverse * coupling, grad_gain)


def rounded(values):
    return lax.reduce_precision(values, exponent_bits=8, mantissa_bits=7)


def three_parts(values):
    first = rounded(values)
    second = rounded(values - first)
    third = values - first - second
    return (first.astype(bf16), second.astype(bf16), third.astype(bf16))


def masked_scores(query, keys, allowed):
    scores = jnp.einsum("qkgd,skd->kgqs", query, keys, preferred_element_type=f32)
    return jnp.where(allowed[None, None], scores * HEAD_DIM ** (-0.5), -1e30)


def attend_forward(query, keys, values, allowed):
    scores = masked_scores(query, keys, allowed)
    highest = jnp.max(scores, axis=-1, keepdims=True)
    log_total = highest + jnp.log(jnp.sum(jnp.exp(scores - highest), axis=-1, keepdims=True))
    weights = jnp.exp(scores - log_total).astype(bf16)
    mixed = jnp.einsum("kgqs,skd->qkgd", weights, values, preferred_element_type=f32)
    return (mixed.astype(bf16), log_total)


def experts_first_body(x_ref, g_ref, pre_w_ref, down_w_ref, hidden_ref, grads_ref, back_ref):
    pre = dot(x_ref[...], pre_w_ref[...], NT)
    grad_hidden = dot(g_ref[...], down_w_ref[...], NT)
    back = None
    for b in range(FF // BLOCK):
        gate = pre[:, 2 * b * BLOCK : (2 * b + 1) * BLOCK]
        up = pre[:, (2 * b + 1) * BLOCK : (2 * b + 2) * BLOCK]
        grad_h = grad_hidden[:, b * BLOCK : (b + 1) * BLOCK]
        sigmoid_gate = 1.0 / (1.0 + jnp.exp(-gate))
        silu = gate * sigmoid_gate
        hidden_ref[:, b * BLOCK : (b + 1) * BLOCK] = (silu * up).astype(bf16)
        grad_gate = (grad_h * up * sigmoid_gate * (1.0 + gate * (1.0 - sigmoid_gate))).astype(bf16)
        grad_up = (grad_h * gate * sigmoid_gate).astype(bf16)
        both = jnp.concatenate([grad_gate, grad_up], axis=1)
        grads_ref[:, 2 * b * BLOCK : (2 * b + 2) * BLOCK] = both
        part = dot(both, pre_w_ref[2 * b * BLOCK : (2 * b + 2) * BLOCK, :]).astype(bf16).astype(f32)
        back = part if back is None else back + part
    back_ref[...] = back.astype(bf16)


def experts_first(arrived, grad_arrived, pre_w, down_w):
    rows, width = arrived.shape
    whole = lambda i: (0, 0)
    by_row = lambda i: (i, 0)
    return pl.pallas_call(
        experts_first_body,
        grid=(rows // ROW_BLOCK,),
        in_specs=[
            pl.BlockSpec((ROW_BLOCK, width), by_row),
            pl.BlockSpec((ROW_BLOCK, width), by_row),
            pl.BlockSpec((2 * FF, width), whole),
            pl.BlockSpec((FF, width), whole),
        ],
        out_specs=[
            pl.BlockSpec((ROW_BLOCK, FF), by_row),
            pl.BlockSpec((ROW_BLOCK, 2 * FF), by_row),
            pl.BlockSpec((ROW_BLOCK, width), by_row),
        ],
        out_shape=[
            jax.ShapeDtypeStruct((rows, FF), bf16),
            jax.ShapeDtypeStruct((rows, 2 * FF), bf16),
            jax.ShapeDtypeStruct((rows, width), bf16),
        ],
        cost_estimate=pl.CostEstimate(
            flops=2 * rows * width * FF * 5,
            bytes_accessed=rows * width * 2 * 5,
            transcendentals=rows * FF,
        ),
        name="experts_first",
    )(arrived, grad_arrived, pre_w, down_w)


def experts_second_body(
    x_ref,
    g_ref,
    hidden_ref,
    grads_ref,
    down_w_ref,
    out_ref,
    total_ref,
    rest_ref,
    theirs,
    came,
    last,
    low,
    low_came,
    send_sem,
    recv_sem,
):
    seq, chip, core = (lax.axis_index(name) for name in ("seq", "chip", "core"))
    partner = (seq, chip, 1 - core)
    mirror = (1 - seq, chip, core)
    barrier = pltpu.get_barrier_semaphore()
    for other in (partner, mirror):
        pl.semaphore_signal(barrier, inc=1, device_id=other, device_id_type=MESH_ID)
    pl.semaphore_wait(barrier, 2)
    width = x_ref.shape[1]

    def send(i, src, dst, to):
        return pltpu.make_async_remote_copy(
            src_ref=src,
            dst_ref=dst,
            send_sem=send_sem.at[i],
            recv_sem=recv_sem.at[i],
            device_id=to,
            device_id_type=MESH_ID,
        )

    def unit_grads(block, kind, target):
        if kind < 2:
            at = (2 * block + kind) * BLOCK
            left, right = (grads_ref, x_ref)
        else:
            at = block * BLOCK
            left, right = (hidden_ref, g_ref)

        @pl.loop(0, width // BLOCK)
        def _(n):
            columns = pl.ds(pl.multiple_of(n * BLOCK, BLOCK), BLOCK)
            target[:, columns] = dot(left[:, at : at + BLOCK], right[:, columns], TN)

    away = [send(k, theirs.at[k], came.at[k], partner) for k in range(3)]
    across = [send(3 + k, low.at[k], low_came.at[k], mirror) for k in range(1)]
    mine = [total_ref, last.at[0], last.at[1]]
    lows = [low.at[0], rest_ref.at[0], rest_ref.at[1]]
    for k in range(3):
        unit_grads(1, k, theirs.at[k])
        if k:
            away[k - 1].start()
    unit_grads(0, 0, mine[0])
    away[2].start()

    def join(k):
        away[k].wait_recv()

        @pl.loop(0, BLOCK // 32)
        def _(r):
            rows = pl.ds(pl.multiple_of(r * 32, 32), 32)
            lows[k][rows, :] = (mine[k][rows, :] + came[k, rows, :]).astype(bf16)

    for k in range(3):
        join(k)
        if k < 2:
            unit_grads(0, k + 1, mine[k + 1])
        if k < len(across):
            across[k].start()

    @pl.loop(0, x_ref.shape[0] // ROW_BLOCK)
    def _(r):
        rows = pl.ds(pl.multiple_of(r * ROW_BLOCK, ROW_BLOCK), ROW_BLOCK)
        out = None
        for b in range(FF // BLOCK):
            units = slice(b * BLOCK, (b + 1) * BLOCK)
            part = dot(hidden_ref[rows, units], down_w_ref[units, :]).astype(bf16).astype(f32)
            out = part if out is None else out + part
        out_ref[rows, :] = out.astype(bf16)

    for k in range(len(across)):
        across[k].wait_recv()

        @pl.loop(0, BLOCK // 32)
        def _(r):
            rows = pl.ds(pl.multiple_of(r * 32, 32), 32)
            mine[k][rows, :] = low[k, rows, :].astype(f32) + low_came[k, rows, :].astype(f32)

    for copy in away + across:
        copy.wait_send()


def experts_second(arrived, grad_arrived, hidden, grads, down_w):
    rows, width = arrived.shape
    return pl.pallas_call(
        experts_second_body,
        in_specs=[pl.BlockSpec(memory_space=pltpu.VMEM)] * 5,
        out_specs=[pl.BlockSpec(memory_space=pltpu.VMEM)] * 3,
        out_shape=[
            jax.ShapeDtypeStruct((rows, width), bf16),
            jax.ShapeDtypeStruct((BLOCK, width), f32),
            jax.ShapeDtypeStruct((2, BLOCK, width), bf16),
        ],
        scratch_shapes=[
            pltpu.VMEM((3, BLOCK, width), f32),
            pltpu.VMEM((3, BLOCK, width), f32),
            pltpu.VMEM((2, BLOCK, width), f32),
            pltpu.VMEM((1, BLOCK, width), bf16),
            pltpu.VMEM((1, BLOCK, width), bf16),
            pltpu.SemaphoreType.DMA((4,)),
            pltpu.SemaphoreType.DMA((4,)),
        ],
        compiler_params=pltpu.CompilerParams(collective_id=1, has_side_effects=True),
        cost_estimate=pl.CostEstimate(
            flops=2 * rows * width * FF * 4,
            bytes_accessed=rows * width * 2 * 20,
            transcendentals=0,
        ),
        name="experts_second",
    )(arrived, grad_arrived, hidden, grads, down_w)


def gather_body(in_ref, project_ref, gains_ref, out_ref, shard_ref, send_sem, recv_sem, local_sem):
    seq, chip, core = (lax.axis_index(name) for name in ("seq", "chip", "core"))
    y, z, half = (chip // (2 * RING), (chip // 2) % RING, chip % 2)

    def device(to_y, to_z, to_half, to_core):
        return (seq, (to_y * RING + to_z) * 2 + to_half, to_core)

    def first(step):
        return device((y + core * step) % RING, (z + (1 - core) * step) % RING, half, core)

    def last(step):
        return device((y + (1 - core) * step) % RING, (z + core * step) % RING, half, core)

    partner = device(y, z, half, 1 - core)
    across = (1 - seq, chip + 1 - 2 * half, core)
    ahead, behind = (1, RING - 1)
    cut = in_ref.shape[1]
    wide = cut + project_ref.shape[1]
    shard_ref[:, :cut] = in_ref[...]
    shard_ref[:, cut:wide] = project_ref[...]
    shard_ref[:, wide:] = gains_ref[...]
    barrier = pltpu.get_barrier_semaphore()
    for other in (partner, across, first(ahead), first(behind), last(ahead), last(behind)):
        pl.semaphore_signal(barrier, inc=1, device_id=other, device_id_type=MESH_ID)
    pl.semaphore_wait(barrier, 6)

    def send(i, src, dst, to):
        return pltpu.make_async_remote_copy(
            src_ref=src,
            dst_ref=dst,
            send_sem=send_sem.at[i],
            recv_sem=recv_sem.at[i],
            device_id=to,
            device_id_type=MESH_ID,
        )

    def pair(c, f, l, part=None):
        cut = slice(None) if part is None else part
        to_y, to_z = (l, f) if c == 0 else (f, l)
        return out_ref.at[(y + to_y) % RING, (z + to_z) % RING, cut, c]

    def run(c):
        sent = []

        def go(i, region, to):
            copy = send(i, region, region, to)
            copy.start()
            sent.append(copy)

        def arrive(i, region):
            send(i, region, region, partner).wait_recv()

        def spread(f):
            go(5 + 2 * f, pair(c, f, 0), last(ahead))
            go(6 + 2 * f, pair(c, f, 0), last(behind))
            go(21 + 5 * f, pair(c, f, 0), partner)

        def relay(f):
            arrive(5 + 2 * f, pair(c, f, behind))
            go(13 + 2 * f, pair(c, f, behind, 0), last(ahead))
            go(22 + 5 * f, pair(c, f, behind), partner)
            arrive(6 + 2 * f, pair(c, f, ahead))
            go(14 + 2 * f, pair(c, f, ahead, 1), last(behind))
            go(23 + 5 * f, pair(c, f, ahead), partner)

        own = out_ref.at[y, z, half, c]
        copy = send(0, shard_ref, own, across)
        copy.start()
        sent.append(copy)
        local = pltpu.make_async_copy(shard_ref, own, local_sem)
        local.start()
        local.wait()
        arrive(0, out_ref.at[y, z, 1 - half, c])
        go(1, pair(c, 0, 0), first(ahead))
        go(2, pair(c, 0, 0), first(behind))
        spread(0)
        arrive(1, pair(c, behind, 0))
        go(3, pair(c, behind, 0, 0), first(ahead))
        spread(behind)
        arrive(2, pair(c, ahead, 0))
        go(4, pair(c, ahead, 0, 1), first(behind))
        spread(ahead)
        relay(0)
        arrive(3, pair(c, 2, 0, 0))
        arrive(4, pair(c, 2, 0, 1))
        spread(2)
        for f in (behind, ahead, 2):
            relay(f)
        for f in (0, behind, ahead, 2):
            for part in range(2):
                arrive(13 + 2 * f + part, pair(c, f, 2, part))
                go(24 + 5 * f + part, pair(c, f, 2, part), partner)
        for f in (0, behind, ahead, 2):
            arrive(21 + 5 * f, pair(1 - c, f, 0))
            arrive(22 + 5 * f, pair(1 - c, f, behind))
            arrive(23 + 5 * f, pair(1 - c, f, ahead))
            for part in range(2):
                arrive(24 + 5 * f + part, pair(1 - c, f, 2, part))
        for copy in sent:
            copy.wait_send()

    for c in (0, 1):
        pl.when(core == c)(lambda c=c: run(c))


def gather_weights(project_in, project_out, gains):
    parts = (project_in, project_out, gains)
    rows, width = (gains.shape[0], sum(part.shape[1] for part in parts))
    out = pl.pallas_call(
        gather_body,
        out_shape=jax.ShapeDtypeStruct((RING, RING, 2, 2, rows, width), bf16),
        in_specs=[pl.BlockSpec(memory_space=pltpu.VMEM)] * 3,
        out_specs=pl.BlockSpec(memory_space=pl.ANY),
        scratch_shapes=[
            pltpu.VMEM((rows, width), bf16),
            pltpu.SemaphoreType.DMA((41,)),
            pltpu.SemaphoreType.DMA((41,)),
            pltpu.SemaphoreType.DMA,
        ],
        compiler_params=pltpu.CompilerParams(collective_id=0, has_side_effects=True),
        cost_estimate=pl.CostEstimate(
            flops=0, bytes_accessed=rows * width * 2 * 4 * RING * RING * 8, transcendentals=0
        ),
        name="gather_weights",
    )(*parts)
    return out.reshape(4 * RING * RING * rows, width)


def projection_grads_body(
    mine_ref,
    sent_ref,
    gq_ref,
    gkv_ref,
    gr_ref,
    gains_ref,
    chosen_mine_ref,
    chosen_sent_ref,
    total_ref,
    away_ref,
):
    query = gq_ref.shape[1]
    width = query + gkv_ref.shape[1]
    wide = width + gr_ref.shape[1]
    spread = lax.broadcasted_iota(jnp.int32, (8, 128), 0)
    lane = lax.broadcasted_iota(jnp.int32, (8, 128), 1)
    apart = ((spread == lane) & (spread < 6)).astype(bf16)
    tokens = gq_ref.shape[0]
    halves = (
        (mine_ref, total_ref, chosen_mine_ref),
        (sent_ref, away_ref, chosen_sent_ref),
    )
    for ref, out_ref, chosen_ref in halves:
        out_ref[:, :query] = dot(ref[:tokens, :], gq_ref[...], TN).astype(out_ref.dtype)
        out_ref[:, query:width] = dot(ref[: 2 * tokens, :], gkv_ref[...], TN).astype(out_ref.dtype)
        out_ref[:, width:wide] = dot(ref[2 * tokens :, :], gr_ref[...], TN).astype(out_ref.dtype)
        picked = dot(gains_ref[...], chosen_ref[...]).astype(bf16)
        out_ref[:, wide:] = dot(picked, apart, TN).astype(out_ref.dtype)


def projection_grads(rows_mine, rows_sent, grad_query, grad_kv, grad_res_low, gains, chosen):
    count = rows_mine.shape[1]
    width = grad_query.shape[1] + grad_kv.shape[1] + grad_res_low.shape[1] + 128
    tile = 128
    whole = lambda i: (0, 0)
    by_column = lambda i: (0, i)
    by_row = lambda i: (i, 0)
    return pl.pallas_call(
        projection_grads_body,
        grid=(count // tile,),
        in_specs=[
            pl.BlockSpec((rows_mine.shape[0], tile), by_column),
            pl.BlockSpec((rows_sent.shape[0], tile), by_column),
            pl.BlockSpec(grad_query.shape, whole),
            pl.BlockSpec(grad_kv.shape, whole),
            pl.BlockSpec(grad_res_low.shape, whole),
            pl.BlockSpec(gains.shape, whole),
            pl.BlockSpec((chosen.shape[0], tile), by_column),
            pl.BlockSpec((chosen.shape[0], tile), lambda i: (0, i + count // tile)),
        ],
        out_specs=[pl.BlockSpec((tile, width), by_row), pl.BlockSpec((tile, width), by_row)],
        out_shape=[
            jax.ShapeDtypeStruct((count, width), f32),
            jax.ShapeDtypeStruct((count, width), bf16),
        ],
        name="projection_grads",
    )(rows_mine, rows_sent, grad_query, grad_kv, grad_res_low, gains, chosen, chosen)


def packed(values):
    lane = lax.broadcasted_iota(jnp.int32, (values.shape[0], 128), 1)
    wide = values.shape[1] - 128
    parts = values[:, wide:]
    total = parts + pltpu.roll(parts, 126, 1) + pltpu.roll(parts, 124, 1)
    total = jnp.where(lane < 2, total, 0.0)
    one = total.astype(bf16).astype(f32)
    two = (total - one).astype(bf16).astype(f32)
    three = total - one - two
    tail = one + pltpu.roll(two, 2, 1) + pltpu.roll(three, 4, 1)
    return jnp.concatenate([values[:, :wide].astype(bf16), tail.astype(bf16)], axis=1)


def reduce_body(
    mine_hbm,
    sent,
    low,
    in_ref,
    out_ref,
    gain_ref,
    up_ref,
    down_ref,
    came,
    acc,
    stage,
    in1,
    in2,
    stage_a,
    in_a1,
    in_a2,
    stage_x,
    in_x,
    own,
    in_own,
    low_came,
    mine,
    mine_sem,
    chip_send,
    chip_recv,
    ring_send,
    ring_recv,
):
    seq, chip, core = (lax.axis_index(name) for name in ("seq", "chip", "core"))
    y, z, half = (chip // (2 * RING), (chip // 2) % RING, chip % 2)
    flip = 1 - core
    at_last = flip * y + core * z
    at_first = flip * z + core * y

    def device(to_y, to_z, to_half, to_core):
        return (seq, (to_y * RING + to_z) * 2 + to_half, to_core)

    def first(step):
        return device((y + core * step) % RING, (z + flip * step) % RING, half, core)

    def last(step):
        return device((y + flip * step) % RING, (z + core * step) % RING, half, core)

    partner = device(y, z, half, flip)
    across = (1 - seq, chip + 1 - 2 * half, core)
    mirror = (1 - seq, chip, core)
    ahead, behind = (1, RING - 1)
    fetch = pltpu.make_async_copy(mine_hbm, mine, mine_sem)
    fetch.start()
    barrier = pltpu.get_barrier_semaphore()
    others = (partner, across, mirror, first(ahead), first(behind), last(ahead), last(behind))
    for other in others:
        pl.semaphore_signal(barrier, inc=1, device_id=other, device_id_type=MESH_ID)
    pl.semaphore_wait(barrier, len(others))

    def send(i, src, dst, to):
        return pltpu.make_async_remote_copy(
            src_ref=src,
            dst_ref=dst,
            send_sem=ring_send.at[i],
            recv_sem=ring_recv.at[i],
            device_id=to,
            device_id_type=MESH_ID,
        )

    def on_chip(s, j, of_core):
        line = ((1 - of_core) * y + of_core * z + s) % RING
        a = (1 - of_core) * line + of_core * j
        b = (1 - of_core) * j + of_core * line
        return (
            a,
            b,
            pltpu.make_async_remote_copy(
                src_ref=sent.at[a, b],
                dst_ref=came.at[a, b],
                send_sem=chip_send.at[s, j],
                recv_sem=chip_recv.at[s, j],
                device_id=partner,
                device_id_type=MESH_ID,
            ),
        )

    order = (2, ahead, behind, 0)
    two = RING // 2
    units = send(12, low, low_came, mirror)
    units.start()
    for s in order:

        @pl.loop(0, RING)
        def _(j):
            on_chip(s, j, flip)[2].start()

    ring = [
        send(0, stage.at[2, :two], in1.at[0], last(ahead)),
        send(1, stage.at[2, two:], in1.at[1], last(behind)),
        send(2, stage.at[1, two:], in2.at[0, two:], last(ahead)),
        send(3, stage.at[1, :two], in2.at[0, :two], last(ahead)),
        send(4, stage.at[3, :two], in2.at[1, :two], last(behind)),
        send(5, stage.at[3, two:], in2.at[1, two:], last(behind)),
        send(6, stage_a.at[2, 0], in_a1.at[0], first(ahead)),
        send(7, stage_a.at[2, 1], in_a1.at[1], first(behind)),
        send(8, stage_a.at[1], in_a2.at[0], first(ahead)),
        send(9, stage_a.at[3], in_a2.at[1], first(behind)),
        send(10, stage_x, in_x, across),
        send(11, own, in_own, mirror),
    ]

    def merge(s, low_j, high_j, to_stage):
        @pl.loop(low_j, high_j)
        def _(j):
            a, b, copy = on_chip(s, j, core)
            copy.wait_recv()
            for h in range(2):
                value = mine[a, b, h] + came[a, b, h].astype(f32)
                if to_stage:
                    stage[s, j, h] = packed(value)
                if not to_stage or s != 2:
                    acc[s, j, h] = value

    fetch.wait()
    merge(2, 0, RING, True)
    ring[0].start()
    ring[1].start()
    merge(ahead, 0, RING, True)
    ring[2].start()
    merge(behind, 0, RING, True)
    ring[4].start()
    merge(0, 0, RING, False)
    for i, s, source, first_j in ((0, ahead, 0, 0), (1, behind, 1, two)):
        ring[i].wait_recv()

        @pl.loop(0, two)
        def _(k):
            for h in range(2):
                value = acc[s, first_j + k, h] + in1[source, k, h].astype(f32)
                stage[s, first_j + k, h] = packed(value)

        ring[3 if i == 0 else 5].start()

    for i, source, first_j in ((2, 0, two), (4, 1, 0), (3, 0, 0), (5, 1, two)):
        ring[i].wait_recv()

        @pl.loop(first_j, first_j + two)
        def _(j):
            for h in range(2):
                acc[0, j, h] = acc[0, j, h] + in2[source, j, h].astype(f32)

    def at(step):
        return (at_first + step) % RING

    for h in range(2):
        stage_a[2, h] = packed(acc[0, at(2), h])
    ring[6].start()
    ring[7].start()
    stage_a[1, 1] = packed(acc[0, at(ahead), 1])
    stage_a[3, 0] = packed(acc[0, at(behind), 0])
    ring[6].wait_recv()
    stage_a[1, 0] = packed(acc[0, at(ahead), 0] + in_a1[0].astype(f32))
    ring[8].start()
    ring[7].wait_recv()
    stage_a[3, 1] = packed(acc[0, at(behind), 1] + in_a1[1].astype(f32))
    ring[9].start()
    ring[8].wait_recv()
    ring[9].wait_recv()
    away = 1 - half
    stage_x[...] = packed(
        acc[0, at_first, away] + in_a2[0, away].astype(f32) + in_a2[1, away].astype(f32)
    )
    ring[10].start()
    own[...] = acc[0, at_first, half] + in_a2[0, half].astype(f32) + in_a2[1, half].astype(f32)
    ring[10].wait_recv()
    own[...] = own[...] + in_x[...].astype(f32)
    ring[11].start()
    units.wait_recv()

    @pl.loop(0, low.shape[1] // 32)
    def _(r):
        rows = pl.ds(pl.multiple_of(r * 32, 32), 32)
        up_ref[rows, :] = low[0, rows, :].astype(f32) + low_came[0, rows, :].astype(f32)
        down_ref[rows, :] = low[1, rows, :].astype(f32) + low_came[1, rows, :].astype(f32)

    ring[11].wait_recv()
    total = own[...] + in_own[...]
    cut = in_ref.shape[1]
    wide = cut + out_ref.shape[1]
    in_ref[...] = total[:, :cut]
    out_ref[...] = total[:, cut:wide]
    gain_ref[...] = total[:, wide:]
    units.wait_send()
    for copy in ring:
        copy.wait_send()
    for s in order:

        @pl.loop(0, RING)
        def _(j):
            on_chip(s, j, flip)[2].wait_send()


def reduce_grads(mine, sent, low, cut):
    width = mine.shape[1]
    share = mine.shape[0] // (2 * RING * RING)
    shape = (RING, RING, 2, share, width)
    two = RING // 2
    pair = (2, share, width)
    return pl.pallas_call(
        reduce_body,
        in_specs=[pl.BlockSpec(memory_space=pl.ANY)] * 2 + [pl.BlockSpec(memory_space=pltpu.VMEM)],
        out_specs=[pl.BlockSpec(memory_space=pltpu.VMEM)] * 5,
        out_shape=[
            jax.ShapeDtypeStruct((share, cut), f32),
            jax.ShapeDtypeStruct((share, width - cut - 128), f32),
            jax.ShapeDtypeStruct((share, 128), f32),
            jax.ShapeDtypeStruct(low.shape[1:], f32),
            jax.ShapeDtypeStruct(low.shape[1:], f32),
        ],
        scratch_shapes=[
            pltpu.VMEM(shape, bf16),
            pltpu.VMEM(shape, f32),
            pltpu.VMEM(shape, bf16),
            pltpu.VMEM((2, two) + pair, bf16),
            pltpu.VMEM((2, RING) + pair, bf16),
            pltpu.VMEM((RING,) + pair, bf16),
            pltpu.VMEM(pair, bf16),
            pltpu.VMEM((2,) + pair, bf16),
            pltpu.VMEM((share, width), bf16),
            pltpu.VMEM((share, width), bf16),
            pltpu.VMEM((share, width), f32),
            pltpu.VMEM((share, width), f32),
            pltpu.VMEM(low.shape, bf16),
            pltpu.VMEM(shape, f32),
            pltpu.SemaphoreType.DMA,
            pltpu.SemaphoreType.DMA((RING, RING)),
            pltpu.SemaphoreType.DMA((RING, RING)),
            pltpu.SemaphoreType.DMA((13,)),
            pltpu.SemaphoreType.DMA((13,)),
        ],
        compiler_params=pltpu.CompilerParams(collective_id=2, has_side_effects=True),
        cost_estimate=pl.CostEstimate(
            flops=mine.size * 8, bytes_accessed=mine.size * 60, transcendentals=0
        ),
        name="reduce_grads",
    )(mine.reshape(shape), sent.reshape(shape), low)


def rotated(block, cosine, sine, first_half):
    partner = jnp.where(first_half, pltpu.roll(block, 96, 1), pltpu.roll(block, 32, 1))
    return block * cosine + partner * sine


def block_backward_body(
    placed_ref,
    back_ref,
    residual_ref,
    inverse_ref,
    gain_ref,
    cotangent_ref,
    weights_hbm,
    query_ref,
    keys_ref,
    values_ref,
    allowed_ref,
    attended_ref,
    log_ref,
    cosine_ref,
    sine_ref,
    own_ref,
    other_ref,
    residual_out,
    low_out,
    query_out,
    kv_out,
    from_out,
    gains_out,
    weights,
    sems,
):
    tokens, width = residual_ref.shape
    kv_width = keys_ref.shape[1]
    in_width = width + 2 * kv_width
    out_part = pltpu.make_async_copy(
        weights_hbm.at[:, in_width : in_width + width],
        weights.at[:, in_width : in_width + width],
        sems.at[0],
    )
    in_part = pltpu.make_async_copy(
        weights_hbm.at[:, :in_width], weights.at[:, :in_width], sems.at[1]
    )
    out_part.start()
    in_part.start()
    residual = residual_ref[...]
    inverse = inverse_ref[...]
    upstream = dot(placed_ref[...], back_ref[...], TN)
    gain_two = jnp.sum(upstream * residual * inverse, axis=0, keepdims=True)
    scaled = upstream * gain_ref[...]
    coupling = jnp.mean(scaled * residual, axis=-1, keepdims=True)
    grad = inverse * scaled - residual * inverse * inverse * inverse * coupling
    grad = cotangent_ref[...].astype(f32) + grad
    residual_out[...] = grad
    low = grad.astype(bf16)
    low_out[...] = low
    out_part.wait()
    grad_mixed = dot(low, weights[:, in_width : in_width + width], NT).astype(bf16)

    lane = lax.broadcasted_iota(jnp.int32, (1, 128), 1)
    low_lanes = lane < HEAD_DIM
    first_half = lane % HEAD_DIM < HEAD_DIM // 2
    allowed = allowed_ref[...] != 0
    cosine, sine = (cosine_ref[...], sine_ref[...])
    scale = HEAD_DIM ** (-0.5)

    def doubled(block, place):
        wide = block.astype(f32)
        turned = pltpu.roll(wide, HEAD_DIM, 1)
        pair = (wide, turned) if place == 0 else (turned, wide)
        return jnp.where(low_lanes, pair[0], pair[1]).astype(bf16)

    for m in range(KV_HEADS // 2):
        kv_lanes = slice(m * 128, (m + 1) * 128)
        key_parts, value_parts = ([], [])
        for place in range(2):
            j = 2 * m + place
            lanes = slice(j * 128, (j + 1) * 128)
            keys = doubled(keys_ref[:, kv_lanes], place)
            values = doubled(values_ref[:, kv_lanes], place)
            grad_block = grad_mixed[:, lanes].astype(f32)
            product = grad_block * attended_ref[:, lanes].astype(f32)
            query_block = query_ref[:, lanes].astype(f32)
            grad_query = []
            grad_keys, grad_values = (None, None)
            for part in range(2):
                mine = low_lanes if part == 0 else jnp.logical_not(low_lanes)
                query = jnp.where(mine, query_block, 0.0).astype(bf16)
                upper = jnp.where(mine, grad_block, 0.0).astype(bf16)
                scores = jnp.where(allowed, dot(query, keys, NT) * scale, -1e30)
                exact = jnp.exp(scores - log_ref[:, 2 * j + part : 2 * j + part + 1])
                delta = jnp.sum(jnp.where(mine, product, 0.0), axis=-1, keepdims=True)
                grad_scores = (exact * (dot(upper, values, NT) - delta)).astype(bf16)
                grad_query.append(dot(grad_scores, keys))
                to_keys = dot(grad_scores, query, TN)
                to_values = dot(exact.astype(bf16), upper, TN)
                grad_keys = to_keys if part == 0 else grad_keys + to_keys
                grad_values = to_values if part == 0 else grad_values + to_values
            both = jnp.where(low_lanes, grad_query[0], grad_query[1]) * scale
            both = rotated(both, cosine[:tokens], sine[:tokens], first_half)
            query_out[:, lanes] = both.astype(bf16)
            key_parts.append(grad_keys + pltpu.roll(grad_keys, HEAD_DIM, 1))
            value_parts.append(grad_values + pltpu.roll(grad_values, HEAD_DIM, 1))
        grad_keys = jnp.where(low_lanes, key_parts[0], key_parts[1]) * scale
        kv_out[:, kv_lanes] = rotated(grad_keys, cosine, sine, first_half).astype(bf16)
        value_lanes = slice(kv_width + m * 128, kv_width + (m + 1) * 128)
        kv_out[:, value_lanes] = jnp.where(low_lanes, value_parts[0], value_parts[1]).astype(bf16)

    in_part.wait()
    from_kv = dot(kv_out[...], weights[:, width:in_width], NT)
    from_own = dot(query_out[...], weights[:, :width], NT) + from_kv[:tokens]
    from_out[...] = from_own
    gain = jnp.sum(from_own * own_ref[...], axis=0, keepdims=True)
    gain += jnp.sum(from_kv[tokens:] * other_ref[...], axis=0, keepdims=True)
    gains = jnp.concatenate([gain, gain_two], axis=0)
    one = gains.astype(bf16).astype(f32)
    two = (gains - one).astype(bf16).astype(f32)
    three = gains - one - two
    parts = jnp.concatenate([one, two, three, jnp.zeros_like(gains)], axis=0)
    gains_out[...] = parts.astype(bf16)


def block_backward(
    placed, back, residual, inverse, gain, cotangent, weights, heads, masks, tables, scaled_inputs
):
    tokens, width = residual.shape
    query, keys, values = heads
    vmem = pl.BlockSpec(memory_space=pltpu.VMEM)
    return pl.pallas_call(
        block_backward_body,
        in_specs=[vmem] * 6 + [pl.BlockSpec(memory_space=pl.ANY)] + [vmem] * 10,
        out_specs=[vmem] * 6,
        out_shape=[
            jax.ShapeDtypeStruct((tokens, width), f32),
            jax.ShapeDtypeStruct((tokens, width), bf16),
            jax.ShapeDtypeStruct((tokens, width), bf16),
            jax.ShapeDtypeStruct((2 * tokens, 2 * keys.shape[1]), bf16),
            jax.ShapeDtypeStruct((tokens, width), f32),
            jax.ShapeDtypeStruct((8, width), bf16),
        ],
        scratch_shapes=[pltpu.VMEM(weights.shape, bf16), pltpu.SemaphoreType.DMA((2,))],
        cost_estimate=pl.CostEstimate(
            flops=3_000_000_000, bytes_accessed=12_000_000, transcendentals=600_000
        ),
        name="block_backward",
    )(
        placed,
        back,
        residual,
        inverse,
        gain,
        cotangent,
        weights,
        query,
        keys,
        values,
        *masks,
        *tables,
        *scaled_inputs,
    )


def spread_plan(route_ids, mix_weights):
    token_count = route_ids.shape[0]
    expert_ids = jnp.arange(EXPERTS)[None, None, :]
    named = route_ids[:, :, None] == expert_ids
    picked = jnp.any(named, axis=1)
    token_weight = jnp.sum(jnp.where(named, mix_weights[:, :, None], 0.0), axis=1)
    earlier = jnp.arange(token_count)[None, :] < jnp.arange(token_count)[:, None]
    rank = dot(earlier.astype(bf16), picked.astype(bf16)).astype(jnp.int32)
    at_slot = jnp.where(picked, rank, -1).T[:, None, :] == jnp.arange(SLOTS)[None, :, None]
    placed = at_slot.astype(bf16).reshape(EXPERTS * SLOTS, token_count)
    weighted = jnp.where(at_slot, token_weight.T[:, None, :], 0.0)
    slot_weight = jnp.sum(weighted, axis=2).reshape(EXPERTS * SLOTS, 1)
    mixers = [part.reshape(EXPERTS * SLOTS, token_count) for part in three_parts(weighted)]
    return (placed, slot_weight, mixers)


def exchange(rows):
    width = rows.shape[-1]
    blocks = rows.reshape(EXPERTS, -1, width)
    groups = [[(g ^ (c % 2)) * EXPERTS + c for c in range(EXPERTS)] for g in range(2)]
    landed = lax.all_to_all(
        blocks,
        ("seq", "chip"),
        split_axis=0,
        concat_axis=0,
        axis_index_groups=groups,
        tiled=True,
    )
    return landed.reshape(-1, width)


def on_device(
    inputs,
    project_in,
    project_out,
    gain_attend,
    gain_expert,
    expert_gate,
    expert_up,
    expert_down,
    routes,
    route_weights,
    segments,
    cotangent,
):
    token_count = inputs.shape[1]
    model_width = inputs.shape[2]
    query_width = HEADS * HEAD_DIM
    kv_width = KV_HEADS * HEAD_DIM
    group = HEADS // KV_HEADS
    seq = lax.axis_index("seq")
    core = lax.axis_index("core")
    own_low = inputs[0]
    other_low = lax.ppermute(own_low, "seq", SWAP)

    placed, slot_weight, mixers = spread_plan(routes[0], route_weights[0])
    grad_rows = (dot(placed, cotangent[0]) * slot_weight).astype(bf16)

    own_units = jnp.concatenate([expert_gate, expert_up, expert_down], axis=0)
    other_units = lax.ppermute(own_units, "core", SWAP)
    pre_w = jnp.concatenate([own_units[: 2 * BLOCK], other_units[: 2 * BLOCK]], axis=0)
    down_w = jnp.concatenate([expert_down, other_units[2 * BLOCK :]], axis=0)

    share = gain_attend.shape[0]
    wide = query_width + 2 * kv_width + query_width
    gain_rows = jnp.stack([gain_attend, gain_expert], axis=0)
    gain_rows = jnp.pad(gain_rows, ((0, share - 2), (0, 128 - share)))
    gathered = gather_weights(project_in, project_out, gain_rows)
    gathered, grad_rows = lax.optimization_barrier((gathered, grad_rows))
    grad_arrived = exchange(grad_rows)
    in_full = gathered[:, : query_width + 2 * kv_width]
    out_full = gathered[:, query_width + 2 * kv_width : wide]
    gain_rows = gathered[:, wide : wide + share].reshape(-1, share, share)
    gain_one, gain_two = (gain_rows[:, 0].reshape(-1), gain_rows[:, 1].reshape(-1))

    row_values = own_low.astype(f32)
    normed_one, inverse_one = norm_forward(row_values, gain_one)
    normed_other, inverse_other = norm_forward(other_low.astype(f32), gain_one)
    kv_w = in_full[:, query_width:]
    projected = dot(normed_one, in_full)
    projected_other = dot(normed_other, kv_w)
    own_at = seq * token_count + jnp.arange(token_count)
    other_at = (1 - seq) * token_count + jnp.arange(token_count)
    own_cos, own_sin = rope_tables(own_at)
    other_cos, other_sin = rope_tables(other_at)
    query = rotate_wide(projected[:, :query_width], own_cos, own_sin, 1.0).astype(bf16)
    key_cut = query_width + kv_width
    own_keys = rotate_wide(projected[:, query_width:key_cut], own_cos, own_sin, 1.0)
    other_keys = rotate_wide(projected_other[:, :kv_width], other_cos, other_sin, 1.0)
    keys = jnp.concatenate([own_keys, other_keys], axis=0).astype(bf16)
    values = jnp.concatenate([projected[:, key_cut:], projected_other[:, kv_width:]], axis=0)
    flat_heads = (query, keys, values.astype(bf16))
    query = query.reshape(token_count, KV_HEADS, group, HEAD_DIM)
    keys = keys.reshape(2 * token_count, KV_HEADS, HEAD_DIM)
    values = values.astype(bf16).reshape(2 * token_count, KV_HEADS, HEAD_DIM)
    seq_ids = segments[0]
    own_ids = lax.dynamic_slice(seq_ids, (seq * token_count,), (token_count,))
    other_ids = lax.dynamic_slice(seq_ids, ((1 - seq) * token_count,), (token_count,))
    key_at = jnp.concatenate([own_at, other_at])
    key_ids = jnp.concatenate([own_ids, other_ids])
    allowed = (key_at[None, :] <= own_at[:, None]) & (key_ids[None, :] == own_ids[:, None])
    attended, log_total = attend_forward(query, keys, values, allowed)
    mixed = attended.reshape(token_count, query_width)
    residual = row_values + dot(mixed, out_full)
    normed_two, inverse_two = norm_forward(residual, gain_two)

    rows = dot(placed, normed_two).astype(bf16)
    rows, grad_arrived = lax.optimization_barrier((rows, grad_arrived))
    arrived = exchange(rows)

    log_rows = log_total.reshape(HEADS, token_count).T
    cosine, sine = wide_tables(key_at)
    feature = jnp.arange(model_width)[:, None]
    slot = jnp.arange(model_width)[None, :]
    half_width = model_width // 2
    of_core = jnp.where(slot < half_width, core, 1 - core)
    at = slot % half_width
    chosen_half = feature == (2 * (at // share) + of_core) * share + at % share
    chosen_half = chosen_half.astype(bf16)
    features = jnp.concatenate([normed_one, normed_other, mixed], axis=0)
    features = dot(features, chosen_half).astype(bf16)
    ready = (
        features[:, :half_width],
        features[:, half_width:],
        chosen_half,
        flat_heads,
        (allowed.astype(jnp.int32), mixed, log_rows),
        (cosine, sine),
        (row_values * inverse_one, other_low.astype(f32) * inverse_other),
    )
    arrived, ready = lax.optimization_barrier((arrived, ready))
    features_mine, features_sent, chosen_half, flat_heads, masks, tables, scaled_inputs = ready

    hidden, grads, back = experts_first(arrived, grad_arrived, pre_w, down_w)
    grad_back = exchange(back)
    out_rows, gate_total, rest_low = experts_second(arrived, grad_arrived, hidden, grads, down_w)
    grad_back, out_rows = lax.optimization_barrier((grad_back, out_rows))
    returned = exchange(out_rows)

    grad_residual, grad_res_low, grad_query, grad_kv, from_own, gain_parts = block_backward(
        placed,
        grad_back,
        residual,
        inverse_two,
        gain_two.astype(f32)[None, :],
        cotangent[0],
        gathered,
        flat_heads,
        masks,
        tables,
        scaled_inputs,
    )
    came = lax.ppermute(grad_kv[token_count:], "seq", SWAP)

    grads_mine, grads_sent = projection_grads(
        features_mine, features_sent, grad_query, grad_kv, grad_res_low, gain_parts, chosen_half
    )
    in_width = query_width + 2 * kv_width
    in_total, out_total, gain_total, up_total, down_total = reduce_grads(
        grads_mine, grads_sent, rest_low, in_width
    )
    gain_total = gain_total[:, :2] + gain_total[:, 2:4] + gain_total[:, 4:6]

    came, gain_total = lax.optimization_barrier((came, gain_total))
    grad_normed_one = from_own + dot(came, kv_w, NT)
    grad_norm_one, _ = norm_backward(row_values, inverse_one, gain_one, grad_normed_one)
    grad_inputs = (grad_residual + grad_norm_one).astype(bf16)

    mix = jnp.concatenate(mixers, axis=1)
    chosen = dot(mix, returned, TN).reshape(3, token_count, model_width)
    output = (residual + (chosen[2] + chosen[1] + chosen[0])).astype(bf16)
    return (
        output.reshape(1, token_count, model_width),
        grad_inputs.reshape(1, token_count, model_width),
        in_total,
        out_total,
        gain_total[:, 0],
        gain_total[:, 1],
        gate_total,
        up_total,
        down_total,
    )


def solution(mesh):
    devices = mesh.devices
    cores = Mesh(devices.reshape(devices.shape[0], -1, 2), ("seq", "chip", "core"))
    every = ("chip", "core")
    by_token = P(every, "seq", None)
    by_row = P(every, None)
    in_specs = (
        by_token,
        by_row,
        by_row,
        P(every),
        P(every),
        by_row,
        by_row,
        by_row,
        by_token,
        by_token,
        by_row,
        by_token,
    )
    out_specs = (by_token, by_token, by_row, by_row, P(every), P(every), by_row, by_row, by_row)
    return jax.shard_map(
        on_device, mesh=cores, in_specs=in_specs, out_specs=out_specs, check_vma=False
    )
```

```python
import jax
import jax.numpy as jnp
from jax import lax
from jax.experimental import pallas as pl
from jax.experimental.pallas import tpu as pltpu
from jax.sharding import Mesh, PartitionSpec as P

HEADS = 16
KV_HEADS = 8
HEAD_DIM = 64
EXPERTS = 32
FF = 512
TOP = 8
CAP = 36
SLOTS = 40
BLOCK = 256
ROW_BLOCK = 256

EPSILON = 1e-06
ROPE_BASE = 10000.0

f32 = jnp.float32
bf16 = jnp.bfloat16

RING = 4
MESH_ID = pl.DeviceIdType.MESH
SWAP = [(0, 1), (1, 0)]
NT = (((1,), (1,)), ((), ()))
TN = (((0,), (0,)), ((), ()))


def dot(a, b, dims=(((1,), (0,)), ((), ()))):
    return lax.dot_general(a, b, dims, preferred_element_type=f32)


def rope_tables(positions):
    half_dim = HEAD_DIM // 2
    powers = jnp.arange(half_dim).astype(f32) * (2.0 / HEAD_DIM)
    inverse_freq = ROPE_BASE ** (-powers)
    angles = positions.astype(f32)[:, None] * inverse_freq[None, :]
    return (jnp.cos(angles), jnp.sin(angles))


def wide_tables(positions):
    place = jnp.arange(128) % HEAD_DIM
    powers = (place % (HEAD_DIM // 2)).astype(f32) * (2.0 / HEAD_DIM)
    angles = positions.astype(f32)[:, None] * (ROPE_BASE ** (-powers))[None, :]
    sine = jnp.sin(angles)
    return (jnp.cos(angles), jnp.where(place < HEAD_DIM // 2, sine, -sine))


def rotate(values, cosine_table, sine_table, turn_sign):
    half_dim = values.shape[-1] // 2
    leading = values[..., :half_dim]
    trailing = values[..., half_dim:]
    cosine_b = cosine_table[:, None, :]
    sine_b = sine_table[:, None, :] * turn_sign
    return jnp.concatenate(
        [leading * cosine_b - trailing * sine_b, trailing * cosine_b + leading * sine_b], axis=-1
    )


def rotate_wide(values, cosine_table, sine_table, turn_sign):
    rows, width = values.shape
    heads = values.reshape(rows, width // HEAD_DIM, HEAD_DIM)
    return rotate(heads, cosine_table, sine_table, turn_sign).reshape(rows, width)


def norm_forward(values, gain_vector):
    inverse = lax.rsqrt(jnp.mean(values * values, axis=-1, keepdims=True) + EPSILON)
    return ((values * inverse * gain_vector.astype(f32)).astype(bf16), inverse)


def rounded(values):
    return lax.reduce_precision(values, exponent_bits=8, mantissa_bits=7)


def three_parts(values):
    first = rounded(values)
    second = rounded(values - first)
    third = values - first - second
    return (first.astype(bf16), second.astype(bf16), third.astype(bf16))


def masked_scores(query, keys, allowed):
    scores = jnp.einsum("qkgd,skd->kgqs", query, keys, preferred_element_type=f32)
    return jnp.where(allowed[None, None], scores * HEAD_DIM ** (-0.5), -1e30)


def attend_forward(query, keys, values, allowed):
    scores = masked_scores(query, keys, allowed)
    highest = jnp.max(scores, axis=-1, keepdims=True)
    log_total = highest + jnp.log(jnp.sum(jnp.exp(scores - highest), axis=-1, keepdims=True))
    weights = jnp.exp(scores - log_total).astype(bf16)
    mixed = jnp.einsum("kgqs,skd->qkgd", weights, values, preferred_element_type=f32)
    return (mixed.astype(bf16), log_total)


def experts_first_body(x_ref, g_ref, pre_w_ref, down_w_ref, hidden_ref, grads_ref, back_ref):
    pre = dot(x_ref[...], pre_w_ref[...], NT)
    grad_hidden = dot(g_ref[...], down_w_ref[...], NT)
    back = None
    for b in range(FF // BLOCK):
        gate = pre[:, 2 * b * BLOCK : (2 * b + 1) * BLOCK]
        up = pre[:, (2 * b + 1) * BLOCK : (2 * b + 2) * BLOCK]
        grad_h = grad_hidden[:, b * BLOCK : (b + 1) * BLOCK]
        sigmoid_gate = 1.0 / (1.0 + jnp.exp(-gate))
        silu = gate * sigmoid_gate
        hidden_ref[:, b * BLOCK : (b + 1) * BLOCK] = (silu * up).astype(bf16)
        grad_gate = (grad_h * up * sigmoid_gate * (1.0 + gate * (1.0 - sigmoid_gate))).astype(bf16)
        grad_up = (grad_h * gate * sigmoid_gate).astype(bf16)
        both = jnp.concatenate([grad_gate, grad_up], axis=1)
        grads_ref[:, 2 * b * BLOCK : (2 * b + 2) * BLOCK] = both
        part = dot(both, pre_w_ref[2 * b * BLOCK : (2 * b + 2) * BLOCK, :]).astype(bf16).astype(f32)
        back = part if back is None else back + part
    back_ref[...] = back.astype(bf16)


def experts_first(arrived, grad_arrived, pre_w, down_w):
    rows, width = arrived.shape
    whole = lambda i: (0, 0)
    by_row = lambda i: (i, 0)
    return pl.pallas_call(
        experts_first_body,
        grid=(rows // ROW_BLOCK,),
        in_specs=[
            pl.BlockSpec((ROW_BLOCK, width), by_row),
            pl.BlockSpec((ROW_BLOCK, width), by_row),
            pl.BlockSpec((2 * FF, width), whole),
            pl.BlockSpec((FF, width), whole),
        ],
        out_specs=[
            pl.BlockSpec((ROW_BLOCK, FF), by_row),
            pl.BlockSpec((ROW_BLOCK, 2 * FF), by_row),
            pl.BlockSpec((ROW_BLOCK, width), by_row),
        ],
        out_shape=[
            jax.ShapeDtypeStruct((rows, FF), bf16),
            jax.ShapeDtypeStruct((rows, 2 * FF), bf16),
            jax.ShapeDtypeStruct((rows, width), bf16),
        ],
        cost_estimate=pl.CostEstimate(
            flops=2 * rows * width * FF * 5,
            bytes_accessed=rows * width * 2 * 5,
            transcendentals=rows * FF,
        ),
        name="experts_first",
    )(arrived, grad_arrived, pre_w, down_w)


def experts_second_body(
    x_ref,
    g_ref,
    hidden_ref,
    grads_ref,
    down_w_ref,
    out_ref,
    total_ref,
    rest_ref,
    theirs,
    came,
    last,
    low,
    low_came,
    send_sem,
    recv_sem,
):
    seq, chip, core = (lax.axis_index(name) for name in ("seq", "chip", "core"))
    partner = (seq, chip, 1 - core)
    mirror = (1 - seq, chip, core)
    barrier = pltpu.get_barrier_semaphore()
    for other in (partner, mirror):
        pl.semaphore_signal(barrier, inc=1, device_id=other, device_id_type=MESH_ID)
    pl.semaphore_wait(barrier, 2)
    width = x_ref.shape[1]

    def send(i, src, dst, to):
        return pltpu.make_async_remote_copy(
            src_ref=src,
            dst_ref=dst,
            send_sem=send_sem.at[i],
            recv_sem=recv_sem.at[i],
            device_id=to,
            device_id_type=MESH_ID,
        )

    def unit_grads(block, kind, target):
        if kind < 2:
            at = (2 * block + kind) * BLOCK
            left, right = (grads_ref, x_ref)
        else:
            at = block * BLOCK
            left, right = (hidden_ref, g_ref)

        @pl.loop(0, width // BLOCK)
        def _(n):
            columns = pl.ds(pl.multiple_of(n * BLOCK, BLOCK), BLOCK)
            target[:, columns] = dot(left[:, at : at + BLOCK], right[:, columns], TN)

    away = [send(k, theirs.at[k], came.at[k], partner) for k in range(3)]
    across = [send(3 + k, low.at[k], low_came.at[k], mirror) for k in range(1)]
    mine = [total_ref, last.at[0], last.at[1]]
    lows = [low.at[0], rest_ref.at[0], rest_ref.at[1]]
    for k in range(3):
        unit_grads(1, k, theirs.at[k])
        if k:
            away[k - 1].start()
    unit_grads(0, 0, mine[0])
    away[2].start()

    def join(k):
        away[k].wait_recv()

        @pl.loop(0, BLOCK // 32)
        def _(r):
            rows = pl.ds(pl.multiple_of(r * 32, 32), 32)
            lows[k][rows, :] = (mine[k][rows, :] + came[k, rows, :]).astype(bf16)

    for k in range(3):
        join(k)
        if k < 2:
            unit_grads(0, k + 1, mine[k + 1])
        if k < len(across):
            across[k].start()

    @pl.loop(0, x_ref.shape[0] // ROW_BLOCK)
    def _(r):
        rows = pl.ds(pl.multiple_of(r * ROW_BLOCK, ROW_BLOCK), ROW_BLOCK)
        out = None
        for b in range(FF // BLOCK):
            units = slice(b * BLOCK, (b + 1) * BLOCK)
            part = dot(hidden_ref[rows, units], down_w_ref[units, :]).astype(bf16).astype(f32)
            out = part if out is None else out + part
        out_ref[rows, :] = out.astype(bf16)

    for k in range(len(across)):
        across[k].wait_recv()

        @pl.loop(0, BLOCK // 32)
        def _(r):
            rows = pl.ds(pl.multiple_of(r * 32, 32), 32)
            mine[k][rows, :] = low[k, rows, :].astype(f32) + low_came[k, rows, :].astype(f32)

    for copy in away + across:
        copy.wait_send()


def experts_second(arrived, grad_arrived, hidden, grads, down_w):
    rows, width = arrived.shape
    return pl.pallas_call(
        experts_second_body,
        in_specs=[pl.BlockSpec(memory_space=pltpu.VMEM)] * 5,
        out_specs=[pl.BlockSpec(memory_space=pltpu.VMEM)] * 3,
        out_shape=[
            jax.ShapeDtypeStruct((rows, width), bf16),
            jax.ShapeDtypeStruct((BLOCK, width), f32),
            jax.ShapeDtypeStruct((2, BLOCK, width), bf16),
        ],
        scratch_shapes=[
            pltpu.VMEM((3, BLOCK, width), f32),
            pltpu.VMEM((3, BLOCK, width), f32),
            pltpu.VMEM((2, BLOCK, width), f32),
            pltpu.VMEM((1, BLOCK, width), bf16),
            pltpu.VMEM((1, BLOCK, width), bf16),
            pltpu.SemaphoreType.DMA((4,)),
            pltpu.SemaphoreType.DMA((4,)),
        ],
        compiler_params=pltpu.CompilerParams(collective_id=1, has_side_effects=True),
        cost_estimate=pl.CostEstimate(
            flops=2 * rows * width * FF * 4,
            bytes_accessed=rows * width * 2 * 20,
            transcendentals=0,
        ),
        name="experts_second",
    )(arrived, grad_arrived, hidden, grads, down_w)


def gather_body(in_ref, project_ref, gains_ref, out_ref, shard_ref, send_sem, recv_sem, local_sem):
    seq, chip, core = (lax.axis_index(name) for name in ("seq", "chip", "core"))
    y, z, half = (chip // (2 * RING), (chip // 2) % RING, chip % 2)

    def device(to_y, to_z, to_half, to_core):
        return (seq, (to_y * RING + to_z) * 2 + to_half, to_core)

    def first(step):
        return device((y + core * step) % RING, (z + (1 - core) * step) % RING, half, core)

    def last(step):
        return device((y + (1 - core) * step) % RING, (z + core * step) % RING, half, core)

    partner = device(y, z, half, 1 - core)
    across = (1 - seq, chip + 1 - 2 * half, core)
    ahead, behind = (1, RING - 1)
    cut = in_ref.shape[1]
    wide = cut + project_ref.shape[1]
    shard_ref[:, :cut] = in_ref[...]
    shard_ref[:, cut:wide] = project_ref[...]
    shard_ref[:, wide:] = gains_ref[...]
    barrier = pltpu.get_barrier_semaphore()
    for other in (partner, across, first(ahead), first(behind), last(ahead), last(behind)):
        pl.semaphore_signal(barrier, inc=1, device_id=other, device_id_type=MESH_ID)
    pl.semaphore_wait(barrier, 6)

    def send(i, src, dst, to):
        return pltpu.make_async_remote_copy(
            src_ref=src,
            dst_ref=dst,
            send_sem=send_sem.at[i],
            recv_sem=recv_sem.at[i],
            device_id=to,
            device_id_type=MESH_ID,
        )

    def pair(c, f, l, part=None):
        cut = slice(None) if part is None else part
        to_y, to_z = (l, f) if c == 0 else (f, l)
        return out_ref.at[(y + to_y) % RING, (z + to_z) % RING, cut, c]

    def run(c):
        sent = []

        def go(i, region, to):
            copy = send(i, region, region, to)
            copy.start()
            sent.append(copy)

        def arrive(i, region):
            send(i, region, region, partner).wait_recv()

        def spread(f):
            go(5 + 2 * f, pair(c, f, 0), last(ahead))
            go(6 + 2 * f, pair(c, f, 0), last(behind))
            go(21 + 5 * f, pair(c, f, 0), partner)

        def relay(f):
            arrive(5 + 2 * f, pair(c, f, behind))
            go(13 + 2 * f, pair(c, f, behind, 0), last(ahead))
            go(22 + 5 * f, pair(c, f, behind), partner)
            arrive(6 + 2 * f, pair(c, f, ahead))
            go(14 + 2 * f, pair(c, f, ahead, 1), last(behind))
            go(23 + 5 * f, pair(c, f, ahead), partner)

        own = out_ref.at[y, z, half, c]
        copy = send(0, shard_ref, own, across)
        copy.start()
        sent.append(copy)
        local = pltpu.make_async_copy(shard_ref, own, local_sem)
        local.start()
        local.wait()
        arrive(0, out_ref.at[y, z, 1 - half, c])
        go(1, pair(c, 0, 0), first(ahead))
        go(2, pair(c, 0, 0), first(behind))
        spread(0)
        arrive(1, pair(c, behind, 0))
        go(3, pair(c, behind, 0, 0), first(ahead))
        spread(behind)
        arrive(2, pair(c, ahead, 0))
        go(4, pair(c, ahead, 0, 1), first(behind))
        spread(ahead)
        relay(0)
        arrive(3, pair(c, 2, 0, 0))
        arrive(4, pair(c, 2, 0, 1))
        spread(2)
        for f in (behind, ahead, 2):
            relay(f)
        for f in (0, behind, ahead, 2):
            for part in range(2):
                arrive(13 + 2 * f + part, pair(c, f, 2, part))
                go(24 + 5 * f + part, pair(c, f, 2, part), partner)
        for f in (0, behind, ahead, 2):
            arrive(21 + 5 * f, pair(1 - c, f, 0))
            arrive(22 + 5 * f, pair(1 - c, f, behind))
            arrive(23 + 5 * f, pair(1 - c, f, ahead))
            for part in range(2):
                arrive(24 + 5 * f + part, pair(1 - c, f, 2, part))
        for copy in sent:
            copy.wait_send()

    for c in (0, 1):
        pl.when(core == c)(lambda c=c: run(c))


def gather_weights(project_in, project_out, gains):
    parts = (project_in, project_out, gains)
    rows, width = (gains.shape[0], sum(part.shape[1] for part in parts))
    out = pl.pallas_call(
        gather_body,
        out_shape=jax.ShapeDtypeStruct((RING, RING, 2, 2, rows, width), bf16),
        in_specs=[pl.BlockSpec(memory_space=pltpu.VMEM)] * 3,
        out_specs=pl.BlockSpec(memory_space=pl.ANY),
        scratch_shapes=[
            pltpu.VMEM((rows, width), bf16),
            pltpu.SemaphoreType.DMA((41,)),
            pltpu.SemaphoreType.DMA((41,)),
            pltpu.SemaphoreType.DMA,
        ],
        compiler_params=pltpu.CompilerParams(collective_id=0, has_side_effects=True),
        cost_estimate=pl.CostEstimate(
            flops=0, bytes_accessed=rows * width * 2 * 4 * RING * RING * 8, transcendentals=0
        ),
        name="gather_weights",
    )(*parts)
    return out.reshape(4 * RING * RING * rows, width)


def projection_grads_body(
    mine_ref,
    sent_ref,
    gq_ref,
    gkv_ref,
    gr_ref,
    gains_ref,
    chosen_mine_ref,
    chosen_sent_ref,
    total_ref,
    away_ref,
):
    query = gq_ref.shape[1]
    width = query + gkv_ref.shape[1]
    wide = width + gr_ref.shape[1]
    spread = lax.broadcasted_iota(jnp.int32, (8, 128), 0)
    lane = lax.broadcasted_iota(jnp.int32, (8, 128), 1)
    apart = ((spread == lane) & (spread < 6)).astype(bf16)
    tokens = gq_ref.shape[0]
    halves = (
        (mine_ref, total_ref, chosen_mine_ref),
        (sent_ref, away_ref, chosen_sent_ref),
    )
    for ref, out_ref, chosen_ref in halves:
        out_ref[:, :query] = dot(ref[:tokens, :], gq_ref[...], TN).astype(out_ref.dtype)
        out_ref[:, query:width] = dot(ref[: 2 * tokens, :], gkv_ref[...], TN).astype(out_ref.dtype)
        out_ref[:, width:wide] = dot(ref[2 * tokens :, :], gr_ref[...], TN).astype(out_ref.dtype)
        picked = dot(gains_ref[...], chosen_ref[...]).astype(bf16)
        out_ref[:, wide:] = dot(picked, apart, TN).astype(out_ref.dtype)


def projection_grads(rows_mine, rows_sent, grad_query, grad_kv, grad_res_low, gains, chosen):
    count = rows_mine.shape[1]
    width = grad_query.shape[1] + grad_kv.shape[1] + grad_res_low.shape[1] + 128
    tile = 128
    whole = lambda i: (0, 0)
    by_column = lambda i: (0, i)
    by_row = lambda i: (i, 0)
    return pl.pallas_call(
        projection_grads_body,
        grid=(count // tile,),
        in_specs=[
            pl.BlockSpec((rows_mine.shape[0], tile), by_column),
            pl.BlockSpec((rows_sent.shape[0], tile), by_column),
            pl.BlockSpec(grad_query.shape, whole),
            pl.BlockSpec(grad_kv.shape, whole),
            pl.BlockSpec(grad_res_low.shape, whole),
            pl.BlockSpec(gains.shape, whole),
            pl.BlockSpec((chosen.shape[0], tile), by_column),
            pl.BlockSpec((chosen.shape[0], tile), lambda i: (0, i + count // tile)),
        ],
        out_specs=[pl.BlockSpec((tile, width), by_row), pl.BlockSpec((tile, width), by_row)],
        out_shape=[
            jax.ShapeDtypeStruct((count, width), f32),
            jax.ShapeDtypeStruct((count, width), bf16),
        ],
        name="projection_grads",
    )(rows_mine, rows_sent, grad_query, grad_kv, grad_res_low, gains, chosen, chosen)


def packed(values):
    lane = lax.broadcasted_iota(jnp.int32, (values.shape[0], 128), 1)
    wide = values.shape[1] - 128
    parts = values[:, wide:]
    total = parts + pltpu.roll(parts, 126, 1) + pltpu.roll(parts, 124, 1)
    total = jnp.where(lane < 2, total, 0.0)
    one = total.astype(bf16).astype(f32)
    two = (total - one).astype(bf16).astype(f32)
    three = total - one - two
    tail = one + pltpu.roll(two, 2, 1) + pltpu.roll(three, 4, 1)
    return jnp.concatenate([values[:, :wide].astype(bf16), tail.astype(bf16)], axis=1)


def reduce_body(
    mine_hbm,
    sent,
    low,
    kv_ref,
    weights_hbm,
    from_ref,
    residual_ref,
    inputs_ref,
    gain_one_ref,
    in_ref,
    out_ref,
    gain_ref,
    up_ref,
    down_ref,
    inputs_out,
    came,
    acc,
    stage,
    in1,
    in2,
    stage_a,
    in_a1,
    in_a2,
    stage_x,
    in_x,
    own,
    in_own,
    low_came,
    mine,
    kv_came,
    kv_weights,
    fetch_sems,
    chip_send,
    chip_recv,
    ring_send,
    ring_recv,
):
    seq, chip, core = (lax.axis_index(name) for name in ("seq", "chip", "core"))
    y, z, half = (chip // (2 * RING), (chip // 2) % RING, chip % 2)
    flip = 1 - core
    at_last = flip * y + core * z
    at_first = flip * z + core * y

    def device(to_y, to_z, to_half, to_core):
        return (seq, (to_y * RING + to_z) * 2 + to_half, to_core)

    def first(step):
        return device((y + core * step) % RING, (z + flip * step) % RING, half, core)

    def last(step):
        return device((y + flip * step) % RING, (z + core * step) % RING, half, core)

    partner = device(y, z, half, flip)
    across = (1 - seq, chip + 1 - 2 * half, core)
    mirror = (1 - seq, chip, core)
    ahead, behind = (1, RING - 1)
    fetch = pltpu.make_async_copy(mine_hbm, mine, fetch_sems.at[0])
    fetch.start()
    tokens, width = from_ref.shape
    fetch_weights = pltpu.make_async_copy(
        weights_hbm.at[:, width : 2 * width], kv_weights, fetch_sems.at[1]
    )
    fetch_weights.start()
    barrier = pltpu.get_barrier_semaphore()
    others = (partner, across, mirror, first(ahead), first(behind), last(ahead), last(behind))
    for other in others:
        pl.semaphore_signal(barrier, inc=1, device_id=other, device_id_type=MESH_ID)
    pl.semaphore_wait(barrier, len(others))

    def send(i, src, dst, to):
        return pltpu.make_async_remote_copy(
            src_ref=src,
            dst_ref=dst,
            send_sem=ring_send.at[i],
            recv_sem=ring_recv.at[i],
            device_id=to,
            device_id_type=MESH_ID,
        )

    def on_chip(s, j, of_core):
        line = ((1 - of_core) * y + of_core * z + s) % RING
        a = (1 - of_core) * line + of_core * j
        b = (1 - of_core) * j + of_core * line
        return (
            a,
            b,
            pltpu.make_async_remote_copy(
                src_ref=sent.at[a, b],
                dst_ref=came.at[a, b],
                send_sem=chip_send.at[s, j],
                recv_sem=chip_recv.at[s, j],
                device_id=partner,
                device_id_type=MESH_ID,
            ),
        )

    order = (2, ahead, behind, 0)
    two = RING // 2
    kv_away = send(13, kv_ref.at[pl.ds(tokens, tokens)], kv_came, mirror)
    kv_away.start()
    units = send(12, low, low_came, mirror)
    units.start()
    for s in order:

        @pl.loop(0, RING)
        def _(j):
            on_chip(s, j, flip)[2].start()

    ring = [
        send(0, stage.at[2, :two], in1.at[0], last(ahead)),
        send(1, stage.at[2, two:], in1.at[1], last(behind)),
        send(2, stage.at[1, two:], in2.at[0, two:], last(ahead)),
        send(3, stage.at[1, :two], in2.at[0, :two], last(ahead)),
        send(4, stage.at[3, :two], in2.at[1, :two], last(behind)),
        send(5, stage.at[3, two:], in2.at[1, two:], last(behind)),
        send(6, stage_a.at[2, 0], in_a1.at[0], first(ahead)),
        send(7, stage_a.at[2, 1], in_a1.at[1], first(behind)),
        send(8, stage_a.at[1], in_a2.at[0], first(ahead)),
        send(9, stage_a.at[3], in_a2.at[1], first(behind)),
        send(10, stage_x, in_x, across),
        send(11, own, in_own, mirror),
    ]

    def merge(s, low_j, high_j, to_stage):
        @pl.loop(low_j, high_j)
        def _(j):
            a, b, copy = on_chip(s, j, core)
            copy.wait_recv()
            for h in range(2):
                value = mine[a, b, h] + came[a, b, h].astype(f32)
                if to_stage:
                    stage[s, j, h] = packed(value)
                if not to_stage or s != 2:
                    acc[s, j, h] = value

    fetch.wait()
    merge(2, 0, RING, True)
    ring[0].start()
    ring[1].start()
    merge(ahead, 0, RING, True)
    ring[2].start()
    merge(behind, 0, RING, True)
    ring[4].start()
    merge(0, 0, RING, False)
    for i, s, source, first_j in ((0, ahead, 0, 0), (1, behind, 1, two)):
        ring[i].wait_recv()

        @pl.loop(0, two)
        def _(k):
            for h in range(2):
                value = acc[s, first_j + k, h] + in1[source, k, h].astype(f32)
                stage[s, first_j + k, h] = packed(value)

        ring[3 if i == 0 else 5].start()

    kv_away.wait_recv()
    fetch_weights.wait()
    values = inputs_ref[...].astype(f32)
    inverse = lax.rsqrt(jnp.mean(values * values, axis=-1, keepdims=True) + EPSILON)
    upstream = from_ref[...] + dot(kv_came[...], kv_weights[...], NT)
    scaled = upstream * gain_one_ref[...]
    coupling = jnp.mean(scaled * values, axis=-1, keepdims=True)
    grad = inverse * scaled - values * inverse * inverse * inverse * coupling
    inputs_out[...] = (residual_ref[...] + grad).astype(bf16)

    for i, source, first_j in ((2, 0, two), (4, 1, 0), (3, 0, 0), (5, 1, two)):
        ring[i].wait_recv()

        @pl.loop(first_j, first_j + two)
        def _(j):
            for h in range(2):
                acc[0, j, h] = acc[0, j, h] + in2[source, j, h].astype(f32)

    def at(step):
        return (at_first + step) % RING

    for h in range(2):
        stage_a[2, h] = packed(acc[0, at(2), h])
    ring[6].start()
    ring[7].start()
    stage_a[1, 1] = packed(acc[0, at(ahead), 1])
    stage_a[3, 0] = packed(acc[0, at(behind), 0])
    ring[6].wait_recv()
    stage_a[1, 0] = packed(acc[0, at(ahead), 0] + in_a1[0].astype(f32))
    ring[8].start()
    ring[7].wait_recv()
    stage_a[3, 1] = packed(acc[0, at(behind), 1] + in_a1[1].astype(f32))
    ring[9].start()
    ring[8].wait_recv()
    ring[9].wait_recv()
    away = 1 - half
    stage_x[...] = packed(
        acc[0, at_first, away] + in_a2[0, away].astype(f32) + in_a2[1, away].astype(f32)
    )
    ring[10].start()
    own[...] = acc[0, at_first, half] + in_a2[0, half].astype(f32) + in_a2[1, half].astype(f32)
    ring[10].wait_recv()
    own[...] = own[...] + in_x[...].astype(f32)
    ring[11].start()
    units.wait_recv()

    @pl.loop(0, low.shape[1] // 32)
    def _(r):
        rows = pl.ds(pl.multiple_of(r * 32, 32), 32)
        up_ref[rows, :] = low[0, rows, :].astype(f32) + low_came[0, rows, :].astype(f32)
        down_ref[rows, :] = low[1, rows, :].astype(f32) + low_came[1, rows, :].astype(f32)

    ring[11].wait_recv()
    total = own[...] + in_own[...]
    cut = in_ref.shape[1]
    wide = cut + out_ref.shape[1]
    in_ref[...] = total[:, :cut]
    out_ref[...] = total[:, cut:wide]
    gain_ref[...] = total[:, wide:]
    units.wait_send()
    kv_away.wait_send()
    for copy in ring:
        copy.wait_send()
    for s in order:

        @pl.loop(0, RING)
        def _(j):
            on_chip(s, j, flip)[2].wait_send()


def reduce_grads(mine, sent, low, cut, kv, weights, for_inputs):
    width = mine.shape[1]
    share = mine.shape[0] // (2 * RING * RING)
    shape = (RING, RING, 2, share, width)
    two = RING // 2
    pair = (2, share, width)
    vmem = pl.BlockSpec(memory_space=pltpu.VMEM)
    away = pl.BlockSpec(memory_space=pl.ANY)
    tokens, kv_width = (kv.shape[0] // 2, kv.shape[1])
    return pl.pallas_call(
        reduce_body,
        in_specs=[away, away, vmem, vmem, away, vmem, vmem, vmem, vmem],
        out_specs=[vmem] * 6,
        out_shape=[
            jax.ShapeDtypeStruct((share, cut), f32),
            jax.ShapeDtypeStruct((share, width - cut - 128), f32),
            jax.ShapeDtypeStruct((share, 128), f32),
            jax.ShapeDtypeStruct(low.shape[1:], f32),
            jax.ShapeDtypeStruct(low.shape[1:], f32),
            jax.ShapeDtypeStruct((tokens, kv_width), bf16),
        ],
        scratch_shapes=[
            pltpu.VMEM(shape, bf16),
            pltpu.VMEM(shape, f32),
            pltpu.VMEM(shape, bf16),
            pltpu.VMEM((2, two) + pair, bf16),
            pltpu.VMEM((2, RING) + pair, bf16),
            pltpu.VMEM((RING,) + pair, bf16),
            pltpu.VMEM(pair, bf16),
            pltpu.VMEM((2,) + pair, bf16),
            pltpu.VMEM((share, width), bf16),
            pltpu.VMEM((share, width), bf16),
            pltpu.VMEM((share, width), f32),
            pltpu.VMEM((share, width), f32),
            pltpu.VMEM(low.shape, bf16),
            pltpu.VMEM(shape, f32),
            pltpu.VMEM((tokens, kv_width), bf16),
            pltpu.VMEM((weights.shape[0], kv_width), bf16),
            pltpu.SemaphoreType.DMA((2,)),
            pltpu.SemaphoreType.DMA((RING, RING)),
            pltpu.SemaphoreType.DMA((RING, RING)),
            pltpu.SemaphoreType.DMA((14,)),
            pltpu.SemaphoreType.DMA((14,)),
        ],
        compiler_params=pltpu.CompilerParams(collective_id=2, has_side_effects=True),
        cost_estimate=pl.CostEstimate(
            flops=mine.size * 8, bytes_accessed=mine.size * 60, transcendentals=0
        ),
        name="reduce_grads",
    )(mine.reshape(shape), sent.reshape(shape), low, kv, weights, *for_inputs)


def rotated(block, cosine, sine, first_half):
    partner = jnp.where(first_half, pltpu.roll(block, 96, 1), pltpu.roll(block, 32, 1))
    return block * cosine + partner * sine


def block_backward_body(
    placed_ref,
    back_ref,
    residual_ref,
    gain_ref,
    cotangent_ref,
    weights_hbm,
    query_ref,
    keys_ref,
    values_ref,
    allowed_ref,
    attended_ref,
    log_ref,
    cosine_ref,
    sine_ref,
    own_ref,
    other_ref,
    residual_out,
    low_out,
    query_out,
    kv_out,
    from_out,
    gains_out,
    weights,
    sems,
):
    tokens, width = residual_ref.shape
    kv_width = keys_ref.shape[1]
    in_width = width + 2 * kv_width
    out_part = pltpu.make_async_copy(
        weights_hbm.at[:, in_width : in_width + width],
        weights.at[:, in_width : in_width + width],
        sems.at[0],
    )
    in_part = pltpu.make_async_copy(
        weights_hbm.at[:, :in_width], weights.at[:, :in_width], sems.at[1]
    )
    out_part.start()
    in_part.start()
    residual = residual_ref[...]
    inverse = lax.rsqrt(jnp.mean(residual * residual, axis=-1, keepdims=True) + EPSILON)
    upstream = dot(placed_ref[...], back_ref[...], TN)
    gain_two = jnp.sum(upstream * residual * inverse, axis=0, keepdims=True)
    scaled = upstream * gain_ref[...]
    coupling = jnp.mean(scaled * residual, axis=-1, keepdims=True)
    grad = inverse * scaled - residual * inverse * inverse * inverse * coupling
    grad = cotangent_ref[...].astype(f32) + grad
    residual_out[...] = grad
    low = grad.astype(bf16)
    low_out[...] = low
    out_part.wait()
    grad_mixed = dot(low, weights[:, in_width : in_width + width], NT).astype(bf16)

    lane = lax.broadcasted_iota(jnp.int32, (1, 128), 1)
    low_lanes = lane < HEAD_DIM
    first_half = lane % HEAD_DIM < HEAD_DIM // 2
    allowed = allowed_ref[...] != 0
    cosine, sine = (cosine_ref[...], sine_ref[...])
    scale = HEAD_DIM ** (-0.5)

    def doubled(block, place):
        wide = block.astype(f32)
        turned = pltpu.roll(wide, HEAD_DIM, 1)
        pair = (wide, turned) if place == 0 else (turned, wide)
        return jnp.where(low_lanes, pair[0], pair[1]).astype(bf16)

    for m in range(KV_HEADS // 2):
        kv_lanes = slice(m * 128, (m + 1) * 128)
        key_parts, value_parts = ([], [])
        for place in range(2):
            j = 2 * m + place
            lanes = slice(j * 128, (j + 1) * 128)
            keys = doubled(keys_ref[:, kv_lanes], place)
            values = doubled(values_ref[:, kv_lanes], place)
            grad_block = grad_mixed[:, lanes].astype(f32)
            product = grad_block * attended_ref[:, lanes].astype(f32)
            query_block = query_ref[:, lanes].astype(f32)
            grad_query = []
            grad_keys, grad_values = (None, None)
            for part in range(2):
                mine = low_lanes if part == 0 else jnp.logical_not(low_lanes)
                query = jnp.where(mine, query_block, 0.0).astype(bf16)
                upper = jnp.where(mine, grad_block, 0.0).astype(bf16)
                scores = jnp.where(allowed, dot(query, keys, NT) * scale, -1e30)
                exact = jnp.exp(scores - log_ref[:, 2 * j + part : 2 * j + part + 1])
                delta = jnp.sum(jnp.where(mine, product, 0.0), axis=-1, keepdims=True)
                grad_scores = (exact * (dot(upper, values, NT) - delta)).astype(bf16)
                grad_query.append(dot(grad_scores, keys))
                to_keys = dot(grad_scores, query, TN)
                to_values = dot(exact.astype(bf16), upper, TN)
                grad_keys = to_keys if part == 0 else grad_keys + to_keys
                grad_values = to_values if part == 0 else grad_values + to_values
            both = jnp.where(low_lanes, grad_query[0], grad_query[1]) * scale
            both = rotated(both, cosine[:tokens], sine[:tokens], first_half)
            query_out[:, lanes] = both.astype(bf16)
            key_parts.append(grad_keys + pltpu.roll(grad_keys, HEAD_DIM, 1))
            value_parts.append(grad_values + pltpu.roll(grad_values, HEAD_DIM, 1))
        grad_keys = jnp.where(low_lanes, key_parts[0], key_parts[1]) * scale
        kv_out[:, kv_lanes] = rotated(grad_keys, cosine, sine, first_half).astype(bf16)
        value_lanes = slice(kv_width + m * 128, kv_width + (m + 1) * 128)
        kv_out[:, value_lanes] = jnp.where(low_lanes, value_parts[0], value_parts[1]).astype(bf16)

    in_part.wait()
    from_kv = dot(kv_out[...], weights[:, width:in_width], NT)
    from_own = dot(query_out[...], weights[:, :width], NT) + from_kv[:tokens]
    from_out[...] = from_own
    gain = jnp.sum(from_own * own_ref[...], axis=0, keepdims=True)
    gain += jnp.sum(from_kv[tokens:] * other_ref[...], axis=0, keepdims=True)
    gains = jnp.concatenate([gain, gain_two], axis=0)
    one = gains.astype(bf16).astype(f32)
    two = (gains - one).astype(bf16).astype(f32)
    three = gains - one - two
    parts = jnp.concatenate([one, two, three, jnp.zeros_like(gains)], axis=0)
    gains_out[...] = parts.astype(bf16)


def block_backward(
    placed, back, residual, gain, cotangent, weights, heads, masks, tables, scaled_inputs
):
    tokens, width = residual.shape
    query, keys, values = heads
    vmem = pl.BlockSpec(memory_space=pltpu.VMEM)
    return pl.pallas_call(
        block_backward_body,
        in_specs=[vmem] * 5 + [pl.BlockSpec(memory_space=pl.ANY)] + [vmem] * 10,
        out_specs=[vmem] * 6,
        out_shape=[
            jax.ShapeDtypeStruct((tokens, width), f32),
            jax.ShapeDtypeStruct((tokens, width), bf16),
            jax.ShapeDtypeStruct((tokens, width), bf16),
            jax.ShapeDtypeStruct((2 * tokens, 2 * keys.shape[1]), bf16),
            jax.ShapeDtypeStruct((tokens, width), f32),
            jax.ShapeDtypeStruct((8, width), bf16),
        ],
        scratch_shapes=[pltpu.VMEM(weights.shape, bf16), pltpu.SemaphoreType.DMA((2,))],
        cost_estimate=pl.CostEstimate(
            flops=3_000_000_000, bytes_accessed=12_000_000, transcendentals=600_000
        ),
        name="block_backward",
    )(
        placed,
        back,
        residual,
        gain,
        cotangent,
        weights,
        query,
        keys,
        values,
        *masks,
        *tables,
        *scaled_inputs,
    )


def spread_plan(route_ids, mix_weights):
    token_count = route_ids.shape[0]
    expert_ids = jnp.arange(EXPERTS)[None, None, :]
    named = route_ids[:, :, None] == expert_ids
    picked = jnp.any(named, axis=1)
    token_weight = jnp.sum(jnp.where(named, mix_weights[:, :, None], 0.0), axis=1)
    earlier = jnp.arange(token_count)[None, :] < jnp.arange(token_count)[:, None]
    rank = dot(earlier.astype(bf16), picked.astype(bf16)).astype(jnp.int32)
    at_slot = jnp.where(picked, rank, -1).T[:, None, :] == jnp.arange(SLOTS)[None, :, None]
    placed = at_slot.astype(bf16).reshape(EXPERTS * SLOTS, token_count)
    weighted = jnp.where(at_slot, token_weight.T[:, None, :], 0.0)
    slot_weight = jnp.sum(weighted, axis=2).reshape(EXPERTS * SLOTS, 1)
    mixers = [part.reshape(EXPERTS * SLOTS, token_count) for part in three_parts(weighted)]
    return (placed, slot_weight, mixers)


def exchange(rows):
    width = rows.shape[-1]
    blocks = rows.reshape(EXPERTS, -1, width)
    groups = [[(g ^ (c % 2)) * EXPERTS + c for c in range(EXPERTS)] for g in range(2)]
    landed = lax.all_to_all(
        blocks,
        ("seq", "chip"),
        split_axis=0,
        concat_axis=0,
        axis_index_groups=groups,
        tiled=True,
    )
    return landed.reshape(-1, width)


def on_device(
    inputs,
    project_in,
    project_out,
    gain_attend,
    gain_expert,
    expert_gate,
    expert_up,
    expert_down,
    routes,
    route_weights,
    segments,
    cotangent,
):
    token_count = inputs.shape[1]
    model_width = inputs.shape[2]
    query_width = HEADS * HEAD_DIM
    kv_width = KV_HEADS * HEAD_DIM
    group = HEADS // KV_HEADS
    seq = lax.axis_index("seq")
    core = lax.axis_index("core")
    own_low = inputs[0]
    other_low = lax.ppermute(own_low, "seq", SWAP)

    placed, slot_weight, mixers = spread_plan(routes[0], route_weights[0])
    grad_rows = (dot(placed, cotangent[0]) * slot_weight).astype(bf16)

    own_units = jnp.concatenate([expert_gate, expert_up, expert_down], axis=0)
    other_units = lax.ppermute(own_units, "core", SWAP)
    pre_w = jnp.concatenate([own_units[: 2 * BLOCK], other_units[: 2 * BLOCK]], axis=0)
    down_w = jnp.concatenate([expert_down, other_units[2 * BLOCK :]], axis=0)

    share = gain_attend.shape[0]
    wide = query_width + 2 * kv_width + query_width
    gain_rows = jnp.stack([gain_attend, gain_expert], axis=0)
    gain_rows = jnp.pad(gain_rows, ((0, share - 2), (0, 128 - share)))
    gathered = gather_weights(project_in, project_out, gain_rows)
    gathered, grad_rows = lax.optimization_barrier((gathered, grad_rows))
    grad_arrived = exchange(grad_rows)
    in_full = gathered[:, : query_width + 2 * kv_width]
    out_full = gathered[:, query_width + 2 * kv_width : wide]
    gain_rows = gathered[:, wide : wide + share].reshape(-1, share, share)
    gain_one, gain_two = (gain_rows[:, 0].reshape(-1), gain_rows[:, 1].reshape(-1))

    row_values = own_low.astype(f32)
    normed_one, inverse_one = norm_forward(row_values, gain_one)
    normed_other, inverse_other = norm_forward(other_low.astype(f32), gain_one)
    kv_w = in_full[:, query_width:]
    projected = dot(normed_one, in_full)
    projected_other = dot(normed_other, kv_w)
    own_at = seq * token_count + jnp.arange(token_count)
    other_at = (1 - seq) * token_count + jnp.arange(token_count)
    own_cos, own_sin = rope_tables(own_at)
    other_cos, other_sin = rope_tables(other_at)
    query = rotate_wide(projected[:, :query_width], own_cos, own_sin, 1.0).astype(bf16)
    key_cut = query_width + kv_width
    own_keys = rotate_wide(projected[:, query_width:key_cut], own_cos, own_sin, 1.0)
    other_keys = rotate_wide(projected_other[:, :kv_width], other_cos, other_sin, 1.0)
    keys = jnp.concatenate([own_keys, other_keys], axis=0).astype(bf16)
    values = jnp.concatenate([projected[:, key_cut:], projected_other[:, kv_width:]], axis=0)
    flat_heads = (query, keys, values.astype(bf16))
    query = query.reshape(token_count, KV_HEADS, group, HEAD_DIM)
    keys = keys.reshape(2 * token_count, KV_HEADS, HEAD_DIM)
    values = values.astype(bf16).reshape(2 * token_count, KV_HEADS, HEAD_DIM)
    seq_ids = segments[0]
    own_ids = lax.dynamic_slice(seq_ids, (seq * token_count,), (token_count,))
    other_ids = lax.dynamic_slice(seq_ids, ((1 - seq) * token_count,), (token_count,))
    key_at = jnp.concatenate([own_at, other_at])
    key_ids = jnp.concatenate([own_ids, other_ids])
    allowed = (key_at[None, :] <= own_at[:, None]) & (key_ids[None, :] == own_ids[:, None])
    attended, log_total = attend_forward(query, keys, values, allowed)
    mixed = attended.reshape(token_count, query_width)
    residual = row_values + dot(mixed, out_full)
    normed_two, _ = norm_forward(residual, gain_two)

    rows = dot(placed, normed_two).astype(bf16)
    rows, grad_arrived = lax.optimization_barrier((rows, grad_arrived))
    arrived = exchange(rows)

    log_rows = log_total.reshape(HEADS, token_count).T
    cosine, sine = wide_tables(key_at)
    feature = jnp.arange(model_width)[:, None]
    slot = jnp.arange(model_width)[None, :]
    half_width = model_width // 2
    of_core = jnp.where(slot < half_width, core, 1 - core)
    at = slot % half_width
    chosen_half = feature == (2 * (at // share) + of_core) * share + at % share
    chosen_half = chosen_half.astype(bf16)
    features = jnp.concatenate([normed_one, normed_other, mixed], axis=0)
    features = dot(features, chosen_half).astype(bf16)
    ready = (
        features[:, :half_width],
        features[:, half_width:],
        chosen_half,
        flat_heads,
        (allowed.astype(jnp.int32), mixed, log_rows),
        (cosine, sine),
        (row_values * inverse_one, other_low.astype(f32) * inverse_other),
        jnp.concatenate(mixers, axis=1),
    )
    arrived, ready = lax.optimization_barrier((arrived, ready))
    features_mine, features_sent, chosen_half, flat_heads, masks, tables, scaled_inputs, mix = ready

    hidden, grads, back = experts_first(arrived, grad_arrived, pre_w, down_w)
    grad_back = exchange(back)
    out_rows, gate_total, rest_low = experts_second(arrived, grad_arrived, hidden, grads, down_w)
    grad_back, out_rows = lax.optimization_barrier((grad_back, out_rows))
    returned = exchange(out_rows)

    grad_residual, grad_res_low, grad_query, grad_kv, from_own, gain_parts = block_backward(
        placed,
        grad_back,
        residual,
        gain_two.astype(f32)[None, :],
        cotangent[0],
        gathered,
        flat_heads,
        masks,
        tables,
        scaled_inputs,
    )

    grads_mine, grads_sent = projection_grads(
        features_mine, features_sent, grad_query, grad_kv, grad_res_low, gain_parts, chosen_half
    )
    in_width = query_width + 2 * kv_width
    in_total, out_total, gain_total, up_total, down_total, grad_inputs = reduce_grads(
        grads_mine,
        grads_sent,
        rest_low,
        in_width,
        grad_kv,
        gathered,
        (from_own, grad_residual, own_low, gain_one.astype(f32)[None, :]),
    )
    gain_total = gain_total[:, :2] + gain_total[:, 2:4] + gain_total[:, 4:6]

    chosen = dot(mix, returned, TN).reshape(3, token_count, model_width)
    output = (residual + (chosen[2] + chosen[1] + chosen[0])).astype(bf16)
    return (
        output.reshape(1, token_count, model_width),
        grad_inputs.reshape(1, token_count, model_width),
        in_total,
        out_total,
        gain_total[:, 0],
        gain_total[:, 1],
        gate_total,
        up_total,
        down_total,
    )


def solution(mesh):
    devices = mesh.devices
    cores = Mesh(devices.reshape(devices.shape[0], -1, 2), ("seq", "chip", "core"))
    every = ("chip", "core")
    by_token = P(every, "seq", None)
    by_row = P(every, None)
    in_specs = (
        by_token,
        by_row,
        by_row,
        P(every),
        P(every),
        by_row,
        by_row,
        by_row,
        by_token,
        by_token,
        by_row,
        by_token,
    )
    out_specs = (by_token, by_token, by_row, by_row, P(every), P(every), by_row, by_row, by_row)
    return jax.shard_map(
        on_device, mesh=cores, in_specs=in_specs, out_specs=out_specs, check_vma=False
    )
```

```python
import jax
import jax.numpy as jnp
from jax import lax
from jax.experimental import pallas as pl
from jax.experimental.pallas import tpu as pltpu
from jax.sharding import Mesh, PartitionSpec as P

HEADS = 16
KV_HEADS = 8
HEAD_DIM = 64
EXPERTS = 32
FF = 512
TOP = 8
CAP = 36
SLOTS = 40
BLOCK = 256
ROW_BLOCK = 256

EPSILON = 1e-06
ROPE_BASE = 10000.0

f32 = jnp.float32
bf16 = jnp.bfloat16

RING = 4
MESH_ID = pl.DeviceIdType.MESH
SWAP = [(0, 1), (1, 0)]
NT = (((1,), (1,)), ((), ()))
TN = (((0,), (0,)), ((), ()))


def dot(a, b, dims=(((1,), (0,)), ((), ()))):
    return lax.dot_general(a, b, dims, preferred_element_type=f32)


def rope_tables(positions):
    half_dim = HEAD_DIM // 2
    powers = jnp.arange(half_dim).astype(f32) * (2.0 / HEAD_DIM)
    inverse_freq = ROPE_BASE ** (-powers)
    angles = positions.astype(f32)[:, None] * inverse_freq[None, :]
    return (jnp.cos(angles), jnp.sin(angles))


def wide_tables(positions):
    place = jnp.arange(128) % HEAD_DIM
    powers = (place % (HEAD_DIM // 2)).astype(f32) * (2.0 / HEAD_DIM)
    angles = positions.astype(f32)[:, None] * (ROPE_BASE ** (-powers))[None, :]
    sine = jnp.sin(angles)
    return (jnp.cos(angles), jnp.where(place < HEAD_DIM // 2, sine, -sine))


def rotate(values, cosine_table, sine_table, turn_sign):
    half_dim = values.shape[-1] // 2
    leading = values[..., :half_dim]
    trailing = values[..., half_dim:]
    cosine_b = cosine_table[:, None, :]
    sine_b = sine_table[:, None, :] * turn_sign
    return jnp.concatenate(
        [leading * cosine_b - trailing * sine_b, trailing * cosine_b + leading * sine_b], axis=-1
    )


def rotate_wide(values, cosine_table, sine_table, turn_sign):
    rows, width = values.shape
    heads = values.reshape(rows, width // HEAD_DIM, HEAD_DIM)
    return rotate(heads, cosine_table, sine_table, turn_sign).reshape(rows, width)


def norm_forward(values, gain_vector):
    inverse = lax.rsqrt(jnp.mean(values * values, axis=-1, keepdims=True) + EPSILON)
    return ((values * inverse * gain_vector.astype(f32)).astype(bf16), inverse)


def rounded(values):
    return lax.reduce_precision(values, exponent_bits=8, mantissa_bits=7)


def three_parts(values):
    first = rounded(values)
    second = rounded(values - first)
    third = values - first - second
    return (first.astype(bf16), second.astype(bf16), third.astype(bf16))


def masked_scores(query, keys, allowed):
    scores = jnp.einsum("qkgd,skd->kgqs", query, keys, preferred_element_type=f32)
    return jnp.where(allowed[None, None], scores * HEAD_DIM ** (-0.5), -1e30)


def attend_forward(query, keys, values, allowed):
    scores = masked_scores(query, keys, allowed)
    highest = jnp.max(scores, axis=-1, keepdims=True)
    log_total = highest + jnp.log(jnp.sum(jnp.exp(scores - highest), axis=-1, keepdims=True))
    weights = jnp.exp(scores - log_total).astype(bf16)
    mixed = jnp.einsum("kgqs,skd->qkgd", weights, values, preferred_element_type=f32)
    return (mixed.astype(bf16), log_total)


def experts_first_body(x_ref, g_ref, pre_w_ref, down_w_ref, hidden_ref, grads_ref, back_ref):
    pre = dot(x_ref[...], pre_w_ref[...], NT)
    grad_hidden = dot(g_ref[...], down_w_ref[...], NT)
    back = None
    for b in range(FF // BLOCK):
        gate = pre[:, 2 * b * BLOCK : (2 * b + 1) * BLOCK]
        up = pre[:, (2 * b + 1) * BLOCK : (2 * b + 2) * BLOCK]
        grad_h = grad_hidden[:, b * BLOCK : (b + 1) * BLOCK]
        sigmoid_gate = 1.0 / (1.0 + jnp.exp(-gate))
        silu = gate * sigmoid_gate
        hidden_ref[:, b * BLOCK : (b + 1) * BLOCK] = (silu * up).astype(bf16)
        grad_gate = (grad_h * up * sigmoid_gate * (1.0 + gate * (1.0 - sigmoid_gate))).astype(bf16)
        grad_up = (grad_h * gate * sigmoid_gate).astype(bf16)
        both = jnp.concatenate([grad_gate, grad_up], axis=1)
        grads_ref[:, 2 * b * BLOCK : (2 * b + 2) * BLOCK] = both
        part = dot(both, pre_w_ref[2 * b * BLOCK : (2 * b + 2) * BLOCK, :]).astype(bf16).astype(f32)
        back = part if back is None else back + part
    back_ref[...] = back.astype(bf16)


def experts_first(arrived, grad_arrived, pre_w, down_w):
    rows, width = arrived.shape
    whole = lambda i: (0, 0)
    by_row = lambda i: (i, 0)
    return pl.pallas_call(
        experts_first_body,
        grid=(rows // ROW_BLOCK,),
        in_specs=[
            pl.BlockSpec((ROW_BLOCK, width), by_row),
            pl.BlockSpec((ROW_BLOCK, width), by_row),
            pl.BlockSpec((2 * FF, width), whole),
            pl.BlockSpec((FF, width), whole),
        ],
        out_specs=[
            pl.BlockSpec((ROW_BLOCK, FF), by_row),
            pl.BlockSpec((ROW_BLOCK, 2 * FF), by_row),
            pl.BlockSpec((ROW_BLOCK, width), by_row),
        ],
        out_shape=[
            jax.ShapeDtypeStruct((rows, FF), bf16),
            jax.ShapeDtypeStruct((rows, 2 * FF), bf16),
            jax.ShapeDtypeStruct((rows, width), bf16),
        ],
        cost_estimate=pl.CostEstimate(
            flops=2 * rows * width * FF * 5,
            bytes_accessed=rows * width * 2 * 5,
            transcendentals=rows * FF,
        ),
        name="experts_first",
    )(arrived, grad_arrived, pre_w, down_w)


def experts_second_body(
    x_ref,
    g_ref,
    hidden_ref,
    grads_ref,
    down_w_ref,
    out_ref,
    gate_ref,
    gate_came_ref,
    rest_ref,
    theirs,
    came,
    last,
    gate,
    low,
    low_came,
    send_sem,
    recv_sem,
):
    seq, chip, core = (lax.axis_index(name) for name in ("seq", "chip", "core"))
    partner = (seq, chip, 1 - core)
    mirror = (1 - seq, chip, core)
    barrier = pltpu.get_barrier_semaphore()
    for other in (partner, mirror):
        pl.semaphore_signal(barrier, inc=1, device_id=other, device_id_type=MESH_ID)
    pl.semaphore_wait(barrier, 2)
    width = x_ref.shape[1]

    def send(i, src, dst, to):
        return pltpu.make_async_remote_copy(
            src_ref=src,
            dst_ref=dst,
            send_sem=send_sem.at[i],
            recv_sem=recv_sem.at[i],
            device_id=to,
            device_id_type=MESH_ID,
        )

    def unit_grads(block, kind, target):
        if kind < 2:
            at = (2 * block + kind) * BLOCK
            left, right = (grads_ref, x_ref)
        else:
            at = block * BLOCK
            left, right = (hidden_ref, g_ref)

        @pl.loop(0, width // BLOCK)
        def _(n):
            columns = pl.ds(pl.multiple_of(n * BLOCK, BLOCK), BLOCK)
            target[:, columns] = dot(left[:, at : at + BLOCK], right[:, columns], TN)

    away = [send(k, theirs.at[k], came.at[k], partner) for k in range(3)]
    across = [send(3 + k, low.at[k], low_came.at[k], mirror) for k in range(1)]
    mine = [gate, last.at[0], last.at[1]]
    lows = [low.at[0], rest_ref.at[0], rest_ref.at[1]]
    for k in range(3):
        unit_grads(1, k, theirs.at[k])
        if k:
            away[k - 1].start()
    unit_grads(0, 0, mine[0])
    away[2].start()

    def join(k):
        away[k].wait_recv()

        @pl.loop(0, BLOCK // 32)
        def _(r):
            rows = pl.ds(pl.multiple_of(r * 32, 32), 32)
            lows[k][rows, :] = (mine[k][rows, :] + came[k, rows, :]).astype(bf16)

    for k in range(3):
        join(k)
        if k < 2:
            unit_grads(0, k + 1, mine[k + 1])
        if k < len(across):
            across[k].start()

    @pl.loop(0, x_ref.shape[0] // ROW_BLOCK)
    def _(r):
        rows = pl.ds(pl.multiple_of(r * ROW_BLOCK, ROW_BLOCK), ROW_BLOCK)
        out = None
        for b in range(FF // BLOCK):
            units = slice(b * BLOCK, (b + 1) * BLOCK)
            part = dot(hidden_ref[rows, units], down_w_ref[units, :]).astype(bf16).astype(f32)
            out = part if out is None else out + part
        out_ref[rows, :] = out.astype(bf16)

    across[0].wait_recv()
    gate_ref[...] = low[0]
    gate_came_ref[...] = low_came[0]
    for copy in away + across:
        copy.wait_send()


def experts_second(arrived, grad_arrived, hidden, grads, down_w):
    rows, width = arrived.shape
    return pl.pallas_call(
        experts_second_body,
        in_specs=[pl.BlockSpec(memory_space=pltpu.VMEM)] * 5,
        out_specs=[pl.BlockSpec(memory_space=pltpu.VMEM)] * 4,
        out_shape=[
            jax.ShapeDtypeStruct((rows, width), bf16),
            jax.ShapeDtypeStruct((BLOCK, width), bf16),
            jax.ShapeDtypeStruct((BLOCK, width), bf16),
            jax.ShapeDtypeStruct((2, BLOCK, width), bf16),
        ],
        scratch_shapes=[
            pltpu.VMEM((3, BLOCK, width), f32),
            pltpu.VMEM((3, BLOCK, width), f32),
            pltpu.VMEM((2, BLOCK, width), f32),
            pltpu.VMEM((BLOCK, width), f32),
            pltpu.VMEM((1, BLOCK, width), bf16),
            pltpu.VMEM((1, BLOCK, width), bf16),
            pltpu.SemaphoreType.DMA((4,)),
            pltpu.SemaphoreType.DMA((4,)),
        ],
        compiler_params=pltpu.CompilerParams(collective_id=1, has_side_effects=True),
        cost_estimate=pl.CostEstimate(
            flops=2 * rows * width * FF * 4,
            bytes_accessed=rows * width * 2 * 20,
            transcendentals=0,
        ),
        name="experts_second",
    )(arrived, grad_arrived, hidden, grads, down_w)


def gather_body(in_ref, project_ref, gains_ref, out_ref, shard_ref, send_sem, recv_sem, local_sem):
    seq, chip, core = (lax.axis_index(name) for name in ("seq", "chip", "core"))
    y, z, half = (chip // (2 * RING), (chip // 2) % RING, chip % 2)

    def device(to_y, to_z, to_half, to_core):
        return (seq, (to_y * RING + to_z) * 2 + to_half, to_core)

    def first(step):
        return device((y + core * step) % RING, (z + (1 - core) * step) % RING, half, core)

    def last(step):
        return device((y + (1 - core) * step) % RING, (z + core * step) % RING, half, core)

    partner = device(y, z, half, 1 - core)
    across = (1 - seq, chip + 1 - 2 * half, core)
    ahead, behind = (1, RING - 1)
    cut = in_ref.shape[1]
    wide = cut + project_ref.shape[1]
    shard_ref[:, :cut] = in_ref[...]
    shard_ref[:, cut:wide] = project_ref[...]
    shard_ref[:, wide:] = gains_ref[...]
    barrier = pltpu.get_barrier_semaphore()
    for other in (partner, across, first(ahead), first(behind), last(ahead), last(behind)):
        pl.semaphore_signal(barrier, inc=1, device_id=other, device_id_type=MESH_ID)
    pl.semaphore_wait(barrier, 6)

    def send(i, src, dst, to):
        return pltpu.make_async_remote_copy(
            src_ref=src,
            dst_ref=dst,
            send_sem=send_sem.at[i],
            recv_sem=recv_sem.at[i],
            device_id=to,
            device_id_type=MESH_ID,
        )

    def pair(c, f, l, part=None):
        cut = slice(None) if part is None else part
        to_y, to_z = (l, f) if c == 0 else (f, l)
        return out_ref.at[(y + to_y) % RING, (z + to_z) % RING, cut, c]

    def run(c):
        sent = []

        def go(i, region, to):
            copy = send(i, region, region, to)
            copy.start()
            sent.append(copy)

        def arrive(i, region):
            send(i, region, region, partner).wait_recv()

        def spread(f):
            go(5 + 2 * f, pair(c, f, 0), last(ahead))
            go(6 + 2 * f, pair(c, f, 0), last(behind))
            go(21 + 5 * f, pair(c, f, 0), partner)

        def relay(f):
            arrive(5 + 2 * f, pair(c, f, behind))
            go(13 + 2 * f, pair(c, f, behind, 0), last(ahead))
            go(22 + 5 * f, pair(c, f, behind), partner)
            arrive(6 + 2 * f, pair(c, f, ahead))
            go(14 + 2 * f, pair(c, f, ahead, 1), last(behind))
            go(23 + 5 * f, pair(c, f, ahead), partner)

        own = out_ref.at[y, z, half, c]
        copy = send(0, shard_ref, own, across)
        copy.start()
        sent.append(copy)
        local = pltpu.make_async_copy(shard_ref, own, local_sem)
        local.start()
        local.wait()
        arrive(0, out_ref.at[y, z, 1 - half, c])
        go(1, pair(c, 0, 0), first(ahead))
        go(2, pair(c, 0, 0), first(behind))
        spread(0)
        arrive(1, pair(c, behind, 0))
        go(3, pair(c, behind, 0, 0), first(ahead))
        spread(behind)
        arrive(2, pair(c, ahead, 0))
        go(4, pair(c, ahead, 0, 1), first(behind))
        spread(ahead)
        relay(0)
        arrive(3, pair(c, 2, 0, 0))
        arrive(4, pair(c, 2, 0, 1))
        spread(2)
        for f in (behind, ahead, 2):
            relay(f)
        for f in (0, behind, ahead, 2):
            for part in range(2):
                arrive(13 + 2 * f + part, pair(c, f, 2, part))
                go(24 + 5 * f + part, pair(c, f, 2, part), partner)
        for f in (0, behind, ahead, 2):
            arrive(21 + 5 * f, pair(1 - c, f, 0))
            arrive(22 + 5 * f, pair(1 - c, f, behind))
            arrive(23 + 5 * f, pair(1 - c, f, ahead))
            for part in range(2):
                arrive(24 + 5 * f + part, pair(1 - c, f, 2, part))
        for copy in sent:
            copy.wait_send()

    for c in (0, 1):
        pl.when(core == c)(lambda c=c: run(c))


def gather_weights(project_in, project_out, gains):
    parts = (project_in, project_out, gains)
    rows, width = (gains.shape[0], sum(part.shape[1] for part in parts))
    out = pl.pallas_call(
        gather_body,
        out_shape=jax.ShapeDtypeStruct((RING, RING, 2, 2, rows, width), bf16),
        in_specs=[pl.BlockSpec(memory_space=pltpu.VMEM)] * 3,
        out_specs=pl.BlockSpec(memory_space=pl.ANY),
        scratch_shapes=[
            pltpu.VMEM((rows, width), bf16),
            pltpu.SemaphoreType.DMA((41,)),
            pltpu.SemaphoreType.DMA((41,)),
            pltpu.SemaphoreType.DMA,
        ],
        compiler_params=pltpu.CompilerParams(collective_id=0, has_side_effects=True),
        cost_estimate=pl.CostEstimate(
            flops=0, bytes_accessed=rows * width * 2 * 4 * RING * RING * 8, transcendentals=0
        ),
        name="gather_weights",
    )(*parts)
    return out.reshape(4 * RING * RING * rows, width)


def projection_grads_body(
    mine_ref,
    sent_ref,
    gq_ref,
    gkv_ref,
    gr_ref,
    gains_ref,
    chosen_mine_ref,
    chosen_sent_ref,
    total_ref,
    away_ref,
):
    query = gq_ref.shape[1]
    width = query + gkv_ref.shape[1]
    wide = width + gr_ref.shape[1]
    spread = lax.broadcasted_iota(jnp.int32, (8, 128), 0)
    lane = lax.broadcasted_iota(jnp.int32, (8, 128), 1)
    apart = ((spread == lane) & (spread < 6)).astype(bf16)
    tokens = gq_ref.shape[0]
    halves = (
        (mine_ref, total_ref, chosen_mine_ref),
        (sent_ref, away_ref, chosen_sent_ref),
    )
    for ref, out_ref, chosen_ref in halves:
        out_ref[:, :query] = dot(ref[:tokens, :], gq_ref[...], TN).astype(out_ref.dtype)
        out_ref[:, query:width] = dot(ref[: 2 * tokens, :], gkv_ref[...], TN).astype(out_ref.dtype)
        out_ref[:, width:wide] = dot(ref[2 * tokens :, :], gr_ref[...], TN).astype(out_ref.dtype)
        picked = dot(gains_ref[...], chosen_ref[...]).astype(bf16)
        out_ref[:, wide:] = dot(picked, apart, TN).astype(out_ref.dtype)


def projection_grads(rows_mine, rows_sent, grad_query, grad_kv, grad_res_low, gains, chosen):
    count = rows_mine.shape[1]
    width = grad_query.shape[1] + grad_kv.shape[1] + grad_res_low.shape[1] + 128
    tile = 256
    whole = lambda i: (0, 0)
    by_column = lambda i: (0, i)
    by_row = lambda i: (i, 0)
    return pl.pallas_call(
        projection_grads_body,
        grid=(count // tile,),
        in_specs=[
            pl.BlockSpec((rows_mine.shape[0], tile), by_column),
            pl.BlockSpec((rows_sent.shape[0], tile), by_column),
            pl.BlockSpec(grad_query.shape, whole),
            pl.BlockSpec(grad_kv.shape, whole),
            pl.BlockSpec(grad_res_low.shape, whole),
            pl.BlockSpec(gains.shape, whole),
            pl.BlockSpec((chosen.shape[0], tile), by_column),
            pl.BlockSpec((chosen.shape[0], tile), lambda i: (0, i + count // tile)),
        ],
        out_specs=[pl.BlockSpec((tile, width), by_row), pl.BlockSpec((tile, width), by_row)],
        out_shape=[
            jax.ShapeDtypeStruct((count, width), f32),
            jax.ShapeDtypeStruct((count, width), bf16),
        ],
        name="projection_grads",
    )(rows_mine, rows_sent, grad_query, grad_kv, grad_res_low, gains, chosen, chosen)


def packed(values):
    lane = lax.broadcasted_iota(jnp.int32, (values.shape[0], 128), 1)
    wide = values.shape[1] - 128
    parts = values[:, wide:]
    total = parts + pltpu.roll(parts, 126, 1) + pltpu.roll(parts, 124, 1)
    total = jnp.where(lane < 2, total, 0.0)
    one = total.astype(bf16).astype(f32)
    two = (total - one).astype(bf16).astype(f32)
    three = total - one - two
    tail = one + pltpu.roll(two, 2, 1) + pltpu.roll(three, 4, 1)
    return jnp.concatenate([values[:, :wide].astype(bf16), tail.astype(bf16)], axis=1)


def reduce_body(
    mine_hbm,
    sent,
    low,
    kv_ref,
    weights_hbm,
    from_ref,
    residual_ref,
    inputs_ref,
    gain_one_ref,
    in_ref,
    out_ref,
    gain_ref,
    up_ref,
    down_ref,
    inputs_out,
    came,
    acc,
    stage,
    in1,
    in2,
    stage_a,
    in_a1,
    in_a2,
    stage_x,
    in_x,
    own,
    in_own,
    low_came,
    mine,
    kv_came,
    kv_weights,
    fetch_sems,
    chip_send,
    chip_recv,
    ring_send,
    ring_recv,
):
    seq, chip, core = (lax.axis_index(name) for name in ("seq", "chip", "core"))
    y, z, half = (chip // (2 * RING), (chip // 2) % RING, chip % 2)
    flip = 1 - core
    at_last = flip * y + core * z
    at_first = flip * z + core * y

    def device(to_y, to_z, to_half, to_core):
        return (seq, (to_y * RING + to_z) * 2 + to_half, to_core)

    def first(step):
        return device((y + core * step) % RING, (z + flip * step) % RING, half, core)

    def last(step):
        return device((y + flip * step) % RING, (z + core * step) % RING, half, core)

    partner = device(y, z, half, flip)
    across = (1 - seq, chip + 1 - 2 * half, core)
    mirror = (1 - seq, chip, core)
    ahead, behind = (1, RING - 1)
    fetch = pltpu.make_async_copy(mine_hbm, mine, fetch_sems.at[0])
    fetch.start()
    tokens, width = from_ref.shape
    fetch_weights = pltpu.make_async_copy(
        weights_hbm.at[:, width : 2 * width], kv_weights, fetch_sems.at[1]
    )
    fetch_weights.start()
    barrier = pltpu.get_barrier_semaphore()
    others = (partner, across, mirror, first(ahead), first(behind), last(ahead), last(behind))
    for other in others:
        pl.semaphore_signal(barrier, inc=1, device_id=other, device_id_type=MESH_ID)
    pl.semaphore_wait(barrier, len(others))

    def send(i, src, dst, to):
        return pltpu.make_async_remote_copy(
            src_ref=src,
            dst_ref=dst,
            send_sem=ring_send.at[i],
            recv_sem=ring_recv.at[i],
            device_id=to,
            device_id_type=MESH_ID,
        )

    def on_chip(s, j, of_core):
        line = ((1 - of_core) * y + of_core * z + s) % RING
        a = (1 - of_core) * line + of_core * j
        b = (1 - of_core) * j + of_core * line
        return (
            a,
            b,
            pltpu.make_async_remote_copy(
                src_ref=sent.at[a, b],
                dst_ref=came.at[a, b],
                send_sem=chip_send.at[s, j],
                recv_sem=chip_recv.at[s, j],
                device_id=partner,
                device_id_type=MESH_ID,
            ),
        )

    order = (2, ahead, behind, 0)
    two = RING // 2
    kv_away = send(13, kv_ref.at[pl.ds(tokens, tokens)], kv_came, mirror)
    kv_away.start()
    units = send(12, low, low_came, mirror)
    units.start()
    for s in order:

        @pl.loop(0, RING)
        def _(j):
            on_chip(s, j, flip)[2].start()

    ring = [
        send(0, stage.at[2, :two], in1.at[0], last(ahead)),
        send(1, stage.at[2, two:], in1.at[1], last(behind)),
        send(2, stage.at[1, two:], in2.at[0, two:], last(ahead)),
        send(3, stage.at[1, :two], in2.at[0, :two], last(ahead)),
        send(4, stage.at[3, :two], in2.at[1, :two], last(behind)),
        send(5, stage.at[3, two:], in2.at[1, two:], last(behind)),
        send(6, stage_a.at[2, 0], in_a1.at[0], first(ahead)),
        send(7, stage_a.at[2, 1], in_a1.at[1], first(behind)),
        send(8, stage_a.at[1], in_a2.at[0], first(ahead)),
        send(9, stage_a.at[3], in_a2.at[1], first(behind)),
        send(10, stage_x, in_x, across),
        send(11, own, in_own, mirror),
    ]

    def merge(s, low_j, high_j, to_stage):
        @pl.loop(low_j, high_j)
        def _(j):
            a, b, copy = on_chip(s, j, core)
            copy.wait_recv()
            for h in range(2):
                value = mine[a, b, h] + came[a, b, h].astype(f32)
                if to_stage:
                    stage[s, j, h] = packed(value)
                if not to_stage or s != 2:
                    acc[s, j, h] = value

    fetch.wait()
    merge(2, 0, RING, True)
    ring[0].start()
    ring[1].start()
    merge(ahead, 0, RING, True)
    ring[2].start()
    merge(behind, 0, RING, True)
    ring[4].start()
    merge(0, 0, RING, False)
    for i, s, source, first_j in ((0, ahead, 0, 0), (1, behind, 1, two)):
        ring[i].wait_recv()

        @pl.loop(0, two)
        def _(k):
            for h in range(2):
                value = acc[s, first_j + k, h] + in1[source, k, h].astype(f32)
                stage[s, first_j + k, h] = packed(value)

        ring[3 if i == 0 else 5].start()

    kv_away.wait_recv()
    fetch_weights.wait()
    values = inputs_ref[...].astype(f32)
    inverse = lax.rsqrt(jnp.mean(values * values, axis=-1, keepdims=True) + EPSILON)
    upstream = from_ref[...] + dot(kv_came[...], kv_weights[...], NT)
    scaled = upstream * gain_one_ref[...]
    coupling = jnp.mean(scaled * values, axis=-1, keepdims=True)
    grad = inverse * scaled - values * inverse * inverse * inverse * coupling
    inputs_out[...] = (residual_ref[...] + grad).astype(bf16)

    for i, source, first_j in ((2, 0, two), (4, 1, 0), (3, 0, 0), (5, 1, two)):
        ring[i].wait_recv()

        @pl.loop(first_j, first_j + two)
        def _(j):
            for h in range(2):
                acc[0, j, h] = acc[0, j, h] + in2[source, j, h].astype(f32)

    def at(step):
        return (at_first + step) % RING

    for h in range(2):
        stage_a[2, h] = packed(acc[0, at(2), h])
    ring[6].start()
    ring[7].start()
    stage_a[1, 1] = packed(acc[0, at(ahead), 1])
    stage_a[3, 0] = packed(acc[0, at(behind), 0])
    ring[6].wait_recv()
    stage_a[1, 0] = packed(acc[0, at(ahead), 0] + in_a1[0].astype(f32))
    ring[8].start()
    ring[7].wait_recv()
    stage_a[3, 1] = packed(acc[0, at(behind), 1] + in_a1[1].astype(f32))
    ring[9].start()
    ring[8].wait_recv()
    ring[9].wait_recv()
    away = 1 - half
    stage_x[...] = packed(
        acc[0, at_first, away] + in_a2[0, away].astype(f32) + in_a2[1, away].astype(f32)
    )
    ring[10].start()
    own[...] = acc[0, at_first, half] + in_a2[0, half].astype(f32) + in_a2[1, half].astype(f32)
    ring[10].wait_recv()
    own[...] = own[...] + in_x[...].astype(f32)
    ring[11].start()
    units.wait_recv()

    @pl.loop(0, low.shape[1] // 32)
    def _(r):
        rows = pl.ds(pl.multiple_of(r * 32, 32), 32)
        up_ref[rows, :] = low[0, rows, :].astype(f32) + low_came[0, rows, :].astype(f32)
        down_ref[rows, :] = low[1, rows, :].astype(f32) + low_came[1, rows, :].astype(f32)

    ring[11].wait_recv()
    total = own[...] + in_own[...]
    cut = in_ref.shape[1]
    wide = cut + out_ref.shape[1]
    in_ref[...] = total[:, :cut]
    out_ref[...] = total[:, cut:wide]
    tail = total[:, wide:]
    gain_ref[...] = tail + pltpu.roll(tail, 126, 1) + pltpu.roll(tail, 124, 1)
    units.wait_send()
    kv_away.wait_send()
    for copy in ring:
        copy.wait_send()
    for s in order:

        @pl.loop(0, RING)
        def _(j):
            on_chip(s, j, flip)[2].wait_send()


def reduce_grads(mine, sent, low, cut, kv, weights, for_inputs):
    width = mine.shape[1]
    share = mine.shape[0] // (2 * RING * RING)
    shape = (RING, RING, 2, share, width)
    two = RING // 2
    pair = (2, share, width)
    vmem = pl.BlockSpec(memory_space=pltpu.VMEM)
    away = pl.BlockSpec(memory_space=pl.ANY)
    tokens, kv_width = (kv.shape[0] // 2, kv.shape[1])
    return pl.pallas_call(
        reduce_body,
        in_specs=[away, away, vmem, vmem, away, vmem, vmem, vmem, vmem],
        out_specs=[vmem] * 6,
        out_shape=[
            jax.ShapeDtypeStruct((share, cut), f32),
            jax.ShapeDtypeStruct((share, width - cut - 128), f32),
            jax.ShapeDtypeStruct((share, 128), f32),
            jax.ShapeDtypeStruct(low.shape[1:], f32),
            jax.ShapeDtypeStruct(low.shape[1:], f32),
            jax.ShapeDtypeStruct((tokens, kv_width), bf16),
        ],
        scratch_shapes=[
            pltpu.VMEM(shape, bf16),
            pltpu.VMEM(shape, f32),
            pltpu.VMEM(shape, bf16),
            pltpu.VMEM((2, two) + pair, bf16),
            pltpu.VMEM((2, RING) + pair, bf16),
            pltpu.VMEM((RING,) + pair, bf16),
            pltpu.VMEM(pair, bf16),
            pltpu.VMEM((2,) + pair, bf16),
            pltpu.VMEM((share, width), bf16),
            pltpu.VMEM((share, width), bf16),
            pltpu.VMEM((share, width), f32),
            pltpu.VMEM((share, width), f32),
            pltpu.VMEM(low.shape, bf16),
            pltpu.VMEM(shape, f32),
            pltpu.VMEM((tokens, kv_width), bf16),
            pltpu.VMEM((weights.shape[0], kv_width), bf16),
            pltpu.SemaphoreType.DMA((2,)),
            pltpu.SemaphoreType.DMA((RING, RING)),
            pltpu.SemaphoreType.DMA((RING, RING)),
            pltpu.SemaphoreType.DMA((14,)),
            pltpu.SemaphoreType.DMA((14,)),
        ],
        compiler_params=pltpu.CompilerParams(collective_id=2, has_side_effects=True),
        cost_estimate=pl.CostEstimate(
            flops=mine.size * 8, bytes_accessed=mine.size * 60, transcendentals=0
        ),
        name="reduce_grads",
    )(mine.reshape(shape), sent.reshape(shape), low, kv, weights, *for_inputs)


def rotated(block, cosine, sine, first_half):
    partner = jnp.where(first_half, pltpu.roll(block, 96, 1), pltpu.roll(block, 32, 1))
    return block * cosine + partner * sine


def block_backward_body(
    placed_ref,
    back_ref,
    residual_ref,
    gain_ref,
    cotangent_ref,
    weights_hbm,
    query_ref,
    keys_ref,
    values_ref,
    allowed_ref,
    attended_ref,
    log_ref,
    cosine_ref,
    sine_ref,
    own_ref,
    other_ref,
    residual_out,
    low_out,
    query_out,
    kv_out,
    from_out,
    gains_out,
    weights,
    sems,
):
    tokens, width = residual_ref.shape
    kv_width = keys_ref.shape[1]
    in_width = width + 2 * kv_width
    out_part = pltpu.make_async_copy(
        weights_hbm.at[:, in_width : in_width + width],
        weights.at[:, in_width : in_width + width],
        sems.at[0],
    )
    in_part = pltpu.make_async_copy(
        weights_hbm.at[:, :in_width], weights.at[:, :in_width], sems.at[1]
    )
    out_part.start()
    in_part.start()
    residual = residual_ref[...]
    inverse = lax.rsqrt(jnp.mean(residual * residual, axis=-1, keepdims=True) + EPSILON)
    upstream = dot(placed_ref[...], back_ref[...], TN)
    gain_two = jnp.sum(upstream * residual * inverse, axis=0, keepdims=True)
    scaled = upstream * gain_ref[...]
    coupling = jnp.mean(scaled * residual, axis=-1, keepdims=True)
    grad = inverse * scaled - residual * inverse * inverse * inverse * coupling
    grad = cotangent_ref[...].astype(f32) + grad
    residual_out[...] = grad
    low = grad.astype(bf16)
    low_out[...] = low
    out_part.wait()
    grad_mixed = dot(low, weights[:, in_width : in_width + width], NT).astype(bf16)

    lane = lax.broadcasted_iota(jnp.int32, (1, 128), 1)
    low_lanes = lane < HEAD_DIM
    first_half = lane % HEAD_DIM < HEAD_DIM // 2
    allowed = allowed_ref[...] != 0
    cosine, sine = (cosine_ref[...], sine_ref[...])
    scale = HEAD_DIM ** (-0.5)

    def doubled(block, place):
        wide = block.astype(f32)
        turned = pltpu.roll(wide, HEAD_DIM, 1)
        pair = (wide, turned) if place == 0 else (turned, wide)
        return jnp.where(low_lanes, pair[0], pair[1]).astype(bf16)

    for m in range(KV_HEADS // 2):
        kv_lanes = slice(m * 128, (m + 1) * 128)
        key_parts, value_parts = ([], [])
        for place in range(2):
            j = 2 * m + place
            lanes = slice(j * 128, (j + 1) * 128)
            keys = doubled(keys_ref[:, kv_lanes], place)
            values = doubled(values_ref[:, kv_lanes], place)
            grad_block = grad_mixed[:, lanes].astype(f32)
            product = grad_block * attended_ref[:, lanes].astype(f32)
            query_block = query_ref[:, lanes].astype(f32)
            grad_query = []
            grad_keys, grad_values = (None, None)
            for part in range(2):
                mine = low_lanes if part == 0 else jnp.logical_not(low_lanes)
                query = jnp.where(mine, query_block, 0.0).astype(bf16)
                upper = jnp.where(mine, grad_block, 0.0).astype(bf16)
                scores = jnp.where(allowed, dot(query, keys, NT) * scale, -1e30)
                exact = jnp.exp(scores - log_ref[:, 2 * j + part : 2 * j + part + 1])
                delta = jnp.sum(jnp.where(mine, product, 0.0), axis=-1, keepdims=True)
                grad_scores = (exact * (dot(upper, values, NT) - delta)).astype(bf16)
                grad_query.append(dot(grad_scores, keys))
                to_keys = dot(grad_scores, query, TN)
                to_values = dot(exact.astype(bf16), upper, TN)
                grad_keys = to_keys if part == 0 else grad_keys + to_keys
                grad_values = to_values if part == 0 else grad_values + to_values
            both = jnp.where(low_lanes, grad_query[0], grad_query[1]) * scale
            both = rotated(both, cosine[:tokens], sine[:tokens], first_half)
            query_out[:, lanes] = both.astype(bf16)
            key_parts.append(grad_keys + pltpu.roll(grad_keys, HEAD_DIM, 1))
            value_parts.append(grad_values + pltpu.roll(grad_values, HEAD_DIM, 1))
        grad_keys = jnp.where(low_lanes, key_parts[0], key_parts[1]) * scale
        kv_out[:, kv_lanes] = rotated(grad_keys, cosine, sine, first_half).astype(bf16)
        value_lanes = slice(kv_width + m * 128, kv_width + (m + 1) * 128)
        kv_out[:, value_lanes] = jnp.where(low_lanes, value_parts[0], value_parts[1]).astype(bf16)

    in_part.wait()
    from_kv = dot(kv_out[...], weights[:, width:in_width], NT)
    from_own = dot(query_out[...], weights[:, :width], NT) + from_kv[:tokens]
    from_out[...] = from_own
    gain = jnp.sum(from_own * own_ref[...], axis=0, keepdims=True)
    gain += jnp.sum(from_kv[tokens:] * other_ref[...], axis=0, keepdims=True)
    gains = jnp.concatenate([gain, gain_two], axis=0)
    one = gains.astype(bf16).astype(f32)
    two = (gains - one).astype(bf16).astype(f32)
    three = gains - one - two
    parts = jnp.concatenate([one, two, three, jnp.zeros_like(gains)], axis=0)
    gains_out[...] = parts.astype(bf16)


def block_backward(
    placed, back, residual, gain, cotangent, weights, heads, masks, tables, scaled_inputs
):
    tokens, width = residual.shape
    query, keys, values = heads
    vmem = pl.BlockSpec(memory_space=pltpu.VMEM)
    return pl.pallas_call(
        block_backward_body,
        in_specs=[vmem] * 5 + [pl.BlockSpec(memory_space=pl.ANY)] + [vmem] * 10,
        out_specs=[vmem] * 6,
        out_shape=[
            jax.ShapeDtypeStruct((tokens, width), f32),
            jax.ShapeDtypeStruct((tokens, width), bf16),
            jax.ShapeDtypeStruct((tokens, width), bf16),
            jax.ShapeDtypeStruct((2 * tokens, 2 * keys.shape[1]), bf16),
            jax.ShapeDtypeStruct((tokens, width), f32),
            jax.ShapeDtypeStruct((8, width), bf16),
        ],
        scratch_shapes=[pltpu.VMEM(weights.shape, bf16), pltpu.SemaphoreType.DMA((2,))],
        cost_estimate=pl.CostEstimate(
            flops=3_000_000_000, bytes_accessed=12_000_000, transcendentals=600_000
        ),
        name="block_backward",
    )(
        placed,
        back,
        residual,
        gain,
        cotangent,
        weights,
        query,
        keys,
        values,
        *masks,
        *tables,
        *scaled_inputs,
    )


def spread_plan(route_ids, mix_weights):
    token_count = route_ids.shape[0]
    expert_ids = jnp.arange(EXPERTS)[None, None, :]
    named = route_ids[:, :, None] == expert_ids
    picked = jnp.any(named, axis=1)
    token_weight = jnp.sum(jnp.where(named, mix_weights[:, :, None], 0.0), axis=1)
    earlier = jnp.arange(token_count)[None, :] < jnp.arange(token_count)[:, None]
    rank = dot(earlier.astype(bf16), picked.astype(bf16)).astype(jnp.int32)
    at_slot = jnp.where(picked, rank, -1).T[:, None, :] == jnp.arange(SLOTS)[None, :, None]
    placed = at_slot.astype(bf16).reshape(EXPERTS * SLOTS, token_count)
    weighted = jnp.where(at_slot, token_weight.T[:, None, :], 0.0)
    slot_weight = jnp.sum(weighted, axis=2).reshape(EXPERTS * SLOTS, 1)
    mixers = [part.reshape(EXPERTS * SLOTS, token_count) for part in three_parts(weighted)]
    return (placed, slot_weight, mixers)


def exchange(rows):
    width = rows.shape[-1]
    blocks = rows.reshape(EXPERTS, -1, width)
    groups = [[(g ^ (c % 2)) * EXPERTS + c for c in range(EXPERTS)] for g in range(2)]
    landed = lax.all_to_all(
        blocks,
        ("seq", "chip"),
        split_axis=0,
        concat_axis=0,
        axis_index_groups=groups,
        tiled=True,
    )
    return landed.reshape(-1, width)


def on_device(
    inputs,
    project_in,
    project_out,
    gain_attend,
    gain_expert,
    expert_gate,
    expert_up,
    expert_down,
    routes,
    route_weights,
    segments,
    cotangent,
):
    token_count = inputs.shape[1]
    model_width = inputs.shape[2]
    query_width = HEADS * HEAD_DIM
    kv_width = KV_HEADS * HEAD_DIM
    group = HEADS // KV_HEADS
    seq = lax.axis_index("seq")
    core = lax.axis_index("core")
    own_low = inputs[0]
    other_low = lax.ppermute(own_low, "seq", SWAP)

    placed, slot_weight, mixers = spread_plan(routes[0], route_weights[0])
    grad_rows = (dot(placed, cotangent[0]) * slot_weight).astype(bf16)

    own_units = jnp.concatenate([expert_gate, expert_up, expert_down], axis=0)
    other_units = lax.ppermute(own_units, "core", SWAP)
    pre_w = jnp.concatenate([own_units[: 2 * BLOCK], other_units[: 2 * BLOCK]], axis=0)
    down_w = jnp.concatenate([expert_down, other_units[2 * BLOCK :]], axis=0)

    share = gain_attend.shape[0]
    wide = query_width + 2 * kv_width + query_width
    gain_rows = jnp.stack([gain_attend, gain_expert], axis=0)
    gain_rows = jnp.pad(gain_rows, ((0, share - 2), (0, 128 - share)))
    gathered = gather_weights(project_in, project_out, gain_rows)
    gathered, grad_rows = lax.optimization_barrier((gathered, grad_rows))
    grad_arrived = exchange(grad_rows)
    in_full = gathered[:, : query_width + 2 * kv_width]
    out_full = gathered[:, query_width + 2 * kv_width : wide]
    gain_rows = gathered[:, wide : wide + share].reshape(-1, share, share)
    gain_one, gain_two = (gain_rows[:, 0].reshape(-1), gain_rows[:, 1].reshape(-1))

    row_values = own_low.astype(f32)
    normed_one, inverse_one = norm_forward(row_values, gain_one)
    normed_other, inverse_other = norm_forward(other_low.astype(f32), gain_one)
    kv_w = in_full[:, query_width:]
    projected = dot(normed_one, in_full)
    projected_other = dot(normed_other, kv_w)
    own_at = seq * token_count + jnp.arange(token_count)
    other_at = (1 - seq) * token_count + jnp.arange(token_count)
    own_cos, own_sin = rope_tables(own_at)
    other_cos, other_sin = rope_tables(other_at)
    query = rotate_wide(projected[:, :query_width], own_cos, own_sin, 1.0).astype(bf16)
    key_cut = query_width + kv_width
    own_keys = rotate_wide(projected[:, query_width:key_cut], own_cos, own_sin, 1.0)
    other_keys = rotate_wide(projected_other[:, :kv_width], other_cos, other_sin, 1.0)
    keys = jnp.concatenate([own_keys, other_keys], axis=0).astype(bf16)
    values = jnp.concatenate([projected[:, key_cut:], projected_other[:, kv_width:]], axis=0)
    flat_heads = (query, keys, values.astype(bf16))
    query = query.reshape(token_count, KV_HEADS, group, HEAD_DIM)
    keys = keys.reshape(2 * token_count, KV_HEADS, HEAD_DIM)
    values = values.astype(bf16).reshape(2 * token_count, KV_HEADS, HEAD_DIM)
    seq_ids = segments[0]
    own_ids = lax.dynamic_slice(seq_ids, (seq * token_count,), (token_count,))
    other_ids = lax.dynamic_slice(seq_ids, ((1 - seq) * token_count,), (token_count,))
    key_at = jnp.concatenate([own_at, other_at])
    key_ids = jnp.concatenate([own_ids, other_ids])
    allowed = (key_at[None, :] <= own_at[:, None]) & (key_ids[None, :] == own_ids[:, None])
    attended, log_total = attend_forward(query, keys, values, allowed)
    mixed = attended.reshape(token_count, query_width)
    residual = row_values + dot(mixed, out_full)
    normed_two, _ = norm_forward(residual, gain_two)

    rows = dot(placed, normed_two).astype(bf16)
    rows, grad_arrived = lax.optimization_barrier((rows, grad_arrived))
    arrived = exchange(rows)

    log_rows = log_total.reshape(HEADS, token_count).T
    cosine, sine = wide_tables(key_at)
    feature = jnp.arange(model_width)[:, None]
    slot = jnp.arange(model_width)[None, :]
    half_width = model_width // 2
    of_core = jnp.where(slot < half_width, core, 1 - core)
    at = slot % half_width
    chosen_half = feature == (2 * (at // share) + of_core) * share + at % share
    chosen_half = chosen_half.astype(bf16)
    features = jnp.concatenate([normed_one, normed_other, mixed], axis=0)
    features = dot(features, chosen_half).astype(bf16)
    ready = (
        features[:, :half_width],
        features[:, half_width:],
        chosen_half,
        flat_heads,
        (allowed.astype(jnp.int32), mixed, log_rows),
        (cosine, sine),
        (row_values * inverse_one, other_low.astype(f32) * inverse_other),
        jnp.concatenate(mixers, axis=1),
    )
    arrived, ready = lax.optimization_barrier((arrived, ready))
    features_mine, features_sent, chosen_half, flat_heads, masks, tables, scaled_inputs, mix = ready

    hidden, grads, back = experts_first(arrived, grad_arrived, pre_w, down_w)
    grad_back = exchange(back)
    out_rows, gate_own, gate_came, rest_low = experts_second(arrived, grad_arrived, hidden, grads, down_w)
    gate_total = gate_own.astype(f32) + gate_came.astype(f32)
    grad_back, out_rows, gate_total = lax.optimization_barrier((grad_back, out_rows, gate_total))
    returned = exchange(out_rows)

    grad_residual, grad_res_low, grad_query, grad_kv, from_own, gain_parts = block_backward(
        placed,
        grad_back,
        residual,
        gain_two.astype(f32)[None, :],
        cotangent[0],
        gathered,
        flat_heads,
        masks,
        tables,
        scaled_inputs,
    )

    grads_mine, grads_sent = projection_grads(
        features_mine, features_sent, grad_query, grad_kv, grad_res_low, gain_parts, chosen_half
    )
    in_width = query_width + 2 * kv_width
    in_total, out_total, gain_total, up_total, down_total, grad_inputs = reduce_grads(
        grads_mine,
        grads_sent,
        rest_low,
        in_width,
        grad_kv,
        gathered,
        (from_own, grad_residual, own_low, gain_one.astype(f32)[None, :]),
    )

    chosen = dot(mix, returned, TN).reshape(3, token_count, model_width)
    output = (residual + (chosen[2] + chosen[1] + chosen[0])).astype(bf16)
    return (
        output.reshape(1, token_count, model_width),
        grad_inputs.reshape(1, token_count, model_width),
        in_total,
        out_total,
        gain_total[:, 0],
        gain_total[:, 1],
        gate_total,
        up_total,
        down_total,
    )


def solution(mesh):
    devices = mesh.devices
    cores = Mesh(devices.reshape(devices.shape[0], -1, 2), ("seq", "chip", "core"))
    every = ("chip", "core")
    by_token = P(every, "seq", None)
    by_row = P(every, None)
    in_specs = (
        by_token,
        by_row,
        by_row,
        P(every),
        P(every),
        by_row,
        by_row,
        by_row,
        by_token,
        by_token,
        by_row,
        by_token,
    )
    out_specs = (by_token, by_token, by_row, by_row, P(every), P(every), by_row, by_row, by_row)
    return jax.shard_map(
        on_device, mesh=cores, in_specs=in_specs, out_specs=out_specs, check_vma=False
    )
```
